32 devices in a mesh: ctx: 8 (over y, x, core), fsdp: 4 (over z).
Axes of the slice: x: 2, y: 2, z: 4, core: 2. Of those that a mesh axis runs over, the one named last changes fastest.
Arguments:
- tokens: bfloat16 [2, 4, 1024, 1024], P(None, 'fsdp', 'ctx'), may hold values from -6 to 6
- doc_ids: int32 [2, 4, 1024], P(None, 'fsdp'), may hold values from 0 to 3, never falling along the last dimension, each value on 1 to 768 neighbouring positions
- routes: int32 [2, 4, 1024, 1], P(None, 'fsdp', 'ctx'), may hold values from 0 to 1; in each aligned block of 128 rows (0 to 127, 128 to 255, ..., all dimensions but the last counted through in order) at most 80 rows name the same one
- cotangent: bfloat16 [2, 4, 1024, 1024], P(None, 'fsdp', 'ctx'), may hold values from -6 to 6
- ln1_gain: bfloat16 [1024], P('fsdp'), may hold values from 0.5 to 1.5
- ln1_shift: bfloat16 [1024], P('fsdp'), may hold values from -1.5 to 1.5
- w_qkv: bfloat16 [3, 1024, 1024], P(None, 'fsdp'), may hold values from -0.1875 to 0.1875
- qv_bias: bfloat16 [2, 1024], P(None, 'fsdp'), may hold values from -1.5 to 1.5
- w_out: bfloat16 [1024, 1024], P('fsdp'), may hold values from -1.5 to 1.5
- out_bias: bfloat16 [1024], P('fsdp'), may hold values from -1.5 to 1.5
- ln2_gain: bfloat16 [1024], P('fsdp'), may hold values from 0.5 to 1.5
- ln2_shift: bfloat16 [1024], P('fsdp'), may hold values from -1.5 to 1.5
- router: bfloat16 [1024, 2], P('fsdp'), may hold values from -0.09375 to 0.09375
- w_in: bfloat16 [2, 1024, 4096], P(None, 'fsdp'), may hold values from -0.1875 to 0.1875
- in_bias: bfloat16 [2, 4096], P(None, 'fsdp'), may hold values from -1.5 to 1.5
- w_back: bfloat16 [2, 4096, 1024], P(None, 'fsdp'), may hold values from -0.1875 to 0.1875
- back_bias: bfloat16 [2, 1024], P(None, 'fsdp'), may hold values from -1.5 to 1.5
Outputs:
- mixed: bfloat16 [2, 4, 1024, 1024], P(None, 'fsdp', 'ctx')
- token_grad: float32 [2, 4, 1024, 1024], P(None, 'fsdp', 'ctx')
- ln1_gain_grad: float32 [1024], P('fsdp')
- ln1_shift_grad: float32 [1024], P('fsdp')
- w_qkv_grad: float32 [3, 1024, 1024], P(None, 'fsdp')
- qv_bias_grad: float32 [2, 1024], P(None, 'fsdp')
- w_out_grad: float32 [1024, 1024], P('fsdp')
- out_bias_grad: float32 [1024], P('fsdp')
- ln2_gain_grad: float32 [1024], P('fsdp')
- ln2_shift_grad: float32 [1024], P('fsdp')
- router_grad: float32 [1024, 2], P('fsdp')
- w_in_grad: float32 [2, 1024, 4096], P(None, 'fsdp')
- in_bias_grad: float32 [2, 4096], P(None, 'fsdp')
- w_back_grad: float32 [2, 4096, 1024], P(None, 'fsdp')
- back_bias_grad: float32 [2, 1024], P(None, 'fsdp')
The draws below stay inside these ranges and needn't reach their ends.
Inputs may be any that keep to these rules, and one draw needn't show every extreme that they name: `doc_ids`: document numbers never fall along a stream's natural positions; a document has at most 768 positions, and one has exactly 768. `routes`: in the 128 storage rows of one device no expert is named more than 80 times, and some device reaches 80.
All inputs are finite; a program needn't handle non-finite values.
Results may differ from the reference program's by a relative error of at most 0.03.
Values may be sent and summed in bfloat16 or wider, within the bound.
A program may use at most 256 MiB of HBM per device.

```python
import math
import jax
import jax.numpy as jnp
import numpy as np
from jax import lax

D = 1024
HEADS = 16
HEAD_DIM = 64
FF = 4096
EXPERTS = 2
MICRO = 2
DOCS = 4
TOK_DEV = 128
CAP = 80
STREAM = 1024
BATCH = 4
DOC_MOST = 768
N_CTX = 8


def steps_of(own_key, extent, split, low, top_value):
    level = 1.0
    for position, parts in split:
        steps = jax.random.uniform(jax.random.fold_in(jax.random.fold_in(own_key, 6), position), (parts,), jnp.float32, low / len(split), top_value / len(split))
        level = level * jnp.repeat(jnp.exp(steps), extent[position] // parts).reshape((-1,) + (1,) * (len(extent) - 1 - position))
    return level


def profile(number_of, total, bound, lean):
    loads = [(1 << 20) // math.isqrt(rank ** lean) + 1 for rank in range(2, number_of + 1)]
    rest, given = total - bound - (number_of - 1), [1] * (number_of - 1)
    while rest > 0:
        movable = [i for i in range(number_of - 1) if given[i] < bound]
        whole, budget = sum([loads[i] for i in movable]), rest
        for i in movable:
            more = min(bound - given[i], max(1, budget * loads[i] // whole), rest)
            given[i] = given[i] + more
            rest = rest - more
    return np.array([bound] + given)


def uneven(stream_key, count, total, bound, lean):
    if count == 2:
        one = jax.random.randint(stream_key, (), max(1, total - bound), min(bound, total - 1) + 1)
        return jnp.stack([one, total - one])
    lengths = jnp.asarray(profile(count, total, bound, lean), jnp.int32)
    pairs = (count - 1) // 2
    giver, sink = lengths[1:1 + 2 * pairs:2], lengths[2:2 + 2 * pairs:2]
    margin = jnp.minimum(giver - 1, bound - sink)
    shifted = jax.random.randint(jax.random.fold_in(stream_key, 1), (pairs,), 0, 1 << 20) % (margin + 1)
    lengths = lengths.at[1:1 + 2 * pairs:2].set(giver - shifted).at[2:2 + 2 * pairs:2].set(sink + shifted)
    return lengths[jax.random.permutation(jax.random.fold_in(stream_key, 2), count)]


def routed_block(key, own, number, rows, number_of, top, limit, slope):
    sequence = jax.random.permutation(key, number_of)
    heavy_load, ordinary = shares(number_of, rows * top, limit, slope, True), shares(number_of, rows * top, limit, slope, False)
    places = jnp.arange(number_of)

    def named(sizes, turn):
        used = int((sizes > 0).sum())
        fixed = max(1, used // 4)
        passed = fixed + (places - fixed + turn * (used - fixed)) % max(1, number_of - fixed)
        return jnp.zeros((number_of,), jnp.int32).at[sequence[jnp.where(places < fixed, places, passed)]].set(jnp.asarray(sizes, jnp.int32))

    sizes = jnp.where(number % 4 == 0, named(heavy_load, number // 4), named(ordinary, number - number // 4 - 1))
    mixed = jax.random.permutation(jax.random.fold_in(own, 3), number_of)
    giver, sink = mixed[0:number_of // 2 * 2:2], mixed[1:number_of // 2 * 2:2]
    slack = jnp.minimum(sizes[giver] - 1, limit - sizes[sink]) // 2
    slack = jnp.where((giver == sequence[0]) | (sink == sequence[0]) | (sizes[sink] == 0), 0, jnp.maximum(slack, 0))
    passed = jax.random.randint(jax.random.fold_in(own, 4), (number_of // 2,), 0, 1 << 20) % (slack + 1)
    sizes = sizes.at[giver].add(-passed).at[sink].add(passed)
    items = jnp.searchsorted(jnp.cumsum(sizes), jnp.arange(rows * top), side="right").astype(jnp.int32)
    listing = items.reshape(top, rows).T
    listing = listing[jax.random.permutation(jax.random.fold_in(own, 1), rows)]
    turn = jax.random.randint(jax.random.fold_in(own, 2), (rows, 1), 0, top)
    return jnp.take_along_axis(listing, (jnp.arange(top)[None, :] + turn) % top, axis=1)


def shares(amount, total, bound, slope, full):
    portions = [(1 << 20) // math.isqrt(grade ** slope) + 1 for grade in range(1, amount + 1)]
    largest = bound if full else min(bound, max(-(-total // amount), total * portions[0] // sum(portions)))
    least = 1 if total - largest >= amount - 1 else 0
    counts, surplus = [largest] + [least] * (amount - 1), total - largest - least * (amount - 1)
    while surplus > 0:
        movable = [i for i in range(1, amount) if counts[i] < largest] or [i for i in range(1, amount) if counts[i] < bound]
        whole, remaining = sum([portions[i] for i in movable]), surplus
        for i in movable:
            addition = min(bound - counts[i], max(1, remaining * portions[i] // whole), surplus)
            counts[i] = counts[i] + addition
            surplus = surplus - addition
    return np.array(counts)


def gaussian(rng, dims, scale, most, cuts=(), held_as=jnp.bfloat16):
    array = jax.random.normal(rng, dims, jnp.float32) * scale
    if len(cuts) > 0:
        array = steps_of(rng, dims, cuts, -0.22, 0.18) * array
    return jnp.clip(array, min=-most, max=most).astype(held_as)


def setup_inputs(seed: int = 0) -> dict:
    arg_keys = jax.random.split(jax.random.key(seed), 18)
    tokens = gaussian(arg_keys[0], (MICRO, BATCH, STREAM, D), 1.0, 6.0, ((1, 4), (2, 8)))
    doc_ids = jax.vmap(lambda own: jnp.searchsorted(jnp.cumsum(uneven(own, DOCS, STREAM, DOC_MOST, 0)), jnp.arange(STREAM), side="right"))(jax.random.split(arg_keys[1], MICRO * BATCH)).reshape((MICRO, BATCH, STREAM)).astype(jnp.int32)
    routes_keys = jax.random.split(jax.random.fold_in(arg_keys[2], 1), MICRO * BATCH * STREAM // TOK_DEV)
    routes_turns = jax.random.permutation(jax.random.fold_in(arg_keys[2], 3), MICRO * BATCH * STREAM // TOK_DEV)
    routes = jax.vmap(lambda own, number: routed_block(jax.random.fold_in(arg_keys[2], 2), own, number, TOK_DEV, EXPERTS, 1, CAP, 1))(routes_keys, routes_turns).reshape((MICRO, BATCH, STREAM, 1))
    cotangent = gaussian(arg_keys[3], (MICRO, BATCH, STREAM, D), 1.0, 6.0, ((1, 4), (2, 8)))
    ln1_gain = jnp.clip(1.0 + 0.1 * jax.random.normal(arg_keys[4], (D,), jnp.float32), 0.5, 1.5).astype(jnp.bfloat16)
    ln1_shift = gaussian(arg_keys[5], (D,), 0.1, 1.5, ((0, 4),))
    w_qkv = gaussian(arg_keys[6], (3, D, D), D ** -0.5, 0.1875, ((1, 4),))
    qv_bias = gaussian(arg_keys[7], (2, D), 0.1, 1.5, ((1, 4),))
    w_out = gaussian(arg_keys[8], (D, D), (D // 64) ** -0.5, 1.5, ((0, 4),))
    out_bias = gaussian(arg_keys[9], (D,), 0.1, 1.5, ((0, 4),))
    ln2_gain = jnp.clip(1.0 + 0.1 * jax.random.normal(arg_keys[10], (D,), jnp.float32), 0.5, 1.5).astype(jnp.bfloat16)
    ln2_shift = gaussian(arg_keys[11], (D,), 0.1, 1.5, ((0, 4),))
    router = gaussian(arg_keys[12], (D, EXPERTS), (4 * D) ** -0.5, 0.09375, ((0, 4),))
    w_in = gaussian(arg_keys[13], (EXPERTS, D, FF), D ** -0.5, 0.1875, ((1, 4),))
    in_bias = gaussian(arg_keys[14], (EXPERTS, FF), 0.1, 1.5, ((1, 4),))
    w_back = gaussian(arg_keys[15], (EXPERTS, FF, D), (FF // 4) ** -0.5, 0.1875, ((1, 4),))
    back_bias = gaussian(arg_keys[16], (EXPERTS, D), 0.1, 1.5, ((1, 4),))
    return dict(tokens=tokens, doc_ids=doc_ids, routes=routes, cotangent=cotangent, ln1_gain=ln1_gain, ln1_shift=ln1_shift, w_qkv=w_qkv, qv_bias=qv_bias, w_out=w_out, out_bias=out_bias, ln2_gain=ln2_gain, ln2_shift=ln2_shift, router=router, w_in=w_in, in_bias=in_bias, w_back=w_back, back_bias=back_bias)


norm_eps = 1e-05
mask_fill = -1e+30

@jax.custom_vjp
def low(v):
    return lax.optimization_barrier(v.astype(jnp.bfloat16)).astype(jnp.float32)

@jax.custom_vjp
def low_back(v):
    return v

def low_keep(v):
    return (low(v), None)

def low_pass(kept, grad):
    return (grad,)

def back_keep(v):
    return (v, None)

def back_low(kept, grad):
    return (low(grad),)
low.defvjp(low_keep, low_pass)
low_back.defvjp(back_keep, back_low)

def matmul(left, right):
    return jnp.dot(left, right, precision=lax.Precision.HIGHEST, preferred_element_type=jnp.float32)

def layer_norm(values, gain, shift):
    mean = lax.optimization_barrier(jnp.mean(values, -1, keepdims=True))
    centred = values - mean
    spread = lax.optimization_barrier(jnp.mean(centred * centred, -1, keepdims=True))
    return centred * lax.rsqrt(spread + norm_eps) * gain + shift

def natural_of_storage():
    half = TOK_DEV // 2
    store = jnp.arange(STREAM, dtype=jnp.int32)
    device = store // TOK_DEV
    slot = store % TOK_DEV
    return jnp.where(slot < half, device * half + slot, (2 * N_CTX - 1 - device) * half + slot - half).astype(jnp.int32)

def storage_of_natural():
    half = TOK_DEV // 2
    natural = jnp.arange(STREAM, dtype=jnp.int32)
    block = natural // half
    within = natural % half
    device = jnp.where(block < N_CTX, block, 2 * N_CTX - 1 - block)
    slot = jnp.where(block < N_CTX, within, half + within)
    return (device * TOK_DEV + slot).astype(jnp.int32)

def attention(queries, key_rows, value_rows, doc_row):
    length = queries.shape[0]
    block = math.gcd(length, 512)
    scale = 1.0 / math.sqrt(HEAD_DIM)
    positions = jnp.arange(length, dtype=jnp.int32)
    query_blocks = queries.reshape(length // block, block, HEADS, HEAD_DIM)
    begins = jnp.arange(length // block, dtype=jnp.int32) * block

    @jax.checkpoint
    def one_block(query_blk, begin):
        query_pos = begin + jnp.arange(block, dtype=jnp.int32)
        query_ids = lax.dynamic_slice_in_dim(doc_row, begin, block, 0)
        scores = jnp.einsum('qhc,khc->hqk', query_blk, key_rows, precision=lax.Precision.HIGHEST) * scale
        scores = low_back(scores)
        allowed = ((positions[None, :] <= query_pos[:, None]) & (doc_row[None, :] == query_ids[:, None]))[None]
        scores = jnp.where(allowed, scores, mask_fill)
        weights = low(jax.nn.softmax(scores, axis=-1))
        return jnp.einsum('hqk,khc->qhc', weights, value_rows, precision=lax.Precision.HIGHEST)

    def map_block(block_pair):
        return one_block(block_pair[0], block_pair[1])
    result = lax.map(map_block, (query_blocks, begins))
    return result.reshape(length, HEADS * HEAD_DIM)

def one_stream(params, inputs, doc_row, route_row):
    ln1_gain, ln1_shift, w_qkv, qv_bias, w_out, out_bias, ln2_gain, ln2_shift, router, w_in, in_bias, w_back, back_bias = params
    length = inputs.shape[0]
    heads_shape = (length, HEADS, HEAD_DIM)
    h_first = low(layer_norm(inputs, ln1_gain, ln1_shift))
    queries = low(low_back(matmul(h_first, w_qkv[0]) + qv_bias[0]))
    key_rows = low(low_back(matmul(h_first, w_qkv[1])))
    value_rows = low(low_back(matmul(h_first, w_qkv[2]) + qv_bias[1]))
    attended = attention(queries.reshape(heads_shape), key_rows.reshape(heads_shape), value_rows.reshape(heads_shape), doc_row)
    attended = low(low_back(attended))
    branch = low_back(matmul(attended, w_out) + out_bias)
    middle = inputs + branch
    h_second = low(layer_norm(middle, ln2_gain, ln2_shift))
    logits = matmul(h_second, router)
    probs = jax.nn.softmax(logits, axis=-1)
    chosen = (route_row[:, None] == jnp.arange(EXPERTS, dtype=jnp.int32)[None, :]).astype(jnp.float32)
    gate = lax.optimization_barrier(jnp.sum(probs * chosen, -1, keepdims=True))
    expert_sum = jnp.zeros(inputs.shape, jnp.float32)
    for expert in range(EXPERTS):
        inner = low_back(matmul(h_second, w_in[expert]) + in_bias[expert])
        active = low(jax.nn.gelu(inner))
        result = low_back(matmul(active, w_back[expert]) + back_bias[expert])
        expert_sum = expert_sum + chosen[:, expert:expert + 1] * result
    return middle + gate * expert_sum

def reference(tokens, doc_ids, routes, cotangent, ln1_gain, ln1_shift, w_qkv, qv_bias, w_out, out_bias, ln2_gain, ln2_shift, router, w_in, in_bias, w_back, back_bias):
    params = (ln1_gain.astype(jnp.float32), ln1_shift.astype(jnp.float32), w_qkv.astype(jnp.float32), qv_bias.astype(jnp.float32), w_out.astype(jnp.float32), out_bias.astype(jnp.float32), ln2_gain.astype(jnp.float32), ln2_shift.astype(jnp.float32), router.astype(jnp.float32), w_in.astype(jnp.float32), in_bias.astype(jnp.float32), w_back.astype(jnp.float32), back_bias.astype(jnp.float32))
    to_natural = storage_of_natural()
    to_storage = natural_of_storage()
    streams = jnp.take(tokens.astype(jnp.float32).reshape(-1, STREAM, D), to_natural, axis=1)
    documents = doc_ids.reshape(-1, STREAM)
    choices_all = jnp.take(routes.reshape(-1, STREAM), to_natural, axis=1)
    upstream = jnp.take(cotangent.astype(jnp.float32).reshape(-1, STREAM, D), to_natural, axis=1)

    def forward(weights, inputs):

        def scan_step(unused, pieces):
            return (unused, jax.checkpoint(one_stream)(weights, pieces[0], pieces[1], pieces[2]))
        _, outputs = lax.scan(scan_step, jnp.float32(0.0), (inputs, documents, choices_all))
        return outputs
    outputs, pull = jax.vjp(forward, params, streams)
    param_grads, stream_grads = pull(upstream)
    g_one, s_one, g_qkv, g_qv, g_out, g_outb, g_two, s_two, g_router, g_in, g_inb, g_back, g_backb = param_grads
    outputs = jnp.take(outputs, to_storage, axis=1)
    stream_grads = jnp.take(stream_grads, to_storage, axis=1)
    return (outputs.reshape(tokens.shape).astype(jnp.bfloat16), stream_grads.reshape(tokens.shape), g_one, s_one, g_qkv, g_qv, g_out, g_outb, g_two, s_two, g_router, g_in, g_inb, g_back, g_backb)
```

```python
import math

import jax
import jax.numpy as jnp
from jax import lax
from jax.experimental import pallas as pl
from jax.experimental.pallas import tpu as pltpu
from jax.sharding import PartitionSpec as P

HEADS = 16
HEAD_DIM = 64
CAP = 80


norm_eps = 1e-05
mask_fill = -1e30


def layer_norm(values, gain, shift):
    mean = jnp.mean(values, -1, keepdims=True)
    centred = values - mean
    spread = jnp.mean(centred * centred, -1, keepdims=True)
    return centred * lax.rsqrt(spread + norm_eps) * gain + shift


def natural_position(store_index, tok_rows, ctx_count):
    half = tok_rows // 2
    device = store_index // tok_rows
    slot = store_index % tok_rows
    return jnp.where(
        slot < half, device * half + slot, (2 * ctx_count - 1 - device) * half + slot - half
    )


def visible(query_pos, query_ids, key_pos, key_ids):
    return (key_pos[None, :] <= query_pos[:, None]) & (key_ids[None, :] == query_ids[:, None])


def block_needed(query_pos, query_ids, key_pos, key_ids):
    return (
        (jnp.min(key_pos) <= jnp.max(query_pos))
        & (jnp.max(key_ids) >= jnp.min(query_ids))
        & (jnp.min(key_ids) <= jnp.max(query_ids))
    )


def attend_keys(
    running, query_heads, query_pos, query_ids, key_part, value_part, pos_part, id_part, scale
):
    length = key_part.shape[0]
    stride = math.gcd(length, 512)
    key_heads = key_part.reshape(length, HEADS, HEAD_DIM)
    value_heads = value_part.reshape(length, HEADS, HEAD_DIM)

    def attend_visit_block(block_index, state):
        offset = block_index * stride
        key_blk = lax.dynamic_slice_in_dim(key_heads, offset, stride, 0)
        value_blk = lax.dynamic_slice_in_dim(value_heads, offset, stride, 0)
        key_pos = lax.dynamic_slice_in_dim(pos_part, offset, stride, 0)
        key_ids = lax.dynamic_slice_in_dim(id_part, offset, stride, 0)
        needed = block_needed(query_pos, query_ids, key_pos, key_ids)

        def update(current):
            best, totals, accum = current
            scores = (
                jnp.einsum("qhc,khc->hqk", query_heads, key_blk, preferred_element_type=jnp.float32)
                * scale
            )
            allowed = visible(query_pos, query_ids, key_pos, key_ids)[None]
            scores = jnp.where(allowed, scores, mask_fill)
            new_best = jnp.maximum(best, jnp.max(scores, -1))
            shrink = jnp.exp(best - new_best)
            weights = jnp.where(allowed, jnp.exp(scores - new_best[..., None]), 0.0)
            totals = totals * shrink + jnp.sum(weights, -1)
            addend = jnp.einsum(
                "hqk,khc->qhc",
                weights.astype(jnp.bfloat16),
                value_blk,
                preferred_element_type=jnp.float32,
            )
            accum = accum * jnp.transpose(shrink)[..., None] + addend
            return (new_best, totals, accum)

        def unchanged(current):
            return current

        return lax.cond(needed, update, unchanged, state)

    return lax.fori_loop(0, length // stride, attend_visit_block, running)


def backward_range(
    query_heads,
    grad_heads,
    log_total,
    delta,
    query_pos,
    query_ids,
    key_part,
    value_part,
    pos_part,
    id_part,
    scale,
):
    length = key_part.shape[0]
    stride = math.gcd(length, 512)
    blocks = length // stride
    key_blocks = key_part.reshape(blocks, stride, HEADS, HEAD_DIM)
    value_blocks = value_part.reshape(blocks, stride, HEADS, HEAD_DIM)
    pos_blocks = pos_part.reshape(blocks, stride)
    id_blocks = id_part.reshape(blocks, stride)
    rows = query_heads.shape[0]

    def backward_visit_block(query_acc, block_data):
        key_blk, value_blk, pos_blk, id_blk = block_data
        needed = block_needed(query_pos, query_ids, pos_blk, id_blk)

        def compute(current):
            scores = (
                jnp.einsum("qhc,khc->hqk", query_heads, key_blk, preferred_element_type=jnp.float32)
                * scale
            )
            allowed = visible(query_pos, query_ids, pos_blk, id_blk)[None]
            weights = jnp.where(allowed, jnp.exp(scores - log_total[..., None]), 0.0)
            weight_grad = jnp.einsum(
                "qhc,khc->hqk", grad_heads, value_blk, preferred_element_type=jnp.float32
            )
            score_grad = (weights * (weight_grad - delta[..., None])).astype(jnp.bfloat16)
            current = (
                current
                + jnp.einsum(
                    "hqk,khc->qhc", score_grad, key_blk, preferred_element_type=jnp.float32
                )
                * scale
            )
            terms = ()
            value_term = jnp.einsum(
                "hqk,qhc->khc",
                weights.astype(jnp.bfloat16),
                grad_heads,
                preferred_element_type=jnp.float32,
            )
            key_term = (
                jnp.einsum(
                    "hqk,qhc->khc", score_grad, query_heads, preferred_element_type=jnp.float32
                )
                * scale
            )
            terms = (key_term, value_term)
            return (current, terms)

        def skipped(current):
            terms = ()
            empty = jnp.zeros((stride, HEADS, HEAD_DIM), jnp.float32)
            terms = (empty, empty)
            return (current, terms)

        query_acc, terms = lax.cond(needed, compute, skipped, query_acc)
        terms = (
            terms[0].reshape(stride, HEADS * HEAD_DIM),
            terms[1].reshape(stride, HEADS * HEAD_DIM),
        )
        return (query_acc, terms)

    start_acc = jnp.zeros((rows, HEADS, HEAD_DIM), jnp.float32)
    query_grad, terms = lax.scan(
        backward_visit_block, start_acc, (key_blocks, value_blocks, pos_blocks, id_blocks)
    )
    return (
        query_grad,
        terms[0].reshape(length, HEADS * HEAD_DIM),
        terms[1].reshape(length, HEADS * HEAD_DIM),
    )


def gather_keys(key_rows, value_rows):
    return (
        lax.all_gather(key_rows, "ctx", axis=0, tiled=True),
        lax.all_gather(value_rows, "ctx", axis=0, tiled=True),
    )


def reduce_grads(attn_terms, expert_terms):
    g_one, s_one, g_qkv, g_qv, g_out, g_outb, g_two, s_two, g_router = attn_terms
    g_in, g_inb, g_back, g_backb = expert_terms
    e_in, e_inb, e_back, e_backb = (
        lax.psum_scatter(g_in.astype(jnp.bfloat16), "fsdp", scatter_dimension=1, tiled=True).astype(
            jnp.float32
        ),
        lax.psum_scatter(
            g_inb.astype(jnp.bfloat16), "fsdp", scatter_dimension=1, tiled=True
        ).astype(jnp.float32),
        lax.psum_scatter(
            g_back.astype(jnp.bfloat16), "fsdp", scatter_dimension=1, tiled=True
        ).astype(jnp.float32),
        lax.psum_scatter(
            g_backb.astype(jnp.bfloat16), "fsdp", scatter_dimension=1, tiled=True
        ).astype(jnp.float32),
    )
    a_one, b_one, a_qkv, a_qv, a_out, a_outb, a_two, b_two, a_router = (
        lax.psum_scatter(
            g_one.astype(jnp.bfloat16), "fsdp", scatter_dimension=0, tiled=True
        ).astype(jnp.float32),
        lax.psum_scatter(
            s_one.astype(jnp.bfloat16), "fsdp", scatter_dimension=0, tiled=True
        ).astype(jnp.float32),
        lax.psum_scatter(
            g_qkv.astype(jnp.bfloat16), "fsdp", scatter_dimension=1, tiled=True
        ).astype(jnp.float32),
        lax.psum_scatter(g_qv.astype(jnp.bfloat16), "fsdp", scatter_dimension=1, tiled=True).astype(
            jnp.float32
        ),
        lax.psum_scatter(
            g_out.astype(jnp.bfloat16), "fsdp", scatter_dimension=0, tiled=True
        ).astype(jnp.float32),
        lax.psum_scatter(
            g_outb.astype(jnp.bfloat16), "fsdp", scatter_dimension=0, tiled=True
        ).astype(jnp.float32),
        lax.psum_scatter(
            g_two.astype(jnp.bfloat16), "fsdp", scatter_dimension=0, tiled=True
        ).astype(jnp.float32),
        lax.psum_scatter(
            s_two.astype(jnp.bfloat16), "fsdp", scatter_dimension=0, tiled=True
        ).astype(jnp.float32),
        lax.psum_scatter(
            g_router.astype(jnp.bfloat16), "fsdp", scatter_dimension=0, tiled=True
        ).astype(jnp.float32),
    )
    return (
        lax.psum(a_one.astype(jnp.bfloat16), "ctx").astype(jnp.float32),
        lax.psum(b_one.astype(jnp.bfloat16), "ctx").astype(jnp.float32),
        lax.psum(a_qkv.astype(jnp.bfloat16), "ctx").astype(jnp.float32),
        lax.psum(a_qv.astype(jnp.bfloat16), "ctx").astype(jnp.float32),
        lax.psum(a_out.astype(jnp.bfloat16), "ctx").astype(jnp.float32),
        lax.psum(a_outb.astype(jnp.bfloat16), "ctx").astype(jnp.float32),
        lax.psum(a_two.astype(jnp.bfloat16), "ctx").astype(jnp.float32),
        lax.psum(b_two.astype(jnp.bfloat16), "ctx").astype(jnp.float32),
        lax.psum(a_router.astype(jnp.bfloat16), "ctx").astype(jnp.float32),
        lax.psum(e_in.astype(jnp.bfloat16), "ctx").astype(jnp.float32),
        lax.psum(e_inb.astype(jnp.bfloat16), "ctx").astype(jnp.float32),
        lax.psum(e_back.astype(jnp.bfloat16), "ctx").astype(jnp.float32),
        lax.psum(e_backb.astype(jnp.bfloat16), "ctx").astype(jnp.float32),
    )


def body(
    tokens,
    doc_ids,
    routes,
    cotangent,
    ln1_gain,
    ln1_shift,
    w_qkv,
    qv_bias,
    w_out,
    out_bias,
    ln2_gain,
    ln2_shift,
    router,
    w_in,
    in_bias,
    w_back,
    back_bias,
):
    gain_one, shift_one, proj_all, bias_qv, proj_out, bias_out, gain_two, shift_two, router_full = (
        lax.all_gather(ln1_gain, "fsdp", axis=0, tiled=True),
        lax.all_gather(ln1_shift, "fsdp", axis=0, tiled=True),
        lax.all_gather(w_qkv, "fsdp", axis=1, tiled=True),
        lax.all_gather(qv_bias, "fsdp", axis=1, tiled=True),
        lax.all_gather(w_out, "fsdp", axis=0, tiled=True),
        lax.all_gather(out_bias, "fsdp", axis=0, tiled=True),
        lax.all_gather(ln2_gain, "fsdp", axis=0, tiled=True),
        lax.all_gather(ln2_shift, "fsdp", axis=0, tiled=True),
        lax.all_gather(router, "fsdp", axis=0, tiled=True),
    )
    inner_full, inner_bias, outer_full, outer_bias = (
        lax.all_gather(w_in, "fsdp", axis=1, tiled=True),
        lax.all_gather(in_bias, "fsdp", axis=1, tiled=True),
        lax.all_gather(w_back, "fsdp", axis=1, tiled=True),
        lax.all_gather(back_bias, "fsdp", axis=1, tiled=True),
    )
    gain_one_f = gain_one.astype(jnp.float32)
    shift_one_f = shift_one.astype(jnp.float32)
    bias_qv_f = bias_qv.astype(jnp.float32)
    bias_out_f = bias_out.astype(jnp.float32)
    gain_two_f = gain_two.astype(jnp.float32)
    shift_two_f = shift_two.astype(jnp.float32)
    router_f = router_full.astype(jnp.float32)
    inner_bias_f = inner_bias.astype(jnp.float32)
    outer_bias_f = outer_bias.astype(jnp.float32)
    micro_count = tokens.shape[0]
    tok_rows = tokens.shape[2]
    width = tokens.shape[3]
    stream_len = doc_ids.shape[2]
    ctx_count = lax.axis_size("ctx")
    expert_count = inner_full.shape[0]
    scale = 1.0 / math.sqrt(HEAD_DIM)
    first_row = lax.axis_index("ctx") * tok_rows
    store_pos = natural_position(lax.iota(jnp.int32, stream_len), tok_rows, ctx_count)
    query_pos = lax.dynamic_slice_in_dim(store_pos, first_row, tok_rows, 0)
    expert_iota = lax.iota(jnp.int32, expert_count)
    slot_iota = lax.iota(jnp.int32, CAP)
    outputs = []
    input_grads = []
    totals = None
    for micro in range(micro_count):
        inputs = tokens[micro, 0].astype(jnp.float32)
        ids_store = jnp.take(doc_ids[micro, 0], store_pos)
        query_ids = lax.dynamic_slice_in_dim(ids_store, first_row, tok_rows, 0)
        picks = routes[micro, 0, :, 0]
        upstream = cotangent[micro, 0].astype(jnp.float32)
        h_first, pull_first = jax.vjp(layer_norm, inputs, gain_one_f, shift_one_f)
        h_first_low = h_first.astype(jnp.bfloat16)
        projected = jnp.einsum(
            "td,jde->jte", h_first_low, proj_all, preferred_element_type=jnp.float32
        )
        queries = (projected[0] + bias_qv_f[0]).astype(jnp.bfloat16)
        key_rows = projected[1].astype(jnp.bfloat16)
        value_rows = (projected[2] + bias_qv_f[1]).astype(jnp.bfloat16)
        query_heads = queries.reshape(tok_rows, HEADS, HEAD_DIM)
        start_state = (
            jnp.full((HEADS, tok_rows), mask_fill, jnp.float32),
            jnp.zeros((HEADS, tok_rows), jnp.float32),
            jnp.zeros((tok_rows, HEADS, HEAD_DIM), jnp.float32),
        )
        best, totals_soft, accum = attend_keys(
            start_state,
            query_heads,
            query_pos,
            query_ids,
            lax.all_gather(key_rows, "ctx", axis=0, tiled=True),
            lax.all_gather(value_rows, "ctx", axis=0, tiled=True),
            store_pos,
            ids_store,
            scale,
        )
        log_total = best + jnp.log(totals_soft)
        attended = accum / jnp.transpose(totals_soft)[..., None]
        attended_low = attended.reshape(tok_rows, width).astype(jnp.bfloat16)
        branch = jnp.dot(attended_low, proj_out, preferred_element_type=jnp.float32) + bias_out_f
        middle = inputs + branch
        h_second, pull_second = jax.vjp(layer_norm, middle, gain_two_f, shift_two_f)
        h_second_low = h_second.astype(jnp.bfloat16)
        logits = jnp.dot(h_second_low, router_full, preferred_element_type=jnp.float32)
        probs = jax.nn.softmax(logits, axis=-1)
        chosen = picks[:, None] == expert_iota[None, :]
        chosen_f = chosen.astype(jnp.float32)
        gate = jnp.sum(probs * chosen_f, -1)
        ranks = jnp.cumsum(chosen.astype(jnp.int32), 0) - 1
        dispatch = (jnp.transpose(ranks)[:, None, :] == slot_iota[None, :, None]) & jnp.transpose(
            chosen
        )[:, None, :]
        dispatch_low = dispatch.astype(jnp.bfloat16)
        dispatch_f = dispatch.astype(jnp.float32)
        slot_inputs = jnp.einsum(
            "ect,td->ecd", dispatch_low, h_second_low, preferred_element_type=jnp.float32
        ).astype(jnp.bfloat16)
        inner = (
            jnp.einsum("ecd,edh->ech", slot_inputs, inner_full, preferred_element_type=jnp.float32)
            + inner_bias_f[:, None, :]
        )
        active, pull_gelu = jax.vjp(jax.nn.gelu, inner)
        active_low = active.astype(jnp.bfloat16)
        result = (
            jnp.einsum("ech,ehd->ecd", active_low, outer_full, preferred_element_type=jnp.float32)
            + outer_bias_f[:, None, :]
        )
        expert_sum = jnp.einsum("ect,ecd->td", dispatch_f, result, precision=lax.Precision.HIGHEST)
        output = middle + gate[:, None] * expert_sum
        outputs.append(output.astype(jnp.bfloat16))
        gate_grad = jnp.sum(upstream * expert_sum, -1)
        slot_grad = jnp.einsum(
            "ect,td->ecd", dispatch_f, gate[:, None] * upstream, precision=lax.Precision.HIGHEST
        ).astype(jnp.bfloat16)
        outer_bias_grad = jnp.sum(slot_grad.astype(jnp.float32), 1)
        outer_grad = jnp.einsum(
            "ech,ecd->ehd", active_low, slot_grad, preferred_element_type=jnp.float32
        )
        active_grad = jnp.einsum(
            "ecd,ehd->ech", slot_grad, outer_full, preferred_element_type=jnp.float32
        )
        inner_grad = pull_gelu(active_grad)[0].astype(jnp.bfloat16)
        inner_bias_grad = jnp.sum(inner_grad.astype(jnp.float32), 1)
        inner_w_grad = jnp.einsum(
            "ecd,ech->edh", slot_inputs, inner_grad, preferred_element_type=jnp.float32
        )
        slot_input_grad = jnp.einsum(
            "ech,edh->ecd", inner_grad, inner_full, preferred_element_type=jnp.float32
        )
        second_grad = jnp.einsum(
            "ect,ecd->td", dispatch_f, slot_input_grad, precision=lax.Precision.HIGHEST
        )
        pick_grad = gate_grad[:, None] * chosen_f
        logit_grad = probs * (pick_grad - jnp.sum(probs * pick_grad, -1, keepdims=True))
        router_grad = jnp.einsum(
            "td,te->de",
            h_second_low.astype(jnp.float32),
            logit_grad,
            precision=lax.Precision.HIGHEST,
        )
        second_grad = second_grad + jnp.einsum(
            "te,de->td", logit_grad, router_f, precision=lax.Precision.HIGHEST
        )
        middle_norm_grad, gain_two_grad, shift_two_grad = pull_second(second_grad)
        middle_grad = upstream + middle_norm_grad
        branch_grad = middle_grad.astype(jnp.bfloat16)
        out_bias_grad = jnp.sum(branch_grad.astype(jnp.float32), 0)
        out_grad = jnp.einsum(
            "td,te->de", attended_low, branch_grad, preferred_element_type=jnp.float32
        )
        attended_grad = jnp.einsum(
            "te,de->td", branch_grad, proj_out, preferred_element_type=jnp.float32
        ).astype(jnp.bfloat16)
        grad_heads = attended_grad.reshape(tok_rows, HEADS, HEAD_DIM)
        delta = jnp.transpose(jnp.sum(grad_heads.astype(jnp.float32) * attended, -1))
        key_all, value_all = gather_keys(key_rows, value_rows)
        query_grad, key_terms, value_terms = backward_range(
            query_heads,
            grad_heads,
            log_total,
            delta,
            query_pos,
            query_ids,
            key_all,
            value_all,
            store_pos,
            ids_store,
            scale,
        )
        key_grad, value_grad = (
            lax.psum_scatter(
                key_terms.astype(jnp.bfloat16), "ctx", scatter_dimension=0, tiled=True
            ).astype(jnp.float32),
            lax.psum_scatter(
                value_terms.astype(jnp.bfloat16), "ctx", scatter_dimension=0, tiled=True
            ).astype(jnp.float32),
        )
        query_low = query_grad.reshape(tok_rows, width).astype(jnp.bfloat16)
        key_low = key_grad.astype(jnp.bfloat16)
        value_low = value_grad.astype(jnp.bfloat16)
        stacked_grad = jnp.stack([query_low, key_low, value_low])
        proj_grad = jnp.einsum(
            "td,jte->jde", h_first_low, stacked_grad, preferred_element_type=jnp.float32
        )
        qv_bias_grad = jnp.stack(
            [jnp.sum(query_low.astype(jnp.float32), 0), jnp.sum(value_low.astype(jnp.float32), 0)]
        )
        first_grad = jnp.einsum(
            "jte,jde->td", stacked_grad, proj_all, preferred_element_type=jnp.float32
        )
        input_norm_grad, gain_one_grad, shift_one_grad = pull_first(first_grad)
        input_grads.append(middle_grad + input_norm_grad)
        attn_terms = (
            gain_one_grad,
            shift_one_grad,
            proj_grad,
            qv_bias_grad,
            out_grad,
            out_bias_grad,
            gain_two_grad,
            shift_two_grad,
            router_grad,
        )
        expert_terms = (inner_w_grad, inner_bias_grad, outer_grad, outer_bias_grad)
        local_terms = attn_terms + expert_terms
        totals = local_terms if totals is None else jax.tree.map(jnp.add, totals, local_terms)
    totals = reduce_grads(totals[:9], totals[9:])
    (
        g_one,
        s_one,
        g_qkv,
        g_qv,
        g_out,
        g_outb,
        g_two,
        s_two,
        g_router,
        g_in,
        g_inb,
        g_back,
        g_backb,
    ) = totals
    mixed = jnp.stack(outputs)[:, None]
    token_grad = jnp.stack(input_grads)[:, None]
    return (
        mixed,
        token_grad,
        g_one,
        s_one,
        g_qkv,
        g_qv,
        g_out,
        g_outb,
        g_two,
        s_two,
        g_router,
        g_in,
        g_inb,
        g_back,
        g_backb,
    )


MESH_ID = pl.DeviceIdType.MESH
BF = jnp.bfloat16
F32 = jnp.float32
DMA = pltpu.SemaphoreType.DMA
VMEM_CAP = 60 * 1024 * 1024
SMALL_ROWS = 32
NT = (((1,), (1,)), ((), ()))
TN = (((0,), (0,)), ((), ()))
NN = (((1,), (0,)), ((), ()))


def mm(left, right, dims=NN):
    return lax.dot_general(left, right, dims, preferred_element_type=F32)


def plane_coords():
    me = lax.axis_index("ctx")
    core = me % 2
    col = (me // 2) % 2
    row = me // 4
    sib = me + 1 - 2 * core
    xn = (row * 2 + 1 - col) * 2 + core
    yn = ((1 - row) * 2 + col) * 2 + core
    dg = ((1 - row) * 2 + 1 - col) * 2 + core
    return me, core, sib, xn, yn, dg


def meet(ctx_peers, fsdp_peers=()):
    sem = pltpu.get_barrier_semaphore()
    for peer in ctx_peers:
        pl.semaphore_signal(sem, inc=1, device_id={"ctx": peer}, device_id_type=MESH_ID)
    for peer in fsdp_peers:
        pl.semaphore_signal(sem, inc=1, device_id={"fsdp": peer}, device_id_type=MESH_ID)
    pl.semaphore_wait(sem, len(ctx_peers) + len(fsdp_peers))


def send_to(src, dst, send_sem, recv_sem, axis, peer):
    return pltpu.make_async_remote_copy(
        src_ref=src,
        dst_ref=dst,
        send_sem=send_sem,
        recv_sem=recv_sem,
        device_id={axis: peer},
        device_id_type=MESH_ID,
    )


def gather_sems(chunks):
    return [
        DMA((2, chunks)),
        DMA((2, chunks)),
        DMA((chunks,)),
        DMA((chunks,)),
        DMA((3, chunks)),
        DMA((3, chunks)),
        DMA((chunks,)),
        DMA((chunks,)),
        DMA((chunks,)),
    ]


def interleave(*parts):
    live = list(parts)
    while live:
        for part in list(live):
            try:
                next(part)
            except StopIteration:
                live.remove(part)


def plane_gather(own, slot, chunks, sems):
    ns, nr, ds, dr, fs, fr, ss, sr, ls = sems
    me, core, sib, xn, yn, dg = plane_coords()
    near = (xn, yn)
    locals_, first, sibs, relays, forwards = [], {}, [], [], []
    for k in range(chunks):
        for i in (0, 1):
            copy = send_to(own(k), slot(me, k), ns.at[i, k], nr.at[i, k], "ctx", near[i])
            copy.start()
            first[i, k] = copy
    for k in range(chunks):
        copy = send_to(own(k), slot(me, k), ss.at[k], sr.at[k], "ctx", sib)
        copy.start()
        sibs.append(copy)
        here = pltpu.make_async_copy(own(k), slot(me, k), ls.at[k])
        here.start()
        locals_.append(here)
    yield
    for k in range(chunks):
        for i in (0, 1):
            first[i, k].wait_recv()
            if k % 2 == i:
                copy = send_to(
                    slot(near[i], k), slot(near[i], k), ds.at[k], dr.at[k], "ctx", near[1 - i]
                )
                copy.start()
                relays.append(copy)
            copy = send_to(
                slot(near[i], k), slot(near[i], k), fs.at[i, k], fr.at[i, k], "ctx", sib
            )
            copy.start()
            forwards.append(copy)
        yield
    for k in range(chunks):
        relays[k].wait_recv()
        copy = send_to(slot(dg, k), slot(dg, k), fs.at[2, k], fr.at[2, k], "ctx", sib)
        copy.start()
        forwards.append(copy)
        yield
    for copy in first.values():
        copy.wait_send()
    for copy in relays:
        copy.wait_send()
    for copy in locals_:
        copy.wait()
    for copy in sibs + forwards:
        copy.wait()


def line_sems(chunks):
    return [DMA((3, chunks)), DMA((3, chunks)), DMA((3, chunks)), DMA((3, chunks)), DMA((chunks,))]


def line_gather(own, slot, chunks, sems):
    us, ur, ws, wr, ls = sems
    z = lax.axis_index("fsdp")

    def up(d, k):
        src = own(k) if d == 0 else slot(z - d, k)
        return send_to(src, slot(z - d, k), us.at[d, k], ur.at[d, k], "fsdp", z + 1)

    def down(d, k):
        src = own(k) if d == 0 else slot(z + d, k)
        return send_to(src, slot(z + d, k), ws.at[d, k], wr.at[d, k], "fsdp", z - 1)

    def from_below(d, k):
        return send_to(own(k), slot(z - d - 1, k), us.at[d, k], ur.at[d, k], "fsdp", z - 1)

    def from_above(d, k):
        return send_to(own(k), slot(z + d + 1, k), ws.at[d, k], wr.at[d, k], "fsdp", z + 1)

    here = []
    for k in range(chunks):
        copy = pltpu.make_async_copy(own(k), slot(z, k), ls.at[k])
        copy.start()
        here.append(copy)
    for d in range(3):
        for k in range(chunks):

            @pl.when((z < 3) & (z >= d))
            def _():
                if d:
                    from_below(d - 1, k).wait_recv()
                up(d, k).start()

            @pl.when((z > 0) & (z + d <= 3))
            def _():
                if d:
                    from_above(d - 1, k).wait_recv()
                down(d, k).start()

            if d:
                yield
    for d in range(3):
        for k in range(chunks):

            @pl.when(z == 3)
            def _():
                from_below(d, k).wait_recv()

            @pl.when(z == 0)
            def _():
                from_above(d, k).wait_recv()

        yield
    for d in range(3):
        for k in range(chunks):

            @pl.when((z < 3) & (z >= d))
            def _():
                up(d, k).wait_send()

            @pl.when((z > 0) & (z + d <= 3))
            def _():
                down(d, k).wait_send()

    for copy in here:
        copy.wait()


def by_rows(count, step, visit):
    def one(index, carry):
        visit(pl.ds(pl.multiple_of(index * step, step), step))
        return carry

    lax.fori_loop(0, count // step, one, 0)


def scatter_scratch(rows, width):
    return [
        pltpu.VMEM((4, rows, width), BF),
        pltpu.VMEM((rows, width), BF),
        pltpu.VMEM((rows, width), BF),
        pltpu.VMEM((rows, width), BF),
        pltpu.VMEM((rows, width), BF),
        pltpu.VMEM((rows, width), BF),
        pltpu.VMEM((rows, width), BF),
        DMA((4,)),
        DMA((4,)),
        DMA((6,)),
        DMA((6,)),
    ]


def plane_scatter(part, rows, out, scratch):
    pair, gs, gr, xs, xr, ys, yr, s1, r1, s2, r2 = scratch
    me, core, sib, xn, yn, dg = plane_coords()
    half = rows // 2
    lo, hi = pl.ds(0, half), pl.ds(half, half)
    step = 32

    def other(peer):
        return peer + 1 - 2 * core

    def f32(value):
        return value.astype(F32)

    first = []
    for i, peer in enumerate((dg, xn, yn, me)):
        copy = send_to(part.at[other(peer)], pair.at[i], s1.at[i], r1.at[i], "ctx", sib)
        copy.start()
        first.append(copy)
    second = []

    def ship(src, dst, index, peer):
        copy = send_to(src, dst, s2.at[index], r2.at[index], "ctx", peer)
        copy.start()
        second.append(copy)

    yield
    first[0].wait_recv()

    def add_diag(rr):
        gs[rr] = (f32(part[dg, rr]) + f32(pair[0, rr])).astype(BF)

    by_rows(rows, step, add_diag)
    ship(gs.at[lo], gr.at[lo], 0, xn)
    ship(gs.at[hi], gr.at[hi], 1, yn)
    yield
    first[1].wait_recv()

    def add_x(rr):
        xs[rr] = (f32(part[xn, rr]) + f32(pair[1, rr])).astype(BF)

    by_rows(half, step, add_x)
    ship(xs.at[lo], xr.at[lo], 2, xn)
    first[2].wait_recv()

    def add_y(index):
        rr = pl.ds(half + index.start, step)
        ys[rr] = (f32(part[yn, rr]) + f32(pair[2, rr])).astype(BF)

    by_rows(half, step, add_y)
    ship(ys.at[hi], yr.at[hi], 3, yn)
    yield
    second[0].wait_recv()

    def join_y(rr):
        ys[rr] = (f32(part[yn, rr]) + f32(pair[2, rr]) + f32(gr[rr])).astype(BF)

    by_rows(half, step, join_y)
    ship(ys.at[lo], yr.at[lo], 4, yn)
    yield
    second[1].wait_recv()

    def join_x(index):
        rr = pl.ds(half + index.start, step)
        xs[rr] = (f32(part[xn, rr]) + f32(pair[1, rr]) + f32(gr[rr])).astype(BF)

    by_rows(half, step, join_x)
    ship(xs.at[hi], xr.at[hi], 5, xn)
    yield
    first[3].wait_recv()
    for index in (2, 3, 4, 5):
        second[index].wait_recv()

    def finish(rr):
        out[rr] = f32(part[me, rr]) + f32(pair[3, rr]) + f32(xr[rr]) + f32(yr[rr])

    by_rows(rows, step, finish)
    for copy in first + second:
        copy.wait_send()


def vmem_spec():
    return pl.BlockSpec(memory_space=pltpu.VMEM)


def any_spec():
    return pl.BlockSpec(memory_space=pl.ANY)


def natural_slot(device, k):
    micro, part = k // 2, k % 2
    return micro * 16 + (device if part == 0 else 15 - device)


def remote_params(ident):
    return pltpu.CompilerParams(
        collective_id=ident, has_side_effects=True, vmem_limit_bytes=VMEM_CAP
    )


def line_peers():
    z = lax.axis_index("fsdp")
    return [(z + d) % 4 for d in (1, 2, 3)]


def entry_kernel(
    x_ref, small_ref, wq_ref, wo_ref, h_ref, params_ref, wqc_ref, woc_ref,
    hs, zs, zr, os, orr, ol, *sems,
):
    me, core, sib, xn, yn, dg = plane_coords()
    z = lax.axis_index("fsdp")
    peers = line_peers()
    meet((sib, xn, yn), peers)
    params_ref[z] = small_ref[...]
    copies = []
    for i, peer in enumerate(peers):
        copy = send_to(small_ref, params_ref.at[z], zs.at[i], zr.at[i], "fsdp", peer)
        copy.start()
        copies.append(copy)
    owner = me // 2
    wo_mine = wo_ref.at[pl.ds(pl.multiple_of(core * 128, 128), 128)]
    columns = pl.ds(pl.multiple_of(me * 128, 128), 128)

    def wq_slot(where, k):
        return wqc_ref.at[k, pl.ds(pl.multiple_of(where * 256, 256), 256)]

    weights = line_gather(lambda k: wq_ref.at[k, :, columns], wq_slot, 3, sems[:5])
    next(weights)

    @pl.when(z == owner)
    def _():
        pltpu.make_async_copy(wo_mine, woc_ref, ol).start()
        for i, peer in enumerate(peers):
            send_to(wo_mine, woc_ref, os.at[i], orr, "fsdp", peer).start()

    for copy in copies:
        copy.wait()

    def full_row(r):
        return jnp.concatenate([params_ref[i, r : r + 1, :] for i in range(4)], axis=1).astype(F32)

    gain, shift = full_row(0), full_row(1)

    def norm(rr):
        values = x_ref[rr].astype(F32)
        mean = jnp.mean(values, -1, keepdims=True)
        centred = values - mean
        spread = jnp.mean(centred * centred, -1, keepdims=True)
        hs[rr] = (centred * lax.rsqrt(spread + norm_eps) * gain + shift).astype(BF)

    by_rows(256, 32, norm)
    tokens_ring = plane_gather(
        lambda k: hs.at[pl.ds(64 * k, 64)],
        lambda device, k: h_ref.at[natural_slot(device, k)],
        4,
        sems[5:],
    )
    interleave(tokens_ring, weights)

    @pl.when(z == owner)
    def _():
        pltpu.make_async_copy(wo_mine, woc_ref, ol).wait()
        for i, peer in enumerate(peers):
            send_to(wo_mine, woc_ref, os.at[i], orr, "fsdp", peer).wait_send()

    @pl.when(z != owner)
    def _():
        send_to(wo_mine, woc_ref, os.at[0], orr, "fsdp", owner).wait_recv()


def entry_call(x, small, w_qkv, w_out):
    return pl.pallas_call(
        entry_kernel,
        out_shape=(
            jax.ShapeDtypeStruct((32, 64, 1024), BF),
            jax.ShapeDtypeStruct((4, SMALL_ROWS, 256), BF),
            jax.ShapeDtypeStruct((3, 1024, 128), BF),
            jax.ShapeDtypeStruct((128, 1024), BF),
        ),
        in_specs=[vmem_spec(), vmem_spec(), any_spec(), any_spec()],
        out_specs=(any_spec(), vmem_spec(), any_spec(), any_spec()),
        scratch_shapes=[
            pltpu.VMEM((256, 1024), BF),
            DMA((3,)),
            DMA((3,)),
            DMA((3,)),
            DMA(()),
            DMA(()),
        ]
        + line_sems(3)
        + gather_sems(4),
        name="entry",
        compiler_params=remote_params(0),
    )(x, small, w_qkv, w_out)


def scatter_call(part, name, ident):
    def kernel(p_ref, o_ref, *scratch):
        me, core, sib, xn, yn, dg = plane_coords()
        meet((sib, xn, yn))
        interleave(plane_scatter(p_ref, 256, o_ref, scratch))

    return pl.pallas_call(
        kernel,
        out_shape=jax.ShapeDtypeStruct((256, 1024), F32),
        in_specs=[vmem_spec()],
        out_specs=vmem_spec(),
        scratch_shapes=scatter_scratch(256, 1024),
        name=name,
        compiler_params=remote_params(ident),
    )(part)


def moe_call(h_slots, d_slots, win, wback, inb):
    def kernel(
        h_ref, d_ref, wi_ref, wb_ref, ib_ref, o_ref, gi_ref, gb_ref, gib_ref,
        rows, gz, slope, dz, part, pair, sent, got,
        ns, nr, fs, fr, ss, sr, ls, s1, r1, s2, r2,
    ):
        me, core, sib, xn, yn, dg = plane_coords()
        expert = me // 4
        meet((sib, xn, yn, dg))
        peers = (dg, xn, yn)
        wanted = (1 - expert, expert, 1 - expert)
        ins = (h_ref, d_ref)

        def away(t, m, i):
            return send_to(
                ins[t].at[wanted[i], m], rows.at[t, m, me], ns.at[t, m, i], nr.at[t, m, i], "ctx", peers[i]
            )

        def beside(t, m):
            return send_to(
                ins[t].at[expert, m], rows.at[t, m, me], ss.at[t, m], sr.at[t, m], "ctx", sib
            )

        def here(t, m):
            return pltpu.make_async_copy(ins[t].at[expert, m], rows.at[t, m, me], ls.at[t, m])

        def onward(t, m, i):
            block = rows.at[t, m, peers[i]]
            return send_to(block, block, fs.at[t, m, i], fr.at[t, m, i], "ctx", sib)

        for t in (0, 1):
            for m in (0, 1):
                for i in range(3):
                    away(t, m, i).start()
        for t in (0, 1):
            for m in (0, 1):
                beside(t, m).start()
                here(t, m).start()

        def arrive(t, m):
            for i in range(3):
                away(t, m, i).wait_recv()
                onward(t, m, i).start()
            here(t, m).wait()
            beside(t, m).wait_recv()
            for i in range(3):
                onward(t, m, i).wait_recv()

        order = (dg, xn, yn, me)

        def to_pair(t, m, i):
            other = order[i] + 1 - 2 * core
            return send_to(
                part.at[t, m, other], pair.at[t, m, i], s1.at[t, m, i], r1.at[t, m, i], "ctx", sib
            )

        def to_home(t, m, i):
            return send_to(
                sent.at[t, m, i], got.at[t, m, i], s2.at[t, m, i], r2.at[t, m, i], "ctx", order[i]
            )

        def join(t, m):
            for i in range(3):
                to_pair(t, m, i).wait_recv()
                mine = order[i]

                def add(rr):
                    sent[t, m, i, rr] = (
                        part[t, m, mine, rr].astype(F32) + pair[t, m, i, rr].astype(F32)
                    ).astype(BF)

                by_rows(CAP, 16, add)
                to_home(t, m, i).start()

        def tile(ref, m, half):
            return ref[0, m, pl.ds(4 * half, 4)].reshape(4 * CAP, 1024)

        def forward(m, carry):
            arrive(0, m)

            def rows_forward(half, inner_carry):
                xs = rows[0, m, pl.ds(4 * half, 4)].reshape(4 * CAP, 1024)
                zed = mm(xs, wi_ref[...]) + ib_ref[...]
                square = zed * zed
                t = jnp.tanh(zed * (GELU_A + GELU_A * GELU_B * square))
                half_up = 0.5 + 0.5 * t
                low = (zed * half_up).astype(BF)
                place = pl.ds(pl.multiple_of(m * 8 * CAP + half * 4 * CAP, 4 * CAP), 4 * CAP)
                gz[place] = low
                slope[place] = half_up + 0.5 * zed * (1.0 - t * t) * (
                    GELU_A + 3.0 * GELU_A * GELU_B * square
                )
                u = mm(low, wb_ref[...]).astype(BF)
                part[0, m, pl.ds(4 * half, 4)] = u.reshape(4, CAP, 1024)
                return inner_carry

            lax.fori_loop(0, 2, rows_forward, 0)
            for i in range(4):
                to_pair(0, m, i).start()
            return carry

        lax.fori_loop(0, 2, forward, 0)
        gib_ref[...] = jnp.zeros_like(gib_ref)

        def backward(m, carry):
            join(0, m)
            arrive(1, m)

            def rows_backward(half, inner_carry):
                du = rows[1, m, pl.ds(4 * half, 4)].reshape(4 * CAP, 1024)
                place = pl.ds(pl.multiple_of(m * 8 * CAP + half * 4 * CAP, 4 * CAP), 4 * CAP)
                low = (mm(du, wb_ref[...], NT) * slope[place]).astype(BF)
                dz[place] = low
                gib_ref[...] += jnp.sum(low.astype(F32), 0, keepdims=True)
                dh = mm(low, wi_ref[...], NT).astype(BF)
                part[1, m, pl.ds(4 * half, 4)] = dh.reshape(4, CAP, 1024)
                return inner_carry

            lax.fori_loop(0, 2, rows_backward, 0)
            for i in range(4):
                to_pair(1, m, i).start()
            return carry

        lax.fori_loop(0, 2, backward, 0)
        for m in (0, 1):
            join(1, m)

        def weight_grads(j, carry):
            column = pl.ds(pl.multiple_of(256 * j, 256), 256)
            du = rows[1].reshape(16 * CAP, 1024)
            gb_ref[column] = mm(gz[:, column], du, TN).astype(BF)
            xs = rows[0, :, :, :, column].reshape(16 * CAP, 256)
            gi_ref[column] = mm(xs, dz[...], TN).astype(BF)
            return carry

        lax.fori_loop(0, 4, weight_grads, 0)
        for t in (0, 1):
            for m in (0, 1):
                to_pair(t, m, 3).wait_recv()
                for i in range(3):
                    to_home(t, m, i).wait_recv()

                def finish(rr):
                    o_ref[expert, t, m, rr] = (
                        part[t, m, me, rr].astype(F32)
                        + pair[t, m, 3, rr].astype(F32)
                        + got[t, m, 1, rr].astype(F32)
                    )
                    o_ref[1 - expert, t, m, rr] = got[t, m, 0, rr].astype(F32) + got[
                        t, m, 2, rr
                    ].astype(F32)

                by_rows(CAP, 16, finish)
        for t in (0, 1):
            for m in (0, 1):
                for i in range(3):
                    away(t, m, i).wait_send()
                    onward(t, m, i).wait_send()
                    to_home(t, m, i).wait_send()
                for i in range(4):
                    to_pair(t, m, i).wait_send()
                beside(t, m).wait_send()

    return pl.pallas_call(
        kernel,
        out_shape=(
            jax.ShapeDtypeStruct((2, 2, 2, CAP, 1024), F32),
            jax.ShapeDtypeStruct((1024, 1024), BF),
            jax.ShapeDtypeStruct((1024, 1024), BF),
            jax.ShapeDtypeStruct((1, 1024), F32),
        ),
        in_specs=[vmem_spec()] * 5,
        out_specs=[vmem_spec()] * 4,
        scratch_shapes=[
            pltpu.VMEM((2, 2, 8, CAP, 1024), BF),
            pltpu.VMEM((16 * CAP, 1024), BF),
            pltpu.VMEM((16 * CAP, 1024), F32),
            pltpu.VMEM((16 * CAP, 1024), BF),
            pltpu.VMEM((2, 2, 8, CAP, 1024), BF),
            pltpu.VMEM((2, 2, 4, CAP, 1024), BF),
            pltpu.VMEM((2, 2, 3, CAP, 1024), BF),
            pltpu.VMEM((2, 2, 3, CAP, 1024), BF),
        ]
        + [DMA((2, 2, 3))] * 4
        + [DMA((2, 2))] * 3
        + [DMA((2, 2, 4))] * 2
        + [DMA((2, 2, 3))] * 2,
        name="moe",
        compiler_params=remote_params(2),
    )(h_slots, d_slots, win, wback, inb)


def gather_back_call(da):
    def kernel(a_ref, o_ref, *scratch):
        me, core, sib, xn, yn, dg = plane_coords()
        meet((sib, xn, yn))
        tokens_ring = plane_gather(
            lambda k: a_ref.at[pl.ds(64 * k, 64)],
            lambda device, k: o_ref.at[natural_slot(device, k)],
            4,
            scratch,
        )
        interleave(tokens_ring)

    return pl.pallas_call(
        kernel,
        out_shape=jax.ShapeDtypeStruct((32, 64, 1024), BF),
        in_specs=[vmem_spec()],
        out_specs=any_spec(),
        scratch_shapes=gather_sems(4),
        name="gather_back",
        compiler_params=remote_params(4),
    )(da)


def final_call(gi, gb, gq, gwo, vectors):
    def kernel(
        gi_ref, gb_ref, gq_ref, go_ref, v_ref,
        oi_ref, ob_ref, oq_ref, oo_ref, ov_ref,
        qgot, qsum, ogot, osum, vgot, vsum, vall,
        qs, qr, os, orr, vs, vr, ps, pr, ws, wr, fs, fr, ol, *sems,
    ):
        me, core, sib, xn, yn, dg = plane_coords()
        z = lax.axis_index("fsdp")
        peers = line_peers()
        others = [(me + d) % 8 for d in range(1, 8)]
        meet(others, peers)
        expert, quarter = me // 4, me % 4
        owner = me // 2

        vcopies = []
        for d in (1, 2, 3):
            peer = (z + d) % 4
            copy = send_to(v_ref.at[peer], vgot.at[d - 1], vs.at[d - 1], vr.at[d - 1], "fsdp", peer)
            copy.start()
            vcopies.append(copy)

        def qblock(where):
            return gq_ref.at[:, pl.ds(pl.multiple_of(where * 256, 256), 256)]

        qcopies = []
        for d in (1, 3, 2):
            peer = (z + d) % 4
            copy = send_to(qblock(peer), qgot.at[d - 1], qs.at[d - 1], qr.at[d - 1], "fsdp", peer)
            copy.start()
            qcopies.append(copy)
        away = (owner - z + 4) % 4

        def to_owner():
            return send_to(go_ref, ogot.at[away - 1], os, orr.at[away - 1], "fsdp", owner)

        @pl.when(z != owner)
        def _():
            to_owner().start()

        def own(k):
            if k < 4:
                return gi_ref.at[:, pl.ds(256 * k, 256)]
            return gb_ref.at[pl.ds(64 * (k - 4), 64)]

        def slot(device, k):
            which, part = device // 4, device % 4
            if k < 4:
                column = pl.multiple_of(k * 1024 + part * 256, 256)
                return oi_ref.at[which, :, pl.ds(column, 256)]
            row = pl.multiple_of(part * 256 + 64 * (k - 4), 64)
            return ob_ref.at[which, pl.ds(row, 64)]

        big = plane_gather(own, slot, 8, sems[:9])
        next(big)
        for copy in vcopies:
            copy.wait()
        vsum[...] = v_ref[z] + vgot[0] + vgot[1] + vgot[2]
        pcopies = []
        for i, peer in enumerate(others):
            copy = send_to(vsum, vall.at[i], ps.at[i], pr.at[i], "ctx", peer)
            copy.start()
            pcopies.append(copy)
        for copy in qcopies:
            copy.wait_recv()
        for j in range(3):

            def add(rr):
                row = pl.ds(pl.multiple_of(z * 256 + rr.start, 32), 32)
                total = gq_ref[j, row].astype(F32)
                for i in range(3):
                    total = total + qgot[i, j, rr].astype(F32)
                qsum[j, rr] = total.astype(BF)

            by_rows(256, 32, add)

        def qslot(device, k):
            return oq_ref.at[k, :, pl.ds(pl.multiple_of(device * 128, 128), 128)]

        second = plane_gather(lambda k: qsum.at[k], qslot, 3, sems[9:18])
        next(second)
        spread = [xn, yn, dg]
        rows_mine = oo_ref.at[pl.ds(pl.multiple_of(core * 128, 128), 128)]
        rows_sib = oo_ref.at[pl.ds(pl.multiple_of((1 - core) * 128, 128), 128)]

        @pl.when(z == owner)
        def _():
            for i in range(3):
                send_to(go_ref, ogot.at[i], os, orr.at[i], "fsdp", (z + 1) % 4).wait_recv()

            def add(rr):
                total = go_ref[rr].astype(F32)
                for i in range(3):
                    total = total + ogot[i, rr].astype(F32)
                osum[rr] = total.astype(BF)

            by_rows(128, 32, add)
            for i, peer in enumerate(spread):
                send_to(osum, rows_mine, ws.at[i], wr, "ctx", peer).start()
            send_to(osum, rows_mine, fs, fr, "ctx", sib).start()
            pltpu.make_async_copy(osum, rows_mine, ol).start()

        interleave(big, second)

        @pl.when(z == owner)
        def _():
            for i, peer in enumerate(spread):
                send_to(osum, rows_mine, ws.at[i], wr, "ctx", peer).wait_send()
            send_to(osum, rows_mine, fs, fr, "ctx", sib).wait_send()
            pltpu.make_async_copy(osum, rows_mine, ol).wait()

        @pl.when(z != owner)
        def _():
            to_owner().wait_send()
            send_to(osum, rows_mine, ws.at[0], wr, "ctx", xn).wait_recv()
            send_to(rows_mine, rows_mine, fs, fr, "ctx", sib).start()
            send_to(rows_mine, rows_mine, fs, fr, "ctx", sib).wait_send()

        send_to(osum, rows_sib, fs, fr, "ctx", sib).wait_recv()
        for copy in qcopies:
            copy.wait_send()
        total = vsum[...]
        for i, copy in enumerate(pcopies):
            copy.wait_recv()
            total = total + vall[i]
        ov_ref[...] = total
        for copy in pcopies:
            copy.wait_send()

    count = vectors.shape[1]
    return pl.pallas_call(
        kernel,
        out_shape=(
            jax.ShapeDtypeStruct((2, 256, 4096), BF),
            jax.ShapeDtypeStruct((2, 1024, 1024), BF),
            jax.ShapeDtypeStruct((3, 256, 1024), BF),
            jax.ShapeDtypeStruct((256, 1024), BF),
            jax.ShapeDtypeStruct((count, 256), F32),
        ),
        in_specs=[vmem_spec()] * 5,
        out_specs=[any_spec()] * 4 + [vmem_spec()],
        scratch_shapes=[
            pltpu.VMEM((3, 3, 256, 128), BF),
            pltpu.VMEM((3, 256, 128), BF),
            pltpu.VMEM((3, 128, 1024), BF),
            pltpu.VMEM((128, 1024), BF),
            pltpu.VMEM((3, count, 256), F32),
            pltpu.VMEM((count, 256), F32),
            pltpu.VMEM((7, count, 256), F32),
            DMA((3,)), DMA((3,)), DMA(()), DMA((3,)), DMA((3,)), DMA((3,)), DMA((7,)), DMA((7,)),
            DMA((3,)), DMA(()), DMA(()), DMA(()), DMA(()),
        ]
        + gather_sems(8)
        + gather_sems(3),
        name="final",
        compiler_params=remote_params(6),
    )(gi, gb, gq, gwo, vectors)


def head_masks(rows):
    lane = lax.broadcasted_iota(jnp.int32, (rows, 128), 1)
    return lane < 64, lane >= 64


def allowed_mask(i, doc_col, doc_row):
    length = 256 * (i + 1)
    qpos = lax.broadcasted_iota(jnp.int32, (256, length), 0) + 256 * i
    kpos = lax.broadcasted_iota(jnp.int32, (256, length), 1)
    return (kpos <= qpos) & (doc_col == doc_row)


def attend_kernel(h_ref, w_ref, b_ref, col_ref, row_ref, wo_ref, qkv_ref, o_ref, of_ref, lse_ref, part_ref):
    h = h_ref[...].reshape(1024, 1024)
    q = (mm(h, w_ref[0]) + b_ref[0:1]).astype(BF)
    k = mm(h, w_ref[1]).astype(BF)
    v = (mm(h, w_ref[2]) + b_ref[1:2]).astype(BF)
    qkv_ref[0] = q
    qkv_ref[1] = k
    qkv_ref[2] = v
    masks = head_masks(256)
    vmasks = head_masks(1024)
    zero = jnp.zeros((), BF)
    vh = [jnp.where(vmasks[j], v, zero) for j in (0, 1)]
    for i in range(4):
        length = 256 * (i + 1)
        qi = q[256 * i : 256 * (i + 1)] * jnp.asarray(0.125, BF)
        allowed = allowed_mask(i, col_ref[0, 256 * i : 256 * (i + 1)], row_ref[0, :, :length])
        total = None
        stats = []
        for j in (0, 1):
            s = mm(jnp.where(masks[j], qi, zero), k[:length], NT)
            s = jnp.where(allowed, s, mask_fill)
            top = jnp.max(s, -1, keepdims=True)
            e = jnp.exp(s - top)
            den = jnp.sum(e, -1, keepdims=True)
            p = (e * (1.0 / den)).astype(BF)
            term = mm(p, vh[j][:length])
            total = term if total is None else total + term
            stats.append(top + jnp.log(den))
        lse_ref[256 * i : 256 * (i + 1)] = jnp.where(masks[0], stats[0], stats[1])
        of_ref[256 * i : 256 * (i + 1)] = total
        low = total.astype(BF)
        o_ref[256 * i : 256 * (i + 1)] = low
        a = mm(low, wo_ref[...]).astype(BF)
        for b in range(4):
            block = 4 * i + b
            dest, part = (block, 0) if block < 8 else (15 - block, 1)
            part_ref[dest, 0, part] = a[64 * b : 64 * (b + 1)]


def attend_call(h, wqkv, bias, doc_col, doc_row, wout):
    const2 = lambda m: (0, 0)
    const3 = lambda m: (0, 0, 0)
    return pl.pallas_call(
        attend_kernel,
        grid=(2,),
        out_shape=(
            jax.ShapeDtypeStruct((3, 2048, 128), BF),
            jax.ShapeDtypeStruct((2048, 128), BF),
            jax.ShapeDtypeStruct((2048, 128), F32),
            jax.ShapeDtypeStruct((2048, 128), F32),
            jax.ShapeDtypeStruct((8, 2, 2, 64, 1024), BF),
        ),
        in_specs=[
            pl.BlockSpec((16, 64, 1024), lambda m: (m, 0, 0)),
            pl.BlockSpec((3, 1024, 128), const3),
            pl.BlockSpec((2, 128), const2),
            pl.BlockSpec((1, 1024, 1), lambda m: (m, 0, 0)),
            pl.BlockSpec((1, 1, 1024), lambda m: (m, 0, 0)),
            pl.BlockSpec((128, 1024), const2),
        ],
        out_specs=(
            pl.BlockSpec((3, 1024, 128), lambda m: (0, m, 0)),
            pl.BlockSpec((1024, 128), lambda m: (m, 0)),
            pl.BlockSpec((1024, 128), lambda m: (m, 0)),
            pl.BlockSpec((1024, 128), lambda m: (m, 0)),
            pl.BlockSpec((8, 1, 2, 64, 1024), lambda m: (0, m, 0, 0, 0)),
        ),
        name="attend",
        compiler_params=pltpu.CompilerParams(vmem_limit_bytes=VMEM_CAP),
    )(h, wqkv, bias, doc_col, doc_row, wout)


def attend_back_kernel(
    g_ref, h_ref, qkv_ref, o_ref, of_ref, lse_ref, w_ref, wo_ref, col_ref, row_ref,
    part_ref, gw_ref, gwo_ref, gb_ref, accw, acco, accb, dka, dva,
):
    m = pl.program_id(0)
    g = g_ref[...].reshape(1024, 1024)
    h = h_ref[...].reshape(1024, 1024)
    q, k, v = qkv_ref[0], qkv_ref[1], qkv_ref[2]
    do = mm(g, wo_ref[...], NT).astype(BF)
    masks = head_masks(256)
    kmasks = head_masks(1024)
    zero = jnp.zeros((), BF)
    dka[...] = jnp.zeros_like(dka)
    dva[...] = jnp.zeros_like(dva)
    dqs = []
    kh = [jnp.where(kmasks[j], k, zero) for j in (0, 1)]
    for i in range(4):
        length = 256 * (i + 1)
        rows = slice(256 * i, 256 * (i + 1))
        qi = q[rows] * jnp.asarray(0.125, BF)
        doi = do[rows]
        allowed = allowed_mask(i, col_ref[0, rows], row_ref[0, :, :length])
        prod = doi.astype(F32) * of_ref[rows]
        lse = lse_ref[rows]
        dq = None
        for j in (0, 1):
            qh = jnp.where(masks[j], qi, zero)
            doh = jnp.where(masks[j], doi, zero)
            delta = jnp.sum(jnp.where(masks[j], prod, 0.0), -1, keepdims=True)
            s = mm(qh, k[:length], NT)
            p = jnp.exp(jnp.where(allowed, s, mask_fill) - lse[:, 64 * j : 64 * j + 1])
            dp = mm(doh, v[:length], NT)
            ds = (p * (dp - delta)).astype(BF)
            term = mm(ds, kh[j][:length])
            dq = term if dq is None else dq + term
            dka[:length] += mm(ds, qh, TN)
            dva[:length] += mm(p.astype(BF), doh, TN)
        dqs.append((dq * 0.125).astype(BF))
    dq = jnp.concatenate(dqs, axis=0)
    dk = dka[...].astype(BF)
    dv = dva[...].astype(BF)

    @pl.when(m == 0)
    def _():
        accw[...] = jnp.zeros_like(accw)
        acco[...] = jnp.zeros_like(acco)
        accb[...] = jnp.zeros_like(accb)

    acco[...] += mm(o_ref[...], g, TN)
    for j, d in enumerate((dq, dk, dv)):
        accw[j] += mm(h, d, TN)
    accb[0:1] += jnp.sum(dq.astype(F32), 0, keepdims=True)
    accb[1:2] += jnp.sum(dv.astype(F32), 0, keepdims=True)
    for i in range(4):
        rows = slice(256 * i, 256 * (i + 1))
        a = (mm(dq[rows], w_ref[0], NT) + mm(dk[rows], w_ref[1], NT) + mm(dv[rows], w_ref[2], NT)).astype(BF)
        for b in range(4):
            block = 4 * i + b
            dest, part = (block, 0) if block < 8 else (15 - block, 1)
            part_ref[dest, 0, part] = a[64 * b : 64 * (b + 1)]

    @pl.when(m == 1)
    def _():
        gw_ref[...] = accw[...].astype(BF)
        gwo_ref[...] = acco[...].astype(BF)
        gb_ref[...] = accb[...]


def attend_back_call(g, h, qkv, o, of, lse, wqkv, wout, doc_col, doc_row):
    const2 = lambda m: (0, 0)
    const3 = lambda m: (0, 0, 0)
    return pl.pallas_call(
        attend_back_kernel,
        grid=(2,),
        out_shape=(
            jax.ShapeDtypeStruct((8, 2, 2, 64, 1024), BF),
            jax.ShapeDtypeStruct((3, 1024, 128), BF),
            jax.ShapeDtypeStruct((128, 1024), BF),
            jax.ShapeDtypeStruct((2, 128), F32),
        ),
        in_specs=[
            pl.BlockSpec((16, 64, 1024), lambda m: (m, 0, 0)),
            pl.BlockSpec((16, 64, 1024), lambda m: (m, 0, 0)),
            pl.BlockSpec((3, 1024, 128), lambda m: (0, m, 0)),
            pl.BlockSpec((1024, 128), lambda m: (m, 0)),
            pl.BlockSpec((1024, 128), lambda m: (m, 0)),
            pl.BlockSpec((1024, 128), lambda m: (m, 0)),
            pl.BlockSpec((3, 1024, 128), const3),
            pl.BlockSpec((128, 1024), const2),
            pl.BlockSpec((1, 1024, 1), lambda m: (m, 0, 0)),
            pl.BlockSpec((1, 1, 1024), lambda m: (m, 0, 0)),
        ],
        out_specs=(
            pl.BlockSpec((8, 1, 2, 64, 1024), lambda m: (0, m, 0, 0, 0)),
            pl.BlockSpec((3, 1024, 128), const3),
            pl.BlockSpec((128, 1024), const2),
            pl.BlockSpec((2, 128), const2),
        ),
        scratch_shapes=[
            pltpu.VMEM((3, 1024, 128), F32),
            pltpu.VMEM((128, 1024), F32),
            pltpu.VMEM((2, 128), F32),
            pltpu.VMEM((1024, 128), F32),
            pltpu.VMEM((1024, 128), F32),
        ],
        name="attend_back",
        compiler_params=pltpu.CompilerParams(vmem_limit_bytes=VMEM_CAP),
    )(g, h, qkv, o, of, lse, wqkv, wout, doc_col, doc_row)


GELU_A = math.sqrt(2.0 / math.pi)
GELU_B = 0.044715


def norm_back(values, gain, grad):
    mean = jnp.mean(values, -1, keepdims=True)
    centred = values - mean
    inv = lax.rsqrt(jnp.mean(centred * centred, -1, keepdims=True) + norm_eps)
    unit = centred * inv
    scaled = grad * gain
    back = inv * (
        scaled
        - jnp.mean(scaled, -1, keepdims=True)
        - unit * jnp.mean(scaled * unit, -1, keepdims=True)
    )
    return back, jnp.sum(grad * unit, 0), jnp.sum(grad, 0)


def fast_body(
    tokens, doc_ids, routes, cotangent, ln1_gain, ln1_shift, w_qkv, qv_bias, w_out, out_bias,
    ln2_gain, ln2_shift, router, w_in, in_bias, w_back, back_bias,
):
    c = lax.axis_index("ctx")
    expert, quarter = c // 4, c % 4
    rows = [ln1_gain, ln1_shift, qv_bias[0], qv_bias[1], out_bias, ln2_gain, ln2_shift]
    rows += [router[:, 0], router[:, 1]]
    rows += [in_bias[e, 256 * k : 256 * (k + 1)] for e in (0, 1) for k in range(4)]
    rows += [back_bias[0], back_bias[1]]
    row_iota = lax.broadcasted_iota(jnp.int32, (SMALL_ROWS, 256), 0)
    small = jnp.zeros((SMALL_ROWS, 256), BF)
    for index, row in enumerate(rows):
        small = jnp.where(row_iota == index, row[None], small)
    win_mine = jnp.concatenate(
        [
            lax.dynamic_slice(w_in, (expert, 0, k * 1024 + quarter * 256), (1, 256, 256))[0]
            for k in range(4)
        ],
        axis=1,
    )
    wback_mine = lax.dynamic_slice(w_back, (expert, quarter * 256, 0), (1, 256, 1024))[0]
    x_low = tokens[:, 0].reshape(256, 1024)
    picks = routes[:, 0, :, 0]
    hs, params, wqkv_c, wout_c = entry_call(x_low, small, w_qkv, w_out)
    win_mine, wback_mine, params = lax.optimization_barrier((win_mine, wback_mine, params))
    win_c = lax.all_gather(win_mine, "fsdp", axis=0, tiled=True)
    wback_c = lax.all_gather(wback_mine, "fsdp", axis=0, tiled=True)

    params = params.astype(F32)
    row_of = lambda r: params[:, r].reshape(1024)
    gain1, outb, gain2, shift2 = row_of(0), row_of(4), row_of(5), row_of(6)
    router_t = jnp.stack([row_of(7), row_of(8)])
    backb = jnp.stack([row_of(17), row_of(18)])
    qvb = lax.dynamic_slice_in_dim(jnp.stack([row_of(2), row_of(3)]), c * 128, 128, 1)
    inb = lax.dynamic_index_in_dim(params[:, 9:17], c, 1, keepdims=False).reshape(1, 1024)

    docs = doc_ids[:, 0]
    doc_col, doc_row = docs[:, :, None], docs[:, None, :]
    qkv, o_low, o_full, lse, part_a = attend_call(hs, wqkv_c, qvb, doc_col, doc_row, wout_c)
    branch = scatter_call(part_a.reshape(8, 256, 1024), "scatter_attend", 1)

    x = x_low.astype(F32)
    dy = cotangent[:, 0].reshape(256, 1024).astype(F32)
    y1 = x + (branch + outb)
    h2 = layer_norm(y1, gain2, shift2).astype(BF)
    logits = lax.dot_general(h2, router_t.astype(BF), NT, preferred_element_type=F32)
    probs = jax.nn.softmax(logits, axis=-1)
    flat = picks.reshape(256)
    chosen = (flat[:, None] == lax.iota(jnp.int32, 2)[None, :]).astype(F32)
    gate = jnp.sum(probs * chosen, -1, keepdims=True)
    before = lax.iota(jnp.int32, 128)
    lower = (before[:, None] < before[None, :]).astype(F32)
    picked = (picks[:, None, :] == lax.iota(jnp.int32, 2)[None, :, None]).astype(F32)
    rank = jnp.sum(picked[:, :, :, None] * lower[None, None], 2)
    slots = lax.iota(jnp.int32, CAP).astype(F32)
    dispatch = (rank[:, :, None, :] == slots[None, None, :, None]) & (picked[:, :, None, :] > 0.5)
    dispatch_low = dispatch.astype(BF)
    du = (gate * dy).astype(BF)

    def to_slots(value):
        return jnp.einsum(
            "mest,mtd->emsd", dispatch_low, value.reshape(2, 128, 1024), preferred_element_type=F32
        ).astype(BF)

    both, gi, gb, gib = moe_call(to_slots(h2), to_slots(du), win_c, wback_c, inb)
    gi_sum = lax.psum_scatter(gi, "fsdp", scatter_dimension=0, tiled=True)
    gb_sum = lax.psum_scatter(gb, "fsdp", scatter_dimension=0, tiled=True)
    unsorted = jnp.einsum(
        "mest,eamsd->amtd", dispatch.astype(F32), both,
        precision=lax.Precision.HIGHEST,
    ).reshape(2, 256, 1024)
    u = unsorted[0] + jnp.where(flat[:, None] == 1, backb[1][None], backb[0][None])
    mixed = (y1 + gate * u).astype(BF)
    dgate = jnp.sum(dy * u, -1, keepdims=True)
    pick_grad = dgate * chosen
    dlogits = probs * (pick_grad - jnp.sum(probs * pick_grad, -1, keepdims=True))
    h2f = h2.astype(F32)
    router_grad = jnp.stack([jnp.sum(h2f * dlogits[:, e : e + 1], 0) for e in (0, 1)])
    dh2 = unsorted[1] + dlogits[:, 0:1] * router_t[0][None] + dlogits[:, 1:2] * router_t[1][None]
    back2, g_two, s_two = norm_back(y1, gain2, dh2)
    dy1 = dy + back2
    da = dy1.astype(BF)
    g_outb = jnp.sum(da.astype(F32), 0)
    duf = du.astype(F32)
    g_backb = jnp.stack([jnp.sum(duf * chosen[:, e : e + 1], 0) for e in (0, 1)])
    da_all = gather_back_call(da)
    part_h, gq, gwo, gqv = attend_back_call(
        da_all, hs, qkv, o_low, o_full, lse, wqkv_c, wout_c, doc_col, doc_row
    )
    dh1 = scatter_call(part_h.reshape(8, 256, 1024), "scatter_back", 5)
    back1, g_one, s_one = norm_back(x, gain1, dh1)
    token_grad = (dy1 + back1).reshape(2, 1, 128, 1024)

    qv_full = lax.dynamic_update_slice_in_dim(jnp.zeros((2, 1024), F32), gqv, c * 128, 1)
    vectors = jnp.concatenate(
        [jnp.stack([g_one, s_one]), qv_full, jnp.stack([g_outb, g_two, s_two]), router_grad, g_backb],
        axis=0,
    )
    vectors = jnp.transpose(vectors.reshape(11, 4, 256), (1, 0, 2))
    ib_rows = lax.dynamic_update_slice_in_dim(
        jnp.zeros((4, 8, 256), F32), gib.reshape(4, 1, 256), c, 1
    )
    vectors = jnp.concatenate([vectors, ib_rows, jnp.zeros((4, 5, 256), F32)], axis=1)
    g_in, g_back, g_qkv, g_out, sums = final_call(gi_sum, gb_sum, gq, gwo, vectors)
    return (
        mixed.reshape(2, 1, 128, 1024),
        token_grad,
        sums[0], sums[1], g_qkv.astype(F32), sums[2:4], g_out.astype(F32), sums[4], sums[5], sums[6],
        jnp.transpose(sums[7:9]), g_in.astype(F32), sums[11:19].reshape(2, 1024), g_back.astype(F32),
        sums[9:11],
    )


def solution(mesh):
    small_plane = mesh.shape["ctx"] == 8 and mesh.shape["fsdp"] == 4
    chosen_body = fast_body if small_plane else body
    placed = (
        P(None, "fsdp", "ctx", None),
        P(None, "fsdp", None),
        P(None, "fsdp", "ctx", None),
        P(None, "fsdp", "ctx", None),
        P("fsdp"),
        P("fsdp"),
        P(None, "fsdp", None),
        P(None, "fsdp"),
        P("fsdp", None),
        P("fsdp"),
        P("fsdp"),
        P("fsdp"),
        P("fsdp", None),
        P(None, "fsdp", None),
        P(None, "fsdp"),
        P(None, "fsdp", None),
        P(None, "fsdp"),
    )
    return jax.shard_map(
        chosen_body,
        mesh=mesh,
        in_specs=placed,
        out_specs=(
            P(None, "fsdp", "ctx", None),
            P(None, "fsdp", "ctx", None),
            P("fsdp"),
            P("fsdp"),
            P(None, "fsdp", None),
            P(None, "fsdp"),
            P("fsdp", None),
            P("fsdp"),
            P("fsdp"),
            P("fsdp"),
            P("fsdp", None),
            P(None, "fsdp", None),
            P(None, "fsdp"),
            P(None, "fsdp", None),
            P(None, "fsdp"),
        ),
        check_vma=False,
    )
```

```python
import math

import jax
import jax.numpy as jnp
from jax import lax
from jax.experimental import pallas as pl
from jax.experimental.pallas import tpu as pltpu
from jax.sharding import PartitionSpec as P

HEADS = 16
HEAD_DIM = 64
CAP = 80


norm_eps = 1e-05
mask_fill = -1e30


def layer_norm(values, gain, shift):
    mean = jnp.mean(values, -1, keepdims=True)
    centred = values - mean
    spread = jnp.mean(centred * centred, -1, keepdims=True)
    return centred * lax.rsqrt(spread + norm_eps) * gain + shift


def natural_position(store_index, tok_rows, ctx_count):
    half = tok_rows // 2
    device = store_index // tok_rows
    slot = store_index % tok_rows
    return jnp.where(
        slot < half, device * half + slot, (2 * ctx_count - 1 - device) * half + slot - half
    )


def visible(query_pos, query_ids, key_pos, key_ids):
    return (key_pos[None, :] <= query_pos[:, None]) & (key_ids[None, :] == query_ids[:, None])


def block_needed(query_pos, query_ids, key_pos, key_ids):
    return (
        (jnp.min(key_pos) <= jnp.max(query_pos))
        & (jnp.max(key_ids) >= jnp.min(query_ids))
        & (jnp.min(key_ids) <= jnp.max(query_ids))
    )


def attend_keys(
    running, query_heads, query_pos, query_ids, key_part, value_part, pos_part, id_part, scale
):
    length = key_part.shape[0]
    stride = math.gcd(length, 512)
    key_heads = key_part.reshape(length, HEADS, HEAD_DIM)
    value_heads = value_part.reshape(length, HEADS, HEAD_DIM)

    def attend_visit_block(block_index, state):
        offset = block_index * stride
        key_blk = lax.dynamic_slice_in_dim(key_heads, offset, stride, 0)
        value_blk = lax.dynamic_slice_in_dim(value_heads, offset, stride, 0)
        key_pos = lax.dynamic_slice_in_dim(pos_part, offset, stride, 0)
        key_ids = lax.dynamic_slice_in_dim(id_part, offset, stride, 0)
        needed = block_needed(query_pos, query_ids, key_pos, key_ids)

        def update(current):
            best, totals, accum = current
            scores = (
                jnp.einsum("qhc,khc->hqk", query_heads, key_blk, preferred_element_type=jnp.float32)
                * scale
            )
            allowed = visible(query_pos, query_ids, key_pos, key_ids)[None]
            scores = jnp.where(allowed, scores, mask_fill)
            new_best = jnp.maximum(best, jnp.max(scores, -1))
            shrink = jnp.exp(best - new_best)
            weights = jnp.where(allowed, jnp.exp(scores - new_best[..., None]), 0.0)
            totals = totals * shrink + jnp.sum(weights, -1)
            addend = jnp.einsum(
                "hqk,khc->qhc",
                weights.astype(jnp.bfloat16),
                value_blk,
                preferred_element_type=jnp.float32,
            )
            accum = accum * jnp.transpose(shrink)[..., None] + addend
            return (new_best, totals, accum)

        def unchanged(current):
            return current

        return lax.cond(needed, update, unchanged, state)

    return lax.fori_loop(0, length // stride, attend_visit_block, running)


def backward_range(
    query_heads,
    grad_heads,
    log_total,
    delta,
    query_pos,
    query_ids,
    key_part,
    value_part,
    pos_part,
    id_part,
    scale,
):
    length = key_part.shape[0]
    stride = math.gcd(length, 512)
    blocks = length // stride
    key_blocks = key_part.reshape(blocks, stride, HEADS, HEAD_DIM)
    value_blocks = value_part.reshape(blocks, stride, HEADS, HEAD_DIM)
    pos_blocks = pos_part.reshape(blocks, stride)
    id_blocks = id_part.reshape(blocks, stride)
    rows = query_heads.shape[0]

    def backward_visit_block(query_acc, block_data):
        key_blk, value_blk, pos_blk, id_blk = block_data
        needed = block_needed(query_pos, query_ids, pos_blk, id_blk)

        def compute(current):
            scores = (
                jnp.einsum("qhc,khc->hqk", query_heads, key_blk, preferred_element_type=jnp.float32)
                * scale
            )
            allowed = visible(query_pos, query_ids, pos_blk, id_blk)[None]
            weights = jnp.where(allowed, jnp.exp(scores - log_total[..., None]), 0.0)
            weight_grad = jnp.einsum(
                "qhc,khc->hqk", grad_heads, value_blk, preferred_element_type=jnp.float32
            )
            score_grad = (weights * (weight_grad - delta[..., None])).astype(jnp.bfloat16)
            current = (
                current
                + jnp.einsum(
                    "hqk,khc->qhc", score_grad, key_blk, preferred_element_type=jnp.float32
                )
                * scale
            )
            terms = ()
            value_term = jnp.einsum(
                "hqk,qhc->khc",
                weights.astype(jnp.bfloat16),
                grad_heads,
                preferred_element_type=jnp.float32,
            )
            key_term = (
                jnp.einsum(
                    "hqk,qhc->khc", score_grad, query_heads, preferred_element_type=jnp.float32
                )
                * scale
            )
            terms = (key_term, value_term)
            return (current, terms)

        def skipped(current):
            terms = ()
            empty = jnp.zeros((stride, HEADS, HEAD_DIM), jnp.float32)
            terms = (empty, empty)
            return (current, terms)

        query_acc, terms = lax.cond(needed, compute, skipped, query_acc)
        terms = (
            terms[0].reshape(stride, HEADS * HEAD_DIM),
            terms[1].reshape(stride, HEADS * HEAD_DIM),
        )
        return (query_acc, terms)

    start_acc = jnp.zeros((rows, HEADS, HEAD_DIM), jnp.float32)
    query_grad, terms = lax.scan(
        backward_visit_block, start_acc, (key_blocks, value_blocks, pos_blocks, id_blocks)
    )
    return (
        query_grad,
        terms[0].reshape(length, HEADS * HEAD_DIM),
        terms[1].reshape(length, HEADS * HEAD_DIM),
    )


def gather_keys(key_rows, value_rows):
    return (
        lax.all_gather(key_rows, "ctx", axis=0, tiled=True),
        lax.all_gather(value_rows, "ctx", axis=0, tiled=True),
    )


def reduce_grads(attn_terms, expert_terms):
    g_one, s_one, g_qkv, g_qv, g_out, g_outb, g_two, s_two, g_router = attn_terms
    g_in, g_inb, g_back, g_backb = expert_terms
    e_in, e_inb, e_back, e_backb = (
        lax.psum_scatter(g_in.astype(jnp.bfloat16), "fsdp", scatter_dimension=1, tiled=True).astype(
            jnp.float32
        ),
        lax.psum_scatter(
            g_inb.astype(jnp.bfloat16), "fsdp", scatter_dimension=1, tiled=True
        ).astype(jnp.float32),
        lax.psum_scatter(
            g_back.astype(jnp.bfloat16), "fsdp", scatter_dimension=1, tiled=True
        ).astype(jnp.float32),
        lax.psum_scatter(
            g_backb.astype(jnp.bfloat16), "fsdp", scatter_dimension=1, tiled=True
        ).astype(jnp.float32),
    )
    a_one, b_one, a_qkv, a_qv, a_out, a_outb, a_two, b_two, a_router = (
        lax.psum_scatter(
            g_one.astype(jnp.bfloat16), "fsdp", scatter_dimension=0, tiled=True
        ).astype(jnp.float32),
        lax.psum_scatter(
            s_one.astype(jnp.bfloat16), "fsdp", scatter_dimension=0, tiled=True
        ).astype(jnp.float32),
        lax.psum_scatter(
            g_qkv.astype(jnp.bfloat16), "fsdp", scatter_dimension=1, tiled=True
        ).astype(jnp.float32),
        lax.psum_scatter(g_qv.astype(jnp.bfloat16), "fsdp", scatter_dimension=1, tiled=True).astype(
            jnp.float32
        ),
        lax.psum_scatter(
            g_out.astype(jnp.bfloat16), "fsdp", scatter_dimension=0, tiled=True
        ).astype(jnp.float32),
        lax.psum_scatter(
            g_outb.astype(jnp.bfloat16), "fsdp", scatter_dimension=0, tiled=True
        ).astype(jnp.float32),
        lax.psum_scatter(
            g_two.astype(jnp.bfloat16), "fsdp", scatter_dimension=0, tiled=True
        ).astype(jnp.float32),
        lax.psum_scatter(
            s_two.astype(jnp.bfloat16), "fsdp", scatter_dimension=0, tiled=True
        ).astype(jnp.float32),
        lax.psum_scatter(
            g_router.astype(jnp.bfloat16), "fsdp", scatter_dimension=0, tiled=True
        ).astype(jnp.float32),
    )
    return (
        lax.psum(a_one.astype(jnp.bfloat16), "ctx").astype(jnp.float32),
        lax.psum(b_one.astype(jnp.bfloat16), "ctx").astype(jnp.float32),
        lax.psum(a_qkv.astype(jnp.bfloat16), "ctx").astype(jnp.float32),
        lax.psum(a_qv.astype(jnp.bfloat16), "ctx").astype(jnp.float32),
        lax.psum(a_out.astype(jnp.bfloat16), "ctx").astype(jnp.float32),
        lax.psum(a_outb.astype(jnp.bfloat16), "ctx").astype(jnp.float32),
        lax.psum(a_two.astype(jnp.bfloat16), "ctx").astype(jnp.float32),
        lax.psum(b_two.astype(jnp.bfloat16), "ctx").astype(jnp.float32),
        lax.psum(a_router.astype(jnp.bfloat16), "ctx").astype(jnp.float32),
        lax.psum(e_in.astype(jnp.bfloat16), "ctx").astype(jnp.float32),
        lax.psum(e_inb.astype(jnp.bfloat16), "ctx").astype(jnp.float32),
        lax.psum(e_back.astype(jnp.bfloat16), "ctx").astype(jnp.float32),
        lax.psum(e_backb.astype(jnp.bfloat16), "ctx").astype(jnp.float32),
    )


def body(
    tokens,
    doc_ids,
    routes,
    cotangent,
    ln1_gain,
    ln1_shift,
    w_qkv,
    qv_bias,
    w_out,
    out_bias,
    ln2_gain,
    ln2_shift,
    router,
    w_in,
    in_bias,
    w_back,
    back_bias,
):
    gain_one, shift_one, proj_all, bias_qv, proj_out, bias_out, gain_two, shift_two, router_full = (
        lax.all_gather(ln1_gain, "fsdp", axis=0, tiled=True),
        lax.all_gather(ln1_shift, "fsdp", axis=0, tiled=True),
        lax.all_gather(w_qkv, "fsdp", axis=1, tiled=True),
        lax.all_gather(qv_bias, "fsdp", axis=1, tiled=True),
        lax.all_gather(w_out, "fsdp", axis=0, tiled=True),
        lax.all_gather(out_bias, "fsdp", axis=0, tiled=True),
        lax.all_gather(ln2_gain, "fsdp", axis=0, tiled=True),
        lax.all_gather(ln2_shift, "fsdp", axis=0, tiled=True),
        lax.all_gather(router, "fsdp", axis=0, tiled=True),
    )
    inner_full, inner_bias, outer_full, outer_bias = (
        lax.all_gather(w_in, "fsdp", axis=1, tiled=True),
        lax.all_gather(in_bias, "fsdp", axis=1, tiled=True),
        lax.all_gather(w_back, "fsdp", axis=1, tiled=True),
        lax.all_gather(back_bias, "fsdp", axis=1, tiled=True),
    )
    gain_one_f = gain_one.astype(jnp.float32)
    shift_one_f = shift_one.astype(jnp.float32)
    bias_qv_f = bias_qv.astype(jnp.float32)
    bias_out_f = bias_out.astype(jnp.float32)
    gain_two_f = gain_two.astype(jnp.float32)
    shift_two_f = shift_two.astype(jnp.float32)
    router_f = router_full.astype(jnp.float32)
    inner_bias_f = inner_bias.astype(jnp.float32)
    outer_bias_f = outer_bias.astype(jnp.float32)
    micro_count = tokens.shape[0]
    tok_rows = tokens.shape[2]
    width = tokens.shape[3]
    stream_len = doc_ids.shape[2]
    ctx_count = lax.axis_size("ctx")
    expert_count = inner_full.shape[0]
    scale = 1.0 / math.sqrt(HEAD_DIM)
    first_row = lax.axis_index("ctx") * tok_rows
    store_pos = natural_position(lax.iota(jnp.int32, stream_len), tok_rows, ctx_count)
    query_pos = lax.dynamic_slice_in_dim(store_pos, first_row, tok_rows, 0)
    expert_iota = lax.iota(jnp.int32, expert_count)
    slot_iota = lax.iota(jnp.int32, CAP)
    outputs = []
    input_grads = []
    totals = None
    for micro in range(micro_count):
        inputs = tokens[micro, 0].astype(jnp.float32)
        ids_store = jnp.take(doc_ids[micro, 0], store_pos)
        query_ids = lax.dynamic_slice_in_dim(ids_store, first_row, tok_rows, 0)
        picks = routes[micro, 0, :, 0]
        upstream = cotangent[micro, 0].astype(jnp.float32)
        h_first, pull_first = jax.vjp(layer_norm, inputs, gain_one_f, shift_one_f)
        h_first_low = h_first.astype(jnp.bfloat16)
        projected = jnp.einsum(
            "td,jde->jte", h_first_low, proj_all, preferred_element_type=jnp.float32
        )
        queries = (projected[0] + bias_qv_f[0]).astype(jnp.bfloat16)
        key_rows = projected[1].astype(jnp.bfloat16)
        value_rows = (projected[2] + bias_qv_f[1]).astype(jnp.bfloat16)
        query_heads = queries.reshape(tok_rows, HEADS, HEAD_DIM)
        start_state = (
            jnp.full((HEADS, tok_rows), mask_fill, jnp.float32),
            jnp.zeros((HEADS, tok_rows), jnp.float32),
            jnp.zeros((tok_rows, HEADS, HEAD_DIM), jnp.float32),
        )
        best, totals_soft, accum = attend_keys(
            start_state,
            query_heads,
            query_pos,
            query_ids,
            lax.all_gather(key_rows, "ctx", axis=0, tiled=True),
            lax.all_gather(value_rows, "ctx", axis=0, tiled=True),
            store_pos,
            ids_store,
            scale,
        )
        log_total = best + jnp.log(totals_soft)
        attended = accum / jnp.transpose(totals_soft)[..., None]
        attended_low = attended.reshape(tok_rows, width).astype(jnp.bfloat16)
        branch = jnp.dot(attended_low, proj_out, preferred_element_type=jnp.float32) + bias_out_f
        middle = inputs + branch
        h_second, pull_second = jax.vjp(layer_norm, middle, gain_two_f, shift_two_f)
        h_second_low = h_second.astype(jnp.bfloat16)
        logits = jnp.dot(h_second_low, router_full, preferred_element_type=jnp.float32)
        probs = jax.nn.softmax(logits, axis=-1)
        chosen = picks[:, None] == expert_iota[None, :]
        chosen_f = chosen.astype(jnp.float32)
        gate = jnp.sum(probs * chosen_f, -1)
        ranks = jnp.cumsum(chosen.astype(jnp.int32), 0) - 1
        dispatch = (jnp.transpose(ranks)[:, None, :] == slot_iota[None, :, None]) & jnp.transpose(
            chosen
        )[:, None, :]
        dispatch_low = dispatch.astype(jnp.bfloat16)
        dispatch_f = dispatch.astype(jnp.float32)
        slot_inputs = jnp.einsum(
            "ect,td->ecd", dispatch_low, h_second_low, preferred_element_type=jnp.float32
        ).astype(jnp.bfloat16)
        inner = (
            jnp.einsum("ecd,edh->ech", slot_inputs, inner_full, preferred_element_type=jnp.float32)
            + inner_bias_f[:, None, :]
        )
        active, pull_gelu = jax.vjp(jax.nn.gelu, inner)
        active_low = active.astype(jnp.bfloat16)
        result = (
            jnp.einsum("ech,ehd->ecd", active_low, outer_full, preferred_element_type=jnp.float32)
            + outer_bias_f[:, None, :]
        )
        expert_sum = jnp.einsum("ect,ecd->td", dispatch_f, result, precision=lax.Precision.HIGHEST)
        output = middle + gate[:, None] * expert_sum
        outputs.append(output.astype(jnp.bfloat16))
        gate_grad = jnp.sum(upstream * expert_sum, -1)
        slot_grad = jnp.einsum(
            "ect,td->ecd", dispatch_f, gate[:, None] * upstream, precision=lax.Precision.HIGHEST
        ).astype(jnp.bfloat16)
        outer_bias_grad = jnp.sum(slot_grad.astype(jnp.float32), 1)
        outer_grad = jnp.einsum(
            "ech,ecd->ehd", active_low, slot_grad, preferred_element_type=jnp.float32
        )
        active_grad = jnp.einsum(
            "ecd,ehd->ech", slot_grad, outer_full, preferred_element_type=jnp.float32
        )
        inner_grad = pull_gelu(active_grad)[0].astype(jnp.bfloat16)
        inner_bias_grad = jnp.sum(inner_grad.astype(jnp.float32), 1)
        inner_w_grad = jnp.einsum(
            "ecd,ech->edh", slot_inputs, inner_grad, preferred_element_type=jnp.float32
        )
        slot_input_grad = jnp.einsum(
            "ech,edh->ecd", inner_grad, inner_full, preferred_element_type=jnp.float32
        )
        second_grad = jnp.einsum(
            "ect,ecd->td", dispatch_f, slot_input_grad, precision=lax.Precision.HIGHEST
        )
        pick_grad = gate_grad[:, None] * chosen_f
        logit_grad = probs * (pick_grad - jnp.sum(probs * pick_grad, -1, keepdims=True))
        router_grad = jnp.einsum(
            "td,te->de",
            h_second_low.astype(jnp.float32),
            logit_grad,
            precision=lax.Precision.HIGHEST,
        )
        second_grad = second_grad + jnp.einsum(
            "te,de->td", logit_grad, router_f, precision=lax.Precision.HIGHEST
        )
        middle_norm_grad, gain_two_grad, shift_two_grad = pull_second(second_grad)
        middle_grad = upstream + middle_norm_grad
        branch_grad = middle_grad.astype(jnp.bfloat16)
        out_bias_grad = jnp.sum(branch_grad.astype(jnp.float32), 0)
        out_grad = jnp.einsum(
            "td,te->de", attended_low, branch_grad, preferred_element_type=jnp.float32
        )
        attended_grad = jnp.einsum(
            "te,de->td", branch_grad, proj_out, preferred_element_type=jnp.float32
        ).astype(jnp.bfloat16)
        grad_heads = attended_grad.reshape(tok_rows, HEADS, HEAD_DIM)
        delta = jnp.transpose(jnp.sum(grad_heads.astype(jnp.float32) * attended, -1))
        key_all, value_all = gather_keys(key_rows, value_rows)
        query_grad, key_terms, value_terms = backward_range(
            query_heads,
            grad_heads,
            log_total,
            delta,
            query_pos,
            query_ids,
            key_all,
            value_all,
            store_pos,
            ids_store,
            scale,
        )
        key_grad, value_grad = (
            lax.psum_scatter(
                key_terms.astype(jnp.bfloat16), "ctx", scatter_dimension=0, tiled=True
            ).astype(jnp.float32),
            lax.psum_scatter(
                value_terms.astype(jnp.bfloat16), "ctx", scatter_dimension=0, tiled=True
            ).astype(jnp.float32),
        )
        query_low = query_grad.reshape(tok_rows, width).astype(jnp.bfloat16)
        key_low = key_grad.astype(jnp.bfloat16)
        value_low = value_grad.astype(jnp.bfloat16)
        stacked_grad = jnp.stack([query_low, key_low, value_low])
        proj_grad = jnp.einsum(
            "td,jte->jde", h_first_low, stacked_grad, preferred_element_type=jnp.float32
        )
        qv_bias_grad = jnp.stack(
            [jnp.sum(query_low.astype(jnp.float32), 0), jnp.sum(value_low.astype(jnp.float32), 0)]
        )
        first_grad = jnp.einsum(
            "jte,jde->td", stacked_grad, proj_all, preferred_element_type=jnp.float32
        )
        input_norm_grad, gain_one_grad, shift_one_grad = pull_first(first_grad)
        input_grads.append(middle_grad + input_norm_grad)
        attn_terms = (
            gain_one_grad,
            shift_one_grad,
            proj_grad,
            qv_bias_grad,
            out_grad,
            out_bias_grad,
            gain_two_grad,
            shift_two_grad,
            router_grad,
        )
        expert_terms = (inner_w_grad, inner_bias_grad, outer_grad, outer_bias_grad)
        local_terms = attn_terms + expert_terms
        totals = local_terms if totals is None else jax.tree.map(jnp.add, totals, local_terms)
    totals = reduce_grads(totals[:9], totals[9:])
    (
        g_one,
        s_one,
        g_qkv,
        g_qv,
        g_out,
        g_outb,
        g_two,
        s_two,
        g_router,
        g_in,
        g_inb,
        g_back,
        g_backb,
    ) = totals
    mixed = jnp.stack(outputs)[:, None]
    token_grad = jnp.stack(input_grads)[:, None]
    return (
        mixed,
        token_grad,
        g_one,
        s_one,
        g_qkv,
        g_qv,
        g_out,
        g_outb,
        g_two,
        s_two,
        g_router,
        g_in,
        g_inb,
        g_back,
        g_backb,
    )


MESH_ID = pl.DeviceIdType.MESH
BF = jnp.bfloat16
F32 = jnp.float32
DMA = pltpu.SemaphoreType.DMA
VMEM_CAP = 60 * 1024 * 1024
SMALL_ROWS = 32
NT = (((1,), (1,)), ((), ()))
TN = (((0,), (0,)), ((), ()))
NN = (((1,), (0,)), ((), ()))


def mm(left, right, dims=NN):
    return lax.dot_general(left, right, dims, preferred_element_type=F32)


def plane_coords():
    me = lax.axis_index("ctx")
    core = me % 2
    col = (me // 2) % 2
    row = me // 4
    sib = me + 1 - 2 * core
    xn = (row * 2 + 1 - col) * 2 + core
    yn = ((1 - row) * 2 + col) * 2 + core
    dg = ((1 - row) * 2 + 1 - col) * 2 + core
    return me, core, sib, xn, yn, dg


def meet(ctx_peers, fsdp_peers=()):
    sem = pltpu.get_barrier_semaphore()
    for peer in ctx_peers:
        pl.semaphore_signal(sem, inc=1, device_id={"ctx": peer}, device_id_type=MESH_ID)
    for peer in fsdp_peers:
        pl.semaphore_signal(sem, inc=1, device_id={"fsdp": peer}, device_id_type=MESH_ID)
    pl.semaphore_wait(sem, len(ctx_peers) + len(fsdp_peers))


def send_to(src, dst, send_sem, recv_sem, axis, peer):
    return pltpu.make_async_remote_copy(
        src_ref=src,
        dst_ref=dst,
        send_sem=send_sem,
        recv_sem=recv_sem,
        device_id={axis: peer},
        device_id_type=MESH_ID,
    )


def gather_sems(chunks):
    return [
        DMA((2, chunks)),
        DMA((2, chunks)),
        DMA((chunks,)),
        DMA((chunks,)),
        DMA((3, chunks)),
        DMA((3, chunks)),
        DMA((chunks,)),
        DMA((chunks,)),
        DMA((chunks,)),
    ]


def interleave(*parts):
    live = list(parts)
    while live:
        for part in list(live):
            try:
                next(part)
            except StopIteration:
                live.remove(part)


def plane_gather(own, slot, chunks, sems):
    ns, nr, ds, dr, fs, fr, ss, sr, ls = sems
    me, core, sib, xn, yn, dg = plane_coords()
    near = (xn, yn)
    locals_, first, sibs, relays, forwards = [], {}, [], [], []
    for k in range(chunks):
        for i in (0, 1):
            copy = send_to(own(k), slot(me, k), ns.at[i, k], nr.at[i, k], "ctx", near[i])
            copy.start()
            first[i, k] = copy
    for k in range(chunks):
        copy = send_to(own(k), slot(me, k), ss.at[k], sr.at[k], "ctx", sib)
        copy.start()
        sibs.append(copy)
        here = pltpu.make_async_copy(own(k), slot(me, k), ls.at[k])
        here.start()
        locals_.append(here)
    yield
    for k in range(chunks):
        for i in (0, 1):
            first[i, k].wait_recv()
            if k % 2 == i:
                copy = send_to(
                    slot(near[i], k), slot(near[i], k), ds.at[k], dr.at[k], "ctx", near[1 - i]
                )
                copy.start()
                relays.append(copy)
            copy = send_to(
                slot(near[i], k), slot(near[i], k), fs.at[i, k], fr.at[i, k], "ctx", sib
            )
            copy.start()
            forwards.append(copy)
        yield
    for k in range(chunks):
        relays[k].wait_recv()
        copy = send_to(slot(dg, k), slot(dg, k), fs.at[2, k], fr.at[2, k], "ctx", sib)
        copy.start()
        forwards.append(copy)
        yield
    for copy in first.values():
        copy.wait_send()
    for copy in relays:
        copy.wait_send()
    for copy in locals_:
        copy.wait()
    for copy in sibs + forwards:
        copy.wait()


def line_sems(chunks):
    return [DMA((3, chunks)), DMA((3, chunks)), DMA((3, chunks)), DMA((3, chunks)), DMA((chunks,))]


def by_rows(count, step, visit):
    def one(index, carry):
        visit(pl.ds(pl.multiple_of(index * step, step), step))
        return carry

    lax.fori_loop(0, count // step, one, 0)


def scatter_scratch(rows, width):
    return [
        pltpu.VMEM((4, rows, width), BF),
        pltpu.VMEM((rows, width), BF),
        pltpu.VMEM((rows, width), BF),
        pltpu.VMEM((rows, width), BF),
        pltpu.VMEM((rows, width), BF),
        pltpu.VMEM((rows, width), BF),
        pltpu.VMEM((rows, width), BF),
        DMA((4,)),
        DMA((4,)),
        DMA((6,)),
        DMA((6,)),
    ]


def plane_scatter(part, rows, out, scratch):
    pair, gs, gr, xs, xr, ys, yr, s1, r1, s2, r2 = scratch
    me, core, sib, xn, yn, dg = plane_coords()
    half = rows // 2
    lo, hi = pl.ds(0, half), pl.ds(half, half)
    step = 32

    def other(peer):
        return peer + 1 - 2 * core

    def f32(value):
        return value.astype(F32)

    first = []
    for i, peer in enumerate((dg, xn, yn, me)):
        copy = send_to(part.at[other(peer)], pair.at[i], s1.at[i], r1.at[i], "ctx", sib)
        copy.start()
        first.append(copy)
    second = []

    def ship(src, dst, index, peer):
        copy = send_to(src, dst, s2.at[index], r2.at[index], "ctx", peer)
        copy.start()
        second.append(copy)

    yield
    first[0].wait_recv()

    def add_diag(rr):
        gs[rr] = (f32(part[dg, rr]) + f32(pair[0, rr])).astype(BF)

    by_rows(rows, step, add_diag)
    ship(gs.at[lo], gr.at[lo], 0, xn)
    ship(gs.at[hi], gr.at[hi], 1, yn)
    yield
    first[1].wait_recv()

    def add_x(rr):
        xs[rr] = (f32(part[xn, rr]) + f32(pair[1, rr])).astype(BF)

    by_rows(half, step, add_x)
    ship(xs.at[lo], xr.at[lo], 2, xn)
    first[2].wait_recv()

    def add_y(index):
        rr = pl.ds(half + index.start, step)
        ys[rr] = (f32(part[yn, rr]) + f32(pair[2, rr])).astype(BF)

    by_rows(half, step, add_y)
    ship(ys.at[hi], yr.at[hi], 3, yn)
    yield
    second[0].wait_recv()

    def join_y(rr):
        ys[rr] = (f32(part[yn, rr]) + f32(pair[2, rr]) + f32(gr[rr])).astype(BF)

    by_rows(half, step, join_y)
    ship(ys.at[lo], yr.at[lo], 4, yn)
    yield
    second[1].wait_recv()

    def join_x(index):
        rr = pl.ds(half + index.start, step)
        xs[rr] = (f32(part[xn, rr]) + f32(pair[1, rr]) + f32(gr[rr])).astype(BF)

    by_rows(half, step, join_x)
    ship(xs.at[hi], xr.at[hi], 5, xn)
    yield
    first[3].wait_recv()
    for index in (2, 3, 4, 5):
        second[index].wait_recv()

    def finish(rr):
        out[rr] = f32(part[me, rr]) + f32(pair[3, rr]) + f32(xr[rr]) + f32(yr[rr])

    by_rows(rows, step, finish)
    for copy in first + second:
        copy.wait_send()


def ring_ops(own, slot, sems):
    ns, nr, ds, dr, fs, fr, ss, sr, ls = sems
    me, core, sib, xn, yn, dg = plane_coords()
    near = (xn, yn)

    def away(i, k):
        return send_to(own(k), slot(me, k), ns.at[i, k], nr.at[i, k], "ctx", near[i])

    def beside(k):
        return send_to(own(k), slot(me, k), ss.at[k], sr.at[k], "ctx", sib)

    def here(k):
        return pltpu.make_async_copy(own(k), slot(me, k), ls.at[k])

    def passed(k):
        block = slot(near[k % 2], k)
        return send_to(block, block, ds.at[k], dr.at[k], "ctx", near[1 - k % 2])

    def onward(i, k):
        block = slot((xn, yn, dg)[i], k)
        return send_to(block, block, fs.at[i, k], fr.at[i, k], "ctx", sib)

    def begin(k):
        for i in (0, 1):
            away(i, k).start()
        beside(k).start()
        here(k).start()

    def relay(k):
        for i in (k % 2, 1 - k % 2):
            away(i, k).wait_recv()
            if i == k % 2:
                passed(k).start()
            onward(i, k).start()

    def diag(k):
        passed(k).wait_recv()
        onward(2, k).start()

    def done(k):
        here(k).wait()
        beside(k).wait_recv()
        for i in range(3):
            onward(i, k).wait_recv()

    def finish(k):
        for i in (0, 1):
            away(i, k).wait_send()
        beside(k).wait_send()
        passed(k).wait_send()
        for i in range(3):
            onward(i, k).wait_send()

    return begin, relay, diag, done, finish


def line_ops(own, slot, chunks, sems):
    us, ur, ws, wr, ls = sems
    z = lax.axis_index("fsdp")

    def up(d, k):
        src = own(k) if d == 0 else slot(z - d, k)
        return send_to(src, slot(z - d, k), us.at[d, k], ur.at[d, k], "fsdp", z + 1)

    def down(d, k):
        src = own(k) if d == 0 else slot(z + d, k)
        return send_to(src, slot(z + d, k), ws.at[d, k], wr.at[d, k], "fsdp", z - 1)

    def from_below(d, k):
        return send_to(own(k), slot(z - d - 1, k), us.at[d, k], ur.at[d, k], "fsdp", z - 1)

    def from_above(d, k):
        return send_to(own(k), slot(z + d + 1, k), ws.at[d, k], wr.at[d, k], "fsdp", z + 1)

    def here(k):
        return pltpu.make_async_copy(own(k), slot(z, k), ls.at[k])

    def pass_one(d, k):
        @pl.when((z < 3) & (z >= d))
        def _():
            if d:
                from_below(d - 1, k).wait_recv()
            up(d, k).start()

        @pl.when((z > 0) & (z + d <= 3))
        def _():
            if d:
                from_above(d - 1, k).wait_recv()
            down(d, k).start()

    def pass_on(d, which=None):
        for k in range(chunks) if which is None else which:
            pass_one(d, k)

    def begin():
        for k in range(chunks):
            here(k).start()
        pass_on(0)

    def arrive():
        for d in range(3):
            for k in range(chunks):

                @pl.when(z == 3)
                def _():
                    from_below(d, k).wait_recv()

                @pl.when(z == 0)
                def _():
                    from_above(d, k).wait_recv()

        for k in range(chunks):
            here(k).wait()

    def finish():
        for d in range(3):
            for k in range(chunks):

                @pl.when((z < 3) & (z >= d))
                def _():
                    up(d, k).wait_send()

                @pl.when((z > 0) & (z + d <= 3))
                def _():
                    down(d, k).wait_send()

    return begin, pass_on, arrive, finish


def sum_scratch():
    return [pltpu.VMEM((2, 4, 128, 1024), BF)] + [pltpu.VMEM((2, 128, 1024), BF)] * 6 + [
        DMA((2, 4)), DMA((2, 4)), DMA((2, 6)), DMA((2, 6)),
    ]


def sum_ops(part, m, out, scratch):
    pair, gs, gr, xs, xr, ys, yr = [ref.at[m] for ref in scratch[:7]]
    s1, r1, s2, r2 = scratch[7:]
    me, core, sib, xn, yn, dg = plane_coords()
    order = (dg, xn, yn, me)
    lo, hi = pl.ds(0, 64), pl.ds(64, 64)

    def to_pair(i):
        other = order[i] + 1 - 2 * core
        return send_to(part.at[m, other], pair.at[i], s1.at[m, i], r1.at[m, i], "ctx", sib)

    def ship(index):
        src, dst, peer = (
            (gs.at[lo], gr.at[lo], xn),
            (gs.at[hi], gr.at[hi], yn),
            (xs.at[lo], xr.at[lo], xn),
            (ys.at[hi], yr.at[hi], yn),
            (ys.at[lo], yr.at[lo], yn),
            (xs.at[hi], xr.at[hi], xn),
        )[index]
        return send_to(src, dst, s2.at[m, index], r2.at[m, index], "ctx", peer)

    def f32(value):
        return value.astype(F32)

    def both(i, rr):
        return f32(part[m, order[i], rr]) + f32(pair[i, rr])

    def begin():
        for i in range(4):
            to_pair(i).start()

    def span(offset, count, visit):
        def one(index):
            visit(pl.ds(offset + index.start, 32))

        by_rows(count, 32, one)

    def diag():
        to_pair(0).wait_recv()

        def add(rr):
            gs[rr] = both(0, rr).astype(BF)

        span(0, 128, add)
        ship(0).start()
        ship(1).start()

    def near():
        to_pair(1).wait_recv()

        def add_x(rr):
            xs[rr] = both(1, rr).astype(BF)

        span(0, 64, add_x)
        ship(2).start()
        to_pair(2).wait_recv()

        def add_y(rr):
            ys[rr] = both(2, rr).astype(BF)

        span(64, 64, add_y)
        ship(3).start()

    def join():
        ship(0).wait_recv()

        def add_y(rr):
            ys[rr] = (both(2, rr) + f32(gr[rr])).astype(BF)

        span(0, 64, add_y)
        ship(4).start()
        ship(1).wait_recv()

        def add_x(rr):
            xs[rr] = (both(1, rr) + f32(gr[rr])).astype(BF)

        span(64, 64, add_x)
        ship(5).start()

    def finish():
        to_pair(3).wait_recv()
        for index in (2, 3, 4, 5):
            ship(index).wait_recv()

        def add(rr):
            place = pl.ds(m * 128 + rr.start, 32)
            out[place] = both(3, rr) + f32(xr[rr]) + f32(yr[rr])

        span(0, 128, add)
        for i in range(4):
            to_pair(i).wait_send()
        for index in range(6):
            ship(index).wait_send()

    return begin, diag, near, join, finish


def vmem_spec():
    return pl.BlockSpec(memory_space=pltpu.VMEM)


def any_spec():
    return pl.BlockSpec(memory_space=pl.ANY)


def natural_slot(device, k):
    micro, part = k // 2, k % 2
    return micro * 16 + (device if part == 0 else 15 - device)


def remote_params(ident):
    return pltpu.CompilerParams(
        collective_id=ident, has_side_effects=True, vmem_limit_bytes=VMEM_CAP
    )


def line_peers():
    z = lax.axis_index("fsdp")
    return [(z + d) % 4 for d in (1, 2, 3)]


def token_docs(row_ref, m):
    row = jnp.broadcast_to(row_ref[pl.ds(m, 1), :].astype(F32), (8, 1024))
    return row[0:1], jnp.transpose(row)[:, 0:1]


def front_kernel(
    x_ref, small_ref, doc_ref, wq_ref, wo_ref, wi_ref,
    h_ref, params_ref, wqc_ref, woc_ref, wic_ref, qkv_ref, of_ref, lse_ref, out_ref,
    hs, units, part, zs, zr, os, orr, ol, *sems,
):
    me, core, sib, xn, yn, dg = plane_coords()
    z = lax.axis_index("fsdp")
    peers = line_peers()
    meet((sib, xn, yn), peers)
    params_ref[z] = small_ref[...]
    copies = []
    for i, peer in enumerate(peers):
        copy = send_to(small_ref, params_ref.at[z], zs.at[i], zr.at[i], "fsdp", peer)
        copy.start()
        copies.append(copy)
    owner = me // 2
    columns = pl.ds(pl.multiple_of(me * 128, 128), 128)
    expert, quarter = me // 4, me % 4

    def wq_slot(where, k):
        return wqc_ref.at[k, pl.ds(pl.multiple_of(where * 256, 256), 256)]

    def wi_own(k):
        return wi_ref.at[expert, :, pl.ds(pl.multiple_of(k * 1024 + quarter * 256, 256), 256)]

    def wi_slot(where, k):
        return wic_ref.at[pl.ds(pl.multiple_of(where * 256, 256), 256), pl.ds(256 * k, 256)]

    q_begin, q_pass, q_arrive, q_finish = line_ops(
        lambda k: wq_ref.at[k, :, columns], wq_slot, 3, sems[:5]
    )
    i_begin, i_pass, i_arrive, i_finish = line_ops(wi_own, wi_slot, 4, sems[5:10])
    begin, relay, diag, done, finish = ring_ops(
        lambda k: hs.at[pl.ds(64 * k, 64)],
        lambda device, k: h_ref.at[natural_slot(device, k)],
        sems[10:19],
    )
    sums = [sum_ops(part, m, out_ref, sems[19:]) for m in (0, 1)]
    q_begin()

    wo_own = wo_ref.at[pl.ds(pl.multiple_of(core * 128, 128), 128)]

    def wo_step(src, side):
        return send_to(
            src, woc_ref, os.at[side], orr.at[side], "fsdp", z + 1 if side == 0 else z - 1
        )

    def wo_both(act):
        @pl.when((z >= owner) & (z < 3))
        def _():
            act(0)

        @pl.when((z <= owner) & (z > 0))
        def _():
            act(1)

    def wo_begin():
        @pl.when(z == owner)
        def _():
            pltpu.make_async_copy(wo_own, woc_ref, ol).start()
            wo_both(lambda side: wo_step(wo_own, side).start())

    def wo_arrive():
        @pl.when(z > owner)
        def _():
            wo_step(woc_ref, 0).wait_recv()

        @pl.when(z < owner)
        def _():
            wo_step(woc_ref, 1).wait_recv()

    def wo_pass(d):
        @pl.when((z == owner + d) | (z == owner - d))
        def _():
            wo_arrive()
            wo_both(lambda side: wo_step(woc_ref, side).start())

    def wo_last():
        @pl.when((z == owner + 3) | (z == owner - 3))
        def _():
            wo_arrive()

        @pl.when(z == owner)
        def _():
            pltpu.make_async_copy(wo_own, woc_ref, ol).wait()

    wo_begin()

    def unit(rr):
        values = x_ref[rr].astype(F32)
        centred = values - jnp.mean(values, -1, keepdims=True)
        spread = jnp.mean(centred * centred, -1, keepdims=True)
        units[rr] = centred * lax.rsqrt(spread + norm_eps)

    by_rows(256, 32, unit)
    for copy in copies:
        copy.wait()

    def full_row(r):
        return jnp.concatenate([params_ref[i, r : r + 1, :] for i in range(4)], axis=1).astype(F32)

    gain, shift = full_row(0), full_row(1)

    def norm(rr):
        hs[rr] = (units[rr] * gain + shift).astype(BF)

    by_rows(256, 32, norm)
    begin(0)
    begin(1)
    q_pass(1)
    relay(0)
    relay(1)
    begin(2)
    begin(3)
    wo_pass(1)
    q_pass(2)
    i_begin()
    diag(0)
    diag(1)
    wo_pass(2)
    done(0)
    done(1)
    q_arrive()
    half = pl.ds(pl.multiple_of(core * 128, 128), 128)
    q_bias = params_ref[owner, 2:3, half].astype(F32)
    v_bias = params_ref[owner, 3:4, half].astype(F32)
    masks = head_masks(256)
    vmasks = head_masks(1024)
    zero = jnp.zeros((), BF)

    def micro(m, carry):
        @pl.when(m == 1)
        def _():
            done(2)
            done(3)

        h = h_ref[pl.ds(16 * m, 16)].reshape(1024, 1024)
        place = pl.ds(pl.multiple_of(m * 1024, 1024), 1024)
        q = (mm(h, wqc_ref[0]) + q_bias).astype(BF)
        k = mm(h, wqc_ref[1]).astype(BF)
        v = (mm(h, wqc_ref[2]) + v_bias).astype(BF)
        qkv_ref[0, place] = q
        qkv_ref[1, place] = k
        qkv_ref[2, place] = v
        vh = [jnp.where(vmasks[j], v, zero) for j in (0, 1)]
        doc_row, doc_col = token_docs(doc_ref, m)
        for i in range(4):
            length = 256 * (i + 1)
            rows = slice(256 * i, 256 * (i + 1))
            qi = q[rows] * jnp.asarray(0.125, BF)
            allowed = allowed_mask(i, doc_col[rows], doc_row[:, :length])
            total = None
            stats = []
            for j in (0, 1):
                s = mm(jnp.where(masks[j], qi, zero), k[:length], NT)
                s = jnp.where(allowed, s, mask_fill)
                top = jnp.max(s, -1, keepdims=True)
                e = jnp.exp(s - top)
                den = jnp.sum(e, -1, keepdims=True)
                p = (e * (1.0 / den)).astype(BF)
                term = mm(p, vh[j][:length])
                total = term if total is None else total + term
                stats.append(top + jnp.log(den))
            at = pl.ds(pl.multiple_of(m * 1024 + 256 * i, 256), 256)
            lse_ref[at] = jnp.where(masks[0], stats[0], stats[1])
            of_ref[at] = total

            @pl.when(m == 0)
            def _():
                if i == 0:
                    relay(2)
                    relay(3)
                if i == 1:
                    i_pass(1, (0,))
                    diag(2)
                if i == 2:
                    i_pass(1, (1,))
                    diag(3)
                if i == 3:
                    wo_last()

            @pl.when(m == 1)
            def _():
                if i == 1:
                    sums[0][3]()
                if i == 3:
                    i_pass(2, (0,))

        for i in range(4):
            at = pl.ds(pl.multiple_of(m * 1024 + 256 * i, 256), 256)
            a = mm(of_ref[at].astype(BF), woc_ref[...]).astype(BF)
            for b in range(4):
                block = 4 * i + b
                dest, side = (block, 0) if block < 8 else (15 - block, 1)
                part[m, dest, 64 * side : 64 * (side + 1)] = a[64 * b : 64 * (b + 1)]

        for n in (0, 1):

            @pl.when(m == n)
            def _():
                for step in sums[n][:3]:
                    step()
                if n == 0:
                    i_pass(1, (2, 3))

        return carry

    lax.fori_loop(0, 2, micro, 0)
    i_pass(2, (1,))
    sums[1][3]()
    i_pass(2, (2, 3))
    sums[0][4]()
    sums[1][4]()
    i_arrive()
    wo_both(lambda side: wo_step(woc_ref, side).wait_send())
    q_finish()
    i_finish()
    for k in range(4):
        finish(k)


def front_call(x, small, docs, w_qkv, w_out, w_in):
    return pl.pallas_call(
        front_kernel,
        out_shape=(
            jax.ShapeDtypeStruct((32, 64, 1024), BF),
            jax.ShapeDtypeStruct((4, SMALL_ROWS, 256), BF),
            jax.ShapeDtypeStruct((3, 1024, 128), BF),
            jax.ShapeDtypeStruct((128, 1024), BF),
            jax.ShapeDtypeStruct((1024, 1024), BF),
            jax.ShapeDtypeStruct((3, 2048, 128), BF),
            jax.ShapeDtypeStruct((2048, 128), F32),
            jax.ShapeDtypeStruct((2048, 128), F32),
            jax.ShapeDtypeStruct((256, 1024), F32),
        ),
        in_specs=[vmem_spec()] * 3 + [any_spec()] * 3,
        out_specs=[vmem_spec()] * 4 + [any_spec()] + [vmem_spec()] * 4,
        scratch_shapes=[
            pltpu.VMEM((256, 1024), BF),
            pltpu.VMEM((256, 1024), F32),
            pltpu.VMEM((2, 8, 128, 1024), BF),
            DMA((3,)),
            DMA((3,)),
            DMA((2,)),
            DMA((2,)),
            DMA(()),
        ]
        + line_sems(3)
        + line_sems(4)
        + gather_sems(4)
        + sum_scratch(),
        name="front",
        compiler_params=remote_params(0),
    )(x, small, docs, w_qkv, w_out, w_in)


def scatter_call(part, name, ident):
    def kernel(p_ref, o_ref, *scratch):
        me, core, sib, xn, yn, dg = plane_coords()
        meet((sib, xn, yn))
        interleave(plane_scatter(p_ref, 256, o_ref, scratch))

    return pl.pallas_call(
        kernel,
        out_shape=jax.ShapeDtypeStruct((256, 1024), F32),
        in_specs=[vmem_spec()],
        out_specs=vmem_spec(),
        scratch_shapes=scatter_scratch(256, 1024),
        name=name,
        compiler_params=remote_params(ident),
    )(part)


def moe_call(h_slots, d_slots, win, w_back, inb):
    def kernel(
        h_ref, d_ref, wi_ref, wall_ref, ib_ref, o_ref, gi_ref, gb_ref, gib_ref,
        wb_ref, rows, gz, slope, dz, part, pair, sent, got,
        ns, nr, fs, fr, ss, sr, ls, s1, r1, s2, r2, *wsems,
    ):
        me, core, sib, xn, yn, dg = plane_coords()
        expert, quarter = me // 4, me % 4
        meet((sib, xn, yn, dg), line_peers())
        w_begin, w_pass, w_arrive, w_finish = line_ops(
            lambda k: wall_ref.at[expert, pl.ds(pl.multiple_of(quarter * 256 + 64 * k, 64), 64)],
            lambda where, k: wb_ref.at[pl.ds(pl.multiple_of(where * 256 + 64 * k, 64), 64)],
            4,
            wsems,
        )
        w_begin()
        peers = (dg, xn, yn)
        wanted = (1 - expert, expert, 1 - expert)
        ins = (h_ref, d_ref)

        def away(t, m, i):
            return send_to(
                ins[t].at[wanted[i], m], rows.at[t, m, me], ns.at[t, m, i], nr.at[t, m, i], "ctx", peers[i]
            )

        def beside(t, m):
            return send_to(
                ins[t].at[expert, m], rows.at[t, m, me], ss.at[t, m], sr.at[t, m], "ctx", sib
            )

        def here(t, m):
            return pltpu.make_async_copy(ins[t].at[expert, m], rows.at[t, m, me], ls.at[t, m])

        def onward(t, m, i):
            block = rows.at[t, m, peers[i]]
            return send_to(block, block, fs.at[t, m, i], fr.at[t, m, i], "ctx", sib)

        for t in (0, 1):
            for m in (0, 1):
                for i in range(3):
                    away(t, m, i).start()
        for t in (0, 1):
            for m in (0, 1):
                beside(t, m).start()
                here(t, m).start()

        def arrive(t, m):
            for i in range(3):
                away(t, m, i).wait_recv()
                onward(t, m, i).start()
            here(t, m).wait()
            beside(t, m).wait_recv()
            for i in range(3):
                onward(t, m, i).wait_recv()

        order = (dg, xn, yn, me)

        def to_pair(t, m, i):
            other = order[i] + 1 - 2 * core
            return send_to(
                part.at[t, m, other], pair.at[t, m, i], s1.at[t, m, i], r1.at[t, m, i], "ctx", sib
            )

        def to_home(t, m, i):
            return send_to(
                sent.at[t, m, i], got.at[t, m, i], s2.at[t, m, i], r2.at[t, m, i], "ctx", order[i]
            )

        def join(t, m):
            for i in range(3):
                to_pair(t, m, i).wait_recv()
                mine = order[i]

                def add(rr):
                    sent[t, m, i, rr] = (
                        part[t, m, mine, rr].astype(F32) + pair[t, m, i, rr].astype(F32)
                    ).astype(BF)

                by_rows(CAP, 16, add)
                to_home(t, m, i).start()

        def inner_rows(m):
            def visit(half, carry):
                xs = rows[0, m, pl.ds(4 * half, 4)].reshape(4 * CAP, 1024)
                zed = mm(xs, wi_ref[...]) + ib_ref[...]
                square = zed * zed
                t = jnp.tanh(zed * (GELU_A + GELU_A * GELU_B * square))
                half_up = 0.5 + 0.5 * t
                place = pl.ds(pl.multiple_of(m * 8 * CAP + half * 4 * CAP, 4 * CAP), 4 * CAP)
                gz[place] = (zed * half_up).astype(BF)
                slope[place] = half_up + 0.5 * zed * (1.0 - t * t) * (
                    GELU_A + 3.0 * GELU_A * GELU_B * square
                )
                return carry

            lax.fori_loop(0, 2, visit, 0)

        def inner(m, carry):
            @pl.when(m == 0)
            def _():
                w_pass(1, (0, 1))

            arrive(0, m)

            @pl.when(m == 0)
            def _():
                w_pass(1, (2,))

            inner_rows(m)

            @pl.when(m == 0)
            def _():
                w_pass(1, (3,))

            return carry

        lax.fori_loop(0, 2, inner, 0)
        w_pass(2, (0, 1))
        arrive(1, 0)
        w_pass(2, (2, 3))
        arrive(1, 1)
        w_arrive()

        def forward(m, carry):
            def visit(half, inner_carry):
                place = pl.ds(pl.multiple_of(m * 8 * CAP + half * 4 * CAP, 4 * CAP), 4 * CAP)
                u = mm(gz[place], wb_ref[...]).astype(BF)
                part[0, m, pl.ds(4 * half, 4)] = u.reshape(4, CAP, 1024)
                return inner_carry

            lax.fori_loop(0, 2, visit, 0)
            for i in range(4):
                to_pair(0, m, i).start()
            return carry

        lax.fori_loop(0, 2, forward, 0)
        join(0, 0)
        join(0, 1)
        gib_ref[...] = jnp.zeros_like(gib_ref)

        def backward(m, carry):
            def rows_backward(half, inner_carry):
                du = rows[1, m, pl.ds(4 * half, 4)].reshape(4 * CAP, 1024)
                place = pl.ds(pl.multiple_of(m * 8 * CAP + half * 4 * CAP, 4 * CAP), 4 * CAP)
                low = (mm(du, wb_ref[...], NT) * slope[place]).astype(BF)
                dz[place] = low
                gib_ref[...] += jnp.sum(low.astype(F32), 0, keepdims=True)
                dh = mm(low, wi_ref[...], NT).astype(BF)
                part[1, m, pl.ds(4 * half, 4)] = dh.reshape(4, CAP, 1024)
                return inner_carry

            lax.fori_loop(0, 2, rows_backward, 0)
            for i in range(4):
                to_pair(1, m, i).start()
            join(1, m)
            return carry

        lax.fori_loop(0, 2, backward, 0)

        def back_grads(j, carry):
            column = pl.ds(pl.multiple_of(256 * j, 256), 256)
            du = rows[1].reshape(16 * CAP, 1024)
            gb_ref[column] = mm(gz[:, column], du, TN).astype(BF)
            return carry

        lax.fori_loop(0, 4, back_grads, 0)

        def weight_grads(j, carry):
            column = pl.ds(pl.multiple_of(256 * j, 256), 256)
            xs = rows[0, :, :, :, column].reshape(16 * CAP, 256)
            gi_ref[column] = mm(xs, dz[...], TN).astype(BF)
            return carry

        lax.fori_loop(0, 4, weight_grads, 0)
        for t in (0, 1):
            for m in (0, 1):
                to_pair(t, m, 3).wait_recv()
                for i in range(3):
                    to_home(t, m, i).wait_recv()

                def finish(rr):
                    o_ref[expert, t, m, rr] = (
                        part[t, m, me, rr].astype(F32)
                        + pair[t, m, 3, rr].astype(F32)
                        + got[t, m, 1, rr].astype(F32)
                    )
                    o_ref[1 - expert, t, m, rr] = got[t, m, 0, rr].astype(F32) + got[
                        t, m, 2, rr
                    ].astype(F32)

                by_rows(CAP, 16, finish)
        for t in (0, 1):
            for m in (0, 1):
                for i in range(3):
                    away(t, m, i).wait_send()
                    onward(t, m, i).wait_send()
                    to_home(t, m, i).wait_send()
                for i in range(4):
                    to_pair(t, m, i).wait_send()
                beside(t, m).wait_send()
        w_finish()

    return pl.pallas_call(
        kernel,
        out_shape=(
            jax.ShapeDtypeStruct((2, 2, 2, CAP, 1024), F32),
            jax.ShapeDtypeStruct((1024, 1024), BF),
            jax.ShapeDtypeStruct((1024, 1024), BF),
            jax.ShapeDtypeStruct((1, 1024), F32),
        ),
        in_specs=[vmem_spec()] * 3 + [any_spec(), vmem_spec()],
        out_specs=[vmem_spec()] * 4,
        scratch_shapes=[
            pltpu.VMEM((1024, 1024), BF),
            pltpu.VMEM((2, 2, 8, CAP, 1024), BF),
            pltpu.VMEM((16 * CAP, 1024), BF),
            pltpu.VMEM((16 * CAP, 1024), F32),
            pltpu.VMEM((16 * CAP, 1024), BF),
            pltpu.VMEM((2, 2, 8, CAP, 1024), BF),
            pltpu.VMEM((2, 2, 4, CAP, 1024), BF),
            pltpu.VMEM((2, 2, 3, CAP, 1024), BF),
            pltpu.VMEM((2, 2, 3, CAP, 1024), BF),
        ]
        + [DMA((2, 2, 3))] * 4
        + [DMA((2, 2))] * 3
        + [DMA((2, 2, 4))] * 2
        + [DMA((2, 2, 3))] * 2
        + line_sems(4),
        name="moe",
        compiler_params=remote_params(2),
    )(h_slots, d_slots, win, w_back, inb)


def gather_back_call(da):
    def kernel(a_ref, o_ref, *scratch):
        me, core, sib, xn, yn, dg = plane_coords()
        meet((sib, xn, yn))
        tokens_ring = plane_gather(
            lambda k: a_ref.at[pl.ds(64 * k, 64)],
            lambda device, k: o_ref.at[natural_slot(device, k)],
            4,
            scratch,
        )
        interleave(tokens_ring)

    return pl.pallas_call(
        kernel,
        out_shape=jax.ShapeDtypeStruct((32, 64, 1024), BF),
        in_specs=[vmem_spec()],
        out_specs=any_spec(),
        scratch_shapes=gather_sems(4),
        name="gather_back",
        compiler_params=remote_params(4),
    )(da)


def final_call(gi, gb, gq, gwo, vectors):
    def kernel(
        gi_ref, gb_ref, gq_ref, go_ref, v_ref,
        oi_ref, ob_ref, oq_ref, oo_ref, ov_ref,
        qgot, qsum, ogot, osum, vgot, vsum, vall,
        qs, qr, os, orr, vs, vr, ps, pr, ws, wr, fs, fr, ol, *sems,
    ):
        me, core, sib, xn, yn, dg = plane_coords()
        z = lax.axis_index("fsdp")
        peers = line_peers()
        others = [(me + d) % 8 for d in range(1, 8)]
        meet(others, peers)
        expert, quarter = me // 4, me % 4
        owner = me // 2

        vcopies = []
        for d in (1, 2, 3):
            peer = (z + d) % 4
            copy = send_to(v_ref.at[peer], vgot.at[d - 1], vs.at[d - 1], vr.at[d - 1], "fsdp", peer)
            copy.start()
            vcopies.append(copy)

        def qblock(where):
            return gq_ref.at[:, pl.ds(pl.multiple_of(where * 256, 256), 256)]

        qcopies = []
        for d in (1, 3, 2):
            peer = (z + d) % 4
            copy = send_to(qblock(peer), qgot.at[d - 1], qs.at[d - 1], qr.at[d - 1], "fsdp", peer)
            copy.start()
            qcopies.append(copy)
        away = (owner - z + 4) % 4

        def to_owner():
            return send_to(go_ref, ogot.at[away - 1], os, orr.at[away - 1], "fsdp", owner)

        @pl.when(z != owner)
        def _():
            to_owner().start()

        def own(k):
            if k < 4:
                return gi_ref.at[:, pl.ds(256 * k, 256)]
            return gb_ref.at[pl.ds(64 * (k - 4), 64)]

        def slot(device, k):
            which, part = device // 4, device % 4
            if k < 4:
                column = pl.multiple_of(k * 1024 + part * 256, 256)
                return oi_ref.at[which, :, pl.ds(column, 256)]
            row = pl.multiple_of(part * 256 + 64 * (k - 4), 64)
            return ob_ref.at[which, pl.ds(row, 64)]

        big = plane_gather(own, slot, 8, sems[:9])
        next(big)
        for copy in vcopies:
            copy.wait()
        vsum[...] = v_ref[z] + vgot[0] + vgot[1] + vgot[2]
        pcopies = []
        for i, peer in enumerate(others):
            copy = send_to(vsum, vall.at[i], ps.at[i], pr.at[i], "ctx", peer)
            copy.start()
            pcopies.append(copy)
        for copy in qcopies:
            copy.wait_recv()
        for j in range(3):

            def add(rr):
                row = pl.ds(pl.multiple_of(z * 256 + rr.start, 32), 32)
                total = gq_ref[j, row].astype(F32)
                for i in range(3):
                    total = total + qgot[i, j, rr].astype(F32)
                qsum[j, rr] = total.astype(BF)

            by_rows(256, 32, add)

        def qslot(device, k):
            return oq_ref.at[k, :, pl.ds(pl.multiple_of(device * 128, 128), 128)]

        second = plane_gather(lambda k: qsum.at[k], qslot, 3, sems[9:18])
        next(second)
        spread = [xn, yn, dg]
        rows_mine = oo_ref.at[pl.ds(pl.multiple_of(core * 128, 128), 128)]
        rows_sib = oo_ref.at[pl.ds(pl.multiple_of((1 - core) * 128, 128), 128)]

        @pl.when(z == owner)
        def _():
            for i in range(3):
                send_to(go_ref, ogot.at[i], os, orr.at[i], "fsdp", (z + 1) % 4).wait_recv()

            def add(rr):
                total = go_ref[rr].astype(F32)
                for i in range(3):
                    total = total + ogot[i, rr].astype(F32)
                osum[rr] = total.astype(BF)

            by_rows(128, 32, add)
            for i, peer in enumerate(spread):
                send_to(osum, rows_mine, ws.at[i], wr, "ctx", peer).start()
            send_to(osum, rows_mine, fs, fr, "ctx", sib).start()
            pltpu.make_async_copy(osum, rows_mine, ol).start()

        interleave(big, second)

        @pl.when(z == owner)
        def _():
            for i, peer in enumerate(spread):
                send_to(osum, rows_mine, ws.at[i], wr, "ctx", peer).wait_send()
            send_to(osum, rows_mine, fs, fr, "ctx", sib).wait_send()
            pltpu.make_async_copy(osum, rows_mine, ol).wait()

        @pl.when(z != owner)
        def _():
            to_owner().wait_send()
            send_to(osum, rows_mine, ws.at[0], wr, "ctx", xn).wait_recv()
            send_to(rows_mine, rows_mine, fs, fr, "ctx", sib).start()
            send_to(rows_mine, rows_mine, fs, fr, "ctx", sib).wait_send()

        send_to(osum, rows_sib, fs, fr, "ctx", sib).wait_recv()
        for copy in qcopies:
            copy.wait_send()
        total = vsum[...]
        for i, copy in enumerate(pcopies):
            copy.wait_recv()
            total = total + vall[i]
        ov_ref[...] = total
        for copy in pcopies:
            copy.wait_send()

    count = vectors.shape[1]
    return pl.pallas_call(
        kernel,
        out_shape=(
            jax.ShapeDtypeStruct((2, 256, 4096), BF),
            jax.ShapeDtypeStruct((2, 1024, 1024), BF),
            jax.ShapeDtypeStruct((3, 256, 1024), BF),
            jax.ShapeDtypeStruct((256, 1024), BF),
            jax.ShapeDtypeStruct((count, 256), F32),
        ),
        in_specs=[vmem_spec()] * 5,
        out_specs=[any_spec()] * 4 + [vmem_spec()],
        scratch_shapes=[
            pltpu.VMEM((3, 3, 256, 128), BF),
            pltpu.VMEM((3, 256, 128), BF),
            pltpu.VMEM((3, 128, 1024), BF),
            pltpu.VMEM((128, 1024), BF),
            pltpu.VMEM((3, count, 256), F32),
            pltpu.VMEM((count, 256), F32),
            pltpu.VMEM((7, count, 256), F32),
            DMA((3,)), DMA((3,)), DMA(()), DMA((3,)), DMA((3,)), DMA((3,)), DMA((7,)), DMA((7,)),
            DMA((3,)), DMA(()), DMA(()), DMA(()), DMA(()),
        ]
        + gather_sems(8)
        + gather_sems(3),
        name="final",
        compiler_params=remote_params(6),
    )(gi, gb, gq, gwo, vectors)


def head_masks(rows):
    lane = lax.broadcasted_iota(jnp.int32, (rows, 128), 1)
    return lane < 64, lane >= 64


def allowed_mask(i, doc_col, doc_row):
    length = 256 * (i + 1)
    qpos = lax.broadcasted_iota(jnp.int32, (256, length), 0) + 256 * i
    kpos = lax.broadcasted_iota(jnp.int32, (256, length), 1)
    return (kpos <= qpos) & (doc_col == doc_row)


def attend_back_kernel(
    g_ref, h_ref, qkv_ref, of_ref, lse_ref, w_ref, wo_ref, doc_ref,
    part_ref, gw_ref, gwo_ref, gb_ref, accw, acco, accb, dka, dva,
):
    m = pl.program_id(0)
    g = g_ref[...].reshape(1024, 1024)
    h = h_ref[...].reshape(1024, 1024)
    q, k, v = qkv_ref[0], qkv_ref[1], qkv_ref[2]
    doc_row, doc_col = token_docs(doc_ref, m)
    do = mm(g, wo_ref[...], NT).astype(BF)
    masks = head_masks(256)
    kmasks = head_masks(1024)
    zero = jnp.zeros((), BF)
    dka[...] = jnp.zeros_like(dka)
    dva[...] = jnp.zeros_like(dva)
    dqs = []
    kh = [jnp.where(kmasks[j], k, zero) for j in (0, 1)]
    for i in range(4):
        length = 256 * (i + 1)
        rows = slice(256 * i, 256 * (i + 1))
        qi = q[rows] * jnp.asarray(0.125, BF)
        doi = do[rows]
        allowed = allowed_mask(i, doc_col[rows], doc_row[:, :length])
        prod = doi.astype(F32) * of_ref[rows]
        lse = lse_ref[rows]
        dq = None
        for j in (0, 1):
            qh = jnp.where(masks[j], qi, zero)
            doh = jnp.where(masks[j], doi, zero)
            delta = jnp.sum(jnp.where(masks[j], prod, 0.0), -1, keepdims=True)
            s = mm(qh, k[:length], NT)
            p = jnp.exp(jnp.where(allowed, s, mask_fill) - lse[:, 64 * j : 64 * j + 1])
            dp = mm(doh, v[:length], NT)
            ds = (p * (dp - delta)).astype(BF)
            term = mm(ds, kh[j][:length])
            dq = term if dq is None else dq + term
            dka[:length] += mm(ds, qh, TN)
            dva[:length] += mm(p.astype(BF), doh, TN)
        dqs.append((dq * 0.125).astype(BF))
    dq = jnp.concatenate(dqs, axis=0)
    dk = dka[...].astype(BF)
    dv = dva[...].astype(BF)

    @pl.when(m == 0)
    def _():
        accw[...] = jnp.zeros_like(accw)
        acco[...] = jnp.zeros_like(acco)
        accb[...] = jnp.zeros_like(accb)

    acco[...] += mm(of_ref[...].astype(BF), g, TN)
    for j, d in enumerate((dq, dk, dv)):
        accw[j] += mm(h, d, TN)
    accb[0:1] += jnp.sum(dq.astype(F32), 0, keepdims=True)
    accb[1:2] += jnp.sum(dv.astype(F32), 0, keepdims=True)
    for i in range(4):
        rows = slice(256 * i, 256 * (i + 1))
        a = (mm(dq[rows], w_ref[0], NT) + mm(dk[rows], w_ref[1], NT) + mm(dv[rows], w_ref[2], NT)).astype(BF)
        for b in range(4):
            block = 4 * i + b
            dest, part = (block, 0) if block < 8 else (15 - block, 1)
            part_ref[dest, 0, part] = a[64 * b : 64 * (b + 1)]

    @pl.when(m == 1)
    def _():
        gw_ref[...] = accw[...].astype(BF)
        gwo_ref[...] = acco[...].astype(BF)
        gb_ref[...] = accb[...]


def attend_back_call(g, h, qkv, of, lse, wqkv, wout, docs):
    const2 = lambda m: (0, 0)
    const3 = lambda m: (0, 0, 0)
    return pl.pallas_call(
        attend_back_kernel,
        grid=(2,),
        out_shape=(
            jax.ShapeDtypeStruct((8, 2, 2, 64, 1024), BF),
            jax.ShapeDtypeStruct((3, 1024, 128), BF),
            jax.ShapeDtypeStruct((128, 1024), BF),
            jax.ShapeDtypeStruct((2, 128), F32),
        ),
        in_specs=[
            pl.BlockSpec((16, 64, 1024), lambda m: (m, 0, 0)),
            pl.BlockSpec((16, 64, 1024), lambda m: (m, 0, 0)),
            pl.BlockSpec((3, 1024, 128), lambda m: (0, m, 0)),
            pl.BlockSpec((1024, 128), lambda m: (m, 0)),
            pl.BlockSpec((1024, 128), lambda m: (m, 0)),
            pl.BlockSpec((3, 1024, 128), const3),
            pl.BlockSpec((128, 1024), const2),
            pl.BlockSpec((2, 1024), const2),
        ],
        out_specs=(
            pl.BlockSpec((8, 1, 2, 64, 1024), lambda m: (0, m, 0, 0, 0)),
            pl.BlockSpec((3, 1024, 128), const3),
            pl.BlockSpec((128, 1024), const2),
            pl.BlockSpec((2, 128), const2),
        ),
        scratch_shapes=[
            pltpu.VMEM((3, 1024, 128), F32),
            pltpu.VMEM((128, 1024), F32),
            pltpu.VMEM((2, 128), F32),
            pltpu.VMEM((1024, 128), F32),
            pltpu.VMEM((1024, 128), F32),
        ],
        name="attend_back",
        compiler_params=pltpu.CompilerParams(vmem_limit_bytes=VMEM_CAP),
    )(g, h, qkv, of, lse, wqkv, wout, docs)


GELU_A = math.sqrt(2.0 / math.pi)
GELU_B = 0.044715


def norm_back(values, gain, grad):
    mean = jnp.mean(values, -1, keepdims=True)
    centred = values - mean
    inv = lax.rsqrt(jnp.mean(centred * centred, -1, keepdims=True) + norm_eps)
    unit = centred * inv
    scaled = grad * gain
    back = inv * (
        scaled
        - jnp.mean(scaled, -1, keepdims=True)
        - unit * jnp.mean(scaled * unit, -1, keepdims=True)
    )
    return back, jnp.sum(grad * unit, 0), jnp.sum(grad, 0)


def fast_body(
    tokens, doc_ids, routes, cotangent, ln1_gain, ln1_shift, w_qkv, qv_bias, w_out, out_bias,
    ln2_gain, ln2_shift, router, w_in, in_bias, w_back, back_bias,
):
    c = lax.axis_index("ctx")
    rows = [ln1_gain, ln1_shift, qv_bias[0], qv_bias[1], out_bias, ln2_gain, ln2_shift]
    rows += [router[:, 0], router[:, 1]]
    rows += [in_bias[e, 256 * k : 256 * (k + 1)] for e in (0, 1) for k in range(4)]
    rows += [back_bias[0], back_bias[1]]
    row_iota = lax.broadcasted_iota(jnp.int32, (SMALL_ROWS, 256), 0)
    small = jnp.zeros((SMALL_ROWS, 256), BF)
    for index, row in enumerate(rows):
        small = jnp.where(row_iota == index, row[None], small)
    x_low = tokens[:, 0].reshape(256, 1024)
    picks = routes[:, 0, :, 0]
    docs = doc_ids[:, 0]
    hs, params, wqkv_c, wout_c, win_c, qkv, o_full, lse, branch = front_call(
        x_low, small, docs, w_qkv, w_out, w_in
    )
    params = params.astype(F32)
    row_of = lambda r: params[:, r].reshape(1024)
    gain1, outb, gain2, shift2 = row_of(0), row_of(4), row_of(5), row_of(6)
    router_t = jnp.stack([row_of(7), row_of(8)])
    backb = jnp.stack([row_of(17), row_of(18)])
    inb = lax.dynamic_index_in_dim(params[:, 9:17], c, 1, keepdims=False).reshape(1, 1024)

    x = x_low.astype(F32)
    dy = cotangent[:, 0].reshape(256, 1024).astype(F32)
    y1 = x + (branch + outb)
    h2 = layer_norm(y1, gain2, shift2).astype(BF)
    logits = lax.dot_general(h2, router_t.astype(BF), NT, preferred_element_type=F32)
    probs = jax.nn.softmax(logits, axis=-1)
    flat = picks.reshape(256)
    chosen = (flat[:, None] == lax.iota(jnp.int32, 2)[None, :]).astype(F32)
    gate = jnp.sum(probs * chosen, -1, keepdims=True)
    before = lax.iota(jnp.int32, 128)
    lower = (before[:, None] < before[None, :]).astype(F32)
    picked = (picks[:, None, :] == lax.iota(jnp.int32, 2)[None, :, None]).astype(F32)
    rank = jnp.sum(picked[:, :, :, None] * lower[None, None], 2)
    slots = lax.iota(jnp.int32, CAP).astype(F32)
    dispatch = (rank[:, :, None, :] == slots[None, None, :, None]) & (picked[:, :, None, :] > 0.5)
    dispatch_low = dispatch.astype(BF)
    du = (gate * dy).astype(BF)

    def to_slots(value):
        return jnp.einsum(
            "mest,mtd->emsd", dispatch_low, value.reshape(2, 128, 1024), preferred_element_type=F32
        ).astype(BF)

    both, gi, gb, gib = moe_call(to_slots(h2), to_slots(du), win_c, w_back, inb)
    gi_sum = lax.psum_scatter(gi, "fsdp", scatter_dimension=0, tiled=True)
    gb_sum = lax.psum_scatter(gb, "fsdp", scatter_dimension=0, tiled=True)
    unsorted = jnp.einsum(
        "mest,eamsd->amtd", dispatch.astype(F32), both,
        precision=lax.Precision.HIGHEST,
    ).reshape(2, 256, 1024)
    u = unsorted[0] + jnp.where(flat[:, None] == 1, backb[1][None], backb[0][None])
    mixed = (y1 + gate * u).astype(BF)
    dgate = jnp.sum(dy * u, -1, keepdims=True)
    pick_grad = dgate * chosen
    dlogits = probs * (pick_grad - jnp.sum(probs * pick_grad, -1, keepdims=True))
    h2f = h2.astype(F32)
    router_grad = jnp.stack([jnp.sum(h2f * dlogits[:, e : e + 1], 0) for e in (0, 1)])
    dh2 = unsorted[1] + dlogits[:, 0:1] * router_t[0][None] + dlogits[:, 1:2] * router_t[1][None]
    back2, g_two, s_two = norm_back(y1, gain2, dh2)
    dy1 = dy + back2
    da = dy1.astype(BF)
    g_outb = jnp.sum(da.astype(F32), 0)
    duf = du.astype(F32)
    g_backb = jnp.stack([jnp.sum(duf * chosen[:, e : e + 1], 0) for e in (0, 1)])
    da_all = gather_back_call(da)
    part_h, gq, gwo, gqv = attend_back_call(
        da_all, hs, qkv, o_full, lse, wqkv_c, wout_c, docs
    )
    dh1 = scatter_call(part_h.reshape(8, 256, 1024), "scatter_back", 5)
    back1, g_one, s_one = norm_back(x, gain1, dh1)
    token_grad = (dy1 + back1).reshape(2, 1, 128, 1024)

    qv_full = lax.dynamic_update_slice_in_dim(jnp.zeros((2, 1024), F32), gqv, c * 128, 1)
    vectors = jnp.concatenate(
        [jnp.stack([g_one, s_one]), qv_full, jnp.stack([g_outb, g_two, s_two]), router_grad, g_backb],
        axis=0,
    )
    vectors = jnp.transpose(vectors.reshape(11, 4, 256), (1, 0, 2))
    ib_rows = lax.dynamic_update_slice_in_dim(
        jnp.zeros((4, 8, 256), F32), gib.reshape(4, 1, 256), c, 1
    )
    vectors = jnp.concatenate([vectors, ib_rows, jnp.zeros((4, 5, 256), F32)], axis=1)
    g_in, g_back, g_qkv, g_out, sums = final_call(gi_sum, gb_sum, gq, gwo, vectors)
    return (
        mixed.reshape(2, 1, 128, 1024),
        token_grad,
        sums[0], sums[1], g_qkv.astype(F32), sums[2:4], g_out.astype(F32), sums[4], sums[5], sums[6],
        jnp.transpose(sums[7:9]), g_in.astype(F32), sums[11:19].reshape(2, 1024), g_back.astype(F32),
        sums[9:11],
    )


def solution(mesh):
    small_plane = mesh.shape["ctx"] == 8 and mesh.shape["fsdp"] == 4
    chosen_body = fast_body if small_plane else body
    placed = (
        P(None, "fsdp", "ctx", None),
        P(None, "fsdp", None),
        P(None, "fsdp", "ctx", None),
        P(None, "fsdp", "ctx", None),
        P("fsdp"),
        P("fsdp"),
        P(None, "fsdp", None),
        P(None, "fsdp"),
        P("fsdp", None),
        P("fsdp"),
        P("fsdp"),
        P("fsdp"),
        P("fsdp", None),
        P(None, "fsdp", None),
        P(None, "fsdp"),
        P(None, "fsdp", None),
        P(None, "fsdp"),
    )
    return jax.shard_map(
        chosen_body,
        mesh=mesh,
        in_specs=placed,
        out_specs=(
            P(None, "fsdp", "ctx", None),
            P(None, "fsdp", "ctx", None),
            P("fsdp"),
            P("fsdp"),
            P(None, "fsdp", None),
            P(None, "fsdp"),
            P("fsdp", None),
            P("fsdp"),
            P("fsdp"),
            P("fsdp"),
            P("fsdp", None),
            P(None, "fsdp", None),
            P(None, "fsdp"),
            P(None, "fsdp", None),
            P(None, "fsdp"),
        ),
        check_vma=False,
    )
```

```python
import math

import jax
import jax.numpy as jnp
from jax import lax
from jax.experimental import pallas as pl
from jax.experimental.pallas import tpu as pltpu
from jax.sharding import PartitionSpec as P

HEADS = 16
HEAD_DIM = 64
CAP = 80


norm_eps = 1e-05
mask_fill = -1e30


def layer_norm(values, gain, shift):
    mean = jnp.mean(values, -1, keepdims=True)
    centred = values - mean
    spread = jnp.mean(centred * centred, -1, keepdims=True)
    return centred * lax.rsqrt(spread + norm_eps) * gain + shift


def natural_position(store_index, tok_rows, ctx_count):
    half = tok_rows // 2
    device = store_index // tok_rows
    slot = store_index % tok_rows
    return jnp.where(
        slot < half, device * half + slot, (2 * ctx_count - 1 - device) * half + slot - half
    )


def visible(query_pos, query_ids, key_pos, key_ids):
    return (key_pos[None, :] <= query_pos[:, None]) & (key_ids[None, :] == query_ids[:, None])


def block_needed(query_pos, query_ids, key_pos, key_ids):
    return (
        (jnp.min(key_pos) <= jnp.max(query_pos))
        & (jnp.max(key_ids) >= jnp.min(query_ids))
        & (jnp.min(key_ids) <= jnp.max(query_ids))
    )


def attend_keys(
    running, query_heads, query_pos, query_ids, key_part, value_part, pos_part, id_part, scale
):
    length = key_part.shape[0]
    stride = math.gcd(length, 512)
    key_heads = key_part.reshape(length, HEADS, HEAD_DIM)
    value_heads = value_part.reshape(length, HEADS, HEAD_DIM)

    def attend_visit_block(block_index, state):
        offset = block_index * stride
        key_blk = lax.dynamic_slice_in_dim(key_heads, offset, stride, 0)
        value_blk = lax.dynamic_slice_in_dim(value_heads, offset, stride, 0)
        key_pos = lax.dynamic_slice_in_dim(pos_part, offset, stride, 0)
        key_ids = lax.dynamic_slice_in_dim(id_part, offset, stride, 0)
        needed = block_needed(query_pos, query_ids, key_pos, key_ids)

        def update(current):
            best, totals, accum = current
            scores = (
                jnp.einsum("qhc,khc->hqk", query_heads, key_blk, preferred_element_type=jnp.float32)
                * scale
            )
            allowed = visible(query_pos, query_ids, key_pos, key_ids)[None]
            scores = jnp.where(allowed, scores, mask_fill)
            new_best = jnp.maximum(best, jnp.max(scores, -1))
            shrink = jnp.exp(best - new_best)
            weights = jnp.where(allowed, jnp.exp(scores - new_best[..., None]), 0.0)
            totals = totals * shrink + jnp.sum(weights, -1)
            addend = jnp.einsum(
                "hqk,khc->qhc",
                weights.astype(jnp.bfloat16),
                value_blk,
                preferred_element_type=jnp.float32,
            )
            accum = accum * jnp.transpose(shrink)[..., None] + addend
            return (new_best, totals, accum)

        def unchanged(current):
            return current

        return lax.cond(needed, update, unchanged, state)

    return lax.fori_loop(0, length // stride, attend_visit_block, running)


def backward_range(
    query_heads,
    grad_heads,
    log_total,
    delta,
    query_pos,
    query_ids,
    key_part,
    value_part,
    pos_part,
    id_part,
    scale,
):
    length = key_part.shape[0]
    stride = math.gcd(length, 512)
    blocks = length // stride
    key_blocks = key_part.reshape(blocks, stride, HEADS, HEAD_DIM)
    value_blocks = value_part.reshape(blocks, stride, HEADS, HEAD_DIM)
    pos_blocks = pos_part.reshape(blocks, stride)
    id_blocks = id_part.reshape(blocks, stride)
    rows = query_heads.shape[0]

    def backward_visit_block(query_acc, block_data):
        key_blk, value_blk, pos_blk, id_blk = block_data
        needed = block_needed(query_pos, query_ids, pos_blk, id_blk)

        def compute(current):
            scores = (
                jnp.einsum("qhc,khc->hqk", query_heads, key_blk, preferred_element_type=jnp.float32)
                * scale
            )
            allowed = visible(query_pos, query_ids, pos_blk, id_blk)[None]
            weights = jnp.where(allowed, jnp.exp(scores - log_total[..., None]), 0.0)
            weight_grad = jnp.einsum(
                "qhc,khc->hqk", grad_heads, value_blk, preferred_element_type=jnp.float32
            )
            score_grad = (weights * (weight_grad - delta[..., None])).astype(jnp.bfloat16)
            current = (
                current
                + jnp.einsum(
                    "hqk,khc->qhc", score_grad, key_blk, preferred_element_type=jnp.float32
                )
                * scale
            )
            terms = ()
            value_term = jnp.einsum(
                "hqk,qhc->khc",
                weights.astype(jnp.bfloat16),
                grad_heads,
                preferred_element_type=jnp.float32,
            )
            key_term = (
                jnp.einsum(
                    "hqk,qhc->khc", score_grad, query_heads, preferred_element_type=jnp.float32
                )
                * scale
            )
            terms = (key_term, value_term)
            return (current, terms)

        def skipped(current):
            terms = ()
            empty = jnp.zeros((stride, HEADS, HEAD_DIM), jnp.float32)
            terms = (empty, empty)
            return (current, terms)

        query_acc, terms = lax.cond(needed, compute, skipped, query_acc)
        terms = (
            terms[0].reshape(stride, HEADS * HEAD_DIM),
            terms[1].reshape(stride, HEADS * HEAD_DIM),
        )
        return (query_acc, terms)

    start_acc = jnp.zeros((rows, HEADS, HEAD_DIM), jnp.float32)
    query_grad, terms = lax.scan(
        backward_visit_block, start_acc, (key_blocks, value_blocks, pos_blocks, id_blocks)
    )
    return (
        query_grad,
        terms[0].reshape(length, HEADS * HEAD_DIM),
        terms[1].reshape(length, HEADS * HEAD_DIM),
    )


def gather_keys(key_rows, value_rows):
    return (
        lax.all_gather(key_rows, "ctx", axis=0, tiled=True),
        lax.all_gather(value_rows, "ctx", axis=0, tiled=True),
    )


def reduce_grads(attn_terms, expert_terms):
    g_one, s_one, g_qkv, g_qv, g_out, g_outb, g_two, s_two, g_router = attn_terms
    g_in, g_inb, g_back, g_backb = expert_terms
    e_in, e_inb, e_back, e_backb = (
        lax.psum_scatter(g_in.astype(jnp.bfloat16), "fsdp", scatter_dimension=1, tiled=True).astype(
            jnp.float32
        ),
        lax.psum_scatter(
            g_inb.astype(jnp.bfloat16), "fsdp", scatter_dimension=1, tiled=True
        ).astype(jnp.float32),
        lax.psum_scatter(
            g_back.astype(jnp.bfloat16), "fsdp", scatter_dimension=1, tiled=True
        ).astype(jnp.float32),
        lax.psum_scatter(
            g_backb.astype(jnp.bfloat16), "fsdp", scatter_dimension=1, tiled=True
        ).astype(jnp.float32),
    )
    a_one, b_one, a_qkv, a_qv, a_out, a_outb, a_two, b_two, a_router = (
        lax.psum_scatter(
            g_one.astype(jnp.bfloat16), "fsdp", scatter_dimension=0, tiled=True
        ).astype(jnp.float32),
        lax.psum_scatter(
            s_one.astype(jnp.bfloat16), "fsdp", scatter_dimension=0, tiled=True
        ).astype(jnp.float32),
        lax.psum_scatter(
            g_qkv.astype(jnp.bfloat16), "fsdp", scatter_dimension=1, tiled=True
        ).astype(jnp.float32),
        lax.psum_scatter(g_qv.astype(jnp.bfloat16), "fsdp", scatter_dimension=1, tiled=True).astype(
            jnp.float32
        ),
        lax.psum_scatter(
            g_out.astype(jnp.bfloat16), "fsdp", scatter_dimension=0, tiled=True
        ).astype(jnp.float32),
        lax.psum_scatter(
            g_outb.astype(jnp.bfloat16), "fsdp", scatter_dimension=0, tiled=True
        ).astype(jnp.float32),
        lax.psum_scatter(
            g_two.astype(jnp.bfloat16), "fsdp", scatter_dimension=0, tiled=True
        ).astype(jnp.float32),
        lax.psum_scatter(
            s_two.astype(jnp.bfloat16), "fsdp", scatter_dimension=0, tiled=True
        ).astype(jnp.float32),
        lax.psum_scatter(
            g_router.astype(jnp.bfloat16), "fsdp", scatter_dimension=0, tiled=True
        ).astype(jnp.float32),
    )
    return (
        lax.psum(a_one.astype(jnp.bfloat16), "ctx").astype(jnp.float32),
        lax.psum(b_one.astype(jnp.bfloat16), "ctx").astype(jnp.float32),
        lax.psum(a_qkv.astype(jnp.bfloat16), "ctx").astype(jnp.float32),
        lax.psum(a_qv.astype(jnp.bfloat16), "ctx").astype(jnp.float32),
        lax.psum(a_out.astype(jnp.bfloat16), "ctx").astype(jnp.float32),
        lax.psum(a_outb.astype(jnp.bfloat16), "ctx").astype(jnp.float32),
        lax.psum(a_two.astype(jnp.bfloat16), "ctx").astype(jnp.float32),
        lax.psum(b_two.astype(jnp.bfloat16), "ctx").astype(jnp.float32),
        lax.psum(a_router.astype(jnp.bfloat16), "ctx").astype(jnp.float32),
        lax.psum(e_in.astype(jnp.bfloat16), "ctx").astype(jnp.float32),
        lax.psum(e_inb.astype(jnp.bfloat16), "ctx").astype(jnp.float32),
        lax.psum(e_back.astype(jnp.bfloat16), "ctx").astype(jnp.float32),
        lax.psum(e_backb.astype(jnp.bfloat16), "ctx").astype(jnp.float32),
    )


def body(
    tokens,
    doc_ids,
    routes,
    cotangent,
    ln1_gain,
    ln1_shift,
    w_qkv,
    qv_bias,
    w_out,
    out_bias,
    ln2_gain,
    ln2_shift,
    router,
    w_in,
    in_bias,
    w_back,
    back_bias,
):
    gain_one, shift_one, proj_all, bias_qv, proj_out, bias_out, gain_two, shift_two, router_full = (
        lax.all_gather(ln1_gain, "fsdp", axis=0, tiled=True),
        lax.all_gather(ln1_shift, "fsdp", axis=0, tiled=True),
        lax.all_gather(w_qkv, "fsdp", axis=1, tiled=True),
        lax.all_gather(qv_bias, "fsdp", axis=1, tiled=True),
        lax.all_gather(w_out, "fsdp", axis=0, tiled=True),
        lax.all_gather(out_bias, "fsdp", axis=0, tiled=True),
        lax.all_gather(ln2_gain, "fsdp", axis=0, tiled=True),
        lax.all_gather(ln2_shift, "fsdp", axis=0, tiled=True),
        lax.all_gather(router, "fsdp", axis=0, tiled=True),
    )
    inner_full, inner_bias, outer_full, outer_bias = (
        lax.all_gather(w_in, "fsdp", axis=1, tiled=True),
        lax.all_gather(in_bias, "fsdp", axis=1, tiled=True),
        lax.all_gather(w_back, "fsdp", axis=1, tiled=True),
        lax.all_gather(back_bias, "fsdp", axis=1, tiled=True),
    )
    gain_one_f = gain_one.astype(jnp.float32)
    shift_one_f = shift_one.astype(jnp.float32)
    bias_qv_f = bias_qv.astype(jnp.float32)
    bias_out_f = bias_out.astype(jnp.float32)
    gain_two_f = gain_two.astype(jnp.float32)
    shift_two_f = shift_two.astype(jnp.float32)
    router_f = router_full.astype(jnp.float32)
    inner_bias_f = inner_bias.astype(jnp.float32)
    outer_bias_f = outer_bias.astype(jnp.float32)
    micro_count = tokens.shape[0]
    tok_rows = tokens.shape[2]
    width = tokens.shape[3]
    stream_len = doc_ids.shape[2]
    ctx_count = lax.axis_size("ctx")
    expert_count = inner_full.shape[0]
    scale = 1.0 / math.sqrt(HEAD_DIM)
    first_row = lax.axis_index("ctx") * tok_rows
    store_pos = natural_position(lax.iota(jnp.int32, stream_len), tok_rows, ctx_count)
    query_pos = lax.dynamic_slice_in_dim(store_pos, first_row, tok_rows, 0)
    expert_iota = lax.iota(jnp.int32, expert_count)
    slot_iota = lax.iota(jnp.int32, CAP)
    outputs = []
    input_grads = []
    totals = None
    for micro in range(micro_count):
        inputs = tokens[micro, 0].astype(jnp.float32)
        ids_store = jnp.take(doc_ids[micro, 0], store_pos)
        query_ids = lax.dynamic_slice_in_dim(ids_store, first_row, tok_rows, 0)
        picks = routes[micro, 0, :, 0]
        upstream = cotangent[micro, 0].astype(jnp.float32)
        h_first, pull_first = jax.vjp(layer_norm, inputs, gain_one_f, shift_one_f)
        h_first_low = h_first.astype(jnp.bfloat16)
        projected = jnp.einsum(
            "td,jde->jte", h_first_low, proj_all, preferred_element_type=jnp.float32
        )
        queries = (projected[0] + bias_qv_f[0]).astype(jnp.bfloat16)
        key_rows = projected[1].astype(jnp.bfloat16)
        value_rows = (projected[2] + bias_qv_f[1]).astype(jnp.bfloat16)
        query_heads = queries.reshape(tok_rows, HEADS, HEAD_DIM)
        start_state = (
            jnp.full((HEADS, tok_rows), mask_fill, jnp.float32),
            jnp.zeros((HEADS, tok_rows), jnp.float32),
            jnp.zeros((tok_rows, HEADS, HEAD_DIM), jnp.float32),
        )
        best, totals_soft, accum = attend_keys(
            start_state,
            query_heads,
            query_pos,
            query_ids,
            lax.all_gather(key_rows, "ctx", axis=0, tiled=True),
            lax.all_gather(value_rows, "ctx", axis=0, tiled=True),
            store_pos,
            ids_store,
            scale,
        )
        log_total = best + jnp.log(totals_soft)
        attended = accum / jnp.transpose(totals_soft)[..., None]
        attended_low = attended.reshape(tok_rows, width).astype(jnp.bfloat16)
        branch = jnp.dot(attended_low, proj_out, preferred_element_type=jnp.float32) + bias_out_f
        middle = inputs + branch
        h_second, pull_second = jax.vjp(layer_norm, middle, gain_two_f, shift_two_f)
        h_second_low = h_second.astype(jnp.bfloat16)
        logits = jnp.dot(h_second_low, router_full, preferred_element_type=jnp.float32)
        probs = jax.nn.softmax(logits, axis=-1)
        chosen = picks[:, None] == expert_iota[None, :]
        chosen_f = chosen.astype(jnp.float32)
        gate = jnp.sum(probs * chosen_f, -1)
        ranks = jnp.cumsum(chosen.astype(jnp.int32), 0) - 1
        dispatch = (jnp.transpose(ranks)[:, None, :] == slot_iota[None, :, None]) & jnp.transpose(
            chosen
        )[:, None, :]
        dispatch_low = dispatch.astype(jnp.bfloat16)
        dispatch_f = dispatch.astype(jnp.float32)
        slot_inputs = jnp.einsum(
            "ect,td->ecd", dispatch_low, h_second_low, preferred_element_type=jnp.float32
        ).astype(jnp.bfloat16)
        inner = (
            jnp.einsum("ecd,edh->ech", slot_inputs, inner_full, preferred_element_type=jnp.float32)
            + inner_bias_f[:, None, :]
        )
        active, pull_gelu = jax.vjp(jax.nn.gelu, inner)
        active_low = active.astype(jnp.bfloat16)
        result = (
            jnp.einsum("ech,ehd->ecd", active_low, outer_full, preferred_element_type=jnp.float32)
            + outer_bias_f[:, None, :]
        )
        expert_sum = jnp.einsum("ect,ecd->td", dispatch_f, result, precision=lax.Precision.HIGHEST)
        output = middle + gate[:, None] * expert_sum
        outputs.append(output.astype(jnp.bfloat16))
        gate_grad = jnp.sum(upstream * expert_sum, -1)
        slot_grad = jnp.einsum(
            "ect,td->ecd", dispatch_f, gate[:, None] * upstream, precision=lax.Precision.HIGHEST
        ).astype(jnp.bfloat16)
        outer_bias_grad = jnp.sum(slot_grad.astype(jnp.float32), 1)
        outer_grad = jnp.einsum(
            "ech,ecd->ehd", active_low, slot_grad, preferred_element_type=jnp.float32
        )
        active_grad = jnp.einsum(
            "ecd,ehd->ech", slot_grad, outer_full, preferred_element_type=jnp.float32
        )
        inner_grad = pull_gelu(active_grad)[0].astype(jnp.bfloat16)
        inner_bias_grad = jnp.sum(inner_grad.astype(jnp.float32), 1)
        inner_w_grad = jnp.einsum(
            "ecd,ech->edh", slot_inputs, inner_grad, preferred_element_type=jnp.float32
        )
        slot_input_grad = jnp.einsum(
            "ech,edh->ecd", inner_grad, inner_full, preferred_element_type=jnp.float32
        )
        second_grad = jnp.einsum(
            "ect,ecd->td", dispatch_f, slot_input_grad, precision=lax.Precision.HIGHEST
        )
        pick_grad = gate_grad[:, None] * chosen_f
        logit_grad = probs * (pick_grad - jnp.sum(probs * pick_grad, -1, keepdims=True))
        router_grad = jnp.einsum(
            "td,te->de",
            h_second_low.astype(jnp.float32),
            logit_grad,
            precision=lax.Precision.HIGHEST,
        )
        second_grad = second_grad + jnp.einsum(
            "te,de->td", logit_grad, router_f, precision=lax.Precision.HIGHEST
        )
        middle_norm_grad, gain_two_grad, shift_two_grad = pull_second(second_grad)
        middle_grad = upstream + middle_norm_grad
        branch_grad = middle_grad.astype(jnp.bfloat16)
        out_bias_grad = jnp.sum(branch_grad.astype(jnp.float32), 0)
        out_grad = jnp.einsum(
            "td,te->de", attended_low, branch_grad, preferred_element_type=jnp.float32
        )
        attended_grad = jnp.einsum(
            "te,de->td", branch_grad, proj_out, preferred_element_type=jnp.float32
        ).astype(jnp.bfloat16)
        grad_heads = attended_grad.reshape(tok_rows, HEADS, HEAD_DIM)
        delta = jnp.transpose(jnp.sum(grad_heads.astype(jnp.float32) * attended, -1))
        key_all, value_all = gather_keys(key_rows, value_rows)
        query_grad, key_terms, value_terms = backward_range(
            query_heads,
            grad_heads,
            log_total,
            delta,
            query_pos,
            query_ids,
            key_all,
            value_all,
            store_pos,
            ids_store,
            scale,
        )
        key_grad, value_grad = (
            lax.psum_scatter(
                key_terms.astype(jnp.bfloat16), "ctx", scatter_dimension=0, tiled=True
            ).astype(jnp.float32),
            lax.psum_scatter(
                value_terms.astype(jnp.bfloat16), "ctx", scatter_dimension=0, tiled=True
            ).astype(jnp.float32),
        )
        query_low = query_grad.reshape(tok_rows, width).astype(jnp.bfloat16)
        key_low = key_grad.astype(jnp.bfloat16)
        value_low = value_grad.astype(jnp.bfloat16)
        stacked_grad = jnp.stack([query_low, key_low, value_low])
        proj_grad = jnp.einsum(
            "td,jte->jde", h_first_low, stacked_grad, preferred_element_type=jnp.float32
        )
        qv_bias_grad = jnp.stack(
            [jnp.sum(query_low.astype(jnp.float32), 0), jnp.sum(value_low.astype(jnp.float32), 0)]
        )
        first_grad = jnp.einsum(
            "jte,jde->td", stacked_grad, proj_all, preferred_element_type=jnp.float32
        )
        input_norm_grad, gain_one_grad, shift_one_grad = pull_first(first_grad)
        input_grads.append(middle_grad + input_norm_grad)
        attn_terms = (
            gain_one_grad,
            shift_one_grad,
            proj_grad,
            qv_bias_grad,
            out_grad,
            out_bias_grad,
            gain_two_grad,
            shift_two_grad,
            router_grad,
        )
        expert_terms = (inner_w_grad, inner_bias_grad, outer_grad, outer_bias_grad)
        local_terms = attn_terms + expert_terms
        totals = local_terms if totals is None else jax.tree.map(jnp.add, totals, local_terms)
    totals = reduce_grads(totals[:9], totals[9:])
    (
        g_one,
        s_one,
        g_qkv,
        g_qv,
        g_out,
        g_outb,
        g_two,
        s_two,
        g_router,
        g_in,
        g_inb,
        g_back,
        g_backb,
    ) = totals
    mixed = jnp.stack(outputs)[:, None]
    token_grad = jnp.stack(input_grads)[:, None]
    return (
        mixed,
        token_grad,
        g_one,
        s_one,
        g_qkv,
        g_qv,
        g_out,
        g_outb,
        g_two,
        s_two,
        g_router,
        g_in,
        g_inb,
        g_back,
        g_backb,
    )


MESH_ID = pl.DeviceIdType.MESH
BF = jnp.bfloat16
F32 = jnp.float32
DMA = pltpu.SemaphoreType.DMA
VMEM_CAP = 60 * 1024 * 1024
SMALL_ROWS = 32
NT = (((1,), (1,)), ((), ()))
TN = (((0,), (0,)), ((), ()))
NN = (((1,), (0,)), ((), ()))


def mm(left, right, dims=NN):
    return lax.dot_general(left, right, dims, preferred_element_type=F32)


def plane_coords():
    me = lax.axis_index("ctx")
    core = me % 2
    col = (me // 2) % 2
    row = me // 4
    sib = me + 1 - 2 * core
    xn = (row * 2 + 1 - col) * 2 + core
    yn = ((1 - row) * 2 + col) * 2 + core
    dg = ((1 - row) * 2 + 1 - col) * 2 + core
    return me, core, sib, xn, yn, dg


def meet(ctx_peers, fsdp_peers=()):
    sem = pltpu.get_barrier_semaphore()
    for peer in ctx_peers:
        pl.semaphore_signal(sem, inc=1, device_id={"ctx": peer}, device_id_type=MESH_ID)
    for peer in fsdp_peers:
        pl.semaphore_signal(sem, inc=1, device_id={"fsdp": peer}, device_id_type=MESH_ID)
    pl.semaphore_wait(sem, len(ctx_peers) + len(fsdp_peers))


def send_to(src, dst, send_sem, recv_sem, axis, peer):
    return pltpu.make_async_remote_copy(
        src_ref=src,
        dst_ref=dst,
        send_sem=send_sem,
        recv_sem=recv_sem,
        device_id={axis: peer},
        device_id_type=MESH_ID,
    )


def gather_sems(chunks):
    return [
        DMA((2, chunks)),
        DMA((2, chunks)),
        DMA((chunks,)),
        DMA((chunks,)),
        DMA((3, chunks)),
        DMA((3, chunks)),
        DMA((chunks,)),
        DMA((chunks,)),
        DMA((chunks,)),
    ]


def line_sems(chunks):
    return [DMA((3, chunks)), DMA((3, chunks)), DMA((3, chunks)), DMA((3, chunks)), DMA((chunks,))]


def by_rows(count, step, visit):
    def one(index, carry):
        visit(pl.ds(pl.multiple_of(index * step, step), step))
        return carry

    lax.fori_loop(0, count // step, one, 0)


def ring_ops(own, slot, sems):
    ns, nr, ds, dr, fs, fr, ss, sr, ls = sems
    me, core, sib, xn, yn, dg = plane_coords()
    near = (xn, yn)

    def away(i, k):
        return send_to(own(k), slot(me, k), ns.at[i, k], nr.at[i, k], "ctx", near[i])

    def beside(k):
        return send_to(own(k), slot(me, k), ss.at[k], sr.at[k], "ctx", sib)

    def here(k):
        return pltpu.make_async_copy(own(k), slot(me, k), ls.at[k])

    def passed(k):
        block = slot(near[k % 2], k)
        return send_to(block, block, ds.at[k], dr.at[k], "ctx", near[1 - k % 2])

    def onward(i, k):
        block = slot((xn, yn, dg)[i], k)
        return send_to(block, block, fs.at[i, k], fr.at[i, k], "ctx", sib)

    def begin(k):
        for i in (0, 1):
            away(i, k).start()
        beside(k).start()
        here(k).start()

    def relay(k):
        for i in (k % 2, 1 - k % 2):
            away(i, k).wait_recv()
            if i == k % 2:
                passed(k).start()
            onward(i, k).start()

    def diag(k):
        passed(k).wait_recv()
        onward(2, k).start()

    def done(k):
        here(k).wait()
        beside(k).wait_recv()
        for i in range(3):
            onward(i, k).wait_recv()

    def finish(k):
        for i in (0, 1):
            away(i, k).wait_send()
        beside(k).wait_send()
        passed(k).wait_send()
        for i in range(3):
            onward(i, k).wait_send()

    return begin, relay, diag, done, finish


def line_ops(own, slot, chunks, sems):
    us, ur, ws, wr, ls = sems
    z = lax.axis_index("fsdp")

    def up(d, k):
        src = own(k) if d == 0 else slot(z - d, k)
        return send_to(src, slot(z - d, k), us.at[d, k], ur.at[d, k], "fsdp", z + 1)

    def down(d, k):
        src = own(k) if d == 0 else slot(z + d, k)
        return send_to(src, slot(z + d, k), ws.at[d, k], wr.at[d, k], "fsdp", z - 1)

    def from_below(d, k):
        return send_to(own(k), slot(z - d - 1, k), us.at[d, k], ur.at[d, k], "fsdp", z - 1)

    def from_above(d, k):
        return send_to(own(k), slot(z + d + 1, k), ws.at[d, k], wr.at[d, k], "fsdp", z + 1)

    def here(k):
        return pltpu.make_async_copy(own(k), slot(z, k), ls.at[k])

    def pass_one(d, k):
        @pl.when((z < 3) & (z >= d))
        def _():
            if d:
                from_below(d - 1, k).wait_recv()
            up(d, k).start()

        @pl.when((z > 0) & (z + d <= 3))
        def _():
            if d:
                from_above(d - 1, k).wait_recv()
            down(d, k).start()

    def pass_on(d, which=None):
        for k in range(chunks) if which is None else which:
            pass_one(d, k)

    def begin():
        for k in range(chunks):
            here(k).start()
        pass_on(0)

    def arrive():
        for d in range(3):
            for k in range(chunks):

                @pl.when(z == 3)
                def _():
                    from_below(d, k).wait_recv()

                @pl.when(z == 0)
                def _():
                    from_above(d, k).wait_recv()

        for k in range(chunks):
            here(k).wait()

    def finish():
        for d in range(3):
            for k in range(chunks):

                @pl.when((z < 3) & (z >= d))
                def _():
                    up(d, k).wait_send()

                @pl.when((z > 0) & (z + d <= 3))
                def _():
                    down(d, k).wait_send()

    return begin, pass_on, arrive, finish


def sum_scratch():
    return [pltpu.VMEM((2, 4, 128, 1024), BF)] + [pltpu.VMEM((2, 128, 1024), BF)] * 6 + [
        DMA((2, 4)), DMA((2, 4)), DMA((2, 6)), DMA((2, 6)),
    ]


def sum_ops(part, m, out, scratch):
    pair, gs, gr, xs, xr, ys, yr = [ref.at[m] for ref in scratch[:7]]
    s1, r1, s2, r2 = scratch[7:]
    me, core, sib, xn, yn, dg = plane_coords()
    order = (dg, xn, yn, me)
    lo, hi = pl.ds(0, 64), pl.ds(64, 64)

    def to_pair(i):
        other = order[i] + 1 - 2 * core
        return send_to(part.at[m, other], pair.at[i], s1.at[m, i], r1.at[m, i], "ctx", sib)

    def ship(index):
        src, dst, peer = (
            (gs.at[lo], gr.at[lo], xn),
            (gs.at[hi], gr.at[hi], yn),
            (xs.at[lo], xr.at[lo], xn),
            (ys.at[hi], yr.at[hi], yn),
            (ys.at[lo], yr.at[lo], yn),
            (xs.at[hi], xr.at[hi], xn),
        )[index]
        return send_to(src, dst, s2.at[m, index], r2.at[m, index], "ctx", peer)

    def f32(value):
        return value.astype(F32)

    def both(i, rr):
        return f32(part[m, order[i], rr]) + f32(pair[i, rr])

    def begin():
        for i in range(4):
            to_pair(i).start()

    def span(offset, count, visit):
        def one(index):
            visit(pl.ds(offset + index.start, 32))

        by_rows(count, 32, one)

    def diag():
        to_pair(0).wait_recv()

        def add(rr):
            gs[rr] = both(0, rr).astype(BF)

        span(0, 128, add)
        ship(0).start()
        ship(1).start()

    def near():
        to_pair(1).wait_recv()

        def add_x(rr):
            xs[rr] = both(1, rr).astype(BF)

        span(0, 64, add_x)
        ship(2).start()
        to_pair(2).wait_recv()

        def add_y(rr):
            ys[rr] = both(2, rr).astype(BF)

        span(64, 64, add_y)
        ship(3).start()

    def join():
        ship(0).wait_recv()

        def add_y(rr):
            ys[rr] = (both(2, rr) + f32(gr[rr])).astype(BF)

        span(0, 64, add_y)
        ship(4).start()
        ship(1).wait_recv()

        def add_x(rr):
            xs[rr] = (both(1, rr) + f32(gr[rr])).astype(BF)

        span(64, 64, add_x)
        ship(5).start()

    def finish():
        to_pair(3).wait_recv()
        for index in (2, 3, 4, 5):
            ship(index).wait_recv()

        def add(rr):
            place = pl.ds(m * 128 + rr.start, 32)
            out[place] = both(3, rr) + f32(xr[rr]) + f32(yr[rr])

        span(0, 128, add)
        for i in range(4):
            to_pair(i).wait_send()
        for index in range(6):
            ship(index).wait_send()

    return begin, diag, near, join, finish


def fold_scratch(rows):
    return [
        pltpu.VMEM((2, 3, rows, 1024), BF),
        pltpu.VMEM((2, 2, rows, 1024), BF),
        DMA((2, 3, 2)),
        DMA((2, 3, 2)),
    ]


def fold_ops(block, rows, out, scratch):
    got, sent, ss, rs = scratch
    z = lax.axis_index("fsdp")
    half = rows // 2
    places = (z, 3 - z)
    nexts = ((z + 1) % 4, (z + 3) % 4)

    def target(side, q):
        return q if side == 0 else 3 - q

    def piece(ref, h):
        return ref.at[pl.ds(half * h, half)]

    def message(src, side, q, h):
        return send_to(
            piece(src, h), piece(got.at[side, q - 1], h), ss.at[side, q - 1, h], rs.at[side, q - 1, h],
            "fsdp", nexts[side],
        )

    def first(side, q, h):
        return message(block(target(side, q)), side, q, h)

    def later(side, q, h):
        return message(sent.at[side, q - 2], side, q, h)

    def begin():
        for side in (0, 1):

            @pl.when(places[side] == 0)
            def _():
                for q in (3, 2, 1):
                    for h in (0, 1):
                        first(side, q, h).start()

    def relay(at, q, h):
        for side in (0, 1):

            @pl.when(places[side] == at)
            def _():
                later(side, q, h).wait_recv()
                mine = block(target(side, q))

                def add(index):
                    rr = pl.ds(half * h + index.start, 32)
                    total = mine[rr].astype(F32) + got[side, q - 1, rr].astype(F32)
                    sent[side, q - 2, rr] = total.astype(BF)

                by_rows(half, 32, add)
                later(side, q, h).start()

    def step(n):
        for at, q, h in (((1, 3, 0),), ((1, 3, 1), (2, 3, 0)), ((1, 2, 0), (2, 3, 1)), ((1, 2, 1),))[n]:
            relay(at, q, h)

    def finish():
        mine = block(z)
        for side in (0, 1):

            @pl.when(places[side] > 0)
            def _():
                for h in (0, 1):
                    q = places[side]
                    send_to(
                        piece(mine, h), piece(got.at[side, q - 1], h), ss.at[side, q - 1, h],
                        rs.at[side, q - 1, h], "fsdp", nexts[side],
                    ).wait_recv()

        def add_all(sides):
            def add(rr):
                total = mine[rr].astype(F32)
                for side in sides:
                    total = total + got[side, places[side] - 1, rr].astype(F32)
                out[rr] = total.astype(BF)

            by_rows(rows, 32, add)

        @pl.when(z == 0)
        def _():
            add_all((1,))

        @pl.when(z == 3)
        def _():
            add_all((0,))

        @pl.when((z > 0) & (z < 3))
        def _():
            add_all((0, 1))

        for side in (0, 1):
            for at, qs in ((0, (3, 2, 1)), (1, (3, 2)), (2, (3,))):

                @pl.when(places[side] == at)
                def _():
                    for q in qs:
                        for h in (0, 1):
                            first(side, q, h).wait_send()

    return begin, step, finish


def vmem_spec():
    return pl.BlockSpec(memory_space=pltpu.VMEM)


def any_spec():
    return pl.BlockSpec(memory_space=pl.ANY)


def natural_slot(device, k):
    micro, part = k // 2, k % 2
    return micro * 16 + (device if part == 0 else 15 - device)


def remote_params(ident):
    return pltpu.CompilerParams(
        collective_id=ident, has_side_effects=True, vmem_limit_bytes=VMEM_CAP
    )


def line_peers():
    z = lax.axis_index("fsdp")
    return [(z + d) % 4 for d in (1, 2, 3)]


def token_docs(row_ref, m):
    row = jnp.broadcast_to(row_ref[pl.ds(m, 1), :].astype(F32), (8, 1024))
    return row[0:1], jnp.transpose(row)[:, 0:1]


def front_kernel(
    x_ref, small_ref, doc_ref, wq_ref, wo_ref, wi_ref,
    h_ref, params_ref, wqc_ref, woc_ref, wic_ref, qkv_ref, of_ref, lse_ref, out_ref,
    hs, units, part, zs, zr, os, orr, ol, *sems,
):
    me, core, sib, xn, yn, dg = plane_coords()
    z = lax.axis_index("fsdp")
    peers = line_peers()
    meet((sib, xn, yn), peers)
    params_ref[z] = small_ref[...]
    copies = []
    for i, peer in enumerate(peers):
        copy = send_to(small_ref, params_ref.at[z], zs.at[i], zr.at[i], "fsdp", peer)
        copy.start()
        copies.append(copy)
    owner = me // 2
    columns = pl.ds(pl.multiple_of(me * 128, 128), 128)
    expert, quarter = me // 4, me % 4

    def wq_slot(where, k):
        return wqc_ref.at[k, pl.ds(pl.multiple_of(where * 256, 256), 256)]

    def wi_own(k):
        return wi_ref.at[expert, :, pl.ds(pl.multiple_of(k * 1024 + quarter * 256, 256), 256)]

    def wi_slot(where, k):
        return wic_ref.at[pl.ds(pl.multiple_of(where * 256, 256), 256), pl.ds(256 * k, 256)]

    q_begin, q_pass, q_arrive, q_finish = line_ops(
        lambda k: wq_ref.at[k, :, columns], wq_slot, 3, sems[:5]
    )
    i_begin, i_pass, i_arrive, i_finish = line_ops(wi_own, wi_slot, 4, sems[5:10])
    begin, relay, diag, done, finish = ring_ops(
        lambda k: hs.at[pl.ds(64 * k, 64)],
        lambda device, k: h_ref.at[natural_slot(device, k)],
        sems[10:19],
    )
    sums = [sum_ops(part, m, out_ref, sems[19:]) for m in (0, 1)]
    q_begin()

    wo_own = wo_ref.at[pl.ds(pl.multiple_of(core * 128, 128), 128)]

    def wo_step(src, side):
        return send_to(
            src, woc_ref, os.at[side], orr.at[side], "fsdp", z + 1 if side == 0 else z - 1
        )

    def wo_both(act):
        @pl.when((z >= owner) & (z < 3))
        def _():
            act(0)

        @pl.when((z <= owner) & (z > 0))
        def _():
            act(1)

    def wo_begin():
        @pl.when(z == owner)
        def _():
            pltpu.make_async_copy(wo_own, woc_ref, ol).start()
            wo_both(lambda side: wo_step(wo_own, side).start())

    def wo_arrive():
        @pl.when(z > owner)
        def _():
            wo_step(woc_ref, 0).wait_recv()

        @pl.when(z < owner)
        def _():
            wo_step(woc_ref, 1).wait_recv()

    def wo_pass(d):
        @pl.when((z == owner + d) | (z == owner - d))
        def _():
            wo_arrive()
            wo_both(lambda side: wo_step(woc_ref, side).start())

    def wo_last():
        @pl.when((z == owner + 3) | (z == owner - 3))
        def _():
            wo_arrive()

        @pl.when(z == owner)
        def _():
            pltpu.make_async_copy(wo_own, woc_ref, ol).wait()

    wo_begin()

    def unit(rr):
        values = x_ref[rr].astype(F32)
        centred = values - jnp.mean(values, -1, keepdims=True)
        spread = jnp.mean(centred * centred, -1, keepdims=True)
        units[rr] = centred * lax.rsqrt(spread + norm_eps)

    by_rows(256, 32, unit)
    for copy in copies:
        copy.wait()

    def full_row(r):
        return jnp.concatenate([params_ref[i, r : r + 1, :] for i in range(4)], axis=1).astype(F32)

    gain, shift = full_row(0), full_row(1)

    def norm(rr):
        hs[rr] = (units[rr] * gain + shift).astype(BF)

    by_rows(256, 32, norm)
    begin(0)
    begin(1)
    q_pass(1)
    relay(0)
    relay(1)
    begin(2)
    begin(3)
    wo_pass(1)
    q_pass(2)
    i_begin()
    diag(0)
    diag(1)
    wo_pass(2)
    done(0)
    done(1)
    q_arrive()
    half = pl.ds(pl.multiple_of(core * 128, 128), 128)
    q_bias = params_ref[owner, 2:3, half].astype(F32)
    v_bias = params_ref[owner, 3:4, half].astype(F32)
    masks = head_masks(256)
    vmasks = head_masks(1024)
    zero = jnp.zeros((), BF)

    def micro(m, carry):
        @pl.when(m == 1)
        def _():
            done(2)
            done(3)

        h = h_ref[pl.ds(16 * m, 16)].reshape(1024, 1024)
        place = pl.ds(pl.multiple_of(m * 1024, 1024), 1024)
        q = (mm(h, wqc_ref[0]) + q_bias).astype(BF)
        k = mm(h, wqc_ref[1]).astype(BF)
        v = (mm(h, wqc_ref[2]) + v_bias).astype(BF)
        qkv_ref[0, place] = q
        qkv_ref[1, place] = k
        qkv_ref[2, place] = v
        vh = [jnp.where(vmasks[j], v, zero) for j in (0, 1)]
        doc_row, doc_col = token_docs(doc_ref, m)
        for i in range(4):
            length = 256 * (i + 1)
            rows = slice(256 * i, 256 * (i + 1))
            qi = q[rows] * jnp.asarray(0.125, BF)
            allowed = allowed_mask(i, doc_col[rows], doc_row[:, :length])
            total = None
            stats = []
            for j in (0, 1):
                s = mm(jnp.where(masks[j], qi, zero), k[:length], NT)
                s = jnp.where(allowed, s, mask_fill)
                top = jnp.max(s, -1, keepdims=True)
                e = jnp.exp(s - top)
                den = jnp.sum(e, -1, keepdims=True)
                p = (e * (1.0 / den)).astype(BF)
                term = mm(p, vh[j][:length])
                total = term if total is None else total + term
                stats.append(top + jnp.log(den))
            at = pl.ds(pl.multiple_of(m * 1024 + 256 * i, 256), 256)
            lse_ref[at] = jnp.where(masks[0], stats[0], stats[1])
            of_ref[at] = total

            @pl.when(m == 0)
            def _():
                if i == 0:
                    relay(2)
                    relay(3)
                if i == 1:
                    i_pass(1, (0,))
                    diag(2)
                if i == 2:
                    i_pass(1, (1,))
                    diag(3)
                if i == 3:
                    wo_last()

            @pl.when(m == 1)
            def _():
                if i == 1:
                    sums[0][3]()
                if i == 3:
                    i_pass(2, (0,))

        for i in range(4):
            at = pl.ds(pl.multiple_of(m * 1024 + 256 * i, 256), 256)
            a = mm(of_ref[at].astype(BF), woc_ref[...]).astype(BF)
            for b in range(4):
                block = 4 * i + b
                dest, side = (block, 0) if block < 8 else (15 - block, 1)
                part[m, dest, 64 * side : 64 * (side + 1)] = a[64 * b : 64 * (b + 1)]

        for n in (0, 1):

            @pl.when(m == n)
            def _():
                for step in sums[n][:3]:
                    step()
                if n == 0:
                    i_pass(1, (2, 3))

        return carry

    lax.fori_loop(0, 2, micro, 0)
    i_pass(2, (1,))
    sums[1][3]()
    i_pass(2, (2, 3))
    sums[0][4]()
    sums[1][4]()
    i_arrive()
    wo_both(lambda side: wo_step(woc_ref, side).wait_send())
    q_finish()
    i_finish()
    for k in range(4):
        finish(k)


def front_call(x, small, docs, w_qkv, w_out, w_in):
    return pl.pallas_call(
        front_kernel,
        out_shape=(
            jax.ShapeDtypeStruct((32, 64, 1024), BF),
            jax.ShapeDtypeStruct((4, SMALL_ROWS, 256), BF),
            jax.ShapeDtypeStruct((3, 1024, 128), BF),
            jax.ShapeDtypeStruct((128, 1024), BF),
            jax.ShapeDtypeStruct((1024, 1024), BF),
            jax.ShapeDtypeStruct((3, 2048, 128), BF),
            jax.ShapeDtypeStruct((2048, 128), F32),
            jax.ShapeDtypeStruct((2048, 128), F32),
            jax.ShapeDtypeStruct((256, 1024), F32),
        ),
        in_specs=[vmem_spec()] * 3 + [any_spec()] * 3,
        out_specs=[vmem_spec()] * 4 + [any_spec()] + [vmem_spec()] * 4,
        scratch_shapes=[
            pltpu.VMEM((256, 1024), BF),
            pltpu.VMEM((256, 1024), F32),
            pltpu.VMEM((2, 8, 128, 1024), BF),
            DMA((3,)),
            DMA((3,)),
            DMA((2,)),
            DMA((2,)),
            DMA(()),
        ]
        + line_sems(3)
        + line_sems(4)
        + gather_sems(4)
        + sum_scratch(),
        name="front",
        compiler_params=remote_params(0),
    )(x, small, docs, w_qkv, w_out, w_in)


def moe_call(h_slots, d_slots, win, w_back, inb):
    def kernel(
        h_ref, d_ref, wi_ref, wall_ref, ib_ref, o_ref, gi_ref, gbs_ref, gib_ref,
        wb_ref, gba, rows, gz, slope, dz, part, pair, sent, got,
        ns, nr, fs, fr, ss, sr, ls, s1, r1, s2, r2, *wsems,
    ):
        me, core, sib, xn, yn, dg = plane_coords()
        expert, quarter = me // 4, me % 4
        meet((sib, xn, yn, dg), line_peers())
        w_begin, w_pass, w_arrive, w_finish = line_ops(
            lambda k: wall_ref.at[expert, pl.ds(pl.multiple_of(quarter * 256 + 64 * k, 64), 64)],
            lambda where, k: wb_ref.at[pl.ds(pl.multiple_of(where * 256 + 64 * k, 64), 64)],
            4,
            wsems[:5],
        )
        z_begin, z_step, z_finish = fold_ops(lambda where: gba.at[where], 256, gbs_ref, wsems[5:])
        w_begin()
        peers = (dg, xn, yn)
        wanted = (1 - expert, expert, 1 - expert)
        ins = (h_ref, d_ref)

        def away(t, m, i):
            return send_to(
                ins[t].at[wanted[i], m], rows.at[t, m, me], ns.at[t, m, i], nr.at[t, m, i], "ctx", peers[i]
            )

        def beside(t, m):
            return send_to(
                ins[t].at[expert, m], rows.at[t, m, me], ss.at[t, m], sr.at[t, m], "ctx", sib
            )

        def here(t, m):
            return pltpu.make_async_copy(ins[t].at[expert, m], rows.at[t, m, me], ls.at[t, m])

        def onward(t, m, i):
            block = rows.at[t, m, peers[i]]
            return send_to(block, block, fs.at[t, m, i], fr.at[t, m, i], "ctx", sib)

        for t in (0, 1):
            for m in (0, 1):
                for i in range(3):
                    away(t, m, i).start()
        for t in (0, 1):
            for m in (0, 1):
                beside(t, m).start()
                here(t, m).start()

        def arrive(t, m):
            for i in range(3):
                away(t, m, i).wait_recv()
                onward(t, m, i).start()
            here(t, m).wait()
            beside(t, m).wait_recv()
            for i in range(3):
                onward(t, m, i).wait_recv()

        order = (dg, xn, yn, me)

        def to_pair(t, m, i):
            other = order[i] + 1 - 2 * core
            return send_to(
                part.at[t, m, other], pair.at[t, m, i], s1.at[t, m, i], r1.at[t, m, i], "ctx", sib
            )

        def to_home(t, m, i):
            return send_to(
                sent.at[t, m, i], got.at[t, m, i], s2.at[t, m, i], r2.at[t, m, i], "ctx", order[i]
            )

        def join(t, m):
            for i in range(3):
                to_pair(t, m, i).wait_recv()
                mine = order[i]

                def add(rr):
                    sent[t, m, i, rr] = (
                        part[t, m, mine, rr].astype(F32) + pair[t, m, i, rr].astype(F32)
                    ).astype(BF)

                by_rows(CAP, 16, add)
                to_home(t, m, i).start()

        def inner_rows(m):
            def visit(half, carry):
                xs = rows[0, m, pl.ds(4 * half, 4)].reshape(4 * CAP, 1024)
                zed = mm(xs, wi_ref[...]) + ib_ref[...]
                square = zed * zed
                t = jnp.tanh(zed * (GELU_A + GELU_A * GELU_B * square))
                half_up = 0.5 + 0.5 * t
                place = pl.ds(pl.multiple_of(m * 8 * CAP + half * 4 * CAP, 4 * CAP), 4 * CAP)
                gz[place] = (zed * half_up).astype(BF)
                slope[place] = half_up + 0.5 * zed * (1.0 - t * t) * (
                    GELU_A + 3.0 * GELU_A * GELU_B * square
                )
                return carry

            lax.fori_loop(0, 2, visit, 0)

        def inner(m, carry):
            @pl.when(m == 0)
            def _():
                w_pass(1, (0, 1))

            arrive(0, m)

            @pl.when(m == 0)
            def _():
                w_pass(1, (2,))

            inner_rows(m)

            @pl.when(m == 0)
            def _():
                w_pass(1, (3,))

            return carry

        lax.fori_loop(0, 2, inner, 0)
        w_pass(2, (0, 1))
        arrive(1, 0)
        w_pass(2, (2, 3))
        arrive(1, 1)

        def back_grads(j, carry):
            column = pl.ds(pl.multiple_of(256 * j, 256), 256)
            du = rows[1].reshape(16 * CAP, 1024)
            gba[j] = mm(gz[:, column], du, TN).astype(BF)
            return carry

        lax.fori_loop(0, 4, back_grads, 0)
        z_begin()
        w_arrive()

        def forward(m, carry):
            def visit(half, inner_carry):
                place = pl.ds(pl.multiple_of(m * 8 * CAP + half * 4 * CAP, 4 * CAP), 4 * CAP)
                u = mm(gz[place], wb_ref[...]).astype(BF)
                part[0, m, pl.ds(4 * half, 4)] = u.reshape(4, CAP, 1024)
                return inner_carry

            lax.fori_loop(0, 2, visit, 0)
            for i in range(4):
                to_pair(0, m, i).start()
            return carry

        lax.fori_loop(0, 2, forward, 0)
        join(0, 0)
        join(0, 1)
        z_step(0)
        gib_ref[...] = jnp.zeros_like(gib_ref)

        def backward(m, carry):
            def rows_backward(half, inner_carry):
                du = rows[1, m, pl.ds(4 * half, 4)].reshape(4 * CAP, 1024)
                place = pl.ds(pl.multiple_of(m * 8 * CAP + half * 4 * CAP, 4 * CAP), 4 * CAP)
                low = (mm(du, wb_ref[...], NT) * slope[place]).astype(BF)
                dz[place] = low
                gib_ref[...] += jnp.sum(low.astype(F32), 0, keepdims=True)
                dh = mm(low, wi_ref[...], NT).astype(BF)
                part[1, m, pl.ds(4 * half, 4)] = dh.reshape(4, CAP, 1024)
                return inner_carry

            lax.fori_loop(0, 2, rows_backward, 0)
            for i in range(4):
                to_pair(1, m, i).start()
            join(1, m)

            @pl.when(m == 0)
            def _():
                z_step(1)

            return carry

        lax.fori_loop(0, 2, backward, 0)
        z_step(2)

        def weight_grads(j, carry):
            column = pl.ds(pl.multiple_of(256 * j, 256), 256)
            xs = rows[0, :, :, :, column].reshape(16 * CAP, 256)
            gi_ref[column] = mm(xs, dz[...], TN).astype(BF)
            return carry

        lax.fori_loop(0, 4, weight_grads, 0)
        z_step(3)
        for t in (0, 1):
            for m in (0, 1):
                to_pair(t, m, 3).wait_recv()
                for i in range(3):
                    to_home(t, m, i).wait_recv()

                def finish(rr):
                    o_ref[expert, t, m, rr] = (
                        part[t, m, me, rr].astype(F32)
                        + pair[t, m, 3, rr].astype(F32)
                        + got[t, m, 1, rr].astype(F32)
                    )
                    o_ref[1 - expert, t, m, rr] = got[t, m, 0, rr].astype(F32) + got[
                        t, m, 2, rr
                    ].astype(F32)

                by_rows(CAP, 16, finish)
        for t in (0, 1):
            for m in (0, 1):
                for i in range(3):
                    away(t, m, i).wait_send()
                    onward(t, m, i).wait_send()
                    to_home(t, m, i).wait_send()
                for i in range(4):
                    to_pair(t, m, i).wait_send()
                beside(t, m).wait_send()
        w_finish()
        z_finish()

    return pl.pallas_call(
        kernel,
        out_shape=(
            jax.ShapeDtypeStruct((2, 2, 2, CAP, 1024), F32),
            jax.ShapeDtypeStruct((1024, 1024), BF),
            jax.ShapeDtypeStruct((256, 1024), BF),
            jax.ShapeDtypeStruct((1, 1024), F32),
        ),
        in_specs=[vmem_spec()] * 3 + [any_spec(), vmem_spec()],
        out_specs=[vmem_spec()] * 4,
        scratch_shapes=[
            pltpu.VMEM((1024, 1024), BF),
            pltpu.VMEM((4, 256, 1024), BF),
            pltpu.VMEM((2, 2, 8, CAP, 1024), BF),
            pltpu.VMEM((16 * CAP, 1024), BF),
            pltpu.VMEM((16 * CAP, 1024), F32),
            pltpu.VMEM((16 * CAP, 1024), BF),
            pltpu.VMEM((2, 2, 8, CAP, 1024), BF),
            pltpu.VMEM((2, 2, 4, CAP, 1024), BF),
            pltpu.VMEM((2, 2, 3, CAP, 1024), BF),
            pltpu.VMEM((2, 2, 3, CAP, 1024), BF),
        ]
        + [DMA((2, 2, 3))] * 4
        + [DMA((2, 2))] * 3
        + [DMA((2, 2, 4))] * 2
        + [DMA((2, 2, 3))] * 2
        + line_sems(4)
        + fold_scratch(256),
        name="moe",
        compiler_params=remote_params(2),
    )(h_slots, d_slots, win, w_back, inb)


def final_call(gi, gb, gq, gwo, vectors):
    def kernel(
        gi_ref, gb_ref, gq_ref, go_ref, v_ref,
        oi_ref, ob_ref, oq_ref, oo_ref, ov_ref,
        qgot, qsum, vgot, vsum, vall,
        qs, qr, vs, vr, ps, pr, ws, wr, hs, hr, fs, fr, ol, *sems,
    ):
        me, core, sib, xn, yn, dg = plane_coords()
        z = lax.axis_index("fsdp")
        others = [(me + d) % 8 for d in range(1, 8)]
        meet(others, line_peers())
        owner = me // 2

        def vector_copy(d):
            peer = (z + d) % 4
            return send_to(v_ref.at[peer], vgot.at[d - 1], vs.at[d - 1], vr.at[d - 1], "fsdp", peer)

        def q_copy(d):
            peer = (z + d) % 4
            block = gq_ref.at[:, pl.ds(pl.multiple_of(peer * 256, 256), 256)]
            return send_to(block, qgot.at[d - 1], qs.at[d - 1], qr.at[d - 1], "fsdp", peer)

        rows_mine = oo_ref.at[pl.ds(pl.multiple_of(core * 128, 128), 128)]
        rows_sib = oo_ref.at[pl.ds(pl.multiple_of((1 - core) * 128, 128), 128)]

        def half(ref, part):
            return ref.at[pl.ds(64 * part, 64)]

        def o_near(i):
            return send_to(go_ref, rows_mine, ws.at[i], wr, "ctx", (xn, yn)[i])

        def o_half(part):
            block = half(rows_mine, part)
            return send_to(block, block, hs, hr.at[part], "ctx", (yn, xn)[part])

        def o_pair(src):
            return send_to(src, rows_mine, fs, fr, "ctx", sib)

        row, col = me // 4, (me // 2) % 2
        own_row, own_col = z // 2, z % 2
        beside_x = (row == own_row) & (col != own_col)
        beside_y = (row != own_row) & (col == own_col)
        across = (row != own_row) & (col != own_col)

        def o_root():
            @pl.when(z == owner)
            def _():
                for i in (0, 1):
                    o_near(i).start()
                o_pair(go_ref).start()
                pltpu.make_async_copy(go_ref, rows_mine, ol).start()

        def o_relay():
            @pl.when(beside_x)
            def _():
                o_near(0).wait_recv()
                o_half(0).start()
                o_pair(rows_mine).start()

            @pl.when(beside_y)
            def _():
                o_near(1).wait_recv()
                o_half(1).start()
                o_pair(rows_mine).start()

        def o_end():
            @pl.when(across)
            def _():
                o_half(0).wait_recv()
                o_half(1).wait_recv()
                o_pair(rows_mine).start()
                o_pair(rows_mine).wait_send()

            @pl.when(z == owner)
            def _():
                for i in (0, 1):
                    o_near(i).wait_send()
                o_pair(go_ref).wait_send()
                pltpu.make_async_copy(go_ref, rows_mine, ol).wait()

            @pl.when(beside_x)
            def _():
                o_half(0).wait_send()
                o_pair(rows_mine).wait_send()

            @pl.when(beside_y)
            def _():
                o_half(1).wait_send()
                o_pair(rows_mine).wait_send()

            send_to(go_ref, rows_sib, fs, fr, "ctx", sib).wait_recv()

        def own(k):
            if k < 4:
                return gi_ref.at[:, pl.ds(256 * k, 256)]
            return gb_ref.at[pl.ds(64 * (k - 4), 64)]

        def slot(device, k):
            which, part = device // 4, device % 4
            if k < 4:
                column = pl.multiple_of(k * 1024 + part * 256, 256)
                return oi_ref.at[which, :, pl.ds(column, 256)]
            row_at = pl.multiple_of(part * 256 + 64 * (k - 4), 64)
            return ob_ref.at[which, pl.ds(row_at, 64)]

        def qslot(device, k):
            return oq_ref.at[k, :, pl.ds(pl.multiple_of(device * 128, 128), 128)]

        begin, relay, diag, done, finish = ring_ops(own, slot, sems[:9])
        q_begin, q_relay, q_diag, q_done, q_finish = ring_ops(lambda k: qsum.at[k], qslot, sems[9:18])
        for d in (1, 2, 3):
            vector_copy(d).start()
        for d in (1, 3, 2):
            q_copy(d).start()
        begin(0)
        begin(1)
        o_root()
        for k in range(2, 8):
            begin(k)
        for d in (1, 2, 3):
            vector_copy(d).wait_recv()
        vsum[...] = v_ref[z] + vgot[0] + vgot[1] + vgot[2]

        def plane_vector(i):
            return send_to(vsum, vall.at[i], ps.at[i], pr.at[i], "ctx", others[i])

        for i in range(7):
            plane_vector(i).start()
        relay(0)
        relay(1)
        relay(2)
        o_relay()
        relay(3)
        relay(4)
        for d in (1, 3, 2):
            q_copy(d).wait_recv()
        for j in range(3):

            def add(rr):
                place = pl.ds(pl.multiple_of(z * 256 + rr.start, 32), 32)
                total = gq_ref[j, place].astype(F32)
                for i in range(3):
                    total = total + qgot[i, j, rr].astype(F32)
                qsum[j, rr] = total.astype(BF)

            by_rows(256, 32, add)
        for k in range(3):
            q_begin(k)
        relay(5)
        diag(0)
        relay(6)
        diag(1)
        relay(7)
        diag(2)
        diag(3)
        for k in range(3):
            q_relay(k)
        for k in range(4, 8):
            diag(k)
        for k in range(3):
            q_diag(k)
        o_end()
        for k in range(8):
            done(k)
        for k in range(3):
            q_done(k)
        total = vsum[...]
        for i in range(7):
            plane_vector(i).wait_recv()
            total = total + vall[i]
        ov_ref[...] = total
        for k in range(8):
            finish(k)
        for k in range(3):
            q_finish(k)
        for d in (1, 2, 3):
            vector_copy(d).wait_send()
            q_copy(d).wait_send()
        for i in range(7):
            plane_vector(i).wait_send()

    count = vectors.shape[1]
    return pl.pallas_call(
        kernel,
        out_shape=(
            jax.ShapeDtypeStruct((2, 256, 4096), BF),
            jax.ShapeDtypeStruct((2, 1024, 1024), BF),
            jax.ShapeDtypeStruct((3, 256, 1024), BF),
            jax.ShapeDtypeStruct((256, 1024), BF),
            jax.ShapeDtypeStruct((count, 256), F32),
        ),
        in_specs=[vmem_spec()] * 5,
        out_specs=[any_spec()] * 4 + [vmem_spec()],
        scratch_shapes=[
            pltpu.VMEM((3, 3, 256, 128), BF),
            pltpu.VMEM((3, 256, 128), BF),
            pltpu.VMEM((3, count, 256), F32),
            pltpu.VMEM((count, 256), F32),
            pltpu.VMEM((7, count, 256), F32),
            DMA((3,)), DMA((3,)), DMA((3,)), DMA((3,)), DMA((7,)), DMA((7,)),
            DMA((2,)), DMA(()), DMA(()), DMA((2,)), DMA(()), DMA(()), DMA(()),
        ]
        + gather_sems(8)
        + gather_sems(3),
        name="final",
        compiler_params=remote_params(6),
    )(gi, gb, gq, gwo, vectors)


def head_masks(rows):
    lane = lax.broadcasted_iota(jnp.int32, (rows, 128), 1)
    return lane < 64, lane >= 64


def allowed_mask(i, doc_col, doc_row):
    length = 256 * (i + 1)
    qpos = lax.broadcasted_iota(jnp.int32, (256, length), 0) + 256 * i
    kpos = lax.broadcasted_iota(jnp.int32, (256, length), 1)
    return (kpos <= qpos) & (doc_col == doc_row)


def back_kernel(
    da_ref, h_ref, qkv_ref, of_ref, lse_ref, w_ref, wo_ref, doc_ref, gi_ref,
    out_ref, gq_ref, gwo_ref, gqv_ref, gis_ref,
    g_all, dqkv, part, dka, dva, probs, gwo, gwo_low, gwo_got, os, orr, *sems,
):
    me, core, sib, xn, yn, dg = plane_coords()
    meet((sib, xn, yn), line_peers())
    begin, relay, diag, done, finish = ring_ops(
        lambda k: da_ref.at[pl.ds(64 * k, 64)],
        lambda device, k: g_all.at[natural_slot(device, k)],
        sems[:9],
    )
    z_begin, z_step, z_finish = fold_ops(
        lambda where: gi_ref.at[pl.ds(pl.multiple_of(where * 256, 256), 256)],
        256,
        gis_ref,
        sems[9:13],
    )
    sums = [sum_ops(part, m, out_ref, sems[13:]) for m in (0, 1)]
    z = lax.axis_index("fsdp")
    owner = me // 2
    away = (owner - z + 4) % 4

    def to_owner():
        return send_to(gwo_low, gwo_got.at[away - 1], os, orr.at[away - 1], "fsdp", owner)

    masks = head_masks(256)
    zero = jnp.zeros((), BF)
    spans = [slice(128 * i * (i + 1), 128 * (i + 1) * (i + 2)) for i in range(4)]
    begin(0)
    begin(1)
    z_begin()

    def weigh(m, carry):
        place = pl.ds(pl.multiple_of(m * 1024, 1024), 1024)
        q, k = qkv_ref[0, place], qkv_ref[1, place]
        doc_row, doc_col = token_docs(doc_ref, m)
        for i in range(4):
            length = 256 * (i + 1)
            rows = slice(256 * i, 256 * (i + 1))
            qi = q[rows] * jnp.asarray(0.125, BF)
            allowed = allowed_mask(i, doc_col[rows], doc_row[:, :length])
            lse = lse_ref[pl.ds(pl.multiple_of(m * 1024 + 256 * i, 256), 256)]
            for j in (0, 1):
                s = mm(jnp.where(masks[j], qi, zero), k[:length], NT)
                probs[m, j, :, spans[i]] = jnp.exp(
                    jnp.where(allowed, s, mask_fill) - lse[:, 64 * j : 64 * j + 1]
                )

        @pl.when(m == 0)
        def _():
            relay(0)
            relay(1)
            begin(2)
            begin(3)

        return carry

    lax.fori_loop(0, 2, weigh, 0)
    z_step(0)
    diag(0)
    diag(1)
    done(0)
    done(1)
    kmasks = head_masks(1024)

    def micro(m, carry):
        @pl.when(m == 1)
        def _():
            done(2)
            done(3)

        place = pl.ds(pl.multiple_of(m * 1024, 1024), 1024)
        g = g_all[pl.ds(16 * m, 16)].reshape(1024, 1024)
        q, k, v = qkv_ref[0, place], qkv_ref[1, place], qkv_ref[2, place]
        do = mm(g, wo_ref[...], NT).astype(BF)
        term = mm(of_ref[place].astype(BF), g, TN)

        @pl.when(m == 0)
        def _():
            gwo[...] = term

        @pl.when(m == 1)
        def _():
            gwo_low[...] = (gwo[...] + term).astype(BF)

            @pl.when(z != owner)
            def _():
                to_owner().start()

        dka[...] = jnp.zeros_like(dka)
        dva[...] = jnp.zeros_like(dva)
        kh = [jnp.where(kmasks[j], k, zero) for j in (0, 1)]
        for i in range(4):
            length = 256 * (i + 1)
            rows = slice(256 * i, 256 * (i + 1))
            at = pl.ds(pl.multiple_of(m * 1024 + 256 * i, 256), 256)
            qi = q[rows] * jnp.asarray(0.125, BF)
            doi = do[rows]
            prod = doi.astype(F32) * of_ref[at]
            dq = None
            for j in (0, 1):
                qh = jnp.where(masks[j], qi, zero)
                doh = jnp.where(masks[j], doi, zero)
                delta = jnp.sum(jnp.where(masks[j], prod, 0.0), -1, keepdims=True)
                p = probs[m, j, :, spans[i]]
                dp = mm(doh, v[:length], NT)
                ds = (p * (dp - delta)).astype(BF)
                term = mm(ds, kh[j][:length])
                dq = term if dq is None else dq + term
                dka[:length] += mm(ds, qh, TN)
                dva[:length] += mm(p.astype(BF), doh, TN)
            dqkv[0, at] = (dq * 0.125).astype(BF)

            @pl.when(m == 0)
            def _():
                if i == 0:
                    relay(2)
                if i == 1:
                    relay(3)
                    z_step(1)
                if i == 3:
                    diag(2)
                    diag(3)
                    z_step(2)

            @pl.when(m == 1)
            def _():
                if i == 0:
                    z_step(3)
                if i == 1:
                    sums[0][3]()

        dqkv[1, place] = dka[...].astype(BF)
        dqkv[2, place] = dva[...].astype(BF)
        for i in range(4):
            at = pl.ds(pl.multiple_of(m * 1024 + 256 * i, 256), 256)
            a = mm(dqkv[0, at], w_ref[0], NT) + mm(dqkv[1, at], w_ref[1], NT)
            a = (a + mm(dqkv[2, at], w_ref[2], NT)).astype(BF)
            for b in range(4):
                block = 4 * i + b
                dest, side = (block, 0) if block < 8 else (15 - block, 1)
                part[m, dest, 64 * side : 64 * (side + 1)] = a[64 * b : 64 * (b + 1)]
        for n in (0, 1):

            @pl.when(m == n)
            def _():
                for step in sums[n][:3]:
                    step()

        return carry

    lax.fori_loop(0, 2, micro, 0)
    sums[1][3]()
    for j in range(3):
        gq_ref[j] = mm(h_ref[...].reshape(2048, 1024), dqkv[j], TN).astype(BF)
    gqv_ref[0:1] = jnp.sum(dqkv[0].astype(F32), 0, keepdims=True)
    gqv_ref[1:2] = jnp.sum(dqkv[2].astype(F32), 0, keepdims=True)
    sums[0][4]()
    sums[1][4]()
    z_finish()

    @pl.when(z != owner)
    def _():
        to_owner().wait_send()

    @pl.when(z == owner)
    def _():
        for i in range(3):
            send_to(gwo_low, gwo_got.at[i], os, orr.at[i], "fsdp", (z + 1) % 4).wait_recv()

        def add(rr):
            total = gwo_low[rr].astype(F32)
            for i in range(3):
                total = total + gwo_got[i, rr].astype(F32)
            gwo_ref[rr] = total.astype(BF)

        by_rows(128, 32, add)

    @pl.when(z != owner)
    def _():
        gwo_ref[...] = jnp.zeros_like(gwo_ref)

    for k in range(4):
        finish(k)


def back_call(da, h, qkv, of, lse, wqkv, wout, docs, gi):
    return pl.pallas_call(
        back_kernel,
        out_shape=(
            jax.ShapeDtypeStruct((256, 1024), F32),
            jax.ShapeDtypeStruct((3, 1024, 128), BF),
            jax.ShapeDtypeStruct((128, 1024), BF),
            jax.ShapeDtypeStruct((2, 128), F32),
            jax.ShapeDtypeStruct((256, 1024), BF),
        ),
        in_specs=[vmem_spec()] * 9,
        out_specs=[vmem_spec()] * 5,
        scratch_shapes=[
            pltpu.VMEM((32, 64, 1024), BF),
            pltpu.VMEM((3, 2048, 128), BF),
            pltpu.VMEM((2, 8, 128, 1024), BF),
            pltpu.VMEM((1024, 128), F32),
            pltpu.VMEM((1024, 128), F32),
            pltpu.VMEM((2, 2, 256, 2560), F32),
            pltpu.VMEM((128, 1024), F32),
            pltpu.VMEM((128, 1024), BF),
            pltpu.VMEM((3, 128, 1024), BF),
            DMA(()),
            DMA((3,)),
        ]
        + gather_sems(4)
        + fold_scratch(256)
        + sum_scratch(),
        name="back",
        compiler_params=remote_params(4),
    )(da, h, qkv, of, lse, wqkv, wout, docs, gi)


GELU_A = math.sqrt(2.0 / math.pi)
GELU_B = 0.044715


def widen_call(arrays):
    count = len(arrays)
    steps = 8

    def kernel(*refs):
        for src, dst in zip(refs[:count], refs[count:]):
            dst[...] = src[...].astype(F32)

    flat = [array.reshape(-1, array.shape[-1]) for array in arrays]
    specs = [pl.BlockSpec((f.shape[0] // steps, f.shape[1]), lambda i: (i, 0)) for f in flat]
    wide = pl.pallas_call(
        kernel,
        grid=(steps,),
        out_shape=[jax.ShapeDtypeStruct(f.shape, F32) for f in flat],
        in_specs=specs,
        out_specs=specs,
        name="widen",
        compiler_params=pltpu.CompilerParams(vmem_limit_bytes=VMEM_CAP),
    )(*flat)
    return [w.reshape(a.shape) for w, a in zip(wide, arrays)]


def norm_back(values, gain, grad):
    mean = jnp.mean(values, -1, keepdims=True)
    centred = values - mean
    inv = lax.rsqrt(jnp.mean(centred * centred, -1, keepdims=True) + norm_eps)
    unit = centred * inv
    scaled = grad * gain
    back = inv * (
        scaled
        - jnp.mean(scaled, -1, keepdims=True)
        - unit * jnp.mean(scaled * unit, -1, keepdims=True)
    )
    return back, jnp.sum(grad * unit, 0), jnp.sum(grad, 0)


def fast_body(
    tokens, doc_ids, routes, cotangent, ln1_gain, ln1_shift, w_qkv, qv_bias, w_out, out_bias,
    ln2_gain, ln2_shift, router, w_in, in_bias, w_back, back_bias,
):
    c = lax.axis_index("ctx")
    rows = [ln1_gain, ln1_shift, qv_bias[0], qv_bias[1], out_bias, ln2_gain, ln2_shift]
    rows += [router[:, 0], router[:, 1]]
    rows += [in_bias[e, 256 * k : 256 * (k + 1)] for e in (0, 1) for k in range(4)]
    rows += [back_bias[0], back_bias[1]]
    row_iota = lax.broadcasted_iota(jnp.int32, (SMALL_ROWS, 256), 0)
    small = jnp.zeros((SMALL_ROWS, 256), BF)
    for index, row in enumerate(rows):
        small = jnp.where(row_iota == index, row[None], small)
    x_low = tokens[:, 0].reshape(256, 1024)
    picks = routes[:, 0, :, 0]
    docs = doc_ids[:, 0]
    hs, params, wqkv_c, wout_c, win_c, qkv, o_full, lse, branch = front_call(
        x_low, small, docs, w_qkv, w_out, w_in
    )
    params = params.astype(F32)
    row_of = lambda r: params[:, r].reshape(1024)
    gain1, outb, gain2, shift2 = row_of(0), row_of(4), row_of(5), row_of(6)
    router_t = jnp.stack([row_of(7), row_of(8)])
    backb = jnp.stack([row_of(17), row_of(18)])
    inb = lax.dynamic_index_in_dim(params[:, 9:17], c, 1, keepdims=False).reshape(1, 1024)

    x = x_low.astype(F32)
    dy = cotangent[:, 0].reshape(256, 1024).astype(F32)
    y1 = x + (branch + outb)
    h2 = layer_norm(y1, gain2, shift2).astype(BF)
    logits = lax.dot_general(h2, router_t.astype(BF), NT, preferred_element_type=F32)
    probs = jax.nn.softmax(logits, axis=-1)
    flat = picks.reshape(256)
    chosen = (flat[:, None] == lax.iota(jnp.int32, 2)[None, :]).astype(F32)
    gate = jnp.sum(probs * chosen, -1, keepdims=True)
    before = lax.iota(jnp.int32, 128)
    lower = (before[:, None] < before[None, :]).astype(F32)
    picked = (picks[:, None, :] == lax.iota(jnp.int32, 2)[None, :, None]).astype(F32)
    rank = jnp.sum(picked[:, :, :, None] * lower[None, None], 2)
    slots = lax.iota(jnp.int32, CAP).astype(F32)
    dispatch = (rank[:, :, None, :] == slots[None, None, :, None]) & (picked[:, :, None, :] > 0.5)
    dispatch_low = dispatch.astype(BF)
    du = (gate * dy).astype(BF)

    def to_slots(value):
        return jnp.einsum(
            "mest,mtd->emsd", dispatch_low, value.reshape(2, 128, 1024), preferred_element_type=F32
        ).astype(BF)

    both, gi, gb_sum, gib = moe_call(to_slots(h2), to_slots(du), win_c, w_back, inb)
    unsorted = jnp.einsum(
        "mest,eamsd->amtd", dispatch.astype(F32), both,
        precision=lax.Precision.HIGHEST,
    ).reshape(2, 256, 1024)
    u = unsorted[0] + jnp.where(flat[:, None] == 1, backb[1][None], backb[0][None])
    mixed = (y1 + gate * u).astype(BF)
    dgate = jnp.sum(dy * u, -1, keepdims=True)
    pick_grad = dgate * chosen
    dlogits = probs * (pick_grad - jnp.sum(probs * pick_grad, -1, keepdims=True))
    h2f = h2.astype(F32)
    router_grad = jnp.stack([jnp.sum(h2f * dlogits[:, e : e + 1], 0) for e in (0, 1)])
    dh2 = unsorted[1] + dlogits[:, 0:1] * router_t[0][None] + dlogits[:, 1:2] * router_t[1][None]
    back2, g_two, s_two = norm_back(y1, gain2, dh2)
    dy1 = dy + back2
    da = dy1.astype(BF)
    g_outb = jnp.sum(da.astype(F32), 0)
    duf = du.astype(F32)
    g_backb = jnp.stack([jnp.sum(duf * chosen[:, e : e + 1], 0) for e in (0, 1)])
    dh1, gq, gwo, gqv, gi_sum = back_call(
        da, hs, qkv, o_full, lse, wqkv_c, wout_c, docs, gi
    )
    back1, g_one, s_one = norm_back(x, gain1, dh1)
    token_grad = (dy1 + back1).reshape(2, 1, 128, 1024)

    qv_full = lax.dynamic_update_slice_in_dim(jnp.zeros((2, 1024), F32), gqv, c * 128, 1)
    vectors = jnp.concatenate(
        [jnp.stack([g_one, s_one]), qv_full, jnp.stack([g_outb, g_two, s_two]), router_grad, g_backb],
        axis=0,
    )
    vectors = jnp.transpose(vectors.reshape(11, 4, 256), (1, 0, 2))
    ib_rows = lax.dynamic_update_slice_in_dim(
        jnp.zeros((4, 8, 256), F32), gib.reshape(4, 1, 256), c, 1
    )
    vectors = jnp.concatenate([vectors, ib_rows, jnp.zeros((4, 5, 256), F32)], axis=1)
    g_in, g_back, g_qkv, g_out, sums = final_call(gi_sum, gb_sum, gq, gwo, vectors)
    g_in, g_back, g_qkv, g_out = widen_call([g_in, g_back, g_qkv, g_out])
    return (
        mixed.reshape(2, 1, 128, 1024),
        token_grad,
        sums[0], sums[1], g_qkv, sums[2:4], g_out, sums[4], sums[5], sums[6],
        jnp.transpose(sums[7:9]), g_in, sums[11:19].reshape(2, 1024), g_back,
        sums[9:11],
    )


def solution(mesh):
    small_plane = mesh.shape["ctx"] == 8 and mesh.shape["fsdp"] == 4
    chosen_body = fast_body if small_plane else body
    placed = (
        P(None, "fsdp", "ctx", None),
        P(None, "fsdp", None),
        P(None, "fsdp", "ctx", None),
        P(None, "fsdp", "ctx", None),
        P("fsdp"),
        P("fsdp"),
        P(None, "fsdp", None),
        P(None, "fsdp"),
        P("fsdp", None),
        P("fsdp"),
        P("fsdp"),
        P("fsdp"),
        P("fsdp", None),
        P(None, "fsdp", None),
        P(None, "fsdp"),
        P(None, "fsdp", None),
        P(None, "fsdp"),
    )
    return jax.shard_map(
        chosen_body,
        mesh=mesh,
        in_specs=placed,
        out_specs=(
            P(None, "fsdp", "ctx", None),
            P(None, "fsdp", "ctx", None),
            P("fsdp"),
            P("fsdp"),
            P(None, "fsdp", None),
            P(None, "fsdp"),
            P("fsdp", None),
            P("fsdp"),
            P("fsdp"),
            P("fsdp"),
            P("fsdp", None),
            P(None, "fsdp", None),
            P(None, "fsdp"),
            P(None, "fsdp", None),
            P(None, "fsdp"),
        ),
        check_vma=False,
    )
```

```python
import math

import jax
import jax.numpy as jnp
from jax import lax
from jax.experimental import pallas as pl
from jax.experimental.pallas import tpu as pltpu
from jax.sharding import PartitionSpec as P

HEADS = 16
HEAD_DIM = 64
CAP = 80


norm_eps = 1e-05
mask_fill = -1e30


def layer_norm(values, gain, shift):
    mean = jnp.mean(values, -1, keepdims=True)
    centred = values - mean
    spread = jnp.mean(centred * centred, -1, keepdims=True)
    return centred * lax.rsqrt(spread + norm_eps) * gain + shift


def natural_position(store_index, tok_rows, ctx_count):
    half = tok_rows // 2
    device = store_index // tok_rows
    slot = store_index % tok_rows
    return jnp.where(
        slot < half, device * half + slot, (2 * ctx_count - 1 - device) * half + slot - half
    )


def visible(query_pos, query_ids, key_pos, key_ids):
    return (key_pos[None, :] <= query_pos[:, None]) & (key_ids[None, :] == query_ids[:, None])


def block_needed(query_pos, query_ids, key_pos, key_ids):
    return (
        (jnp.min(key_pos) <= jnp.max(query_pos))
        & (jnp.max(key_ids) >= jnp.min(query_ids))
        & (jnp.min(key_ids) <= jnp.max(query_ids))
    )


def attend_keys(
    running, query_heads, query_pos, query_ids, key_part, value_part, pos_part, id_part, scale
):
    length = key_part.shape[0]
    stride = math.gcd(length, 512)
    key_heads = key_part.reshape(length, HEADS, HEAD_DIM)
    value_heads = value_part.reshape(length, HEADS, HEAD_DIM)

    def attend_visit_block(block_index, state):
        offset = block_index * stride
        key_blk = lax.dynamic_slice_in_dim(key_heads, offset, stride, 0)
        value_blk = lax.dynamic_slice_in_dim(value_heads, offset, stride, 0)
        key_pos = lax.dynamic_slice_in_dim(pos_part, offset, stride, 0)
        key_ids = lax.dynamic_slice_in_dim(id_part, offset, stride, 0)
        needed = block_needed(query_pos, query_ids, key_pos, key_ids)

        def update(current):
            best, totals, accum = current
            scores = (
                jnp.einsum("qhc,khc->hqk", query_heads, key_blk, preferred_element_type=jnp.float32)
                * scale
            )
            allowed = visible(query_pos, query_ids, key_pos, key_ids)[None]
            scores = jnp.where(allowed, scores, mask_fill)
            new_best = jnp.maximum(best, jnp.max(scores, -1))
            shrink = jnp.exp(best - new_best)
            weights = jnp.where(allowed, jnp.exp(scores - new_best[..., None]), 0.0)
            totals = totals * shrink + jnp.sum(weights, -1)
            addend = jnp.einsum(
                "hqk,khc->qhc",
                weights.astype(jnp.bfloat16),
                value_blk,
                preferred_element_type=jnp.float32,
            )
            accum = accum * jnp.transpose(shrink)[..., None] + addend
            return (new_best, totals, accum)

        def unchanged(current):
            return current

        return lax.cond(needed, update, unchanged, state)

    return lax.fori_loop(0, length // stride, attend_visit_block, running)


def backward_range(
    query_heads,
    grad_heads,
    log_total,
    delta,
    query_pos,
    query_ids,
    key_part,
    value_part,
    pos_part,
    id_part,
    scale,
):
    length = key_part.shape[0]
    stride = math.gcd(length, 512)
    blocks = length // stride
    key_blocks = key_part.reshape(blocks, stride, HEADS, HEAD_DIM)
    value_blocks = value_part.reshape(blocks, stride, HEADS, HEAD_DIM)
    pos_blocks = pos_part.reshape(blocks, stride)
    id_blocks = id_part.reshape(blocks, stride)
    rows = query_heads.shape[0]

    def backward_visit_block(query_acc, block_data):
        key_blk, value_blk, pos_blk, id_blk = block_data
        needed = block_needed(query_pos, query_ids, pos_blk, id_blk)

        def compute(current):
            scores = (
                jnp.einsum("qhc,khc->hqk", query_heads, key_blk, preferred_element_type=jnp.float32)
                * scale
            )
            allowed = visible(query_pos, query_ids, pos_blk, id_blk)[None]
            weights = jnp.where(allowed, jnp.exp(scores - log_total[..., None]), 0.0)
            weight_grad = jnp.einsum(
                "qhc,khc->hqk", grad_heads, value_blk, preferred_element_type=jnp.float32
            )
            score_grad = (weights * (weight_grad - delta[..., None])).astype(jnp.bfloat16)
            current = (
                current
                + jnp.einsum(
                    "hqk,khc->qhc", score_grad, key_blk, preferred_element_type=jnp.float32
                )
                * scale
            )
            terms = ()
            value_term = jnp.einsum(
                "hqk,qhc->khc",
                weights.astype(jnp.bfloat16),
                grad_heads,
                preferred_element_type=jnp.float32,
            )
            key_term = (
                jnp.einsum(
                    "hqk,qhc->khc", score_grad, query_heads, preferred_element_type=jnp.float32
                )
                * scale
            )
            terms = (key_term, value_term)
            return (current, terms)

        def skipped(current):
            terms = ()
            empty = jnp.zeros((stride, HEADS, HEAD_DIM), jnp.float32)
            terms = (empty, empty)
            return (current, terms)

        query_acc, terms = lax.cond(needed, compute, skipped, query_acc)
        terms = (
            terms[0].reshape(stride, HEADS * HEAD_DIM),
            terms[1].reshape(stride, HEADS * HEAD_DIM),
        )
        return (query_acc, terms)

    start_acc = jnp.zeros((rows, HEADS, HEAD_DIM), jnp.float32)
    query_grad, terms = lax.scan(
        backward_visit_block, start_acc, (key_blocks, value_blocks, pos_blocks, id_blocks)
    )
    return (
        query_grad,
        terms[0].reshape(length, HEADS * HEAD_DIM),
        terms[1].reshape(length, HEADS * HEAD_DIM),
    )


def gather_keys(key_rows, value_rows):
    return (
        lax.all_gather(key_rows, "ctx", axis=0, tiled=True),
        lax.all_gather(value_rows, "ctx", axis=0, tiled=True),
    )


def reduce_grads(attn_terms, expert_terms):
    g_one, s_one, g_qkv, g_qv, g_out, g_outb, g_two, s_two, g_router = attn_terms
    g_in, g_inb, g_back, g_backb = expert_terms
    e_in, e_inb, e_back, e_backb = (
        lax.psum_scatter(g_in.astype(jnp.bfloat16), "fsdp", scatter_dimension=1, tiled=True).astype(
            jnp.float32
        ),
        lax.psum_scatter(
            g_inb.astype(jnp.bfloat16), "fsdp", scatter_dimension=1, tiled=True
        ).astype(jnp.float32),
        lax.psum_scatter(
            g_back.astype(jnp.bfloat16), "fsdp", scatter_dimension=1, tiled=True
        ).astype(jnp.float32),
        lax.psum_scatter(
            g_backb.astype(jnp.bfloat16), "fsdp", scatter_dimension=1, tiled=True
        ).astype(jnp.float32),
    )
    a_one, b_one, a_qkv, a_qv, a_out, a_outb, a_two, b_two, a_router = (
        lax.psum_scatter(
            g_one.astype(jnp.bfloat16), "fsdp", scatter_dimension=0, tiled=True
        ).astype(jnp.float32),
        lax.psum_scatter(
            s_one.astype(jnp.bfloat16), "fsdp", scatter_dimension=0, tiled=True
        ).astype(jnp.float32),
        lax.psum_scatter(
            g_qkv.astype(jnp.bfloat16), "fsdp", scatter_dimension=1, tiled=True
        ).astype(jnp.float32),
        lax.psum_scatter(g_qv.astype(jnp.bfloat16), "fsdp", scatter_dimension=1, tiled=True).astype(
            jnp.float32
        ),
        lax.psum_scatter(
            g_out.astype(jnp.bfloat16), "fsdp", scatter_dimension=0, tiled=True
        ).astype(jnp.float32),
        lax.psum_scatter(
            g_outb.astype(jnp.bfloat16), "fsdp", scatter_dimension=0, tiled=True
        ).astype(jnp.float32),
        lax.psum_scatter(
            g_two.astype(jnp.bfloat16), "fsdp", scatter_dimension=0, tiled=True
        ).astype(jnp.float32),
        lax.psum_scatter(
            s_two.astype(jnp.bfloat16), "fsdp", scatter_dimension=0, tiled=True
        ).astype(jnp.float32),
        lax.psum_scatter(
            g_router.astype(jnp.bfloat16), "fsdp", scatter_dimension=0, tiled=True
        ).astype(jnp.float32),
    )
    return (
        lax.psum(a_one.astype(jnp.bfloat16), "ctx").astype(jnp.float32),
        lax.psum(b_one.astype(jnp.bfloat16), "ctx").astype(jnp.float32),
        lax.psum(a_qkv.astype(jnp.bfloat16), "ctx").astype(jnp.float32),
        lax.psum(a_qv.astype(jnp.bfloat16), "ctx").astype(jnp.float32),
        lax.psum(a_out.astype(jnp.bfloat16), "ctx").astype(jnp.float32),
        lax.psum(a_outb.astype(jnp.bfloat16), "ctx").astype(jnp.float32),
        lax.psum(a_two.astype(jnp.bfloat16), "ctx").astype(jnp.float32),
        lax.psum(b_two.astype(jnp.bfloat16), "ctx").astype(jnp.float32),
        lax.psum(a_router.astype(jnp.bfloat16), "ctx").astype(jnp.float32),
        lax.psum(e_in.astype(jnp.bfloat16), "ctx").astype(jnp.float32),
        lax.psum(e_inb.astype(jnp.bfloat16), "ctx").astype(jnp.float32),
        lax.psum(e_back.astype(jnp.bfloat16), "ctx").astype(jnp.float32),
        lax.psum(e_backb.astype(jnp.bfloat16), "ctx").astype(jnp.float32),
    )


def body(
    tokens,
    doc_ids,
    routes,
    cotangent,
    ln1_gain,
    ln1_shift,
    w_qkv,
    qv_bias,
    w_out,
    out_bias,
    ln2_gain,
    ln2_shift,
    router,
    w_in,
    in_bias,
    w_back,
    back_bias,
):
    gain_one, shift_one, proj_all, bias_qv, proj_out, bias_out, gain_two, shift_two, router_full = (
        lax.all_gather(ln1_gain, "fsdp", axis=0, tiled=True),
        lax.all_gather(ln1_shift, "fsdp", axis=0, tiled=True),
        lax.all_gather(w_qkv, "fsdp", axis=1, tiled=True),
        lax.all_gather(qv_bias, "fsdp", axis=1, tiled=True),
        lax.all_gather(w_out, "fsdp", axis=0, tiled=True),
        lax.all_gather(out_bias, "fsdp", axis=0, tiled=True),
        lax.all_gather(ln2_gain, "fsdp", axis=0, tiled=True),
        lax.all_gather(ln2_shift, "fsdp", axis=0, tiled=True),
        lax.all_gather(router, "fsdp", axis=0, tiled=True),
    )
    inner_full, inner_bias, outer_full, outer_bias = (
        lax.all_gather(w_in, "fsdp", axis=1, tiled=True),
        lax.all_gather(in_bias, "fsdp", axis=1, tiled=True),
        lax.all_gather(w_back, "fsdp", axis=1, tiled=True),
        lax.all_gather(back_bias, "fsdp", axis=1, tiled=True),
    )
    gain_one_f = gain_one.astype(jnp.float32)
    shift_one_f = shift_one.astype(jnp.float32)
    bias_qv_f = bias_qv.astype(jnp.float32)
    bias_out_f = bias_out.astype(jnp.float32)
    gain_two_f = gain_two.astype(jnp.float32)
    shift_two_f = shift_two.astype(jnp.float32)
    router_f = router_full.astype(jnp.float32)
    inner_bias_f = inner_bias.astype(jnp.float32)
    outer_bias_f = outer_bias.astype(jnp.float32)
    micro_count = tokens.shape[0]
    tok_rows = tokens.shape[2]
    width = tokens.shape[3]
    stream_len = doc_ids.shape[2]
    ctx_count = lax.axis_size("ctx")
    expert_count = inner_full.shape[0]
    scale = 1.0 / math.sqrt(HEAD_DIM)
    first_row = lax.axis_index("ctx") * tok_rows
    store_pos = natural_position(lax.iota(jnp.int32, stream_len), tok_rows, ctx_count)
    query_pos = lax.dynamic_slice_in_dim(store_pos, first_row, tok_rows, 0)
    expert_iota = lax.iota(jnp.int32, expert_count)
    slot_iota = lax.iota(jnp.int32, CAP)
    outputs = []
    input_grads = []
    totals = None
    for micro in range(micro_count):
        inputs = tokens[micro, 0].astype(jnp.float32)
        ids_store = jnp.take(doc_ids[micro, 0], store_pos)
        query_ids = lax.dynamic_slice_in_dim(ids_store, first_row, tok_rows, 0)
        picks = routes[micro, 0, :, 0]
        upstream = cotangent[micro, 0].astype(jnp.float32)
        h_first, pull_first = jax.vjp(layer_norm, inputs, gain_one_f, shift_one_f)
        h_first_low = h_first.astype(jnp.bfloat16)
        projected = jnp.einsum(
            "td,jde->jte", h_first_low, proj_all, preferred_element_type=jnp.float32
        )
        queries = (projected[0] + bias_qv_f[0]).astype(jnp.bfloat16)
        key_rows = projected[1].astype(jnp.bfloat16)
        value_rows = (projected[2] + bias_qv_f[1]).astype(jnp.bfloat16)
        query_heads = queries.reshape(tok_rows, HEADS, HEAD_DIM)
        start_state = (
            jnp.full((HEADS, tok_rows), mask_fill, jnp.float32),
            jnp.zeros((HEADS, tok_rows), jnp.float32),
            jnp.zeros((tok_rows, HEADS, HEAD_DIM), jnp.float32),
        )
        best, totals_soft, accum = attend_keys(
            start_state,
            query_heads,
            query_pos,
            query_ids,
            lax.all_gather(key_rows, "ctx", axis=0, tiled=True),
            lax.all_gather(value_rows, "ctx", axis=0, tiled=True),
            store_pos,
            ids_store,
            scale,
        )
        log_total = best + jnp.log(totals_soft)
        attended = accum / jnp.transpose(totals_soft)[..., None]
        attended_low = attended.reshape(tok_rows, width).astype(jnp.bfloat16)
        branch = jnp.dot(attended_low, proj_out, preferred_element_type=jnp.float32) + bias_out_f
        middle = inputs + branch
        h_second, pull_second = jax.vjp(layer_norm, middle, gain_two_f, shift_two_f)
        h_second_low = h_second.astype(jnp.bfloat16)
        logits = jnp.dot(h_second_low, router_full, preferred_element_type=jnp.float32)
        probs = jax.nn.softmax(logits, axis=-1)
        chosen = picks[:, None] == expert_iota[None, :]
        chosen_f = chosen.astype(jnp.float32)
        gate = jnp.sum(probs * chosen_f, -1)
        ranks = jnp.cumsum(chosen.astype(jnp.int32), 0) - 1
        dispatch = (jnp.transpose(ranks)[:, None, :] == slot_iota[None, :, None]) & jnp.transpose(
            chosen
        )[:, None, :]
        dispatch_low = dispatch.astype(jnp.bfloat16)
        dispatch_f = dispatch.astype(jnp.float32)
        slot_inputs = jnp.einsum(
            "ect,td->ecd", dispatch_low, h_second_low, preferred_element_type=jnp.float32
        ).astype(jnp.bfloat16)
        inner = (
            jnp.einsum("ecd,edh->ech", slot_inputs, inner_full, preferred_element_type=jnp.float32)
            + inner_bias_f[:, None, :]
        )
        active, pull_gelu = jax.vjp(jax.nn.gelu, inner)
        active_low = active.astype(jnp.bfloat16)
        result = (
            jnp.einsum("ech,ehd->ecd", active_low, outer_full, preferred_element_type=jnp.float32)
            + outer_bias_f[:, None, :]
        )
        expert_sum = jnp.einsum("ect,ecd->td", dispatch_f, result, precision=lax.Precision.HIGHEST)
        output = middle + gate[:, None] * expert_sum
        outputs.append(output.astype(jnp.bfloat16))
        gate_grad = jnp.sum(upstream * expert_sum, -1)
        slot_grad = jnp.einsum(
            "ect,td->ecd", dispatch_f, gate[:, None] * upstream, precision=lax.Precision.HIGHEST
        ).astype(jnp.bfloat16)
        outer_bias_grad = jnp.sum(slot_grad.astype(jnp.float32), 1)
        outer_grad = jnp.einsum(
            "ech,ecd->ehd", active_low, slot_grad, preferred_element_type=jnp.float32
        )
        active_grad = jnp.einsum(
            "ecd,ehd->ech", slot_grad, outer_full, preferred_element_type=jnp.float32
        )
        inner_grad = pull_gelu(active_grad)[0].astype(jnp.bfloat16)
        inner_bias_grad = jnp.sum(inner_grad.astype(jnp.float32), 1)
        inner_w_grad = jnp.einsum(
            "ecd,ech->edh", slot_inputs, inner_grad, preferred_element_type=jnp.float32
        )
        slot_input_grad = jnp.einsum(
            "ech,edh->ecd", inner_grad, inner_full, preferred_element_type=jnp.float32
        )
        second_grad = jnp.einsum(
            "ect,ecd->td", dispatch_f, slot_input_grad, precision=lax.Precision.HIGHEST
        )
        pick_grad = gate_grad[:, None] * chosen_f
        logit_grad = probs * (pick_grad - jnp.sum(probs * pick_grad, -1, keepdims=True))
        router_grad = jnp.einsum(
            "td,te->de",
            h_second_low.astype(jnp.float32),
            logit_grad,
            precision=lax.Precision.HIGHEST,
        )
        second_grad = second_grad + jnp.einsum(
            "te,de->td", logit_grad, router_f, precision=lax.Precision.HIGHEST
        )
        middle_norm_grad, gain_two_grad, shift_two_grad = pull_second(second_grad)
        middle_grad = upstream + middle_norm_grad
        branch_grad = middle_grad.astype(jnp.bfloat16)
        out_bias_grad = jnp.sum(branch_grad.astype(jnp.float32), 0)
        out_grad = jnp.einsum(
            "td,te->de", attended_low, branch_grad, preferred_element_type=jnp.float32
        )
        attended_grad = jnp.einsum(
            "te,de->td", branch_grad, proj_out, preferred_element_type=jnp.float32
        ).astype(jnp.bfloat16)
        grad_heads = attended_grad.reshape(tok_rows, HEADS, HEAD_DIM)
        delta = jnp.transpose(jnp.sum(grad_heads.astype(jnp.float32) * attended, -1))
        key_all, value_all = gather_keys(key_rows, value_rows)
        query_grad, key_terms, value_terms = backward_range(
            query_heads,
            grad_heads,
            log_total,
            delta,
            query_pos,
            query_ids,
            key_all,
            value_all,
            store_pos,
            ids_store,
            scale,
        )
        key_grad, value_grad = (
            lax.psum_scatter(
                key_terms.astype(jnp.bfloat16), "ctx", scatter_dimension=0, tiled=True
            ).astype(jnp.float32),
            lax.psum_scatter(
                value_terms.astype(jnp.bfloat16), "ctx", scatter_dimension=0, tiled=True
            ).astype(jnp.float32),
        )
        query_low = query_grad.reshape(tok_rows, width).astype(jnp.bfloat16)
        key_low = key_grad.astype(jnp.bfloat16)
        value_low = value_grad.astype(jnp.bfloat16)
        stacked_grad = jnp.stack([query_low, key_low, value_low])
        proj_grad = jnp.einsum(
            "td,jte->jde", h_first_low, stacked_grad, preferred_element_type=jnp.float32
        )
        qv_bias_grad = jnp.stack(
            [jnp.sum(query_low.astype(jnp.float32), 0), jnp.sum(value_low.astype(jnp.float32), 0)]
        )
        first_grad = jnp.einsum(
            "jte,jde->td", stacked_grad, proj_all, preferred_element_type=jnp.float32
        )
        input_norm_grad, gain_one_grad, shift_one_grad = pull_first(first_grad)
        input_grads.append(middle_grad + input_norm_grad)
        attn_terms = (
            gain_one_grad,
            shift_one_grad,
            proj_grad,
            qv_bias_grad,
            out_grad,
            out_bias_grad,
            gain_two_grad,
            shift_two_grad,
            router_grad,
        )
        expert_terms = (inner_w_grad, inner_bias_grad, outer_grad, outer_bias_grad)
        local_terms = attn_terms + expert_terms
        totals = local_terms if totals is None else jax.tree.map(jnp.add, totals, local_terms)
    totals = reduce_grads(totals[:9], totals[9:])
    (
        g_one,
        s_one,
        g_qkv,
        g_qv,
        g_out,
        g_outb,
        g_two,
        s_two,
        g_router,
        g_in,
        g_inb,
        g_back,
        g_backb,
    ) = totals
    mixed = jnp.stack(outputs)[:, None]
    token_grad = jnp.stack(input_grads)[:, None]
    return (
        mixed,
        token_grad,
        g_one,
        s_one,
        g_qkv,
        g_qv,
        g_out,
        g_outb,
        g_two,
        s_two,
        g_router,
        g_in,
        g_inb,
        g_back,
        g_backb,
    )


MESH_ID = pl.DeviceIdType.MESH
BF = jnp.bfloat16
F32 = jnp.float32
DMA = pltpu.SemaphoreType.DMA
VMEM_CAP = 60 * 1024 * 1024
SMALL_ROWS = 32
NT = (((1,), (1,)), ((), ()))
TN = (((0,), (0,)), ((), ()))
NN = (((1,), (0,)), ((), ()))


def mm(left, right, dims=NN):
    return lax.dot_general(left, right, dims, preferred_element_type=F32)


def plane_coords():
    me = lax.axis_index("ctx")
    core = me % 2
    col = (me // 2) % 2
    row = me // 4
    sib = me + 1 - 2 * core
    xn = (row * 2 + 1 - col) * 2 + core
    yn = ((1 - row) * 2 + col) * 2 + core
    dg = ((1 - row) * 2 + 1 - col) * 2 + core
    return me, core, sib, xn, yn, dg


def meet(ctx_peers, fsdp_peers=()):
    sem = pltpu.get_barrier_semaphore()
    for peer in ctx_peers:
        pl.semaphore_signal(sem, inc=1, device_id={"ctx": peer}, device_id_type=MESH_ID)
    for peer in fsdp_peers:
        pl.semaphore_signal(sem, inc=1, device_id={"fsdp": peer}, device_id_type=MESH_ID)
    pl.semaphore_wait(sem, len(ctx_peers) + len(fsdp_peers))


def send_to(src, dst, send_sem, recv_sem, axis, peer):
    return pltpu.make_async_remote_copy(
        src_ref=src,
        dst_ref=dst,
        send_sem=send_sem,
        recv_sem=recv_sem,
        device_id={axis: peer},
        device_id_type=MESH_ID,
    )


def gather_sems(chunks):
    return [
        DMA((2, chunks)),
        DMA((2, chunks)),
        DMA((chunks,)),
        DMA((chunks,)),
        DMA((3, chunks)),
        DMA((3, chunks)),
        DMA((chunks,)),
        DMA((chunks,)),
        DMA((chunks,)),
    ]


def line_sems(chunks):
    return [DMA((3, chunks)), DMA((3, chunks)), DMA((3, chunks)), DMA((3, chunks)), DMA((chunks,))]


def by_rows(count, step, visit):
    def one(index, carry):
        visit(pl.ds(pl.multiple_of(index * step, step), step))
        return carry

    lax.fori_loop(0, count // step, one, 0)


def ring_ops(own, slot, sems):
    ns, nr, ds, dr, fs, fr, ss, sr, ls = sems
    me, core, sib, xn, yn, dg = plane_coords()
    near = (xn, yn)

    def away(i, k):
        return send_to(own(k), slot(me, k), ns.at[i, k], nr.at[i, k], "ctx", near[i])

    def beside(k):
        return send_to(own(k), slot(me, k), ss.at[k], sr.at[k], "ctx", sib)

    def here(k):
        return pltpu.make_async_copy(own(k), slot(me, k), ls.at[k])

    def passed(k):
        block = slot(near[k % 2], k)
        return send_to(block, block, ds.at[k], dr.at[k], "ctx", near[1 - k % 2])

    def onward(i, k):
        block = slot((xn, yn, dg)[i], k)
        return send_to(block, block, fs.at[i, k], fr.at[i, k], "ctx", sib)

    def begin(k):
        for i in (0, 1):
            away(i, k).start()
        beside(k).start()
        here(k).start()

    def relay(k):
        for i in (k % 2, 1 - k % 2):
            away(i, k).wait_recv()
            if i == k % 2:
                passed(k).start()
            onward(i, k).start()

    def diag(k):
        passed(k).wait_recv()
        onward(2, k).start()

    def done(k):
        here(k).wait()
        beside(k).wait_recv()
        for i in range(3):
            onward(i, k).wait_recv()

    def finish(k):
        for i in (0, 1):
            away(i, k).wait_send()
        beside(k).wait_send()
        passed(k).wait_send()
        for i in range(3):
            onward(i, k).wait_send()

    return begin, relay, diag, done, finish


def line_ops(own, slot, chunks, sems):
    us, ur, ws, wr, ls = sems
    z = lax.axis_index("fsdp")

    def up(d, k):
        src = own(k) if d == 0 else slot(z - d, k)
        return send_to(src, slot(z - d, k), us.at[d, k], ur.at[d, k], "fsdp", z + 1)

    def down(d, k):
        src = own(k) if d == 0 else slot(z + d, k)
        return send_to(src, slot(z + d, k), ws.at[d, k], wr.at[d, k], "fsdp", z - 1)

    def from_below(d, k):
        return send_to(own(k), slot(z - d - 1, k), us.at[d, k], ur.at[d, k], "fsdp", z - 1)

    def from_above(d, k):
        return send_to(own(k), slot(z + d + 1, k), ws.at[d, k], wr.at[d, k], "fsdp", z + 1)

    def here(k):
        return pltpu.make_async_copy(own(k), slot(z, k), ls.at[k])

    def pass_one(d, k):
        @pl.when((z < 3) & (z >= d))
        def _():
            if d:
                from_below(d - 1, k).wait_recv()
            up(d, k).start()

        @pl.when((z > 0) & (z + d <= 3))
        def _():
            if d:
                from_above(d - 1, k).wait_recv()
            down(d, k).start()

    def pass_on(d, which=None):
        for k in range(chunks) if which is None else which:
            pass_one(d, k)

    def begin():
        for k in range(chunks):
            here(k).start()
        pass_on(0)

    def arrive():
        for d in range(3):
            for k in range(chunks):

                @pl.when(z == 3)
                def _():
                    from_below(d, k).wait_recv()

                @pl.when(z == 0)
                def _():
                    from_above(d, k).wait_recv()

        for k in range(chunks):
            here(k).wait()

    def finish():
        for d in range(3):
            for k in range(chunks):

                @pl.when((z < 3) & (z >= d))
                def _():
                    up(d, k).wait_send()

                @pl.when((z > 0) & (z + d <= 3))
                def _():
                    down(d, k).wait_send()

    return begin, pass_on, arrive, finish


def sum_scratch():
    return [pltpu.VMEM((2, 4, 128, 1024), BF)] + [pltpu.VMEM((2, 128, 1024), BF)] * 6 + [
        DMA((2, 4)), DMA((2, 4)), DMA((2, 6)), DMA((2, 6)),
    ]


def sum_ops(part, m, out, scratch):
    pair, gs, gr, xs, xr, ys, yr = [ref.at[m] for ref in scratch[:7]]
    s1, r1, s2, r2 = scratch[7:]
    me, core, sib, xn, yn, dg = plane_coords()
    order = (dg, xn, yn, me)
    lo, hi = pl.ds(0, 64), pl.ds(64, 64)

    def to_pair(i):
        other = order[i] + 1 - 2 * core
        return send_to(part.at[m, other], pair.at[i], s1.at[m, i], r1.at[m, i], "ctx", sib)

    def ship(index):
        src, dst, peer = (
            (gs.at[lo], gr.at[lo], xn),
            (gs.at[hi], gr.at[hi], yn),
            (xs.at[lo], xr.at[lo], xn),
            (ys.at[hi], yr.at[hi], yn),
            (ys.at[lo], yr.at[lo], yn),
            (xs.at[hi], xr.at[hi], xn),
        )[index]
        return send_to(src, dst, s2.at[m, index], r2.at[m, index], "ctx", peer)

    def f32(value):
        return value.astype(F32)

    def both(i, rr):
        return f32(part[m, order[i], rr]) + f32(pair[i, rr])

    def begin():
        for i in range(4):
            to_pair(i).start()

    def span(offset, count, visit):
        def one(index):
            visit(pl.ds(offset + index.start, 32))

        by_rows(count, 32, one)

    def diag():
        to_pair(0).wait_recv()

        def add(rr):
            gs[rr] = both(0, rr).astype(BF)

        span(0, 128, add)
        ship(0).start()
        ship(1).start()

    def near():
        to_pair(1).wait_recv()

        def add_x(rr):
            xs[rr] = both(1, rr).astype(BF)

        span(0, 64, add_x)
        ship(2).start()
        to_pair(2).wait_recv()

        def add_y(rr):
            ys[rr] = both(2, rr).astype(BF)

        span(64, 64, add_y)
        ship(3).start()

    def join():
        ship(0).wait_recv()

        def add_y(rr):
            ys[rr] = (both(2, rr) + f32(gr[rr])).astype(BF)

        span(0, 64, add_y)
        ship(4).start()
        ship(1).wait_recv()

        def add_x(rr):
            xs[rr] = (both(1, rr) + f32(gr[rr])).astype(BF)

        span(64, 64, add_x)
        ship(5).start()

    def finish():
        to_pair(3).wait_recv()
        for index in (2, 3, 4, 5):
            ship(index).wait_recv()

        def add(rr):
            place = pl.ds(m * 128 + rr.start, 32)
            out[place] = both(3, rr) + f32(xr[rr]) + f32(yr[rr])

        span(0, 128, add)
        for i in range(4):
            to_pair(i).wait_send()
        for index in range(6):
            ship(index).wait_send()

    return begin, diag, near, join, finish


def fold_scratch(rows):
    return [
        pltpu.VMEM((2, 3, rows, 1024), BF),
        pltpu.VMEM((2, 2, rows, 1024), BF),
        DMA((2, 3, 2)),
        DMA((2, 3, 2)),
    ]


def fold_ops(block, rows, out, scratch):
    got, sent, ss, rs = scratch
    z = lax.axis_index("fsdp")
    half = rows // 2
    places = (z, 3 - z)
    nexts = ((z + 1) % 4, (z + 3) % 4)

    def target(side, q):
        return q if side == 0 else 3 - q

    def piece(ref, h):
        return ref.at[pl.ds(half * h, half)]

    def message(src, side, q, h):
        return send_to(
            piece(src, h), piece(got.at[side, q - 1], h), ss.at[side, q - 1, h], rs.at[side, q - 1, h],
            "fsdp", nexts[side],
        )

    def first(side, q, h):
        return message(block(target(side, q)), side, q, h)

    def later(side, q, h):
        return message(sent.at[side, q - 2], side, q, h)

    def begin():
        for side in (0, 1):

            @pl.when(places[side] == 0)
            def _():
                for q in (3, 2, 1):
                    for h in (0, 1):
                        first(side, q, h).start()

    def relay(at, q, h):
        for side in (0, 1):

            @pl.when(places[side] == at)
            def _():
                later(side, q, h).wait_recv()
                mine = block(target(side, q))

                def add(index):
                    rr = pl.ds(half * h + index.start, 32)
                    total = mine[rr].astype(F32) + got[side, q - 1, rr].astype(F32)
                    sent[side, q - 2, rr] = total.astype(BF)

                by_rows(half, 32, add)
                later(side, q, h).start()

    def step(n):
        for at, q, h in (((1, 3, 0),), ((1, 3, 1), (2, 3, 0)), ((1, 2, 0), (2, 3, 1)), ((1, 2, 1),))[n]:
            relay(at, q, h)

    def finish():
        mine = block(z)
        for side in (0, 1):

            @pl.when(places[side] > 0)
            def _():
                for h in (0, 1):
                    q = places[side]
                    send_to(
                        piece(mine, h), piece(got.at[side, q - 1], h), ss.at[side, q - 1, h],
                        rs.at[side, q - 1, h], "fsdp", nexts[side],
                    ).wait_recv()

        def add_all(sides):
            def add(rr):
                total = mine[rr].astype(F32)
                for side in sides:
                    total = total + got[side, places[side] - 1, rr].astype(F32)
                out[rr] = total.astype(BF)

            by_rows(rows, 32, add)

        @pl.when(z == 0)
        def _():
            add_all((1,))

        @pl.when(z == 3)
        def _():
            add_all((0,))

        @pl.when((z > 0) & (z < 3))
        def _():
            add_all((0, 1))

        for side in (0, 1):
            for at, qs in ((0, (3, 2, 1)), (1, (3, 2)), (2, (3,))):

                @pl.when(places[side] == at)
                def _():
                    for q in qs:
                        for h in (0, 1):
                            first(side, q, h).wait_send()

    return begin, step, finish


def vmem_spec():
    return pl.BlockSpec(memory_space=pltpu.VMEM)


def any_spec():
    return pl.BlockSpec(memory_space=pl.ANY)


def natural_slot(device, k):
    micro, part = k // 2, k % 2
    return micro * 16 + (device if part == 0 else 15 - device)


def remote_params(ident):
    return pltpu.CompilerParams(
        collective_id=ident, has_side_effects=True, vmem_limit_bytes=VMEM_CAP
    )


def line_peers():
    z = lax.axis_index("fsdp")
    return [(z + d) % 4 for d in (1, 2, 3)]


def token_docs(row_ref, m):
    row = jnp.broadcast_to(row_ref[m].astype(F32), (8, 1024))
    return row[0:1], jnp.transpose(row)[:, 0:1]


def front_kernel(
    x_ref, small_ref, doc_ref, wq_ref, wo_ref, wi_ref, picks_ref, dy_ref,
    h_ref, params_ref, wqc_ref, woc_ref, wic_ref, qkv_ref, of_ref, lse_ref,
    y_ref, h2_ref, stat_ref, disp_ref, hslot_ref, dslot_ref,
    out_ref, hs, units, part, zs, zr, os, orr, ol, *sems,
):
    me, core, sib, xn, yn, dg = plane_coords()
    z = lax.axis_index("fsdp")
    peers = line_peers()
    meet((sib, xn, yn), peers)
    params_ref[z] = small_ref[...]
    copies = []
    for i, peer in enumerate(peers):
        copy = send_to(small_ref, params_ref.at[z], zs.at[i], zr.at[i], "fsdp", peer)
        copy.start()
        copies.append(copy)
    owner = me // 2
    columns = pl.ds(pl.multiple_of(me * 128, 128), 128)
    expert, quarter = me // 4, me % 4

    def wq_slot(where, k):
        return wqc_ref.at[k, pl.ds(pl.multiple_of(where * 256, 256), 256)]

    def wi_own(k):
        return wi_ref.at[expert, :, pl.ds(pl.multiple_of(k * 1024 + quarter * 256, 256), 256)]

    def wi_slot(where, k):
        return wic_ref.at[pl.ds(pl.multiple_of(where * 256, 256), 256), pl.ds(256 * k, 256)]

    q_begin, q_pass, q_arrive, q_finish = line_ops(
        lambda k: wq_ref.at[k, :, columns], wq_slot, 3, sems[:5]
    )
    i_begin, i_pass, i_arrive, i_finish = line_ops(wi_own, wi_slot, 4, sems[5:10])
    begin, relay, diag, done, finish = ring_ops(
        lambda k: hs.at[pl.ds(64 * k, 64)],
        lambda device, k: h_ref.at[natural_slot(device, k)],
        sems[10:19],
    )
    sums = [sum_ops(part, m, out_ref, sems[19:]) for m in (0, 1)]
    q_begin()

    wo_own = wo_ref.at[pl.ds(pl.multiple_of(core * 128, 128), 128)]

    def wo_step(src, side):
        return send_to(
            src, woc_ref, os.at[side], orr.at[side], "fsdp", z + 1 if side == 0 else z - 1
        )

    def wo_both(act):
        @pl.when((z >= owner) & (z < 3))
        def _():
            act(0)

        @pl.when((z <= owner) & (z > 0))
        def _():
            act(1)

    def wo_begin():
        @pl.when(z == owner)
        def _():
            pltpu.make_async_copy(wo_own, woc_ref, ol).start()
            wo_both(lambda side: wo_step(wo_own, side).start())

    def wo_arrive():
        @pl.when(z > owner)
        def _():
            wo_step(woc_ref, 0).wait_recv()

        @pl.when(z < owner)
        def _():
            wo_step(woc_ref, 1).wait_recv()

    def wo_pass(d):
        @pl.when((z == owner + d) | (z == owner - d))
        def _():
            wo_arrive()
            wo_both(lambda side: wo_step(woc_ref, side).start())

    def wo_last():
        @pl.when((z == owner + 3) | (z == owner - 3))
        def _():
            wo_arrive()

        @pl.when(z == owner)
        def _():
            pltpu.make_async_copy(wo_own, woc_ref, ol).wait()

    wo_begin()

    def unit(rr):
        values = x_ref[rr].astype(F32)
        centred = values - jnp.mean(values, -1, keepdims=True)
        spread = jnp.mean(centred * centred, -1, keepdims=True)
        units[rr] = centred * lax.rsqrt(spread + norm_eps)

    by_rows(256, 32, unit)
    for copy in copies:
        copy.wait()

    def full_row(r):
        return jnp.concatenate([params_ref[i, r : r + 1, :] for i in range(4)], axis=1).astype(F32)

    gain, shift = full_row(0), full_row(1)

    def norm(rr):
        hs[rr] = (units[rr] * gain + shift).astype(BF)

    by_rows(256, 32, norm)
    begin(0)
    begin(1)
    q_pass(1)
    relay(0)
    relay(1)
    begin(2)
    begin(3)
    wo_pass(1)
    q_pass(2)
    i_begin()
    diag(0)
    diag(1)
    wo_pass(2)
    done(0)
    done(1)
    q_arrive()
    half = pl.ds(pl.multiple_of(core * 128, 128), 128)
    q_bias = params_ref[owner, 2:3, half].astype(F32)
    v_bias = params_ref[owner, 3:4, half].astype(F32)
    masks = head_masks(256)
    vmasks = head_masks(1024)
    zero = jnp.zeros((), BF)

    def micro(m, carry):
        @pl.when(m == 1)
        def _():
            done(2)
            done(3)

        h = h_ref[pl.ds(16 * m, 16)].reshape(1024, 1024)
        place = pl.ds(pl.multiple_of(m * 1024, 1024), 1024)
        q = (mm(h, wqc_ref[0]) + q_bias).astype(BF)
        k = mm(h, wqc_ref[1]).astype(BF)
        v = (mm(h, wqc_ref[2]) + v_bias).astype(BF)
        qkv_ref[0, place] = q
        qkv_ref[1, place] = k
        qkv_ref[2, place] = v
        vh = [jnp.where(vmasks[j], v, zero) for j in (0, 1)]
        doc_row, doc_col = token_docs(doc_ref, m)
        for i in range(4):
            length = 256 * (i + 1)
            rows = slice(256 * i, 256 * (i + 1))
            qi = q[rows] * jnp.asarray(0.125, BF)
            allowed = allowed_mask(i, doc_col[rows], doc_row[:, :length])
            total = None
            stats = []
            for j in (0, 1):
                s = mm(jnp.where(masks[j], qi, zero), k[:length], NT)
                s = jnp.where(allowed, s, mask_fill)
                top = jnp.max(s, -1, keepdims=True)
                e = jnp.exp(s - top)
                den = jnp.sum(e, -1, keepdims=True)
                p = (e * (1.0 / den)).astype(BF)
                term = mm(p, vh[j][:length])
                total = term if total is None else total + term
                stats.append(top + jnp.log(den))
            at = pl.ds(pl.multiple_of(m * 1024 + 256 * i, 256), 256)
            lse_ref[at] = jnp.where(masks[0], stats[0], stats[1])
            of_ref[at] = total

            @pl.when(m == 0)
            def _():
                if i == 0:
                    relay(2)
                    relay(3)
                if i == 1:
                    i_pass(1, (0,))
                    diag(2)
                if i == 2:
                    i_pass(1, (1,))
                    diag(3)
                if i == 3:
                    wo_last()

            @pl.when(m == 1)
            def _():
                if i == 1:
                    sums[0][3]()
                if i == 3:
                    i_pass(2, (0,))

        for i in range(4):
            at = pl.ds(pl.multiple_of(m * 1024 + 256 * i, 256), 256)
            a = mm(of_ref[at].astype(BF), woc_ref[...]).astype(BF)
            for b in range(4):
                block = 4 * i + b
                dest, side = (block, 0) if block < 8 else (15 - block, 1)
                part[m, dest, 64 * side : 64 * (side + 1)] = a[64 * b : 64 * (b + 1)]

        for n in (0, 1):

            @pl.when(m == n)
            def _():
                for step in sums[n][:3]:
                    step()
                if n == 0:
                    i_pass(1, (2, 3))

        return carry

    lax.fori_loop(0, 2, micro, 0)
    outb, gain2, shift2 = full_row(4), full_row(5), full_row(6)
    router = jnp.concatenate([full_row(7), full_row(8)], axis=0).astype(BF)

    def route(m):
        picked = jnp.broadcast_to(picks_ref[m : m + 1].astype(F32), (8, 128))
        sub = lax.broadcasted_iota(jnp.int32, (8, 128), 0)
        member = jnp.where(sub == 0, 1.0 - picked, picked)
        earlier = lax.broadcasted_iota(jnp.int32, (128, 128), 0)
        later = lax.broadcasted_iota(jnp.int32, (128, 128), 1)
        rank = mm(member.astype(BF), (earlier < later).astype(BF))
        slot = lax.broadcasted_iota(jnp.int32, (CAP, 128), 0).astype(F32)
        for e in (0, 1):
            hit = (rank[e : e + 1] == slot) & (member[e : e + 1] > 0.5)
            disp_ref[m, e] = hit.astype(BF)
        return jnp.transpose(picked)[:, 0:1]

    def second_norm(m):
        pick = route(m)
        base = 128 * m

        def visit(index):
            rr = pl.ds(base + index.start, 32)
            values = x_ref[rr].astype(F32) + (out_ref[rr] + outb)
            y_ref[rr] = values
            centred = values - jnp.mean(values, -1, keepdims=True)
            spread = jnp.mean(centred * centred, -1, keepdims=True)
            h2_ref[rr] = (centred * lax.rsqrt(spread + norm_eps) * gain2 + shift2).astype(BF)

        by_rows(128, 32, visit)
        span = pl.ds(base, 128)
        h2 = h2_ref[span]
        logits = mm(h2, router, NT)
        top = jnp.max(logits, -1, keepdims=True)
        e = jnp.exp(logits - top)
        probs = e / jnp.sum(e, -1, keepdims=True)
        gate = jnp.where(pick > 0.5, probs[:, 1:2], probs[:, 0:1])
        lane = lax.broadcasted_iota(jnp.int32, (128, 128), 1)
        packed = jnp.where(lane == 0, probs[:, 0:1], probs[:, 1:2])
        packed = jnp.where(lane == 2, gate, packed)
        stat_ref[span] = jnp.where(lane == 3, pick, packed)
        du = (gate * dy_ref[span].astype(F32)).astype(BF)
        for which in (0, 1):
            hslot_ref[which, m] = mm(disp_ref[m, which], h2).astype(BF)
            dslot_ref[which, m] = mm(disp_ref[m, which], du).astype(BF)

    i_pass(2, (1,))
    sums[1][3]()
    i_pass(2, (2, 3))
    sums[0][4]()
    second_norm(0)
    sums[1][4]()
    second_norm(1)
    i_arrive()
    wo_both(lambda side: wo_step(woc_ref, side).wait_send())
    q_finish()
    i_finish()
    for k in range(4):
        finish(k)


def front_call(x, small, docs, w_qkv, w_out, w_in, picks, dy):
    return pl.pallas_call(
        front_kernel,
        out_shape=(
            jax.ShapeDtypeStruct((32, 64, 1024), BF),
            jax.ShapeDtypeStruct((4, SMALL_ROWS, 256), BF),
            jax.ShapeDtypeStruct((3, 1024, 128), BF),
            jax.ShapeDtypeStruct((128, 1024), BF),
            jax.ShapeDtypeStruct((1024, 1024), BF),
            jax.ShapeDtypeStruct((3, 2048, 128), BF),
            jax.ShapeDtypeStruct((2048, 128), F32),
            jax.ShapeDtypeStruct((2048, 128), F32),
            jax.ShapeDtypeStruct((256, 1024), F32),
            jax.ShapeDtypeStruct((256, 1024), BF),
            jax.ShapeDtypeStruct((256, 128), F32),
            jax.ShapeDtypeStruct((2, 2, CAP, 128), BF),
            jax.ShapeDtypeStruct((2, 2, CAP, 1024), BF),
            jax.ShapeDtypeStruct((2, 2, CAP, 1024), BF),
        ),
        in_specs=[vmem_spec()] * 3 + [any_spec()] * 3 + [vmem_spec()] * 2,
        out_specs=[vmem_spec()] * 4 + [any_spec()] + [vmem_spec()] * 9,
        scratch_shapes=[
            pltpu.VMEM((256, 1024), F32),
            pltpu.VMEM((256, 1024), BF),
            pltpu.VMEM((256, 1024), F32),
            pltpu.VMEM((2, 8, 128, 1024), BF),
            DMA((3,)),
            DMA((3,)),
            DMA((2,)),
            DMA((2,)),
            DMA(()),
        ]
        + line_sems(3)
        + line_sems(4)
        + gather_sems(4)
        + sum_scratch(),
        name="front",
        compiler_params=remote_params(0),
    )(x, small, docs, w_qkv, w_out, w_in, picks, dy)


def moe_call(h_slots, d_slots, win, w_back, params, y1, h2, stats, dispatch, dy):
    def kernel(
        h_ref, d_ref, wi_ref, wall_ref, params_ref, y_ref, h2_ref, stat_ref, disp_ref, dy_ref,
        gi_ref, gbs_ref, mixed_ref, dy1_ref, da_ref, v_ref,
        o_ref, gib_ref, acc, wb_ref, gba, u_ref, g_ref, rows, gz, slope, dz, part, pair, sent, got,
        ns, nr, fs, fr, ss, sr, ls, s1, r1, s2, r2, *wsems,
    ):
        me, core, sib, xn, yn, dg = plane_coords()
        expert, quarter = me // 4, me % 4
        meet((sib, xn, yn, dg), line_peers())
        w_begin, w_pass, w_arrive, w_finish = line_ops(
            lambda k: wall_ref.at[expert, pl.ds(pl.multiple_of(quarter * 256 + 64 * k, 64), 64)],
            lambda where, k: wb_ref.at[pl.ds(pl.multiple_of(where * 256 + 64 * k, 64), 64)],
            4,
            wsems[:5],
        )
        z_begin, z_step, z_finish = fold_ops(lambda where: gba.at[where], 256, gbs_ref, wsems[5:])
        w_begin()
        peers = (dg, xn, yn)
        wanted = (1 - expert, expert, 1 - expert)
        ins = (h_ref, d_ref)

        def away(t, m, i):
            return send_to(
                ins[t].at[wanted[i], m], rows.at[t, m, me], ns.at[t, m, i], nr.at[t, m, i], "ctx", peers[i]
            )

        def beside(t, m):
            return send_to(
                ins[t].at[expert, m], rows.at[t, m, me], ss.at[t, m], sr.at[t, m], "ctx", sib
            )

        def here(t, m):
            return pltpu.make_async_copy(ins[t].at[expert, m], rows.at[t, m, me], ls.at[t, m])

        def onward(t, m, i):
            block = rows.at[t, m, peers[i]]
            return send_to(block, block, fs.at[t, m, i], fr.at[t, m, i], "ctx", sib)

        for t in (0, 1):
            for m in (0, 1):
                for i in range(3):
                    away(t, m, i).start()
        for t in (0, 1):
            for m in (0, 1):
                beside(t, m).start()
                here(t, m).start()

        def arrive(t, m):
            for i in range(3):
                away(t, m, i).wait_recv()
                onward(t, m, i).start()
            here(t, m).wait()
            beside(t, m).wait_recv()
            for i in range(3):
                onward(t, m, i).wait_recv()

        order = (dg, xn, yn, me)

        def to_pair(t, m, i):
            other = order[i] + 1 - 2 * core
            return send_to(
                part.at[t, m, other], pair.at[t, m, i], s1.at[t, m, i], r1.at[t, m, i], "ctx", sib
            )

        def to_home(t, m, i):
            return send_to(
                sent.at[t, m, i], got.at[t, m, i], s2.at[t, m, i], r2.at[t, m, i], "ctx", order[i]
            )

        def join(t, m):
            for i in range(3):
                to_pair(t, m, i).wait_recv()
                mine = order[i]

                def add(rr):
                    sent[t, m, i, rr] = (
                        part[t, m, mine, rr].astype(F32) + pair[t, m, i, rr].astype(F32)
                    ).astype(BF)

                by_rows(CAP, 16, add)
                to_home(t, m, i).start()

        mine_row = lax.broadcasted_iota(jnp.int32, (8, 256), 0) == me
        in_bias = jnp.concatenate(
            [
                jnp.sum(
                    jnp.where(mine_row, params_ref[i, 9:17, :].astype(F32), 0.0), 0, keepdims=True
                )
                for i in range(4)
            ],
            axis=1,
        )

        def inner_rows(m):
            def visit(half, carry):
                xs = rows[0, m, pl.ds(4 * half, 4)].reshape(4 * CAP, 1024)
                zed = mm(xs, wi_ref[...]) + in_bias
                square = zed * zed
                t = jnp.tanh(zed * (GELU_A + GELU_A * GELU_B * square))
                half_up = 0.5 + 0.5 * t
                place = pl.ds(pl.multiple_of(m * 8 * CAP + half * 4 * CAP, 4 * CAP), 4 * CAP)
                gz[place] = (zed * half_up).astype(BF)
                slope[place] = half_up + 0.5 * zed * (1.0 - t * t) * (
                    GELU_A + 3.0 * GELU_A * GELU_B * square
                )
                return carry

            lax.fori_loop(0, 2, visit, 0)

        def inner(m, carry):
            @pl.when(m == 0)
            def _():
                w_pass(1, (0, 1))

            arrive(0, m)

            @pl.when(m == 0)
            def _():
                w_pass(1, (2,))

            inner_rows(m)

            @pl.when(m == 0)
            def _():
                w_pass(1, (3,))

            return carry

        lax.fori_loop(0, 2, inner, 0)
        w_pass(2, (0, 1))
        arrive(1, 0)
        w_pass(2, (2, 3))
        arrive(1, 1)

        def back_grads(j, carry):
            column = pl.ds(pl.multiple_of(256 * j, 256), 256)
            du = rows[1].reshape(16 * CAP, 1024)
            gba[j] = mm(gz[:, column], du, TN).astype(BF)
            return carry

        lax.fori_loop(0, 4, back_grads, 0)
        z_begin()
        w_arrive()

        def forward(m, carry):
            def visit(half, inner_carry):
                place = pl.ds(pl.multiple_of(m * 8 * CAP + half * 4 * CAP, 4 * CAP), 4 * CAP)
                u = mm(gz[place], wb_ref[...]).astype(BF)
                part[0, m, pl.ds(4 * half, 4)] = u.reshape(4, CAP, 1024)
                return inner_carry

            lax.fori_loop(0, 2, visit, 0)
            for i in range(4):
                to_pair(0, m, i).start()
            return carry

        lax.fori_loop(0, 2, forward, 0)
        join(0, 0)
        join(0, 1)
        z_step(0)
        gib_ref[...] = jnp.zeros_like(gib_ref)

        def backward(m, carry):
            def rows_backward(half, inner_carry):
                du = rows[1, m, pl.ds(4 * half, 4)].reshape(4 * CAP, 1024)
                place = pl.ds(pl.multiple_of(m * 8 * CAP + half * 4 * CAP, 4 * CAP), 4 * CAP)
                low = (mm(du, wb_ref[...], NT) * slope[place]).astype(BF)
                dz[place] = low
                gib_ref[...] += jnp.sum(low.astype(F32), 0, keepdims=True)
                dh = mm(low, wi_ref[...], NT).astype(BF)
                part[1, m, pl.ds(4 * half, 4)] = dh.reshape(4, CAP, 1024)
                return inner_carry

            lax.fori_loop(0, 2, rows_backward, 0)
            for i in range(4):
                to_pair(1, m, i).start()
            join(1, m)

            @pl.when(m == 0)
            def _():
                z_step(1)

            return carry

        lax.fori_loop(0, 2, backward, 0)
        z_step(2)

        def weight_grads(j, carry):
            column = pl.ds(pl.multiple_of(256 * j, 256), 256)
            xs = rows[0, :, :, :, column].reshape(16 * CAP, 256)
            gi_ref[column] = mm(xs, dz[...], TN).astype(BF)
            return carry

        lax.fori_loop(0, 4, weight_grads, 0)
        z_step(3)

        def full_row(r):
            return jnp.concatenate(
                [params_ref[i, r : r + 1, :] for i in range(4)], axis=1
            ).astype(F32)

        gain2, router0, router1 = full_row(5), full_row(7), full_row(8)
        bias0, bias1 = full_row(17), full_row(18)
        acc[...] = jnp.zeros_like(acc)

        def home(t, m):
            to_pair(t, m, 3).wait_recv()
            for i in range(3):
                to_home(t, m, i).wait_recv()

            def finish(rr):
                o_ref[expert, t, m, rr] = (
                    part[t, m, me, rr].astype(F32)
                    + pair[t, m, 3, rr].astype(F32)
                    + got[t, m, 1, rr].astype(F32)
                )
                o_ref[1 - expert, t, m, rr] = got[t, m, 0, rr].astype(F32) + got[
                    t, m, 2, rr
                ].astype(F32)

            by_rows(CAP, 16, finish)

        def to_tokens(t, m):
            total = None
            for e in (0, 1):
                value = o_ref[e, t, m]
                for _ in range(3):
                    low = value.astype(BF)
                    term = mm(disp_ref[m, e], low, TN)
                    total = term if total is None else total + term
                    value = value - low.astype(F32)
            return total

        def token_rows(m):
            span = pl.ds(128 * m, 128)
            home(0, m)
            u_ref[...] = to_tokens(0, m)
            home(1, m)
            g_ref[...] = to_tokens(1, m)

            def visit(index):
                rr = pl.ds(128 * m + index.start, 32)
                local = pl.ds(index.start, 32)
                stat = stat_ref[rr]
                p0, p1, gate, pick = (stat[:, i : i + 1] for i in range(4))
                dy = dy_ref[rr].astype(F32)
                values = y_ref[rr]
                u = u_ref[local] + jnp.where(pick > 0.5, bias1, bias0)
                mixed_ref[rr] = (values + gate * u).astype(BF)
                dgate = jnp.sum(dy * u, -1, keepdims=True)
                d0, d1 = dgate * (1.0 - pick), dgate * pick
                mean_grad = p0 * d0 + p1 * d1
                l0, l1 = p0 * (d0 - mean_grad), p1 * (d1 - mean_grad)
                grad = g_ref[local] + (l0 * router0 + l1 * router1)
                h2f = h2_ref[rr].astype(F32)
                centred = values - jnp.mean(values, -1, keepdims=True)
                inv = lax.rsqrt(jnp.mean(centred * centred, -1, keepdims=True) + norm_eps)
                unit = centred * inv
                scaled = grad * gain2
                back = inv * (
                    scaled
                    - jnp.mean(scaled, -1, keepdims=True)
                    - unit * jnp.mean(scaled * unit, -1, keepdims=True)
                )
                dy1 = dy + back
                low = dy1.astype(BF)
                dy1_ref[rr] = dy1
                da_ref[rr] = low
                sums = (
                    low.astype(F32), grad * unit, grad, h2f * l0, h2f * l1,
                )
                for row, term in enumerate(sums):
                    acc[row : row + 1] += jnp.sum(term, 0, keepdims=True)

            by_rows(128, 32, visit)

        token_rows(0)
        token_rows(1)
        for e in (0, 1):
            for m in (0, 1):
                acc[5 + e : 6 + e] += jnp.sum(d_ref[e, m].astype(F32), 0, keepdims=True)
        v_ref[...] = jnp.zeros_like(v_ref)
        for i in range(4):
            v_ref[i, 4:11, :] = acc[0:7, 256 * i : 256 * (i + 1)]
            v_ref[i, pl.ds(11 + me, 1), :] = gib_ref[:, 256 * i : 256 * (i + 1)]
        for t in (0, 1):
            for m in (0, 1):
                for i in range(3):
                    away(t, m, i).wait_send()
                    onward(t, m, i).wait_send()
                    to_home(t, m, i).wait_send()
                for i in range(4):
                    to_pair(t, m, i).wait_send()
                beside(t, m).wait_send()
        w_finish()
        z_finish()

    return pl.pallas_call(
        kernel,
        out_shape=(
            jax.ShapeDtypeStruct((1024, 1024), BF),
            jax.ShapeDtypeStruct((256, 1024), BF),
            jax.ShapeDtypeStruct((256, 1024), BF),
            jax.ShapeDtypeStruct((256, 1024), F32),
            jax.ShapeDtypeStruct((256, 1024), BF),
            jax.ShapeDtypeStruct((4, 24, 256), F32),
        ),
        in_specs=[vmem_spec()] * 3 + [any_spec()] + [vmem_spec()] * 6,
        out_specs=[vmem_spec()] * 6,
        scratch_shapes=[
            pltpu.VMEM((2, 2, 2, CAP, 1024), F32),
            pltpu.VMEM((1, 1024), F32),
            pltpu.VMEM((8, 1024), F32),
            pltpu.VMEM((1024, 1024), BF),
            pltpu.VMEM((4, 256, 1024), BF),
            pltpu.VMEM((128, 1024), F32),
            pltpu.VMEM((128, 1024), F32),
            pltpu.VMEM((2, 2, 8, CAP, 1024), BF),
            pltpu.VMEM((16 * CAP, 1024), BF),
            pltpu.VMEM((16 * CAP, 1024), F32),
            pltpu.VMEM((16 * CAP, 1024), BF),
            pltpu.VMEM((2, 2, 8, CAP, 1024), BF),
            pltpu.VMEM((2, 2, 4, CAP, 1024), BF),
            pltpu.VMEM((2, 2, 3, CAP, 1024), BF),
            pltpu.VMEM((2, 2, 3, CAP, 1024), BF),
        ]
        + [DMA((2, 2, 3))] * 4
        + [DMA((2, 2))] * 3
        + [DMA((2, 2, 4))] * 2
        + [DMA((2, 2, 3))] * 2
        + line_sems(4)
        + fold_scratch(256),
        name="moe",
        compiler_params=remote_params(2),
    )(h_slots, d_slots, win, w_back, params, y1, h2, stats, dispatch, dy)


def final_call(gi, gb, gq, gwo, vectors, gqv, x, dh1, dy1, params):
    def kernel(
        gi_ref, gb_ref, gq_ref, go_ref, base_ref, gqv_ref, x_ref, dh_ref, dy_ref, params_ref,
        oi_ref, ob_ref, oq_ref, oo_ref, ov_ref, ot_ref,
        v_ref, acc, qgot, qsum, vgot, vsum, vall,
        qs, qr, vs, vr, ps, pr, ws, wr, hs, hr, fs, fr, ol, *sems,
    ):
        me, core, sib, xn, yn, dg = plane_coords()
        z = lax.axis_index("fsdp")
        others = [(me + d) % 8 for d in range(1, 8)]
        meet(others, line_peers())
        owner = me // 2

        def vector_copy(d):
            peer = (z + d) % 4
            return send_to(v_ref.at[peer], vgot.at[d - 1], vs.at[d - 1], vr.at[d - 1], "fsdp", peer)

        def q_copy(d):
            peer = (z + d) % 4
            block = gq_ref.at[:, pl.ds(pl.multiple_of(peer * 256, 256), 256)]
            return send_to(block, qgot.at[d - 1], qs.at[d - 1], qr.at[d - 1], "fsdp", peer)

        rows_mine = oo_ref.at[pl.ds(pl.multiple_of(core * 128, 128), 128)]
        rows_sib = oo_ref.at[pl.ds(pl.multiple_of((1 - core) * 128, 128), 128)]

        def half(ref, part):
            return ref.at[pl.ds(64 * part, 64)]

        def o_near(i):
            return send_to(go_ref, rows_mine, ws.at[i], wr, "ctx", (xn, yn)[i])

        def o_half(part):
            block = half(rows_mine, part)
            return send_to(block, block, hs, hr.at[part], "ctx", (yn, xn)[part])

        def o_pair(src):
            return send_to(src, rows_mine, fs, fr, "ctx", sib)

        row, col = me // 4, (me // 2) % 2
        own_row, own_col = z // 2, z % 2
        beside_x = (row == own_row) & (col != own_col)
        beside_y = (row != own_row) & (col == own_col)
        across = (row != own_row) & (col != own_col)

        def o_root():
            @pl.when(z == owner)
            def _():
                for i in (0, 1):
                    o_near(i).start()
                o_pair(go_ref).start()
                pltpu.make_async_copy(go_ref, rows_mine, ol).start()

        def o_relay():
            @pl.when(beside_x)
            def _():
                o_near(0).wait_recv()
                o_half(0).start()
                o_pair(rows_mine).start()

            @pl.when(beside_y)
            def _():
                o_near(1).wait_recv()
                o_half(1).start()
                o_pair(rows_mine).start()

        def o_end():
            @pl.when(across)
            def _():
                o_half(0).wait_recv()
                o_half(1).wait_recv()
                o_pair(rows_mine).start()
                o_pair(rows_mine).wait_send()

            @pl.when(z == owner)
            def _():
                for i in (0, 1):
                    o_near(i).wait_send()
                o_pair(go_ref).wait_send()
                pltpu.make_async_copy(go_ref, rows_mine, ol).wait()

            @pl.when(beside_x)
            def _():
                o_half(0).wait_send()
                o_pair(rows_mine).wait_send()

            @pl.when(beside_y)
            def _():
                o_half(1).wait_send()
                o_pair(rows_mine).wait_send()

            send_to(go_ref, rows_sib, fs, fr, "ctx", sib).wait_recv()

        def own(k):
            if k < 4:
                return gi_ref.at[:, pl.ds(256 * k, 256)]
            return gb_ref.at[pl.ds(64 * (k - 4), 64)]

        def slot(device, k):
            which, part = device // 4, device % 4
            if k < 4:
                column = pl.multiple_of(k * 1024 + part * 256, 256)
                return oi_ref.at[which, :, pl.ds(column, 256)]
            row_at = pl.multiple_of(part * 256 + 64 * (k - 4), 64)
            return ob_ref.at[which, pl.ds(row_at, 64)]

        def qslot(device, k):
            return oq_ref.at[k, :, pl.ds(pl.multiple_of(device * 128, 128), 128)]

        begin, relay, diag, done, finish = ring_ops(own, slot, sems[:9])
        q_begin, q_relay, q_diag, q_done, q_finish = ring_ops(lambda k: qsum.at[k], qslot, sems[9:18])
        for d in (1, 3, 2):
            q_copy(d).start()
        begin(0)
        begin(1)
        o_root()
        for k in range(2, 8):
            begin(k)
        gain = jnp.concatenate([params_ref[i, 0:1, :] for i in range(4)], axis=1).astype(F32)
        acc[...] = jnp.zeros_like(acc)

        def norm_rows(rr):
            values = x_ref[rr].astype(F32)
            grad = dh_ref[rr]
            centred = values - jnp.mean(values, -1, keepdims=True)
            inv = lax.rsqrt(jnp.mean(centred * centred, -1, keepdims=True) + norm_eps)
            unit = centred * inv
            scaled = grad * gain
            back = inv * (
                scaled
                - jnp.mean(scaled, -1, keepdims=True)
                - unit * jnp.mean(scaled * unit, -1, keepdims=True)
            )
            ot_ref[rr] = dy_ref[rr] + back
            acc[0:1] += jnp.sum(grad * unit, 0, keepdims=True)
            acc[1:2] += jnp.sum(grad, 0, keepdims=True)

        for k in range(4):

            def part(index):
                norm_rows(pl.ds(64 * k + index.start, 32))

            by_rows(64, 32, part)
            relay(k)
        v_ref[...] = base_ref[...]
        for i in range(4):
            v_ref[i, 0:2, :] = acc[0:2, 256 * i : 256 * (i + 1)]
        v_ref[owner, 2:4, pl.ds(pl.multiple_of(core * 128, 128), 128)] = gqv_ref[...]
        for d in (1, 2, 3):
            vector_copy(d).start()

        def plane_vector(i):
            return send_to(vsum, vall.at[i], ps.at[i], pr.at[i], "ctx", others[i])

        o_relay()
        relay(4)
        for d in (1, 3, 2):
            q_copy(d).wait_recv()
        for j in range(3):

            def add(rr):
                place = pl.ds(pl.multiple_of(z * 256 + rr.start, 32), 32)
                total = gq_ref[j, place].astype(F32)
                for i in range(3):
                    total = total + qgot[i, j, rr].astype(F32)
                qsum[j, rr] = total.astype(BF)

            by_rows(256, 32, add)
        for k in range(3):
            q_begin(k)
        for d in (1, 2, 3):
            vector_copy(d).wait_recv()
        vsum[...] = v_ref[z] + vgot[0] + vgot[1] + vgot[2]
        for i in range(7):
            plane_vector(i).start()
        relay(5)
        diag(0)
        relay(6)
        diag(1)
        relay(7)
        diag(2)
        diag(3)
        for k in range(3):
            q_relay(k)
        for k in range(4, 8):
            diag(k)
        for k in range(3):
            q_diag(k)
        o_end()
        for k in range(8):
            done(k)
        for k in range(3):
            q_done(k)
        total = vsum[...]
        for i in range(7):
            plane_vector(i).wait_recv()
            total = total + vall[i]
        ov_ref[...] = total
        for k in range(8):
            finish(k)
        for k in range(3):
            q_finish(k)
        for d in (1, 2, 3):
            vector_copy(d).wait_send()
            q_copy(d).wait_send()
        for i in range(7):
            plane_vector(i).wait_send()

    count = vectors.shape[1]
    return pl.pallas_call(
        kernel,
        out_shape=(
            jax.ShapeDtypeStruct((2, 256, 4096), BF),
            jax.ShapeDtypeStruct((2, 1024, 1024), BF),
            jax.ShapeDtypeStruct((3, 256, 1024), BF),
            jax.ShapeDtypeStruct((256, 1024), BF),
            jax.ShapeDtypeStruct((count, 256), F32),
            jax.ShapeDtypeStruct((256, 1024), F32),
        ),
        in_specs=[vmem_spec()] * 10,
        out_specs=[any_spec()] * 4 + [vmem_spec()] * 2,
        scratch_shapes=[
            pltpu.VMEM((4, count, 256), F32),
            pltpu.VMEM((8, 1024), F32),
            pltpu.VMEM((3, 3, 256, 128), BF),
            pltpu.VMEM((3, 256, 128), BF),
            pltpu.VMEM((3, count, 256), F32),
            pltpu.VMEM((count, 256), F32),
            pltpu.VMEM((7, count, 256), F32),
            DMA((3,)), DMA((3,)), DMA((3,)), DMA((3,)), DMA((7,)), DMA((7,)),
            DMA((2,)), DMA(()), DMA(()), DMA((2,)), DMA(()), DMA(()), DMA(()),
        ]
        + gather_sems(8)
        + gather_sems(3),
        name="final",
        compiler_params=remote_params(6),
    )(gi, gb, gq, gwo, vectors, gqv, x, dh1, dy1, params)


def head_masks(rows):
    lane = lax.broadcasted_iota(jnp.int32, (rows, 128), 1)
    return lane < 64, lane >= 64


def allowed_mask(i, doc_col, doc_row):
    length = 256 * (i + 1)
    qpos = lax.broadcasted_iota(jnp.int32, (256, length), 0) + 256 * i
    kpos = lax.broadcasted_iota(jnp.int32, (256, length), 1)
    return (kpos <= qpos) & (doc_col == doc_row)


def back_kernel(
    da_ref, h_ref, qkv_ref, of_ref, lse_ref, w_ref, wo_ref, doc_ref, gi_ref,
    out_ref, gq_ref, gwo_ref, gqv_ref, gis_ref,
    g_all, dqkv, part, dka, dva, probs, gwo, gwo_low, gwo_got, os, orr, *sems,
):
    me, core, sib, xn, yn, dg = plane_coords()
    meet((sib, xn, yn), line_peers())
    begin, relay, diag, done, finish = ring_ops(
        lambda k: da_ref.at[pl.ds(64 * k, 64)],
        lambda device, k: g_all.at[natural_slot(device, k)],
        sems[:9],
    )
    z_begin, z_step, z_finish = fold_ops(
        lambda where: gi_ref.at[pl.ds(pl.multiple_of(where * 256, 256), 256)],
        256,
        gis_ref,
        sems[9:13],
    )
    sums = [sum_ops(part, m, out_ref, sems[13:]) for m in (0, 1)]
    z = lax.axis_index("fsdp")
    owner = me // 2
    away = (owner - z + 4) % 4

    def to_owner():
        return send_to(gwo_low, gwo_got.at[away - 1], os, orr.at[away - 1], "fsdp", owner)

    masks = head_masks(256)
    zero = jnp.zeros((), BF)
    spans = [slice(128 * i * (i + 1), 128 * (i + 1) * (i + 2)) for i in range(4)]
    begin(0)
    begin(1)
    z_begin()

    def weigh(m, carry):
        place = pl.ds(pl.multiple_of(m * 1024, 1024), 1024)
        q, k = qkv_ref[0, place], qkv_ref[1, place]
        doc_row, doc_col = token_docs(doc_ref, m)
        for i in range(4):
            length = 256 * (i + 1)
            rows = slice(256 * i, 256 * (i + 1))
            qi = q[rows] * jnp.asarray(0.125, BF)
            allowed = allowed_mask(i, doc_col[rows], doc_row[:, :length])
            lse = lse_ref[pl.ds(pl.multiple_of(m * 1024 + 256 * i, 256), 256)]
            for j in (0, 1):
                s = mm(jnp.where(masks[j], qi, zero), k[:length], NT)
                probs[m, j, :, spans[i]] = jnp.exp(
                    jnp.where(allowed, s, mask_fill) - lse[:, 64 * j : 64 * j + 1]
                )

        @pl.when(m == 0)
        def _():
            relay(0)
            relay(1)
            begin(2)
            begin(3)

        return carry

    lax.fori_loop(0, 2, weigh, 0)
    z_step(0)
    diag(0)
    diag(1)
    done(0)
    done(1)
    kmasks = head_masks(1024)

    def micro(m, carry):
        @pl.when(m == 1)
        def _():
            done(2)
            done(3)

        place = pl.ds(pl.multiple_of(m * 1024, 1024), 1024)
        g = g_all[pl.ds(16 * m, 16)].reshape(1024, 1024)
        q, k, v = qkv_ref[0, place], qkv_ref[1, place], qkv_ref[2, place]
        do = mm(g, wo_ref[...], NT).astype(BF)
        term = mm(of_ref[place].astype(BF), g, TN)

        @pl.when(m == 0)
        def _():
            gwo[...] = term

        @pl.when(m == 1)
        def _():
            gwo_low[...] = (gwo[...] + term).astype(BF)

            @pl.when(z != owner)
            def _():
                to_owner().start()

        dka[...] = jnp.zeros_like(dka)
        dva[...] = jnp.zeros_like(dva)
        kh = [jnp.where(kmasks[j], k, zero) for j in (0, 1)]
        for i in range(4):
            length = 256 * (i + 1)
            rows = slice(256 * i, 256 * (i + 1))
            at = pl.ds(pl.multiple_of(m * 1024 + 256 * i, 256), 256)
            qi = q[rows] * jnp.asarray(0.125, BF)
            doi = do[rows]
            prod = doi.astype(F32) * of_ref[at]
            dq = None
            for j in (0, 1):
                qh = jnp.where(masks[j], qi, zero)
                doh = jnp.where(masks[j], doi, zero)
                delta = jnp.sum(jnp.where(masks[j], prod, 0.0), -1, keepdims=True)
                p = probs[m, j, :, spans[i]]
                dp = mm(doh, v[:length], NT)
                ds = (p * (dp - delta)).astype(BF)
                term = mm(ds, kh[j][:length])
                dq = term if dq is None else dq + term
                dka[:length] += mm(ds, qh, TN)
                dva[:length] += mm(p.astype(BF), doh, TN)
            dqkv[0, at] = (dq * 0.125).astype(BF)

            @pl.when(m == 0)
            def _():
                if i == 0:
                    relay(2)
                if i == 1:
                    relay(3)
                    z_step(1)
                if i == 3:
                    diag(2)
                    diag(3)
                    z_step(2)

            @pl.when(m == 1)
            def _():
                if i == 0:
                    z_step(3)
                if i == 1:
                    sums[0][3]()

        dqkv[1, place] = dka[...].astype(BF)
        dqkv[2, place] = dva[...].astype(BF)
        for i in range(4):
            at = pl.ds(pl.multiple_of(m * 1024 + 256 * i, 256), 256)
            a = mm(dqkv[0, at], w_ref[0], NT) + mm(dqkv[1, at], w_ref[1], NT)
            a = (a + mm(dqkv[2, at], w_ref[2], NT)).astype(BF)
            for b in range(4):
                block = 4 * i + b
                dest, side = (block, 0) if block < 8 else (15 - block, 1)
                part[m, dest, 64 * side : 64 * (side + 1)] = a[64 * b : 64 * (b + 1)]
        for n in (0, 1):

            @pl.when(m == n)
            def _():
                for step in sums[n][:3]:
                    step()

        return carry

    lax.fori_loop(0, 2, micro, 0)
    sums[1][3]()
    for j in range(3):
        gq_ref[j] = mm(h_ref[...].reshape(2048, 1024), dqkv[j], TN).astype(BF)
    gqv_ref[0:1] = jnp.sum(dqkv[0].astype(F32), 0, keepdims=True)
    gqv_ref[1:2] = jnp.sum(dqkv[2].astype(F32), 0, keepdims=True)
    sums[0][4]()
    sums[1][4]()
    z_finish()

    @pl.when(z != owner)
    def _():
        to_owner().wait_send()

    @pl.when(z == owner)
    def _():
        for i in range(3):
            send_to(gwo_low, gwo_got.at[i], os, orr.at[i], "fsdp", (z + 1) % 4).wait_recv()

        def add(rr):
            total = gwo_low[rr].astype(F32)
            for i in range(3):
                total = total + gwo_got[i, rr].astype(F32)
            gwo_ref[rr] = total.astype(BF)

        by_rows(128, 32, add)

    @pl.when(z != owner)
    def _():
        gwo_ref[...] = jnp.zeros_like(gwo_ref)

    for k in range(4):
        finish(k)


def back_call(da, h, qkv, of, lse, wqkv, wout, docs, gi):
    return pl.pallas_call(
        back_kernel,
        out_shape=(
            jax.ShapeDtypeStruct((256, 1024), F32),
            jax.ShapeDtypeStruct((3, 1024, 128), BF),
            jax.ShapeDtypeStruct((128, 1024), BF),
            jax.ShapeDtypeStruct((2, 128), F32),
            jax.ShapeDtypeStruct((256, 1024), BF),
        ),
        in_specs=[vmem_spec()] * 9,
        out_specs=[vmem_spec()] * 5,
        scratch_shapes=[
            pltpu.VMEM((32, 64, 1024), BF),
            pltpu.VMEM((3, 2048, 128), BF),
            pltpu.VMEM((2, 8, 128, 1024), BF),
            pltpu.VMEM((1024, 128), F32),
            pltpu.VMEM((1024, 128), F32),
            pltpu.VMEM((2, 2, 256, 2560), F32),
            pltpu.VMEM((128, 1024), F32),
            pltpu.VMEM((128, 1024), BF),
            pltpu.VMEM((3, 128, 1024), BF),
            DMA(()),
            DMA((3,)),
        ]
        + gather_sems(4)
        + fold_scratch(256)
        + sum_scratch(),
        name="back",
        compiler_params=remote_params(4),
    )(da, h, qkv, of, lse, wqkv, wout, docs, gi)


GELU_A = math.sqrt(2.0 / math.pi)
GELU_B = 0.044715


def widen_call(arrays, sums):
    count = len(arrays)
    steps = 8
    flat = [array.reshape(-1, array.shape[-1]) for array in arrays]
    sizes = [f.shape[0] // steps for f in flat]
    small = [(256,), (256,), (2, 256), (256,), (256,), (256,), (2, 256), (2, 1024), (2, 256)]

    def kernel(*refs):
        step = pl.program_id(0)
        v_ref, wide, outs = refs[count], refs[count + 1 : 2 * count + 1], refs[2 * count + 1 :]
        for src, dst, size in zip(refs[:count], wide, sizes):
            dst[...] = src[pl.ds(pl.multiple_of(step * size, 32), size)].astype(F32)

        @pl.when(step == 0)
        def _():
            for index, row in ((0, 0), (1, 1), (3, 4), (4, 5), (5, 6)):
                outs[index][...] = v_ref[row]
            outs[2][...] = v_ref[2:4]
            outs[6][...] = v_ref[7:9]
            for e in (0, 1):
                for k in range(4):
                    outs[7][e : e + 1, 256 * k : 256 * (k + 1)] = v_ref[11 + 4 * e + k : 12 + 4 * e + k]
            outs[8][...] = v_ref[9:11]

    results = pl.pallas_call(
        kernel,
        grid=(steps,),
        out_shape=[jax.ShapeDtypeStruct(f.shape, F32) for f in flat]
        + [jax.ShapeDtypeStruct(shape, F32) for shape in small],
        in_specs=[vmem_spec()] * (count + 1),
        out_specs=[pl.BlockSpec((n, f.shape[1]), lambda i: (i, 0)) for n, f in zip(sizes, flat)]
        + [vmem_spec()] * len(small),
        name="widen",
        compiler_params=pltpu.CompilerParams(vmem_limit_bytes=VMEM_CAP),
    )(*flat, sums)
    return [w.reshape(a.shape) for w, a in zip(results[:count], arrays)], results[count:]


def fast_body(
    tokens, doc_ids, routes, cotangent, ln1_gain, ln1_shift, w_qkv, qv_bias, w_out, out_bias,
    ln2_gain, ln2_shift, router, w_in, in_bias, w_back, back_bias,
):
    rows = [ln1_gain, ln1_shift, qv_bias[0], qv_bias[1], out_bias, ln2_gain, ln2_shift]
    rows += [router[:, 0], router[:, 1]]
    rows += [in_bias[e, 256 * k : 256 * (k + 1)] for e in (0, 1) for k in range(4)]
    rows += [back_bias[0], back_bias[1]]
    row_iota = lax.broadcasted_iota(jnp.int32, (SMALL_ROWS, 256), 0)
    small = jnp.zeros((SMALL_ROWS, 256), BF)
    for index, row in enumerate(rows):
        small = jnp.where(row_iota == index, row[None], small)
    x_low = tokens[:, 0].reshape(256, 1024)
    picks = routes[:, 0, :, 0]
    dy_low = cotangent[:, 0].reshape(256, 1024)
    hs, params, wqkv_c, wout_c, win_c, qkv, o_full, lse, y1, h2, stats, dispatch, h_slots, d_slots = (
        front_call(x_low, small, doc_ids, w_qkv, w_out, w_in, picks, dy_low)
    )
    gi, gb_sum, mixed, dy1, da, vectors = moe_call(
        h_slots, d_slots, win_c, w_back, params, y1, h2, stats, dispatch, dy_low
    )
    dh1, gq, gwo, gqv, gi_sum = back_call(
        da, hs, qkv, o_full, lse, wqkv_c, wout_c, doc_ids, gi
    )
    g_in, g_back, g_qkv, g_out, sums, token_grad = final_call(
        gi_sum, gb_sum, gq, gwo, vectors, gqv, x_low, dh1, dy1, params
    )
    (g_in, g_back, g_qkv, g_out, token_grad), small_grads = widen_call(
        [g_in, g_back, g_qkv, g_out, token_grad], sums
    )
    g_one, s_one, g_qv, g_outb, g_two, s_two, g_router, g_inb, g_backb = small_grads
    return (
        mixed.reshape(2, 1, 128, 1024),
        token_grad.reshape(2, 1, 128, 1024),
        g_one, s_one, g_qkv, g_qv, g_out, g_outb, g_two, s_two,
        jnp.transpose(g_router), g_in, g_inb, g_back, g_backb,
    )


def solution(mesh):
    small_plane = mesh.shape["ctx"] == 8 and mesh.shape["fsdp"] == 4
    chosen_body = fast_body if small_plane else body
    placed = (
        P(None, "fsdp", "ctx", None),
        P(None, "fsdp", None),
        P(None, "fsdp", "ctx", None),
        P(None, "fsdp", "ctx", None),
        P("fsdp"),
        P("fsdp"),
        P(None, "fsdp", None),
        P(None, "fsdp"),
        P("fsdp", None),
        P("fsdp"),
        P("fsdp"),
        P("fsdp"),
        P("fsdp", None),
        P(None, "fsdp", None),
        P(None, "fsdp"),
        P(None, "fsdp", None),
        P(None, "fsdp"),
    )
    return jax.shard_map(
        chosen_body,
        mesh=mesh,
        in_specs=placed,
        out_specs=(
            P(None, "fsdp", "ctx", None),
            P(None, "fsdp", "ctx", None),
            P("fsdp"),
            P("fsdp"),
            P(None, "fsdp", None),
            P(None, "fsdp"),
            P("fsdp", None),
            P("fsdp"),
            P("fsdp"),
            P("fsdp"),
            P("fsdp", None),
            P(None, "fsdp", None),
            P(None, "fsdp"),
            P(None, "fsdp", None),
            P(None, "fsdp"),
        ),
        check_vma=False,
    )
```

```python
import math

import jax
import jax.numpy as jnp
from jax import lax
from jax.experimental import pallas as pl
from jax.experimental.pallas import tpu as pltpu
from jax.sharding import PartitionSpec as P

HEADS = 16
HEAD_DIM = 64
CAP = 80


norm_eps = 1e-05
mask_fill = -1e30


def layer_norm(values, gain, shift):
    mean = jnp.mean(values, -1, keepdims=True)
    centred = values - mean
    spread = jnp.mean(centred * centred, -1, keepdims=True)
    return centred * lax.rsqrt(spread + norm_eps) * gain + shift


def natural_position(store_index, tok_rows, ctx_count):
    half = tok_rows // 2
    device = store_index // tok_rows
    slot = store_index % tok_rows
    return jnp.where(
        slot < half, device * half + slot, (2 * ctx_count - 1 - device) * half + slot - half
    )


def visible(query_pos, query_ids, key_pos, key_ids):
    return (key_pos[None, :] <= query_pos[:, None]) & (key_ids[None, :] == query_ids[:, None])


def block_needed(query_pos, query_ids, key_pos, key_ids):
    return (
        (jnp.min(key_pos) <= jnp.max(query_pos))
        & (jnp.max(key_ids) >= jnp.min(query_ids))
        & (jnp.min(key_ids) <= jnp.max(query_ids))
    )


def attend_keys(
    running, query_heads, query_pos, query_ids, key_part, value_part, pos_part, id_part, scale
):
    length = key_part.shape[0]
    stride = math.gcd(length, 512)
    key_heads = key_part.reshape(length, HEADS, HEAD_DIM)
    value_heads = value_part.reshape(length, HEADS, HEAD_DIM)

    def attend_visit_block(block_index, state):
        offset = block_index * stride
        key_blk = lax.dynamic_slice_in_dim(key_heads, offset, stride, 0)
        value_blk = lax.dynamic_slice_in_dim(value_heads, offset, stride, 0)
        key_pos = lax.dynamic_slice_in_dim(pos_part, offset, stride, 0)
        key_ids = lax.dynamic_slice_in_dim(id_part, offset, stride, 0)
        needed = block_needed(query_pos, query_ids, key_pos, key_ids)

        def update(current):
            best, totals, accum = current
            scores = (
                jnp.einsum("qhc,khc->hqk", query_heads, key_blk, preferred_element_type=jnp.float32)
                * scale
            )
            allowed = visible(query_pos, query_ids, key_pos, key_ids)[None]
            scores = jnp.where(allowed, scores, mask_fill)
            new_best = jnp.maximum(best, jnp.max(scores, -1))
            shrink = jnp.exp(best - new_best)
            weights = jnp.where(allowed, jnp.exp(scores - new_best[..., None]), 0.0)
            totals = totals * shrink + jnp.sum(weights, -1)
            addend = jnp.einsum(
                "hqk,khc->qhc",
                weights.astype(jnp.bfloat16),
                value_blk,
                preferred_element_type=jnp.float32,
            )
            accum = accum * jnp.transpose(shrink)[..., None] + addend
            return (new_best, totals, accum)

        def unchanged(current):
            return current

        return lax.cond(needed, update, unchanged, state)

    return lax.fori_loop(0, length // stride, attend_visit_block, running)


def backward_range(
    query_heads,
    grad_heads,
    log_total,
    delta,
    query_pos,
    query_ids,
    key_part,
    value_part,
    pos_part,
    id_part,
    scale,
):
    length = key_part.shape[0]
    stride = math.gcd(length, 512)
    blocks = length // stride
    key_blocks = key_part.reshape(blocks, stride, HEADS, HEAD_DIM)
    value_blocks = value_part.reshape(blocks, stride, HEADS, HEAD_DIM)
    pos_blocks = pos_part.reshape(blocks, stride)
    id_blocks = id_part.reshape(blocks, stride)
    rows = query_heads.shape[0]

    def backward_visit_block(query_acc, block_data):
        key_blk, value_blk, pos_blk, id_blk = block_data
        needed = block_needed(query_pos, query_ids, pos_blk, id_blk)

        def compute(current):
            scores = (
                jnp.einsum("qhc,khc->hqk", query_heads, key_blk, preferred_element_type=jnp.float32)
                * scale
            )
            allowed = visible(query_pos, query_ids, pos_blk, id_blk)[None]
            weights = jnp.where(allowed, jnp.exp(scores - log_total[..., None]), 0.0)
            weight_grad = jnp.einsum(
                "qhc,khc->hqk", grad_heads, value_blk, preferred_element_type=jnp.float32
            )
            score_grad = (weights * (weight_grad - delta[..., None])).astype(jnp.bfloat16)
            current = (
                current
                + jnp.einsum(
                    "hqk,khc->qhc", score_grad, key_blk, preferred_element_type=jnp.float32
                )
                * scale
            )
            terms = ()
            value_term = jnp.einsum(
                "hqk,qhc->khc",
                weights.astype(jnp.bfloat16),
                grad_heads,
                preferred_element_type=jnp.float32,
            )
            key_term = (
                jnp.einsum(
                    "hqk,qhc->khc", score_grad, query_heads, preferred_element_type=jnp.float32
                )
                * scale
            )
            terms = (key_term, value_term)
            return (current, terms)

        def skipped(current):
            terms = ()
            empty = jnp.zeros((stride, HEADS, HEAD_DIM), jnp.float32)
            terms = (empty, empty)
            return (current, terms)

        query_acc, terms = lax.cond(needed, compute, skipped, query_acc)
        terms = (
            terms[0].reshape(stride, HEADS * HEAD_DIM),
            terms[1].reshape(stride, HEADS * HEAD_DIM),
        )
        return (query_acc, terms)

    start_acc = jnp.zeros((rows, HEADS, HEAD_DIM), jnp.float32)
    query_grad, terms = lax.scan(
        backward_visit_block, start_acc, (key_blocks, value_blocks, pos_blocks, id_blocks)
    )
    return (
        query_grad,
        terms[0].reshape(length, HEADS * HEAD_DIM),
        terms[1].reshape(length, HEADS * HEAD_DIM),
    )


def gather_keys(key_rows, value_rows):
    return (
        lax.all_gather(key_rows, "ctx", axis=0, tiled=True),
        lax.all_gather(value_rows, "ctx", axis=0, tiled=True),
    )


def reduce_grads(attn_terms, expert_terms):
    g_one, s_one, g_qkv, g_qv, g_out, g_outb, g_two, s_two, g_router = attn_terms
    g_in, g_inb, g_back, g_backb = expert_terms
    e_in, e_inb, e_back, e_backb = (
        lax.psum_scatter(g_in.astype(jnp.bfloat16), "fsdp", scatter_dimension=1, tiled=True).astype(
            jnp.float32
        ),
        lax.psum_scatter(
            g_inb.astype(jnp.bfloat16), "fsdp", scatter_dimension=1, tiled=True
        ).astype(jnp.float32),
        lax.psum_scatter(
            g_back.astype(jnp.bfloat16), "fsdp", scatter_dimension=1, tiled=True
        ).astype(jnp.float32),
        lax.psum_scatter(
            g_backb.astype(jnp.bfloat16), "fsdp", scatter_dimension=1, tiled=True
        ).astype(jnp.float32),
    )
    a_one, b_one, a_qkv, a_qv, a_out, a_outb, a_two, b_two, a_router = (
        lax.psum_scatter(
            g_one.astype(jnp.bfloat16), "fsdp", scatter_dimension=0, tiled=True
        ).astype(jnp.float32),
        lax.psum_scatter(
            s_one.astype(jnp.bfloat16), "fsdp", scatter_dimension=0, tiled=True
        ).astype(jnp.float32),
        lax.psum_scatter(
            g_qkv.astype(jnp.bfloat16), "fsdp", scatter_dimension=1, tiled=True
        ).astype(jnp.float32),
        lax.psum_scatter(g_qv.astype(jnp.bfloat16), "fsdp", scatter_dimension=1, tiled=True).astype(
            jnp.float32
        ),
        lax.psum_scatter(
            g_out.astype(jnp.bfloat16), "fsdp", scatter_dimension=0, tiled=True
        ).astype(jnp.float32),
        lax.psum_scatter(
            g_outb.astype(jnp.bfloat16), "fsdp", scatter_dimension=0, tiled=True
        ).astype(jnp.float32),
        lax.psum_scatter(
            g_two.astype(jnp.bfloat16), "fsdp", scatter_dimension=0, tiled=True
        ).astype(jnp.float32),
        lax.psum_scatter(
            s_two.astype(jnp.bfloat16), "fsdp", scatter_dimension=0, tiled=True
        ).astype(jnp.float32),
        lax.psum_scatter(
            g_router.astype(jnp.bfloat16), "fsdp", scatter_dimension=0, tiled=True
        ).astype(jnp.float32),
    )
    return (
        lax.psum(a_one.astype(jnp.bfloat16), "ctx").astype(jnp.float32),
        lax.psum(b_one.astype(jnp.bfloat16), "ctx").astype(jnp.float32),
        lax.psum(a_qkv.astype(jnp.bfloat16), "ctx").astype(jnp.float32),
        lax.psum(a_qv.astype(jnp.bfloat16), "ctx").astype(jnp.float32),
        lax.psum(a_out.astype(jnp.bfloat16), "ctx").astype(jnp.float32),
        lax.psum(a_outb.astype(jnp.bfloat16), "ctx").astype(jnp.float32),
        lax.psum(a_two.astype(jnp.bfloat16), "ctx").astype(jnp.float32),
        lax.psum(b_two.astype(jnp.bfloat16), "ctx").astype(jnp.float32),
        lax.psum(a_router.astype(jnp.bfloat16), "ctx").astype(jnp.float32),
        lax.psum(e_in.astype(jnp.bfloat16), "ctx").astype(jnp.float32),
        lax.psum(e_inb.astype(jnp.bfloat16), "ctx").astype(jnp.float32),
        lax.psum(e_back.astype(jnp.bfloat16), "ctx").astype(jnp.float32),
        lax.psum(e_backb.astype(jnp.bfloat16), "ctx").astype(jnp.float32),
    )


def body(
    tokens,
    doc_ids,
    routes,
    cotangent,
    ln1_gain,
    ln1_shift,
    w_qkv,
    qv_bias,
    w_out,
    out_bias,
    ln2_gain,
    ln2_shift,
    router,
    w_in,
    in_bias,
    w_back,
    back_bias,
):
    gain_one, shift_one, proj_all, bias_qv, proj_out, bias_out, gain_two, shift_two, router_full = (
        lax.all_gather(ln1_gain, "fsdp", axis=0, tiled=True),
        lax.all_gather(ln1_shift, "fsdp", axis=0, tiled=True),
        lax.all_gather(w_qkv, "fsdp", axis=1, tiled=True),
        lax.all_gather(qv_bias, "fsdp", axis=1, tiled=True),
        lax.all_gather(w_out, "fsdp", axis=0, tiled=True),
        lax.all_gather(out_bias, "fsdp", axis=0, tiled=True),
        lax.all_gather(ln2_gain, "fsdp", axis=0, tiled=True),
        lax.all_gather(ln2_shift, "fsdp", axis=0, tiled=True),
        lax.all_gather(router, "fsdp", axis=0, tiled=True),
    )
    inner_full, inner_bias, outer_full, outer_bias = (
        lax.all_gather(w_in, "fsdp", axis=1, tiled=True),
        lax.all_gather(in_bias, "fsdp", axis=1, tiled=True),
        lax.all_gather(w_back, "fsdp", axis=1, tiled=True),
        lax.all_gather(back_bias, "fsdp", axis=1, tiled=True),
    )
    gain_one_f = gain_one.astype(jnp.float32)
    shift_one_f = shift_one.astype(jnp.float32)
    bias_qv_f = bias_qv.astype(jnp.float32)
    bias_out_f = bias_out.astype(jnp.float32)
    gain_two_f = gain_two.astype(jnp.float32)
    shift_two_f = shift_two.astype(jnp.float32)
    router_f = router_full.astype(jnp.float32)
    inner_bias_f = inner_bias.astype(jnp.float32)
    outer_bias_f = outer_bias.astype(jnp.float32)
    micro_count = tokens.shape[0]
    tok_rows = tokens.shape[2]
    width = tokens.shape[3]
    stream_len = doc_ids.shape[2]
    ctx_count = lax.axis_size("ctx")
    expert_count = inner_full.shape[0]
    scale = 1.0 / math.sqrt(HEAD_DIM)
    first_row = lax.axis_index("ctx") * tok_rows
    store_pos = natural_position(lax.iota(jnp.int32, stream_len), tok_rows, ctx_count)
    query_pos = lax.dynamic_slice_in_dim(store_pos, first_row, tok_rows, 0)
    expert_iota = lax.iota(jnp.int32, expert_count)
    slot_iota = lax.iota(jnp.int32, CAP)
    outputs = []
    input_grads = []
    totals = None
    for micro in range(micro_count):
        inputs = tokens[micro, 0].astype(jnp.float32)
        ids_store = jnp.take(doc_ids[micro, 0], store_pos)
        query_ids = lax.dynamic_slice_in_dim(ids_store, first_row, tok_rows, 0)
        picks = routes[micro, 0, :, 0]
        upstream = cotangent[micro, 0].astype(jnp.float32)
        h_first, pull_first = jax.vjp(layer_norm, inputs, gain_one_f, shift_one_f)
        h_first_low = h_first.astype(jnp.bfloat16)
        projected = jnp.einsum(
            "td,jde->jte", h_first_low, proj_all, preferred_element_type=jnp.float32
        )
        queries = (projected[0] + bias_qv_f[0]).astype(jnp.bfloat16)
        key_rows = projected[1].astype(jnp.bfloat16)
        value_rows = (projected[2] + bias_qv_f[1]).astype(jnp.bfloat16)
        query_heads = queries.reshape(tok_rows, HEADS, HEAD_DIM)
        start_state = (
            jnp.full((HEADS, tok_rows), mask_fill, jnp.float32),
            jnp.zeros((HEADS, tok_rows), jnp.float32),
            jnp.zeros((tok_rows, HEADS, HEAD_DIM), jnp.float32),
        )
        best, totals_soft, accum = attend_keys(
            start_state,
            query_heads,
            query_pos,
            query_ids,
            lax.all_gather(key_rows, "ctx", axis=0, tiled=True),
            lax.all_gather(value_rows, "ctx", axis=0, tiled=True),
            store_pos,
            ids_store,
            scale,
        )
        log_total = best + jnp.log(totals_soft)
        attended = accum / jnp.transpose(totals_soft)[..., None]
        attended_low = attended.reshape(tok_rows, width).astype(jnp.bfloat16)
        branch = jnp.dot(attended_low, proj_out, preferred_element_type=jnp.float32) + bias_out_f
        middle = inputs + branch
        h_second, pull_second = jax.vjp(layer_norm, middle, gain_two_f, shift_two_f)
        h_second_low = h_second.astype(jnp.bfloat16)
        logits = jnp.dot(h_second_low, router_full, preferred_element_type=jnp.float32)
        probs = jax.nn.softmax(logits, axis=-1)
        chosen = picks[:, None] == expert_iota[None, :]
        chosen_f = chosen.astype(jnp.float32)
        gate = jnp.sum(probs * chosen_f, -1)
        ranks = jnp.cumsum(chosen.astype(jnp.int32), 0) - 1
        dispatch = (jnp.transpose(ranks)[:, None, :] == slot_iota[None, :, None]) & jnp.transpose(
            chosen
        )[:, None, :]
        dispatch_low = dispatch.astype(jnp.bfloat16)
        dispatch_f = dispatch.astype(jnp.float32)
        slot_inputs = jnp.einsum(
            "ect,td->ecd", dispatch_low, h_second_low, preferred_element_type=jnp.float32
        ).astype(jnp.bfloat16)
        inner = (
            jnp.einsum("ecd,edh->ech", slot_inputs, inner_full, preferred_element_type=jnp.float32)
            + inner_bias_f[:, None, :]
        )
        active, pull_gelu = jax.vjp(jax.nn.gelu, inner)
        active_low = active.astype(jnp.bfloat16)
        result = (
            jnp.einsum("ech,ehd->ecd", active_low, outer_full, preferred_element_type=jnp.float32)
            + outer_bias_f[:, None, :]
        )
        expert_sum = jnp.einsum("ect,ecd->td", dispatch_f, result, precision=lax.Precision.HIGHEST)
        output = middle + gate[:, None] * expert_sum
        outputs.append(output.astype(jnp.bfloat16))
        gate_grad = jnp.sum(upstream * expert_sum, -1)
        slot_grad = jnp.einsum(
            "ect,td->ecd", dispatch_f, gate[:, None] * upstream, precision=lax.Precision.HIGHEST
        ).astype(jnp.bfloat16)
        outer_bias_grad = jnp.sum(slot_grad.astype(jnp.float32), 1)
        outer_grad = jnp.einsum(
            "ech,ecd->ehd", active_low, slot_grad, preferred_element_type=jnp.float32
        )
        active_grad = jnp.einsum(
            "ecd,ehd->ech", slot_grad, outer_full, preferred_element_type=jnp.float32
        )
        inner_grad = pull_gelu(active_grad)[0].astype(jnp.bfloat16)
        inner_bias_grad = jnp.sum(inner_grad.astype(jnp.float32), 1)
        inner_w_grad = jnp.einsum(
            "ecd,ech->edh", slot_inputs, inner_grad, preferred_element_type=jnp.float32
        )
        slot_input_grad = jnp.einsum(
            "ech,edh->ecd", inner_grad, inner_full, preferred_element_type=jnp.float32
        )
        second_grad = jnp.einsum(
            "ect,ecd->td", dispatch_f, slot_input_grad, precision=lax.Precision.HIGHEST
        )
        pick_grad = gate_grad[:, None] * chosen_f
        logit_grad = probs * (pick_grad - jnp.sum(probs * pick_grad, -1, keepdims=True))
        router_grad = jnp.einsum(
            "td,te->de",
            h_second_low.astype(jnp.float32),
            logit_grad,
            precision=lax.Precision.HIGHEST,
        )
        second_grad = second_grad + jnp.einsum(
            "te,de->td", logit_grad, router_f, precision=lax.Precision.HIGHEST
        )
        middle_norm_grad, gain_two_grad, shift_two_grad = pull_second(second_grad)
        middle_grad = upstream + middle_norm_grad
        branch_grad = middle_grad.astype(jnp.bfloat16)
        out_bias_grad = jnp.sum(branch_grad.astype(jnp.float32), 0)
        out_grad = jnp.einsum(
            "td,te->de", attended_low, branch_grad, preferred_element_type=jnp.float32
        )
        attended_grad = jnp.einsum(
            "te,de->td", branch_grad, proj_out, preferred_element_type=jnp.float32
        ).astype(jnp.bfloat16)
        grad_heads = attended_grad.reshape(tok_rows, HEADS, HEAD_DIM)
        delta = jnp.transpose(jnp.sum(grad_heads.astype(jnp.float32) * attended, -1))
        key_all, value_all = gather_keys(key_rows, value_rows)
        query_grad, key_terms, value_terms = backward_range(
            query_heads,
            grad_heads,
            log_total,
            delta,
            query_pos,
            query_ids,
            key_all,
            value_all,
            store_pos,
            ids_store,
            scale,
        )
        key_grad, value_grad = (
            lax.psum_scatter(
                key_terms.astype(jnp.bfloat16), "ctx", scatter_dimension=0, tiled=True
            ).astype(jnp.float32),
            lax.psum_scatter(
                value_terms.astype(jnp.bfloat16), "ctx", scatter_dimension=0, tiled=True
            ).astype(jnp.float32),
        )
        query_low = query_grad.reshape(tok_rows, width).astype(jnp.bfloat16)
        key_low = key_grad.astype(jnp.bfloat16)
        value_low = value_grad.astype(jnp.bfloat16)
        stacked_grad = jnp.stack([query_low, key_low, value_low])
        proj_grad = jnp.einsum(
            "td,jte->jde", h_first_low, stacked_grad, preferred_element_type=jnp.float32
        )
        qv_bias_grad = jnp.stack(
            [jnp.sum(query_low.astype(jnp.float32), 0), jnp.sum(value_low.astype(jnp.float32), 0)]
        )
        first_grad = jnp.einsum(
            "jte,jde->td", stacked_grad, proj_all, preferred_element_type=jnp.float32
        )
        input_norm_grad, gain_one_grad, shift_one_grad = pull_first(first_grad)
        input_grads.append(middle_grad + input_norm_grad)
        attn_terms = (
            gain_one_grad,
            shift_one_grad,
            proj_grad,
            qv_bias_grad,
            out_grad,
            out_bias_grad,
            gain_two_grad,
            shift_two_grad,
            router_grad,
        )
        expert_terms = (inner_w_grad, inner_bias_grad, outer_grad, outer_bias_grad)
        local_terms = attn_terms + expert_terms
        totals = local_terms if totals is None else jax.tree.map(jnp.add, totals, local_terms)
    totals = reduce_grads(totals[:9], totals[9:])
    (
        g_one,
        s_one,
        g_qkv,
        g_qv,
        g_out,
        g_outb,
        g_two,
        s_two,
        g_router,
        g_in,
        g_inb,
        g_back,
        g_backb,
    ) = totals
    mixed = jnp.stack(outputs)[:, None]
    token_grad = jnp.stack(input_grads)[:, None]
    return (
        mixed,
        token_grad,
        g_one,
        s_one,
        g_qkv,
        g_qv,
        g_out,
        g_outb,
        g_two,
        s_two,
        g_router,
        g_in,
        g_inb,
        g_back,
        g_backb,
    )


MESH_ID = pl.DeviceIdType.MESH
BF = jnp.bfloat16
F32 = jnp.float32
DMA = pltpu.SemaphoreType.DMA
VMEM_CAP = 60 * 1024 * 1024
SMALL_ROWS = 32
NT = (((1,), (1,)), ((), ()))
TN = (((0,), (0,)), ((), ()))
NN = (((1,), (0,)), ((), ()))


def mm(left, right, dims=NN):
    return lax.dot_general(left, right, dims, preferred_element_type=F32)


def plane_coords():
    me = lax.axis_index("ctx")
    core = me % 2
    col = (me // 2) % 2
    row = me // 4
    sib = me + 1 - 2 * core
    xn = (row * 2 + 1 - col) * 2 + core
    yn = ((1 - row) * 2 + col) * 2 + core
    dg = ((1 - row) * 2 + 1 - col) * 2 + core
    return me, core, sib, xn, yn, dg


def meet(ctx_peers, fsdp_peers=()):
    sem = pltpu.get_barrier_semaphore()
    for peer in ctx_peers:
        pl.semaphore_signal(sem, inc=1, device_id={"ctx": peer}, device_id_type=MESH_ID)
    for peer in fsdp_peers:
        pl.semaphore_signal(sem, inc=1, device_id={"fsdp": peer}, device_id_type=MESH_ID)
    pl.semaphore_wait(sem, len(ctx_peers) + len(fsdp_peers))


def send_to(src, dst, send_sem, recv_sem, axis, peer):
    return pltpu.make_async_remote_copy(
        src_ref=src,
        dst_ref=dst,
        send_sem=send_sem,
        recv_sem=recv_sem,
        device_id={axis: peer},
        device_id_type=MESH_ID,
    )


def gather_sems(chunks):
    return [
        DMA((2, chunks)),
        DMA((2, chunks)),
        DMA((chunks,)),
        DMA((chunks,)),
        DMA((3, chunks)),
        DMA((3, chunks)),
        DMA((chunks,)),
        DMA((chunks,)),
        DMA((chunks,)),
    ]


def line_sems(chunks):
    return [DMA((3, chunks)), DMA((3, chunks)), DMA((3, chunks)), DMA((3, chunks)), DMA((chunks,))]


def by_rows(count, step, visit):
    def one(index, carry):
        visit(pl.ds(pl.multiple_of(index * step, step), step))
        return carry

    lax.fori_loop(0, count // step, one, 0)


def ring_ops(own, slot, sems):
    ns, nr, ds, dr, fs, fr, ss, sr, ls = sems
    me, core, sib, xn, yn, dg = plane_coords()
    near = (xn, yn)

    def away(i, k):
        return send_to(own(k), slot(me, k), ns.at[i, k], nr.at[i, k], "ctx", near[i])

    def beside(k):
        return send_to(own(k), slot(me, k), ss.at[k], sr.at[k], "ctx", sib)

    def here(k):
        return pltpu.make_async_copy(own(k), slot(me, k), ls.at[k])

    def passed(k):
        block = slot(near[k % 2], k)
        return send_to(block, block, ds.at[k], dr.at[k], "ctx", near[1 - k % 2])

    def onward(i, k):
        block = slot((xn, yn, dg)[i], k)
        return send_to(block, block, fs.at[i, k], fr.at[i, k], "ctx", sib)

    def begin(k):
        for i in (0, 1):
            away(i, k).start()
        beside(k).start()
        here(k).start()

    def relay(k):
        for i in (k % 2, 1 - k % 2):
            away(i, k).wait_recv()
            if i == k % 2:
                passed(k).start()
            onward(i, k).start()

    def diag(k):
        passed(k).wait_recv()
        onward(2, k).start()

    def done(k):
        here(k).wait()
        beside(k).wait_recv()
        for i in range(3):
            onward(i, k).wait_recv()

    def finish(k):
        for i in (0, 1):
            away(i, k).wait_send()
        beside(k).wait_send()
        passed(k).wait_send()
        for i in range(3):
            onward(i, k).wait_send()

    return begin, relay, diag, done, finish


def line_ops(own, slot, chunks, sems):
    us, ur, ws, wr, ls = sems
    z = lax.axis_index("fsdp")

    def up(d, k):
        src = own(k) if d == 0 else slot(z - d, k)
        return send_to(src, slot(z - d, k), us.at[d, k], ur.at[d, k], "fsdp", z + 1)

    def down(d, k):
        src = own(k) if d == 0 else slot(z + d, k)
        return send_to(src, slot(z + d, k), ws.at[d, k], wr.at[d, k], "fsdp", z - 1)

    def from_below(d, k):
        return send_to(own(k), slot(z - d - 1, k), us.at[d, k], ur.at[d, k], "fsdp", z - 1)

    def from_above(d, k):
        return send_to(own(k), slot(z + d + 1, k), ws.at[d, k], wr.at[d, k], "fsdp", z + 1)

    def here(k):
        return pltpu.make_async_copy(own(k), slot(z, k), ls.at[k])

    def pass_one(d, k):
        @pl.when((z < 3) & (z >= d))
        def _():
            if d:
                from_below(d - 1, k).wait_recv()
            up(d, k).start()

        @pl.when((z > 0) & (z + d <= 3))
        def _():
            if d:
                from_above(d - 1, k).wait_recv()
            down(d, k).start()

    def pass_on(d, which=None):
        for k in range(chunks) if which is None else which:
            pass_one(d, k)

    def begin():
        for k in range(chunks):
            here(k).start()
        pass_on(0)

    def arrive():
        for d in range(3):
            for k in range(chunks):

                @pl.when(z == 3)
                def _():
                    from_below(d, k).wait_recv()

                @pl.when(z == 0)
                def _():
                    from_above(d, k).wait_recv()

        for k in range(chunks):
            here(k).wait()

    def finish():
        for d in range(3):
            for k in range(chunks):

                @pl.when((z < 3) & (z >= d))
                def _():
                    up(d, k).wait_send()

                @pl.when((z > 0) & (z + d <= 3))
                def _():
                    down(d, k).wait_send()

    return begin, pass_on, arrive, finish


def sum_scratch():
    return [pltpu.VMEM((2, 4, 128, 1024), BF)] + [pltpu.VMEM((2, 128, 1024), BF)] * 6 + [
        DMA((2, 4)), DMA((2, 4)), DMA((2, 6)), DMA((2, 6)),
    ]


def sum_ops(part, m, out, scratch):
    pair, gs, gr, xs, xr, ys, yr = [ref.at[m] for ref in scratch[:7]]
    s1, r1, s2, r2 = scratch[7:]
    me, core, sib, xn, yn, dg = plane_coords()
    order = (dg, xn, yn, me)
    lo, hi = pl.ds(0, 64), pl.ds(64, 64)

    def to_pair(i):
        other = order[i] + 1 - 2 * core
        return send_to(part.at[m, other], pair.at[i], s1.at[m, i], r1.at[m, i], "ctx", sib)

    def ship(index):
        src, dst, peer = (
            (gs.at[lo], gr.at[lo], xn),
            (gs.at[hi], gr.at[hi], yn),
            (xs.at[lo], xr.at[lo], xn),
            (ys.at[hi], yr.at[hi], yn),
            (ys.at[lo], yr.at[lo], yn),
            (xs.at[hi], xr.at[hi], xn),
        )[index]
        return send_to(src, dst, s2.at[m, index], r2.at[m, index], "ctx", peer)

    def f32(value):
        return value.astype(F32)

    def both(i, rr):
        return f32(part[m, order[i], rr]) + f32(pair[i, rr])

    def begin():
        for i in range(4):
            to_pair(i).start()

    def span(offset, count, visit):
        def one(index):
            visit(pl.ds(offset + index.start, 32))

        by_rows(count, 32, one)

    def diag():
        to_pair(0).wait_recv()

        def add(rr):
            gs[rr] = both(0, rr).astype(BF)

        span(0, 128, add)
        ship(0).start()
        ship(1).start()

    def near():
        to_pair(1).wait_recv()

        def add_x(rr):
            xs[rr] = both(1, rr).astype(BF)

        span(0, 64, add_x)
        ship(2).start()
        to_pair(2).wait_recv()

        def add_y(rr):
            ys[rr] = both(2, rr).astype(BF)

        span(64, 64, add_y)
        ship(3).start()

    def join():
        ship(0).wait_recv()

        def add_y(rr):
            ys[rr] = (both(2, rr) + f32(gr[rr])).astype(BF)

        span(0, 64, add_y)
        ship(4).start()
        ship(1).wait_recv()

        def add_x(rr):
            xs[rr] = (both(1, rr) + f32(gr[rr])).astype(BF)

        span(64, 64, add_x)
        ship(5).start()

    def finish():
        to_pair(3).wait_recv()
        for index in (2, 3, 4, 5):
            ship(index).wait_recv()

        def add(rr):
            place = pl.ds(m * 128 + rr.start, 32)
            out[place] = both(3, rr) + f32(xr[rr]) + f32(yr[rr])

        span(0, 128, add)
        for i in range(4):
            to_pair(i).wait_send()
        for index in range(6):
            ship(index).wait_send()

    return begin, diag, near, join, finish


def fold_scratch(rows):
    return [
        pltpu.VMEM((2, 3, rows, 1024), BF),
        pltpu.VMEM((2, 2, rows, 1024), BF),
        DMA((2, 3, 2)),
        DMA((2, 3, 2)),
    ]


def fold_ops(block, rows, out, scratch):
    got, sent, ss, rs = scratch
    z = lax.axis_index("fsdp")
    half = rows // 2
    places = (z, 3 - z)
    nexts = ((z + 1) % 4, (z + 3) % 4)

    def target(side, q):
        return q if side == 0 else 3 - q

    def piece(ref, h):
        return ref.at[pl.ds(half * h, half)]

    def message(src, side, q, h):
        return send_to(
            piece(src, h), piece(got.at[side, q - 1], h), ss.at[side, q - 1, h], rs.at[side, q - 1, h],
            "fsdp", nexts[side],
        )

    def first(side, q, h):
        return message(block(target(side, q)), side, q, h)

    def later(side, q, h):
        return message(sent.at[side, q - 2], side, q, h)

    def begin():
        for side in (0, 1):

            @pl.when(places[side] == 0)
            def _():
                for q in (3, 2, 1):
                    for h in (0, 1):
                        first(side, q, h).start()

    def relay(at, q, h):
        for side in (0, 1):

            @pl.when(places[side] == at)
            def _():
                later(side, q, h).wait_recv()
                mine = block(target(side, q))

                def add(index):
                    rr = pl.ds(half * h + index.start, 32)
                    total = mine[rr].astype(F32) + got[side, q - 1, rr].astype(F32)
                    sent[side, q - 2, rr] = total.astype(BF)

                by_rows(half, 32, add)
                later(side, q, h).start()

    def step(n):
        for at, q, h in (((1, 3, 0),), ((1, 3, 1), (2, 3, 0)), ((1, 2, 0), (2, 3, 1)), ((1, 2, 1),))[n]:
            relay(at, q, h)

    def finish():
        mine = block(z)
        for side in (0, 1):

            @pl.when(places[side] > 0)
            def _():
                for h in (0, 1):
                    q = places[side]
                    send_to(
                        piece(mine, h), piece(got.at[side, q - 1], h), ss.at[side, q - 1, h],
                        rs.at[side, q - 1, h], "fsdp", nexts[side],
                    ).wait_recv()

        def add_all(sides):
            def add(rr):
                total = mine[rr].astype(F32)
                for side in sides:
                    total = total + got[side, places[side] - 1, rr].astype(F32)
                out[rr] = total.astype(BF)

            by_rows(rows, 32, add)

        @pl.when(z == 0)
        def _():
            add_all((1,))

        @pl.when(z == 3)
        def _():
            add_all((0,))

        @pl.when((z > 0) & (z < 3))
        def _():
            add_all((0, 1))

        for side in (0, 1):
            for at, qs in ((0, (3, 2, 1)), (1, (3, 2)), (2, (3,))):

                @pl.when(places[side] == at)
                def _():
                    for q in qs:
                        for h in (0, 1):
                            first(side, q, h).wait_send()

    return begin, step, finish


def vmem_spec():
    return pl.BlockSpec(memory_space=pltpu.VMEM)


def any_spec():
    return pl.BlockSpec(memory_space=pl.ANY)


def natural_slot(device, k):
    micro, part = k // 2, k % 2
    return micro * 16 + (device if part == 0 else 15 - device)


def remote_params(ident):
    return pltpu.CompilerParams(
        collective_id=ident, has_side_effects=True, vmem_limit_bytes=VMEM_CAP
    )


def line_peers():
    z = lax.axis_index("fsdp")
    return [(z + d) % 4 for d in (1, 2, 3)]


def token_docs(row_ref, m):
    row = jnp.broadcast_to(row_ref[m].astype(F32), (8, 1024))
    return row[0:1], jnp.transpose(row)[:, 0:1]


def front_kernel(
    x_ref, small_ref, doc_ref, wq_ref, wo_ref, wi_ref, picks_ref, dy_ref,
    h_ref, params_ref, wqc_ref, woc_ref, wic_ref, qkv_ref, of_ref, lse_ref,
    y_ref, h2_ref, stat_ref, disp_ref, hslot_ref, dslot_ref,
    out_ref, hs, units, part, zs, zr, os, orr, ol, *sems,
):
    me, core, sib, xn, yn, dg = plane_coords()
    z = lax.axis_index("fsdp")
    peers = line_peers()
    meet((sib, xn, yn), peers)
    params_ref[z] = small_ref[...]
    copies = []
    for i, peer in enumerate(peers):
        copy = send_to(small_ref, params_ref.at[z], zs.at[i], zr.at[i], "fsdp", peer)
        copy.start()
        copies.append(copy)
    owner = me // 2
    columns = pl.ds(pl.multiple_of(me * 128, 128), 128)
    expert, quarter = me // 4, me % 4

    def wq_slot(where, k):
        return wqc_ref.at[k, pl.ds(pl.multiple_of(where * 256, 256), 256)]

    def wi_own(k):
        return wi_ref.at[expert, :, pl.ds(pl.multiple_of(k * 1024 + quarter * 256, 256), 256)]

    def wi_slot(where, k):
        return wic_ref.at[pl.ds(pl.multiple_of(where * 256, 256), 256), pl.ds(256 * k, 256)]

    q_begin, q_pass, q_arrive, q_finish = line_ops(
        lambda k: wq_ref.at[k, :, columns], wq_slot, 3, sems[:5]
    )
    i_begin, i_pass, i_arrive, i_finish = line_ops(wi_own, wi_slot, 4, sems[5:10])
    begin, relay, diag, done, finish = ring_ops(
        lambda k: hs.at[pl.ds(64 * k, 64)],
        lambda device, k: h_ref.at[natural_slot(device, k)],
        sems[10:19],
    )
    sums = [sum_ops(part, m, out_ref, sems[19:]) for m in (0, 1)]
    q_begin()

    wo_own = wo_ref.at[pl.ds(pl.multiple_of(core * 128, 128), 128)]

    def wo_step(src, side):
        return send_to(
            src, woc_ref, os.at[side], orr.at[side], "fsdp", z + 1 if side == 0 else z - 1
        )

    def wo_both(act):
        @pl.when((z >= owner) & (z < 3))
        def _():
            act(0)

        @pl.when((z <= owner) & (z > 0))
        def _():
            act(1)

    def wo_begin():
        @pl.when(z == owner)
        def _():
            pltpu.make_async_copy(wo_own, woc_ref, ol).start()
            wo_both(lambda side: wo_step(wo_own, side).start())

    def wo_arrive():
        @pl.when(z > owner)
        def _():
            wo_step(woc_ref, 0).wait_recv()

        @pl.when(z < owner)
        def _():
            wo_step(woc_ref, 1).wait_recv()

    def wo_pass(d):
        @pl.when((z == owner + d) | (z == owner - d))
        def _():
            wo_arrive()
            wo_both(lambda side: wo_step(woc_ref, side).start())

    def wo_last():
        @pl.when((z == owner + 3) | (z == owner - 3))
        def _():
            wo_arrive()

        @pl.when(z == owner)
        def _():
            pltpu.make_async_copy(wo_own, woc_ref, ol).wait()

    wo_begin()

    def unit(rr):
        values = x_ref[rr].astype(F32)
        centred = values - jnp.mean(values, -1, keepdims=True)
        spread = jnp.mean(centred * centred, -1, keepdims=True)
        units[rr] = centred * lax.rsqrt(spread + norm_eps)

    by_rows(256, 32, unit)
    for copy in copies:
        copy.wait()

    def full_row(r):
        return jnp.concatenate([params_ref[i, r : r + 1, :] for i in range(4)], axis=1).astype(F32)

    gain, shift = full_row(0), full_row(1)

    def norm(rr):
        hs[rr] = (units[rr] * gain + shift).astype(BF)

    by_rows(256, 32, norm)
    begin(0)
    begin(1)
    q_pass(1)
    relay(0)
    relay(1)
    begin(2)
    begin(3)
    wo_pass(1)
    q_pass(2)
    i_begin()
    diag(0)
    diag(1)
    wo_pass(2)
    done(0)
    done(1)
    q_arrive()
    half = pl.ds(pl.multiple_of(core * 128, 128), 128)
    q_bias = params_ref[owner, 2:3, half].astype(F32)
    v_bias = params_ref[owner, 3:4, half].astype(F32)
    masks = head_masks(256)
    vmasks = head_masks(1024)
    zero = jnp.zeros((), BF)

    def micro(m, carry):
        @pl.when(m == 1)
        def _():
            done(2)
            done(3)

        h = h_ref[pl.ds(16 * m, 16)].reshape(1024, 1024)
        place = pl.ds(pl.multiple_of(m * 1024, 1024), 1024)
        q = (mm(h, wqc_ref[0]) + q_bias).astype(BF)
        k = mm(h, wqc_ref[1]).astype(BF)
        v = (mm(h, wqc_ref[2]) + v_bias).astype(BF)
        qkv_ref[0, place] = q
        qkv_ref[1, place] = k
        qkv_ref[2, place] = v
        vh = [jnp.where(vmasks[j], v, zero) for j in (0, 1)]
        doc_row, doc_col = token_docs(doc_ref, m)
        for i in range(4):
            length = 256 * (i + 1)
            rows = slice(256 * i, 256 * (i + 1))
            qi = q[rows] * jnp.asarray(0.125, BF)
            allowed = allowed_mask(i, doc_col[rows], doc_row[:, :length])
            total = None
            stats = []
            for j in (0, 1):
                s = mm(jnp.where(masks[j], qi, zero), k[:length], NT)
                s = jnp.where(allowed, s, mask_fill)
                top = jnp.max(s, -1, keepdims=True)
                e = jnp.exp(s - top)
                den = jnp.sum(e, -1, keepdims=True)
                p = (e * (1.0 / den)).astype(BF)
                term = mm(p, vh[j][:length])
                total = term if total is None else total + term
                stats.append(top + jnp.log(den))
            at = pl.ds(pl.multiple_of(m * 1024 + 256 * i, 256), 256)
            lse_ref[at] = jnp.where(masks[0], stats[0], stats[1])
            of_ref[at] = total

            @pl.when(m == 0)
            def _():
                if i == 0:
                    relay(2)
                    relay(3)
                if i == 1:
                    i_pass(1, (0,))
                    diag(2)
                if i == 2:
                    i_pass(1, (1,))
                    diag(3)
                if i == 3:
                    wo_last()

            @pl.when(m == 1)
            def _():
                if i == 1:
                    sums[0][3]()
                if i == 3:
                    i_pass(2, (0,))

        for i in range(4):
            at = pl.ds(pl.multiple_of(m * 1024 + 256 * i, 256), 256)
            a = mm(of_ref[at].astype(BF), woc_ref[...]).astype(BF)
            for b in range(4):
                block = 4 * i + b
                dest, side = (block, 0) if block < 8 else (15 - block, 1)
                part[m, dest, 64 * side : 64 * (side + 1)] = a[64 * b : 64 * (b + 1)]

        for n in (0, 1):

            @pl.when(m == n)
            def _():
                for step in sums[n][:3]:
                    step()
                if n == 0:
                    i_pass(1, (2, 3))

        return carry

    lax.fori_loop(0, 2, micro, 0)
    outb, gain2, shift2 = full_row(4), full_row(5), full_row(6)
    router = jnp.concatenate([full_row(7), full_row(8)], axis=0).astype(BF)

    def route(m):
        picked = jnp.broadcast_to(picks_ref[m : m + 1].astype(F32), (8, 128))
        sub = lax.broadcasted_iota(jnp.int32, (8, 128), 0)
        member = jnp.where(sub == 0, 1.0 - picked, picked)
        earlier = lax.broadcasted_iota(jnp.int32, (128, 128), 0)
        later = lax.broadcasted_iota(jnp.int32, (128, 128), 1)
        rank = mm(member.astype(BF), (earlier < later).astype(BF))
        slot = lax.broadcasted_iota(jnp.int32, (CAP, 128), 0).astype(F32)
        for e in (0, 1):
            hit = (rank[e : e + 1] == slot) & (member[e : e + 1] > 0.5)
            disp_ref[m, e] = hit.astype(BF)
        return jnp.transpose(picked)[:, 0:1]

    def second_norm(m):
        pick = route(m)
        base = 128 * m

        def visit(index):
            rr = pl.ds(base + index.start, 32)
            values = x_ref[rr].astype(F32) + (out_ref[rr] + outb)
            y_ref[rr] = values
            centred = values - jnp.mean(values, -1, keepdims=True)
            spread = jnp.mean(centred * centred, -1, keepdims=True)
            h2_ref[rr] = (centred * lax.rsqrt(spread + norm_eps) * gain2 + shift2).astype(BF)

        by_rows(128, 32, visit)
        span = pl.ds(base, 128)
        h2 = h2_ref[span]
        logits = mm(h2, router, NT)
        top = jnp.max(logits, -1, keepdims=True)
        e = jnp.exp(logits - top)
        probs = e / jnp.sum(e, -1, keepdims=True)
        gate = jnp.where(pick > 0.5, probs[:, 1:2], probs[:, 0:1])
        lane = lax.broadcasted_iota(jnp.int32, (128, 128), 1)
        packed = jnp.where(lane == 0, probs[:, 0:1], probs[:, 1:2])
        packed = jnp.where(lane == 2, gate, packed)
        stat_ref[span] = jnp.where(lane == 3, pick, packed)
        du = (gate * dy_ref[span].astype(F32)).astype(BF)
        for which in (0, 1):
            hslot_ref[which, m] = mm(disp_ref[m, which], h2).astype(BF)
            dslot_ref[which, m] = mm(disp_ref[m, which], du).astype(BF)

    i_pass(2, (1,))
    sums[1][3]()
    i_pass(2, (2, 3))
    sums[0][4]()
    second_norm(0)
    sums[1][4]()
    second_norm(1)
    i_arrive()
    wo_both(lambda side: wo_step(woc_ref, side).wait_send())
    q_finish()
    i_finish()
    for k in range(4):
        finish(k)


def front_call(x, small, docs, w_qkv, w_out, w_in, picks, dy):
    return pl.pallas_call(
        front_kernel,
        out_shape=(
            jax.ShapeDtypeStruct((32, 64, 1024), BF),
            jax.ShapeDtypeStruct((4, SMALL_ROWS, 256), BF),
            jax.ShapeDtypeStruct((3, 1024, 128), BF),
            jax.ShapeDtypeStruct((128, 1024), BF),
            jax.ShapeDtypeStruct((1024, 1024), BF),
            jax.ShapeDtypeStruct((3, 2048, 128), BF),
            jax.ShapeDtypeStruct((2048, 128), F32),
            jax.ShapeDtypeStruct((2048, 128), F32),
            jax.ShapeDtypeStruct((256, 1024), F32),
            jax.ShapeDtypeStruct((256, 1024), BF),
            jax.ShapeDtypeStruct((256, 128), F32),
            jax.ShapeDtypeStruct((2, 2, CAP, 128), BF),
            jax.ShapeDtypeStruct((2, 2, CAP, 1024), BF),
            jax.ShapeDtypeStruct((2, 2, CAP, 1024), BF),
        ),
        in_specs=[vmem_spec()] * 3 + [any_spec()] * 3 + [vmem_spec()] * 2,
        out_specs=[vmem_spec()] * 4 + [any_spec()] + [vmem_spec()] * 9,
        scratch_shapes=[
            pltpu.VMEM((256, 1024), F32),
            pltpu.VMEM((256, 1024), BF),
            pltpu.VMEM((256, 1024), F32),
            pltpu.VMEM((2, 8, 128, 1024), BF),
            DMA((3,)),
            DMA((3,)),
            DMA((2,)),
            DMA((2,)),
            DMA(()),
        ]
        + line_sems(3)
        + line_sems(4)
        + gather_sems(4)
        + sum_scratch(),
        name="front",
        compiler_params=remote_params(0),
    )(x, small, docs, w_qkv, w_out, w_in, picks, dy)


def moe_call(h_slots, d_slots, win, w_back, params, y1, h2, stats, dispatch, dy):
    def kernel(
        h_ref, d_ref, wi_ref, wall_ref, params_ref, y_ref, h2_ref, stat_ref, disp_ref, dy_ref,
        gi_ref, gbs_ref, mixed_ref, dy1_ref, da_ref, v_ref,
        o_ref, gib_ref, acc, wb_ref, gba, u_ref, g_ref, rows, gz, slope, dz, part, pair, sent, got,
        ns, nr, fs, fr, ss, sr, ls, s1, r1, s2, r2, *wsems,
    ):
        me, core, sib, xn, yn, dg = plane_coords()
        expert, quarter = me // 4, me % 4
        meet((sib, xn, yn, dg), line_peers())
        w_begin, w_pass, w_arrive, w_finish = line_ops(
            lambda k: wall_ref.at[expert, pl.ds(pl.multiple_of(quarter * 256 + 64 * k, 64), 64)],
            lambda where, k: wb_ref.at[pl.ds(pl.multiple_of(where * 256 + 64 * k, 64), 64)],
            4,
            wsems[:5],
        )
        z_begin, z_step, z_finish = fold_ops(lambda where: gba.at[where], 256, gbs_ref, wsems[5:])
        w_begin()
        peers = (dg, xn, yn)
        wanted = (1 - expert, expert, 1 - expert)
        ins = (h_ref, d_ref)

        def away(t, m, i):
            return send_to(
                ins[t].at[wanted[i], m], rows.at[t, m, me], ns.at[t, m, i], nr.at[t, m, i], "ctx", peers[i]
            )

        def beside(t, m):
            return send_to(
                ins[t].at[expert, m], rows.at[t, m, me], ss.at[t, m], sr.at[t, m], "ctx", sib
            )

        def here(t, m):
            return pltpu.make_async_copy(ins[t].at[expert, m], rows.at[t, m, me], ls.at[t, m])

        def onward(t, m, i):
            block = rows.at[t, m, peers[i]]
            return send_to(block, block, fs.at[t, m, i], fr.at[t, m, i], "ctx", sib)

        for t in (0, 1):
            for m in (0, 1):
                for i in range(3):
                    away(t, m, i).start()
        for t in (0, 1):
            for m in (0, 1):
                beside(t, m).start()
                here(t, m).start()

        def arrive(t, m):
            for i in range(3):
                away(t, m, i).wait_recv()
                onward(t, m, i).start()
            here(t, m).wait()
            beside(t, m).wait_recv()
            for i in range(3):
                onward(t, m, i).wait_recv()

        order = (dg, xn, yn, me)

        def to_pair(t, m, i):
            other = order[i] + 1 - 2 * core
            return send_to(
                part.at[t, m, other], pair.at[t, m, i], s1.at[t, m, i], r1.at[t, m, i], "ctx", sib
            )

        def to_home(t, m, i):
            return send_to(
                sent.at[t, m, i], got.at[t, m, i], s2.at[t, m, i], r2.at[t, m, i], "ctx", order[i]
            )

        def join(t, m):
            for i in range(3):
                to_pair(t, m, i).wait_recv()
                mine = order[i]

                def add(rr):
                    sent[t, m, i, rr] = (
                        part[t, m, mine, rr].astype(F32) + pair[t, m, i, rr].astype(F32)
                    ).astype(BF)

                by_rows(CAP, 16, add)
                to_home(t, m, i).start()

        mine_row = lax.broadcasted_iota(jnp.int32, (8, 256), 0) == me
        in_bias = jnp.concatenate(
            [
                jnp.sum(
                    jnp.where(mine_row, params_ref[i, 9:17, :].astype(F32), 0.0), 0, keepdims=True
                )
                for i in range(4)
            ],
            axis=1,
        )

        def inner_rows(m):
            def visit(half, carry):
                xs = rows[0, m, pl.ds(4 * half, 4)].reshape(4 * CAP, 1024)
                zed = mm(xs, wi_ref[...]) + in_bias
                square = zed * zed
                t = jnp.tanh(zed * (GELU_A + GELU_A * GELU_B * square))
                half_up = 0.5 + 0.5 * t
                place = pl.ds(pl.multiple_of(m * 8 * CAP + half * 4 * CAP, 4 * CAP), 4 * CAP)
                gz[place] = (zed * half_up).astype(BF)
                slope[place] = half_up + 0.5 * zed * (1.0 - t * t) * (
                    GELU_A + 3.0 * GELU_A * GELU_B * square
                )
                return carry

            lax.fori_loop(0, 2, visit, 0)

        def inner(m, carry):
            @pl.when(m == 0)
            def _():
                w_pass(1, (0, 1))

            arrive(0, m)

            @pl.when(m == 0)
            def _():
                w_pass(1, (2,))

            inner_rows(m)

            @pl.when(m == 0)
            def _():
                w_pass(1, (3,))

            return carry

        lax.fori_loop(0, 2, inner, 0)
        w_pass(2, (0, 1))
        arrive(1, 0)
        w_pass(2, (2, 3))
        arrive(1, 1)

        def back_grads(j, carry):
            column = pl.ds(pl.multiple_of(256 * j, 256), 256)
            du = rows[1].reshape(16 * CAP, 1024)
            gba[j] = mm(gz[:, column], du, TN).astype(BF)
            return carry

        lax.fori_loop(0, 4, back_grads, 0)
        z_begin()
        w_arrive()

        def forward(m, carry):
            def visit(half, inner_carry):
                place = pl.ds(pl.multiple_of(m * 8 * CAP + half * 4 * CAP, 4 * CAP), 4 * CAP)
                u = mm(gz[place], wb_ref[...]).astype(BF)
                part[0, m, pl.ds(4 * half, 4)] = u.reshape(4, CAP, 1024)
                return inner_carry

            lax.fori_loop(0, 2, visit, 0)
            for i in range(4):
                to_pair(0, m, i).start()
            join(0, m)
            return carry

        lax.fori_loop(0, 2, forward, 0)
        z_step(0)
        gib_ref[...] = jnp.zeros_like(gib_ref)

        def backward(m, carry):
            def rows_backward(half, inner_carry):
                du = rows[1, m, pl.ds(4 * half, 4)].reshape(4 * CAP, 1024)
                place = pl.ds(pl.multiple_of(m * 8 * CAP + half * 4 * CAP, 4 * CAP), 4 * CAP)
                low = (mm(du, wb_ref[...], NT) * slope[place]).astype(BF)
                dz[place] = low
                gib_ref[...] += jnp.sum(low.astype(F32), 0, keepdims=True)
                dh = mm(low, wi_ref[...], NT).astype(BF)
                part[1, m, pl.ds(4 * half, 4)] = dh.reshape(4, CAP, 1024)
                return inner_carry

            lax.fori_loop(0, 2, rows_backward, 0)
            for i in range(4):
                to_pair(1, m, i).start()
            join(1, m)

            @pl.when(m == 0)
            def _():
                z_step(1)

            return carry

        lax.fori_loop(0, 2, backward, 0)
        z_step(2)

        def weight_grads(j, carry):
            column = pl.ds(pl.multiple_of(256 * j, 256), 256)
            xs = rows[0, :, :, :, column].reshape(16 * CAP, 256)
            gi_ref[column] = mm(xs, dz[...], TN).astype(BF)
            return carry

        lax.fori_loop(0, 4, weight_grads, 0)
        z_step(3)

        def full_row(r):
            return jnp.concatenate(
                [params_ref[i, r : r + 1, :] for i in range(4)], axis=1
            ).astype(F32)

        gain2, router0, router1 = full_row(5), full_row(7), full_row(8)
        bias0, bias1 = full_row(17), full_row(18)
        acc[...] = jnp.zeros_like(acc)

        def home(t, m):
            to_pair(t, m, 3).wait_recv()
            for i in range(3):
                to_home(t, m, i).wait_recv()

            def finish(rr):
                o_ref[expert, t, m, rr] = (
                    part[t, m, me, rr].astype(F32)
                    + pair[t, m, 3, rr].astype(F32)
                    + got[t, m, 1, rr].astype(F32)
                )
                o_ref[1 - expert, t, m, rr] = got[t, m, 0, rr].astype(F32) + got[
                    t, m, 2, rr
                ].astype(F32)

            by_rows(CAP, 16, finish)

        def to_tokens(t, m):
            total = None
            for e in (0, 1):
                value = o_ref[e, t, m]
                for _ in range(3):
                    low = value.astype(BF)
                    term = mm(disp_ref[m, e], low, TN)
                    total = term if total is None else total + term
                    value = value - low.astype(F32)
            return total

        def token_rows(m):
            span = pl.ds(128 * m, 128)
            home(0, m)
            u_ref[...] = to_tokens(0, m)
            home(1, m)
            g_ref[...] = to_tokens(1, m)

            def visit(index):
                rr = pl.ds(128 * m + index.start, 32)
                local = pl.ds(index.start, 32)
                stat = stat_ref[rr]
                p0, p1, gate, pick = (stat[:, i : i + 1] for i in range(4))
                dy = dy_ref[rr].astype(F32)
                values = y_ref[rr]
                u = u_ref[local] + jnp.where(pick > 0.5, bias1, bias0)
                mixed_ref[rr] = (values + gate * u).astype(BF)
                dgate = jnp.sum(dy * u, -1, keepdims=True)
                d0, d1 = dgate * (1.0 - pick), dgate * pick
                mean_grad = p0 * d0 + p1 * d1
                l0, l1 = p0 * (d0 - mean_grad), p1 * (d1 - mean_grad)
                grad = g_ref[local] + (l0 * router0 + l1 * router1)
                h2f = h2_ref[rr].astype(F32)
                centred = values - jnp.mean(values, -1, keepdims=True)
                inv = lax.rsqrt(jnp.mean(centred * centred, -1, keepdims=True) + norm_eps)
                unit = centred * inv
                scaled = grad * gain2
                back = inv * (
                    scaled
                    - jnp.mean(scaled, -1, keepdims=True)
                    - unit * jnp.mean(scaled * unit, -1, keepdims=True)
                )
                dy1 = dy + back
                low = dy1.astype(BF)
                dy1_ref[rr] = dy1
                da_ref[rr] = low
                sums = (
                    low.astype(F32), grad * unit, grad, h2f * l0, h2f * l1,
                )
                for row, term in enumerate(sums):
                    acc[row : row + 1] += jnp.sum(term, 0, keepdims=True)

            by_rows(128, 32, visit)

        token_rows(0)
        token_rows(1)
        for e in (0, 1):
            for m in (0, 1):
                acc[5 + e : 6 + e] += jnp.sum(d_ref[e, m].astype(F32), 0, keepdims=True)
        v_ref[...] = jnp.zeros_like(v_ref)
        for i in range(4):
            v_ref[i, 4:11, :] = acc[0:7, 256 * i : 256 * (i + 1)]
            v_ref[i, pl.ds(11 + me, 1), :] = gib_ref[:, 256 * i : 256 * (i + 1)]
        for t in (0, 1):
            for m in (0, 1):
                for i in range(3):
                    away(t, m, i).wait_send()
                    onward(t, m, i).wait_send()
                    to_home(t, m, i).wait_send()
                for i in range(4):
                    to_pair(t, m, i).wait_send()
                beside(t, m).wait_send()
        w_finish()
        z_finish()

    return pl.pallas_call(
        kernel,
        out_shape=(
            jax.ShapeDtypeStruct((1024, 1024), BF),
            jax.ShapeDtypeStruct((256, 1024), BF),
            jax.ShapeDtypeStruct((256, 1024), BF),
            jax.ShapeDtypeStruct((256, 1024), F32),
            jax.ShapeDtypeStruct((256, 1024), BF),
            jax.ShapeDtypeStruct((4, 24, 256), F32),
        ),
        in_specs=[vmem_spec()] * 3 + [any_spec()] + [vmem_spec()] * 6,
        out_specs=[vmem_spec()] * 6,
        scratch_shapes=[
            pltpu.VMEM((2, 2, 2, CAP, 1024), F32),
            pltpu.VMEM((1, 1024), F32),
            pltpu.VMEM((8, 1024), F32),
            pltpu.VMEM((1024, 1024), BF),
            pltpu.VMEM((4, 256, 1024), BF),
            pltpu.VMEM((128, 1024), F32),
            pltpu.VMEM((128, 1024), F32),
            pltpu.VMEM((2, 2, 8, CAP, 1024), BF),
            pltpu.VMEM((16 * CAP, 1024), BF),
            pltpu.VMEM((16 * CAP, 1024), F32),
            pltpu.VMEM((16 * CAP, 1024), BF),
            pltpu.VMEM((2, 2, 8, CAP, 1024), BF),
            pltpu.VMEM((2, 2, 4, CAP, 1024), BF),
            pltpu.VMEM((2, 2, 3, CAP, 1024), BF),
            pltpu.VMEM((2, 2, 3, CAP, 1024), BF),
        ]
        + [DMA((2, 2, 3))] * 4
        + [DMA((2, 2))] * 3
        + [DMA((2, 2, 4))] * 2
        + [DMA((2, 2, 3))] * 2
        + line_sems(4)
        + fold_scratch(256),
        name="moe",
        compiler_params=remote_params(2),
    )(h_slots, d_slots, win, w_back, params, y1, h2, stats, dispatch, dy)


def final_call(gi, gb, gq, gwo, vectors, gqv, x, dh1, dy1, params):
    def kernel(
        gi_ref, gb_ref, gq_ref, go_ref, base_ref, gqv_ref, x_ref, dh_ref, dy_ref, params_ref,
        oi_ref, ob_ref, oq_ref, oo_ref, ov_ref, ot_ref,
        v_ref, acc, qgot, qsum, vgot, vsum, vall,
        qs, qr, vs, vr, ps, pr, ws, wr, hs, hr, fs, fr, ol, *sems,
    ):
        me, core, sib, xn, yn, dg = plane_coords()
        z = lax.axis_index("fsdp")
        others = [(me + d) % 8 for d in range(1, 8)]
        meet(others, line_peers())
        owner = me // 2

        def vector_copy(d):
            peer = (z + d) % 4
            return send_to(v_ref.at[peer], vgot.at[d - 1], vs.at[d - 1], vr.at[d - 1], "fsdp", peer)

        def q_copy(d):
            peer = (z + d) % 4
            block = gq_ref.at[:, pl.ds(pl.multiple_of(peer * 256, 256), 256)]
            return send_to(block, qgot.at[d - 1], qs.at[d - 1], qr.at[d - 1], "fsdp", peer)

        rows_mine = oo_ref.at[pl.ds(pl.multiple_of(core * 128, 128), 128)]
        rows_sib = oo_ref.at[pl.ds(pl.multiple_of((1 - core) * 128, 128), 128)]

        def half(ref, part):
            return ref.at[pl.ds(64 * part, 64)]

        def o_near(i):
            return send_to(go_ref, rows_mine, ws.at[i], wr, "ctx", (xn, yn)[i])

        def o_half(part):
            block = half(rows_mine, part)
            return send_to(block, block, hs, hr.at[part], "ctx", (yn, xn)[part])

        def o_pair(src):
            return send_to(src, rows_mine, fs, fr, "ctx", sib)

        row, col = me // 4, (me // 2) % 2
        own_row, own_col = z // 2, z % 2
        beside_x = (row == own_row) & (col != own_col)
        beside_y = (row != own_row) & (col == own_col)
        across = (row != own_row) & (col != own_col)

        def o_root():
            @pl.when(z == owner)
            def _():
                for i in (0, 1):
                    o_near(i).start()
                o_pair(go_ref).start()
                pltpu.make_async_copy(go_ref, rows_mine, ol).start()

        def o_relay():
            @pl.when(beside_x)
            def _():
                o_near(0).wait_recv()
                o_half(0).start()
                o_pair(rows_mine).start()

            @pl.when(beside_y)
            def _():
                o_near(1).wait_recv()
                o_half(1).start()
                o_pair(rows_mine).start()

        def o_end():
            @pl.when(across)
            def _():
                o_half(0).wait_recv()
                o_half(1).wait_recv()
                o_pair(rows_mine).start()
                o_pair(rows_mine).wait_send()

            @pl.when(z == owner)
            def _():
                for i in (0, 1):
                    o_near(i).wait_send()
                o_pair(go_ref).wait_send()
                pltpu.make_async_copy(go_ref, rows_mine, ol).wait()

            @pl.when(beside_x)
            def _():
                o_half(0).wait_send()
                o_pair(rows_mine).wait_send()

            @pl.when(beside_y)
            def _():
                o_half(1).wait_send()
                o_pair(rows_mine).wait_send()

            send_to(go_ref, rows_sib, fs, fr, "ctx", sib).wait_recv()

        def own(k):
            if k < 4:
                return gi_ref.at[:, pl.ds(256 * k, 256)]
            return gb_ref.at[pl.ds(64 * (k - 4), 64)]

        def slot(device, k):
            which, part = device // 4, device % 4
            if k < 4:
                column = pl.multiple_of(k * 1024 + part * 256, 256)
                return oi_ref.at[which, :, pl.ds(column, 256)]
            row_at = pl.multiple_of(part * 256 + 64 * (k - 4), 64)
            return ob_ref.at[which, pl.ds(row_at, 64)]

        def qslot(device, k):
            return oq_ref.at[k, :, pl.ds(pl.multiple_of(device * 128, 128), 128)]

        begin, relay, diag, done, finish = ring_ops(own, slot, sems[:9])
        q_begin, q_relay, q_diag, q_done, q_finish = ring_ops(lambda k: qsum.at[k], qslot, sems[9:18])
        for d in (1, 3, 2):
            q_copy(d).start()
        for k in range(8):
            begin(k)
        o_root()
        gain = jnp.concatenate([params_ref[i, 0:1, :] for i in range(4)], axis=1).astype(F32)
        acc[...] = jnp.zeros_like(acc)

        def norm_rows(rr):
            values = x_ref[rr].astype(F32)
            grad = dh_ref[rr]
            centred = values - jnp.mean(values, -1, keepdims=True)
            inv = lax.rsqrt(jnp.mean(centred * centred, -1, keepdims=True) + norm_eps)
            unit = centred * inv
            scaled = grad * gain
            back = inv * (
                scaled
                - jnp.mean(scaled, -1, keepdims=True)
                - unit * jnp.mean(scaled * unit, -1, keepdims=True)
            )
            ot_ref[rr] = dy_ref[rr] + back
            acc[0:1] += jnp.sum(grad * unit, 0, keepdims=True)
            acc[1:2] += jnp.sum(grad, 0, keepdims=True)

        for k in range(4):

            def part(index):
                norm_rows(pl.ds(64 * k + index.start, 32))

            by_rows(64, 32, part)
            relay(k)
        v_ref[...] = base_ref[...]
        for i in range(4):
            v_ref[i, 0:2, :] = acc[0:2, 256 * i : 256 * (i + 1)]
        v_ref[owner, 2:4, pl.ds(pl.multiple_of(core * 128, 128), 128)] = gqv_ref[...]
        for d in (1, 2, 3):
            vector_copy(d).start()

        def plane_vector(i):
            return send_to(vsum, vall.at[i], ps.at[i], pr.at[i], "ctx", others[i])

        relay(4)
        for d in (1, 3, 2):
            q_copy(d).wait_recv()
        for j in range(3):

            def add(rr):
                place = pl.ds(pl.multiple_of(z * 256 + rr.start, 32), 32)
                total = gq_ref[j, place].astype(F32)
                for i in range(3):
                    total = total + qgot[i, j, rr].astype(F32)
                qsum[j, rr] = total.astype(BF)

            by_rows(256, 32, add)
        for k in range(3):
            q_begin(k)
        for d in (1, 2, 3):
            vector_copy(d).wait_recv()
        vsum[...] = v_ref[z] + vgot[0] + vgot[1] + vgot[2]
        for i in range(7):
            plane_vector(i).start()
        relay(5)
        diag(0)
        relay(6)
        diag(1)
        relay(7)
        diag(2)
        o_relay()
        diag(3)
        for k in range(3):
            q_relay(k)
        for k in range(4, 8):
            diag(k)
        for k in range(3):
            q_diag(k)
        o_end()
        for k in range(8):
            done(k)
        for k in range(3):
            q_done(k)
        total = vsum[...]
        for i in range(7):
            plane_vector(i).wait_recv()
            total = total + vall[i]
        ov_ref[...] = total
        for k in range(8):
            finish(k)
        for k in range(3):
            q_finish(k)
        for d in (1, 2, 3):
            vector_copy(d).wait_send()
            q_copy(d).wait_send()
        for i in range(7):
            plane_vector(i).wait_send()

    count = vectors.shape[1]
    return pl.pallas_call(
        kernel,
        out_shape=(
            jax.ShapeDtypeStruct((2, 256, 4096), BF),
            jax.ShapeDtypeStruct((2, 1024, 1024), BF),
            jax.ShapeDtypeStruct((3, 256, 1024), BF),
            jax.ShapeDtypeStruct((256, 1024), BF),
            jax.ShapeDtypeStruct((count, 256), F32),
            jax.ShapeDtypeStruct((256, 1024), F32),
        ),
        in_specs=[vmem_spec()] * 10,
        out_specs=[any_spec()] * 4 + [vmem_spec()] * 2,
        scratch_shapes=[
            pltpu.VMEM((4, count, 256), F32),
            pltpu.VMEM((8, 1024), F32),
            pltpu.VMEM((3, 3, 256, 128), BF),
            pltpu.VMEM((3, 256, 128), BF),
            pltpu.VMEM((3, count, 256), F32),
            pltpu.VMEM((count, 256), F32),
            pltpu.VMEM((7, count, 256), F32),
            DMA((3,)), DMA((3,)), DMA((3,)), DMA((3,)), DMA((7,)), DMA((7,)),
            DMA((2,)), DMA(()), DMA(()), DMA((2,)), DMA(()), DMA(()), DMA(()),
        ]
        + gather_sems(8)
        + gather_sems(3),
        name="final",
        compiler_params=remote_params(6),
    )(gi, gb, gq, gwo, vectors, gqv, x, dh1, dy1, params)


def head_masks(rows):
    lane = lax.broadcasted_iota(jnp.int32, (rows, 128), 1)
    return lane < 64, lane >= 64


def allowed_mask(i, doc_col, doc_row):
    length = 256 * (i + 1)
    qpos = lax.broadcasted_iota(jnp.int32, (256, length), 0) + 256 * i
    kpos = lax.broadcasted_iota(jnp.int32, (256, length), 1)
    return (kpos <= qpos) & (doc_col == doc_row)


def back_kernel(
    da_ref, h_ref, qkv_ref, of_ref, lse_ref, w_ref, wo_ref, doc_ref, gi_ref,
    out_ref, gq_ref, gwo_ref, gqv_ref, gis_ref,
    g_all, dqkv, part, dka, dva, probs, gwo, gwo_low, gwo_got, os, orr, *sems,
):
    me, core, sib, xn, yn, dg = plane_coords()
    meet((sib, xn, yn), line_peers())
    begin, relay, diag, done, finish = ring_ops(
        lambda k: da_ref.at[pl.ds(64 * k, 64)],
        lambda device, k: g_all.at[natural_slot(device, k)],
        sems[:9],
    )
    z_begin, z_step, z_finish = fold_ops(
        lambda where: gi_ref.at[pl.ds(pl.multiple_of(where * 256, 256), 256)],
        256,
        gis_ref,
        sems[9:13],
    )
    sums = [sum_ops(part, m, out_ref, sems[13:]) for m in (0, 1)]
    z = lax.axis_index("fsdp")
    owner = me // 2
    away = (owner - z + 4) % 4

    def to_owner():
        return send_to(gwo_low, gwo_got.at[away - 1], os, orr.at[away - 1], "fsdp", owner)

    masks = head_masks(256)
    zero = jnp.zeros((), BF)
    spans = [slice(128 * i * (i + 1), 128 * (i + 1) * (i + 2)) for i in range(4)]
    begin(0)
    begin(1)
    z_begin()

    def weigh(m, carry):
        place = pl.ds(pl.multiple_of(m * 1024, 1024), 1024)
        q, k = qkv_ref[0, place], qkv_ref[1, place]
        doc_row, doc_col = token_docs(doc_ref, m)
        for i in range(4):
            length = 256 * (i + 1)
            rows = slice(256 * i, 256 * (i + 1))
            qi = q[rows] * jnp.asarray(0.125, BF)
            allowed = allowed_mask(i, doc_col[rows], doc_row[:, :length])
            lse = lse_ref[pl.ds(pl.multiple_of(m * 1024 + 256 * i, 256), 256)]
            for j in (0, 1):
                s = mm(jnp.where(masks[j], qi, zero), k[:length], NT)
                probs[m, j, :, spans[i]] = jnp.exp(
                    jnp.where(allowed, s, mask_fill) - lse[:, 64 * j : 64 * j + 1]
                )

        @pl.when(m == 0)
        def _():
            relay(0)
            relay(1)
            begin(2)
            begin(3)

        return carry

    lax.fori_loop(0, 2, weigh, 0)
    z_step(0)
    diag(0)
    diag(1)
    done(0)
    done(1)
    kmasks = head_masks(1024)

    def micro(m, carry):
        @pl.when(m == 1)
        def _():
            done(2)
            done(3)

        place = pl.ds(pl.multiple_of(m * 1024, 1024), 1024)
        g = g_all[pl.ds(16 * m, 16)].reshape(1024, 1024)
        q, k, v = qkv_ref[0, place], qkv_ref[1, place], qkv_ref[2, place]
        do = mm(g, wo_ref[...], NT).astype(BF)
        term = mm(of_ref[place].astype(BF), g, TN)

        @pl.when(m == 0)
        def _():
            gwo[...] = term

        @pl.when(m == 1)
        def _():
            gwo_low[...] = (gwo[...] + term).astype(BF)

            @pl.when(z != owner)
            def _():
                to_owner().start()

        dka[...] = jnp.zeros_like(dka)
        dva[...] = jnp.zeros_like(dva)
        kh = [jnp.where(kmasks[j], k, zero) for j in (0, 1)]
        for i in range(4):
            length = 256 * (i + 1)
            rows = slice(256 * i, 256 * (i + 1))
            at = pl.ds(pl.multiple_of(m * 1024 + 256 * i, 256), 256)
            qi = q[rows] * jnp.asarray(0.125, BF)
            doi = do[rows]
            prod = doi.astype(F32) * of_ref[at]
            dq = None
            for j in (0, 1):
                qh = jnp.where(masks[j], qi, zero)
                doh = jnp.where(masks[j], doi, zero)
                delta = jnp.sum(jnp.where(masks[j], prod, 0.0), -1, keepdims=True)
                p = probs[m, j, :, spans[i]]
                dp = mm(doh, v[:length], NT)
                ds = (p * (dp - delta)).astype(BF)
                term = mm(ds, kh[j][:length])
                dq = term if dq is None else dq + term
                dka[:, :length] += mm(qh, ds, TN)
                dva[:, :length] += mm(doh, p.astype(BF), TN)
            dqkv[0, at] = (dq * 0.125).astype(BF)

            @pl.when(m == 0)
            def _():
                if i == 0:
                    relay(2)
                if i == 1:
                    relay(3)
                    z_step(1)
                if i == 3:
                    diag(2)
                    diag(3)
                    z_step(2)

            @pl.when(m == 1)
            def _():
                if i == 0:
                    z_step(3)
                if i == 1:
                    sums[0][3]()

        dqkv[1, place] = jnp.transpose(dka[...]).astype(BF)
        dqkv[2, place] = jnp.transpose(dva[...]).astype(BF)
        for i in range(4):
            at = pl.ds(pl.multiple_of(m * 1024 + 256 * i, 256), 256)
            a = mm(dqkv[0, at], w_ref[0], NT) + mm(dqkv[1, at], w_ref[1], NT)
            a = (a + mm(dqkv[2, at], w_ref[2], NT)).astype(BF)
            for b in range(4):
                block = 4 * i + b
                dest, side = (block, 0) if block < 8 else (15 - block, 1)
                part[m, dest, 64 * side : 64 * (side + 1)] = a[64 * b : 64 * (b + 1)]
        for n in (0, 1):

            @pl.when(m == n)
            def _():
                for step in sums[n][:3]:
                    step()

        return carry

    lax.fori_loop(0, 2, micro, 0)
    sums[1][3]()
    for j in range(3):
        gq_ref[j] = jnp.transpose(mm(dqkv[j], h_ref[...].reshape(2048, 1024), TN)).astype(BF)
    gqv_ref[0:1] = jnp.sum(dqkv[0].astype(F32), 0, keepdims=True)
    gqv_ref[1:2] = jnp.sum(dqkv[2].astype(F32), 0, keepdims=True)
    sums[0][4]()
    sums[1][4]()
    z_finish()

    @pl.when(z != owner)
    def _():
        to_owner().wait_send()

    @pl.when(z == owner)
    def _():
        for i in range(3):
            send_to(gwo_low, gwo_got.at[i], os, orr.at[i], "fsdp", (z + 1) % 4).wait_recv()

        def add(rr):
            total = gwo_low[rr].astype(F32)
            for i in range(3):
                total = total + gwo_got[i, rr].astype(F32)
            gwo_ref[rr] = total.astype(BF)

        by_rows(128, 32, add)

    @pl.when(z != owner)
    def _():
        gwo_ref[...] = jnp.zeros_like(gwo_ref)

    for k in range(4):
        finish(k)


def back_call(da, h, qkv, of, lse, wqkv, wout, docs, gi):
    return pl.pallas_call(
        back_kernel,
        out_shape=(
            jax.ShapeDtypeStruct((256, 1024), F32),
            jax.ShapeDtypeStruct((3, 1024, 128), BF),
            jax.ShapeDtypeStruct((128, 1024), BF),
            jax.ShapeDtypeStruct((2, 128), F32),
            jax.ShapeDtypeStruct((256, 1024), BF),
        ),
        in_specs=[vmem_spec()] * 9,
        out_specs=[vmem_spec()] * 5,
        scratch_shapes=[
            pltpu.VMEM((32, 64, 1024), BF),
            pltpu.VMEM((3, 2048, 128), BF),
            pltpu.VMEM((2, 8, 128, 1024), BF),
            pltpu.VMEM((128, 1024), F32),
            pltpu.VMEM((128, 1024), F32),
            pltpu.VMEM((2, 2, 256, 2560), F32),
            pltpu.VMEM((128, 1024), F32),
            pltpu.VMEM((128, 1024), BF),
            pltpu.VMEM((3, 128, 1024), BF),
            DMA(()),
            DMA((3,)),
        ]
        + gather_sems(4)
        + fold_scratch(256)
        + sum_scratch(),
        name="back",
        compiler_params=remote_params(4),
    )(da, h, qkv, of, lse, wqkv, wout, docs, gi)


GELU_A = math.sqrt(2.0 / math.pi)
GELU_B = 0.044715


def widen_call(arrays, kinds, sums):
    count = len(arrays)
    steps = 8
    flat = [array.reshape(-1, array.shape[-1]) for array in arrays]
    sizes = [f.shape[0] // steps for f in flat]
    small = [(256,), (256,), (2, 256), (256,), (256,), (256,), (2, 256), (2, 1024), (2, 256)]

    def kernel(*refs):
        step = pl.program_id(0)
        v_ref, wide, outs = refs[count], refs[count + 1 : 2 * count + 1], refs[2 * count + 1 :]
        for src, dst, size in zip(refs[:count], wide, sizes):
            dst[...] = src[pl.ds(pl.multiple_of(step * size, 16), size)].astype(dst.dtype)

        @pl.when(step == 0)
        def _():
            for index, row in ((0, 0), (1, 1), (3, 4), (4, 5), (5, 6)):
                outs[index][...] = v_ref[row]
            outs[2][...] = v_ref[2:4]
            outs[6][...] = v_ref[7:9]
            for e in (0, 1):
                for k in range(4):
                    outs[7][e : e + 1, 256 * k : 256 * (k + 1)] = v_ref[11 + 4 * e + k : 12 + 4 * e + k]
            outs[8][...] = v_ref[9:11]

    results = pl.pallas_call(
        kernel,
        grid=(steps,),
        out_shape=[jax.ShapeDtypeStruct(f.shape, kind) for f, kind in zip(flat, kinds)]
        + [jax.ShapeDtypeStruct(shape, F32) for shape in small],
        in_specs=[vmem_spec()] * (count + 1),
        out_specs=[pl.BlockSpec((n, f.shape[1]), lambda i: (i, 0)) for n, f in zip(sizes, flat)]
        + [vmem_spec()] * len(small),
        name="widen",
        compiler_params=pltpu.CompilerParams(vmem_limit_bytes=VMEM_CAP),
    )(*flat, sums)
    return [w.reshape(a.shape) for w, a in zip(results[:count], arrays)], results[count:]


def fast_body(
    tokens, doc_ids, routes, cotangent, ln1_gain, ln1_shift, w_qkv, qv_bias, w_out, out_bias,
    ln2_gain, ln2_shift, router, w_in, in_bias, w_back, back_bias,
):
    router_t = jnp.transpose(router)
    rows = [ln1_gain[None], ln1_shift[None], qv_bias[0:1], qv_bias[1:2], out_bias[None]]
    rows += [ln2_gain[None], ln2_shift[None], router_t[0:1], router_t[1:2]]
    rows += [in_bias[e : e + 1, 256 * k : 256 * (k + 1)] for e in (0, 1) for k in range(4)]
    rows += [back_bias[0:1], back_bias[1:2]]
    row_iota = lax.broadcasted_iota(jnp.int32, (SMALL_ROWS, 256), 0)
    small = jnp.zeros((SMALL_ROWS, 256), BF)
    for index, row in enumerate(rows):
        small = jnp.where(row_iota == index, row, small)
    x_low = tokens[:, 0].reshape(256, 1024)
    picks = routes[:, 0, :, 0]
    dy_low = cotangent[:, 0].reshape(256, 1024)
    hs, params, wqkv_c, wout_c, win_c, qkv, o_full, lse, y1, h2, stats, dispatch, h_slots, d_slots = (
        front_call(x_low, small, doc_ids, w_qkv, w_out, w_in, picks, dy_low)
    )
    gi, gb_sum, mixed, dy1, da, vectors = moe_call(
        h_slots, d_slots, win_c, w_back, params, y1, h2, stats, dispatch, dy_low
    )
    dh1, gq, gwo, gqv, gi_sum = back_call(
        da, hs, qkv, o_full, lse, wqkv_c, wout_c, doc_ids, gi
    )
    g_in, g_back, g_qkv, g_out, sums, token_grad = final_call(
        gi_sum, gb_sum, gq, gwo, vectors, gqv, x_low, dh1, dy1, params
    )
    (g_in, g_back, g_qkv, g_out, token_grad, mixed), small_grads = widen_call(
        [g_in, g_back, g_qkv, g_out, token_grad, mixed], [F32] * 5 + [BF], sums
    )
    g_one, s_one, g_qv, g_outb, g_two, s_two, g_router, g_inb, g_backb = small_grads
    return (
        mixed.reshape(2, 1, 128, 1024),
        token_grad.reshape(2, 1, 128, 1024),
        g_one, s_one, g_qkv, g_qv, g_out, g_outb, g_two, s_two,
        jnp.transpose(g_router), g_in, g_inb, g_back, g_backb,
    )


def solution(mesh):
    small_plane = mesh.shape["ctx"] == 8 and mesh.shape["fsdp"] == 4
    chosen_body = fast_body if small_plane else body
    placed = (
        P(None, "fsdp", "ctx", None),
        P(None, "fsdp", None),
        P(None, "fsdp", "ctx", None),
        P(None, "fsdp", "ctx", None),
        P("fsdp"),
        P("fsdp"),
        P(None, "fsdp", None),
        P(None, "fsdp"),
        P("fsdp", None),
        P("fsdp"),
        P("fsdp"),
        P("fsdp"),
        P("fsdp", None),
        P(None, "fsdp", None),
        P(None, "fsdp"),
        P(None, "fsdp", None),
        P(None, "fsdp"),
    )
    return jax.shard_map(
        chosen_body,
        mesh=mesh,
        in_specs=placed,
        out_specs=(
            P(None, "fsdp", "ctx", None),
            P(None, "fsdp", "ctx", None),
            P("fsdp"),
            P("fsdp"),
            P(None, "fsdp", None),
            P(None, "fsdp"),
            P("fsdp", None),
            P("fsdp"),
            P("fsdp"),
            P("fsdp"),
            P("fsdp", None),
            P(None, "fsdp", None),
            P(None, "fsdp"),
            P(None, "fsdp", None),
            P(None, "fsdp"),
        ),
        check_vma=False,
    )
```

```python
import math

import jax
import jax.numpy as jnp
from jax import lax
from jax.experimental import pallas as pl
from jax.experimental.pallas import tpu as pltpu
from jax.sharding import PartitionSpec as P

HEADS = 16
HEAD_DIM = 64
CAP = 80


norm_eps = 1e-05
mask_fill = -1e30


def layer_norm(values, gain, shift):
    mean = jnp.mean(values, -1, keepdims=True)
    centred = values - mean
    spread = jnp.mean(centred * centred, -1, keepdims=True)
    return centred * lax.rsqrt(spread + norm_eps) * gain + shift


def natural_position(store_index, tok_rows, ctx_count):
    half = tok_rows // 2
    device = store_index // tok_rows
    slot = store_index % tok_rows
    return jnp.where(
        slot < half, device * half + slot, (2 * ctx_count - 1 - device) * half + slot - half
    )


def visible(query_pos, query_ids, key_pos, key_ids):
    return (key_pos[None, :] <= query_pos[:, None]) & (key_ids[None, :] == query_ids[:, None])


def block_needed(query_pos, query_ids, key_pos, key_ids):
    return (
        (jnp.min(key_pos) <= jnp.max(query_pos))
        & (jnp.max(key_ids) >= jnp.min(query_ids))
        & (jnp.min(key_ids) <= jnp.max(query_ids))
    )


def attend_keys(
    running, query_heads, query_pos, query_ids, key_part, value_part, pos_part, id_part, scale
):
    length = key_part.shape[0]
    stride = math.gcd(length, 512)
    key_heads = key_part.reshape(length, HEADS, HEAD_DIM)
    value_heads = value_part.reshape(length, HEADS, HEAD_DIM)

    def attend_visit_block(block_index, state):
        offset = block_index * stride
        key_blk = lax.dynamic_slice_in_dim(key_heads, offset, stride, 0)
        value_blk = lax.dynamic_slice_in_dim(value_heads, offset, stride, 0)
        key_pos = lax.dynamic_slice_in_dim(pos_part, offset, stride, 0)
        key_ids = lax.dynamic_slice_in_dim(id_part, offset, stride, 0)
        needed = block_needed(query_pos, query_ids, key_pos, key_ids)

        def update(current):
            best, totals, accum = current
            scores = (
                jnp.einsum("qhc,khc->hqk", query_heads, key_blk, preferred_element_type=jnp.float32)
                * scale
            )
            allowed = visible(query_pos, query_ids, key_pos, key_ids)[None]
            scores = jnp.where(allowed, scores, mask_fill)
            new_best = jnp.maximum(best, jnp.max(scores, -1))
            shrink = jnp.exp(best - new_best)
            weights = jnp.where(allowed, jnp.exp(scores - new_best[..., None]), 0.0)
            totals = totals * shrink + jnp.sum(weights, -1)
            addend = jnp.einsum(
                "hqk,khc->qhc",
                weights.astype(jnp.bfloat16),
                value_blk,
                preferred_element_type=jnp.float32,
            )
            accum = accum * jnp.transpose(shrink)[..., None] + addend
            return (new_best, totals, accum)

        def unchanged(current):
            return current

        return lax.cond(needed, update, unchanged, state)

    return lax.fori_loop(0, length // stride, attend_visit_block, running)


def backward_range(
    query_heads,
    grad_heads,
    log_total,
    delta,
    query_pos,
    query_ids,
    key_part,
    value_part,
    pos_part,
    id_part,
    scale,
):
    length = key_part.shape[0]
    stride = math.gcd(length, 512)
    blocks = length // stride
    key_blocks = key_part.reshape(blocks, stride, HEADS, HEAD_DIM)
    value_blocks = value_part.reshape(blocks, stride, HEADS, HEAD_DIM)
    pos_blocks = pos_part.reshape(blocks, stride)
    id_blocks = id_part.reshape(blocks, stride)
    rows = query_heads.shape[0]

    def backward_visit_block(query_acc, block_data):
        key_blk, value_blk, pos_blk, id_blk = block_data
        needed = block_needed(query_pos, query_ids, pos_blk, id_blk)

        def compute(current):
            scores = (
                jnp.einsum("qhc,khc->hqk", query_heads, key_blk, preferred_element_type=jnp.float32)
                * scale
            )
            allowed = visible(query_pos, query_ids, pos_blk, id_blk)[None]
            weights = jnp.where(allowed, jnp.exp(scores - log_total[..., None]), 0.0)
            weight_grad = jnp.einsum(
                "qhc,khc->hqk", grad_heads, value_blk, preferred_element_type=jnp.float32
            )
            score_grad = (weights * (weight_grad - delta[..., None])).astype(jnp.bfloat16)
            current = (
                current
                + jnp.einsum(
                    "hqk,khc->qhc", score_grad, key_blk, preferred_element_type=jnp.float32
                )
                * scale
            )
            terms = ()
            value_term = jnp.einsum(
                "hqk,qhc->khc",
                weights.astype(jnp.bfloat16),
                grad_heads,
                preferred_element_type=jnp.float32,
            )
            key_term = (
                jnp.einsum(
                    "hqk,qhc->khc", score_grad, query_heads, preferred_element_type=jnp.float32
                )
                * scale
            )
            terms = (key_term, value_term)
            return (current, terms)

        def skipped(current):
            terms = ()
            empty = jnp.zeros((stride, HEADS, HEAD_DIM), jnp.float32)
            terms = (empty, empty)
            return (current, terms)

        query_acc, terms = lax.cond(needed, compute, skipped, query_acc)
        terms = (
            terms[0].reshape(stride, HEADS * HEAD_DIM),
            terms[1].reshape(stride, HEADS * HEAD_DIM),
        )
        return (query_acc, terms)

    start_acc = jnp.zeros((rows, HEADS, HEAD_DIM), jnp.float32)
    query_grad, terms = lax.scan(
        backward_visit_block, start_acc, (key_blocks, value_blocks, pos_blocks, id_blocks)
    )
    return (
        query_grad,
        terms[0].reshape(length, HEADS * HEAD_DIM),
        terms[1].reshape(length, HEADS * HEAD_DIM),
    )


def gather_keys(key_rows, value_rows):
    return (
        lax.all_gather(key_rows, "ctx", axis=0, tiled=True),
        lax.all_gather(value_rows, "ctx", axis=0, tiled=True),
    )


def reduce_grads(attn_terms, expert_terms):
    g_one, s_one, g_qkv, g_qv, g_out, g_outb, g_two, s_two, g_router = attn_terms
    g_in, g_inb, g_back, g_backb = expert_terms
    e_in, e_inb, e_back, e_backb = (
        lax.psum_scatter(g_in.astype(jnp.bfloat16), "fsdp", scatter_dimension=1, tiled=True).astype(
            jnp.float32
        ),
        lax.psum_scatter(
            g_inb.astype(jnp.bfloat16), "fsdp", scatter_dimension=1, tiled=True
        ).astype(jnp.float32),
        lax.psum_scatter(
            g_back.astype(jnp.bfloat16), "fsdp", scatter_dimension=1, tiled=True
        ).astype(jnp.float32),
        lax.psum_scatter(
            g_backb.astype(jnp.bfloat16), "fsdp", scatter_dimension=1, tiled=True
        ).astype(jnp.float32),
    )
    a_one, b_one, a_qkv, a_qv, a_out, a_outb, a_two, b_two, a_router = (
        lax.psum_scatter(
            g_one.astype(jnp.bfloat16), "fsdp", scatter_dimension=0, tiled=True
        ).astype(jnp.float32),
        lax.psum_scatter(
            s_one.astype(jnp.bfloat16), "fsdp", scatter_dimension=0, tiled=True
        ).astype(jnp.float32),
        lax.psum_scatter(
            g_qkv.astype(jnp.bfloat16), "fsdp", scatter_dimension=1, tiled=True
        ).astype(jnp.float32),
        lax.psum_scatter(g_qv.astype(jnp.bfloat16), "fsdp", scatter_dimension=1, tiled=True).astype(
            jnp.float32
        ),
        lax.psum_scatter(
            g_out.astype(jnp.bfloat16), "fsdp", scatter_dimension=0, tiled=True
        ).astype(jnp.float32),
        lax.psum_scatter(
            g_outb.astype(jnp.bfloat16), "fsdp", scatter_dimension=0, tiled=True
        ).astype(jnp.float32),
        lax.psum_scatter(
            g_two.astype(jnp.bfloat16), "fsdp", scatter_dimension=0, tiled=True
        ).astype(jnp.float32),
        lax.psum_scatter(
            s_two.astype(jnp.bfloat16), "fsdp", scatter_dimension=0, tiled=True
        ).astype(jnp.float32),
        lax.psum_scatter(
            g_router.astype(jnp.bfloat16), "fsdp", scatter_dimension=0, tiled=True
        ).astype(jnp.float32),
    )
    return (
        lax.psum(a_one.astype(jnp.bfloat16), "ctx").astype(jnp.float32),
        lax.psum(b_one.astype(jnp.bfloat16), "ctx").astype(jnp.float32),
        lax.psum(a_qkv.astype(jnp.bfloat16), "ctx").astype(jnp.float32),
        lax.psum(a_qv.astype(jnp.bfloat16), "ctx").astype(jnp.float32),
        lax.psum(a_out.astype(jnp.bfloat16), "ctx").astype(jnp.float32),
        lax.psum(a_outb.astype(jnp.bfloat16), "ctx").astype(jnp.float32),
        lax.psum(a_two.astype(jnp.bfloat16), "ctx").astype(jnp.float32),
        lax.psum(b_two.astype(jnp.bfloat16), "ctx").astype(jnp.float32),
        lax.psum(a_router.astype(jnp.bfloat16), "ctx").astype(jnp.float32),
        lax.psum(e_in.astype(jnp.bfloat16), "ctx").astype(jnp.float32),
        lax.psum(e_inb.astype(jnp.bfloat16), "ctx").astype(jnp.float32),
        lax.psum(e_back.astype(jnp.bfloat16), "ctx").astype(jnp.float32),
        lax.psum(e_backb.astype(jnp.bfloat16), "ctx").astype(jnp.float32),
    )


def body(
    tokens,
    doc_ids,
    routes,
    cotangent,
    ln1_gain,
    ln1_shift,
    w_qkv,
    qv_bias,
    w_out,
    out_bias,
    ln2_gain,
    ln2_shift,
    router,
    w_in,
    in_bias,
    w_back,
    back_bias,
):
    gain_one, shift_one, proj_all, bias_qv, proj_out, bias_out, gain_two, shift_two, router_full = (
        lax.all_gather(ln1_gain, "fsdp", axis=0, tiled=True),
        lax.all_gather(ln1_shift, "fsdp", axis=0, tiled=True),
        lax.all_gather(w_qkv, "fsdp", axis=1, tiled=True),
        lax.all_gather(qv_bias, "fsdp", axis=1, tiled=True),
        lax.all_gather(w_out, "fsdp", axis=0, tiled=True),
        lax.all_gather(out_bias, "fsdp", axis=0, tiled=True),
        lax.all_gather(ln2_gain, "fsdp", axis=0, tiled=True),
        lax.all_gather(ln2_shift, "fsdp", axis=0, tiled=True),
        lax.all_gather(router, "fsdp", axis=0, tiled=True),
    )
    inner_full, inner_bias, outer_full, outer_bias = (
        lax.all_gather(w_in, "fsdp", axis=1, tiled=True),
        lax.all_gather(in_bias, "fsdp", axis=1, tiled=True),
        lax.all_gather(w_back, "fsdp", axis=1, tiled=True),
        lax.all_gather(back_bias, "fsdp", axis=1, tiled=True),
    )
    gain_one_f = gain_one.astype(jnp.float32)
    shift_one_f = shift_one.astype(jnp.float32)
    bias_qv_f = bias_qv.astype(jnp.float32)
    bias_out_f = bias_out.astype(jnp.float32)
    gain_two_f = gain_two.astype(jnp.float32)
    shift_two_f = shift_two.astype(jnp.float32)
    router_f = router_full.astype(jnp.float32)
    inner_bias_f = inner_bias.astype(jnp.float32)
    outer_bias_f = outer_bias.astype(jnp.float32)
    micro_count = tokens.shape[0]
    tok_rows = tokens.shape[2]
    width = tokens.shape[3]
    stream_len = doc_ids.shape[2]
    ctx_count = lax.axis_size("ctx")
    expert_count = inner_full.shape[0]
    scale = 1.0 / math.sqrt(HEAD_DIM)
    first_row = lax.axis_index("ctx") * tok_rows
    store_pos = natural_position(lax.iota(jnp.int32, stream_len), tok_rows, ctx_count)
    query_pos = lax.dynamic_slice_in_dim(store_pos, first_row, tok_rows, 0)
    expert_iota = lax.iota(jnp.int32, expert_count)
    slot_iota = lax.iota(jnp.int32, CAP)
    outputs = []
    input_grads = []
    totals = None
    for micro in range(micro_count):
        inputs = tokens[micro, 0].astype(jnp.float32)
        ids_store = jnp.take(doc_ids[micro, 0], store_pos)
        query_ids = lax.dynamic_slice_in_dim(ids_store, first_row, tok_rows, 0)
        picks = routes[micro, 0, :, 0]
        upstream = cotangent[micro, 0].astype(jnp.float32)
        h_first, pull_first = jax.vjp(layer_norm, inputs, gain_one_f, shift_one_f)
        h_first_low = h_first.astype(jnp.bfloat16)
        projected = jnp.einsum(
            "td,jde->jte", h_first_low, proj_all, preferred_element_type=jnp.float32
        )
        queries = (projected[0] + bias_qv_f[0]).astype(jnp.bfloat16)
        key_rows = projected[1].astype(jnp.bfloat16)
        value_rows = (projected[2] + bias_qv_f[1]).astype(jnp.bfloat16)
        query_heads = queries.reshape(tok_rows, HEADS, HEAD_DIM)
        start_state = (
            jnp.full((HEADS, tok_rows), mask_fill, jnp.float32),
            jnp.zeros((HEADS, tok_rows), jnp.float32),
            jnp.zeros((tok_rows, HEADS, HEAD_DIM), jnp.float32),
        )
        best, totals_soft, accum = attend_keys(
            start_state,
            query_heads,
            query_pos,
            query_ids,
            lax.all_gather(key_rows, "ctx", axis=0, tiled=True),
            lax.all_gather(value_rows, "ctx", axis=0, tiled=True),
            store_pos,
            ids_store,
            scale,
        )
        log_total = best + jnp.log(totals_soft)
        attended = accum / jnp.transpose(totals_soft)[..., None]
        attended_low = attended.reshape(tok_rows, width).astype(jnp.bfloat16)
        branch = jnp.dot(attended_low, proj_out, preferred_element_type=jnp.float32) + bias_out_f
        middle = inputs + branch
        h_second, pull_second = jax.vjp(layer_norm, middle, gain_two_f, shift_two_f)
        h_second_low = h_second.astype(jnp.bfloat16)
        logits = jnp.dot(h_second_low, router_full, preferred_element_type=jnp.float32)
        probs = jax.nn.softmax(logits, axis=-1)
        chosen = picks[:, None] == expert_iota[None, :]
        chosen_f = chosen.astype(jnp.float32)
        gate = jnp.sum(probs * chosen_f, -1)
        ranks = jnp.cumsum(chosen.astype(jnp.int32), 0) - 1
        dispatch = (jnp.transpose(ranks)[:, None, :] == slot_iota[None, :, None]) & jnp.transpose(
            chosen
        )[:, None, :]
        dispatch_low = dispatch.astype(jnp.bfloat16)
        dispatch_f = dispatch.astype(jnp.float32)
        slot_inputs = jnp.einsum(
            "ect,td->ecd", dispatch_low, h_second_low, preferred_element_type=jnp.float32
        ).astype(jnp.bfloat16)
        inner = (
            jnp.einsum("ecd,edh->ech", slot_inputs, inner_full, preferred_element_type=jnp.float32)
            + inner_bias_f[:, None, :]
        )
        active, pull_gelu = jax.vjp(jax.nn.gelu, inner)
        active_low = active.astype(jnp.bfloat16)
        result = (
            jnp.einsum("ech,ehd->ecd", active_low, outer_full, preferred_element_type=jnp.float32)
            + outer_bias_f[:, None, :]
        )
        expert_sum = jnp.einsum("ect,ecd->td", dispatch_f, result, precision=lax.Precision.HIGHEST)
        output = middle + gate[:, None] * expert_sum
        outputs.append(output.astype(jnp.bfloat16))
        gate_grad = jnp.sum(upstream * expert_sum, -1)
        slot_grad = jnp.einsum(
            "ect,td->ecd", dispatch_f, gate[:, None] * upstream, precision=lax.Precision.HIGHEST
        ).astype(jnp.bfloat16)
        outer_bias_grad = jnp.sum(slot_grad.astype(jnp.float32), 1)
        outer_grad = jnp.einsum(
            "ech,ecd->ehd", active_low, slot_grad, preferred_element_type=jnp.float32
        )
        active_grad = jnp.einsum(
            "ecd,ehd->ech", slot_grad, outer_full, preferred_element_type=jnp.float32
        )
        inner_grad = pull_gelu(active_grad)[0].astype(jnp.bfloat16)
        inner_bias_grad = jnp.sum(inner_grad.astype(jnp.float32), 1)
        inner_w_grad = jnp.einsum(
            "ecd,ech->edh", slot_inputs, inner_grad, preferred_element_type=jnp.float32
        )
        slot_input_grad = jnp.einsum(
            "ech,edh->ecd", inner_grad, inner_full, preferred_element_type=jnp.float32
        )
        second_grad = jnp.einsum(
            "ect,ecd->td", dispatch_f, slot_input_grad, precision=lax.Precision.HIGHEST
        )
        pick_grad = gate_grad[:, None] * chosen_f
        logit_grad = probs * (pick_grad - jnp.sum(probs * pick_grad, -1, keepdims=True))
        router_grad = jnp.einsum(
            "td,te->de",
            h_second_low.astype(jnp.float32),
            logit_grad,
            precision=lax.Precision.HIGHEST,
        )
        second_grad = second_grad + jnp.einsum(
            "te,de->td", logit_grad, router_f, precision=lax.Precision.HIGHEST
        )
        middle_norm_grad, gain_two_grad, shift_two_grad = pull_second(second_grad)
        middle_grad = upstream + middle_norm_grad
        branch_grad = middle_grad.astype(jnp.bfloat16)
        out_bias_grad = jnp.sum(branch_grad.astype(jnp.float32), 0)
        out_grad = jnp.einsum(
            "td,te->de", attended_low, branch_grad, preferred_element_type=jnp.float32
        )
        attended_grad = jnp.einsum(
            "te,de->td", branch_grad, proj_out, preferred_element_type=jnp.float32
        ).astype(jnp.bfloat16)
        grad_heads = attended_grad.reshape(tok_rows, HEADS, HEAD_DIM)
        delta = jnp.transpose(jnp.sum(grad_heads.astype(jnp.float32) * attended, -1))
        key_all, value_all = gather_keys(key_rows, value_rows)
        query_grad, key_terms, value_terms = backward_range(
            query_heads,
            grad_heads,
            log_total,
            delta,
            query_pos,
            query_ids,
            key_all,
            value_all,
            store_pos,
            ids_store,
            scale,
        )
        key_grad, value_grad = (
            lax.psum_scatter(
                key_terms.astype(jnp.bfloat16), "ctx", scatter_dimension=0, tiled=True
            ).astype(jnp.float32),
            lax.psum_scatter(
                value_terms.astype(jnp.bfloat16), "ctx", scatter_dimension=0, tiled=True
            ).astype(jnp.float32),
        )
        query_low = query_grad.reshape(tok_rows, width).astype(jnp.bfloat16)
        key_low = key_grad.astype(jnp.bfloat16)
        value_low = value_grad.astype(jnp.bfloat16)
        stacked_grad = jnp.stack([query_low, key_low, value_low])
        proj_grad = jnp.einsum(
            "td,jte->jde", h_first_low, stacked_grad, preferred_element_type=jnp.float32
        )
        qv_bias_grad = jnp.stack(
            [jnp.sum(query_low.astype(jnp.float32), 0), jnp.sum(value_low.astype(jnp.float32), 0)]
        )
        first_grad = jnp.einsum(
            "jte,jde->td", stacked_grad, proj_all, preferred_element_type=jnp.float32
        )
        input_norm_grad, gain_one_grad, shift_one_grad = pull_first(first_grad)
        input_grads.append(middle_grad + input_norm_grad)
        attn_terms = (
            gain_one_grad,
            shift_one_grad,
            proj_grad,
            qv_bias_grad,
            out_grad,
            out_bias_grad,
            gain_two_grad,
            shift_two_grad,
            router_grad,
        )
        expert_terms = (inner_w_grad, inner_bias_grad, outer_grad, outer_bias_grad)
        local_terms = attn_terms + expert_terms
        totals = local_terms if totals is None else jax.tree.map(jnp.add, totals, local_terms)
    totals = reduce_grads(totals[:9], totals[9:])
    (
        g_one,
        s_one,
        g_qkv,
        g_qv,
        g_out,
        g_outb,
        g_two,
        s_two,
        g_router,
        g_in,
        g_inb,
        g_back,
        g_backb,
    ) = totals
    mixed = jnp.stack(outputs)[:, None]
    token_grad = jnp.stack(input_grads)[:, None]
    return (
        mixed,
        token_grad,
        g_one,
        s_one,
        g_qkv,
        g_qv,
        g_out,
        g_outb,
        g_two,
        s_two,
        g_router,
        g_in,
        g_inb,
        g_back,
        g_backb,
    )


MESH_ID = pl.DeviceIdType.MESH
BF = jnp.bfloat16
F32 = jnp.float32
DMA = pltpu.SemaphoreType.DMA
VMEM_CAP = 60 * 1024 * 1024
SMALL_ROWS = 32
NT = (((1,), (1,)), ((), ()))
TN = (((0,), (0,)), ((), ()))
NN = (((1,), (0,)), ((), ()))


def mm(left, right, dims=NN):
    return lax.dot_general(left, right, dims, preferred_element_type=F32)


def plane_coords():
    me = lax.axis_index("ctx")
    core = me % 2
    col = (me // 2) % 2
    row = me // 4
    sib = me + 1 - 2 * core
    xn = (row * 2 + 1 - col) * 2 + core
    yn = ((1 - row) * 2 + col) * 2 + core
    dg = ((1 - row) * 2 + 1 - col) * 2 + core
    return me, core, sib, xn, yn, dg


def meet(ctx_peers, fsdp_peers=()):
    sem = pltpu.get_barrier_semaphore()
    for peer in ctx_peers:
        pl.semaphore_signal(sem, inc=1, device_id={"ctx": peer}, device_id_type=MESH_ID)
    for peer in fsdp_peers:
        pl.semaphore_signal(sem, inc=1, device_id={"fsdp": peer}, device_id_type=MESH_ID)
    pl.semaphore_wait(sem, len(ctx_peers) + len(fsdp_peers))


def send_to(src, dst, send_sem, recv_sem, axis, peer):
    return pltpu.make_async_remote_copy(
        src_ref=src,
        dst_ref=dst,
        send_sem=send_sem,
        recv_sem=recv_sem,
        device_id={axis: peer},
        device_id_type=MESH_ID,
    )


def gather_sems(chunks):
    return [
        DMA((2, chunks)),
        DMA((2, chunks)),
        DMA((chunks,)),
        DMA((chunks,)),
        DMA((3, chunks)),
        DMA((3, chunks)),
        DMA((chunks,)),
        DMA((chunks,)),
        DMA((chunks,)),
    ]


def line_sems(chunks):
    return [DMA((3, chunks)), DMA((3, chunks)), DMA((3, chunks)), DMA((3, chunks)), DMA((chunks,))]


def by_rows(count, step, visit):
    def one(index, carry):
        visit(pl.ds(pl.multiple_of(index * step, step), step))
        return carry

    lax.fori_loop(0, count // step, one, 0)


def ring_ops(own, slot, sems):
    ns, nr, ds, dr, fs, fr, ss, sr, ls = sems
    me, core, sib, xn, yn, dg = plane_coords()
    near = (xn, yn)

    def away(i, k):
        return send_to(own(k), slot(me, k), ns.at[i, k], nr.at[i, k], "ctx", near[i])

    def beside(k):
        return send_to(own(k), slot(me, k), ss.at[k], sr.at[k], "ctx", sib)

    def here(k):
        return pltpu.make_async_copy(own(k), slot(me, k), ls.at[k])

    def passed(k):
        block = slot(near[k % 2], k)
        return send_to(block, block, ds.at[k], dr.at[k], "ctx", near[1 - k % 2])

    def onward(i, k):
        block = slot((xn, yn, dg)[i], k)
        return send_to(block, block, fs.at[i, k], fr.at[i, k], "ctx", sib)

    def begin(k):
        for i in (0, 1):
            away(i, k).start()
        beside(k).start()
        here(k).start()

    def relay(k):
        for i in (k % 2, 1 - k % 2):
            away(i, k).wait_recv()
            if i == k % 2:
                passed(k).start()
            onward(i, k).start()

    def diag(k):
        passed(k).wait_recv()
        onward(2, k).start()

    def done(k):
        here(k).wait()
        beside(k).wait_recv()
        for i in range(3):
            onward(i, k).wait_recv()

    def finish(k):
        for i in (0, 1):
            away(i, k).wait_send()
        beside(k).wait_send()
        passed(k).wait_send()
        for i in range(3):
            onward(i, k).wait_send()

    return begin, relay, diag, done, finish


def line_ops(own, slot, chunks, sems):
    us, ur, ws, wr, ls = sems
    z = lax.axis_index("fsdp")

    def up(d, k):
        src = own(k) if d == 0 else slot(z - d, k)
        return send_to(src, slot(z - d, k), us.at[d, k], ur.at[d, k], "fsdp", z + 1)

    def down(d, k):
        src = own(k) if d == 0 else slot(z + d, k)
        return send_to(src, slot(z + d, k), ws.at[d, k], wr.at[d, k], "fsdp", z - 1)

    def from_below(d, k):
        return send_to(own(k), slot(z - d - 1, k), us.at[d, k], ur.at[d, k], "fsdp", z - 1)

    def from_above(d, k):
        return send_to(own(k), slot(z + d + 1, k), ws.at[d, k], wr.at[d, k], "fsdp", z + 1)

    def here(k):
        return pltpu.make_async_copy(own(k), slot(z, k), ls.at[k])

    def pass_one(d, k):
        @pl.when((z < 3) & (z >= d))
        def _():
            if d:
                from_below(d - 1, k).wait_recv()
            up(d, k).start()

        @pl.when((z > 0) & (z + d <= 3))
        def _():
            if d:
                from_above(d - 1, k).wait_recv()
            down(d, k).start()

    def pass_on(d, which=None):
        for k in range(chunks) if which is None else which:
            pass_one(d, k)

    def begin():
        for k in range(chunks):
            here(k).start()
        pass_on(0)

    def arrive():
        for d in range(3):
            for k in range(chunks):

                @pl.when(z == 3)
                def _():
                    from_below(d, k).wait_recv()

                @pl.when(z == 0)
                def _():
                    from_above(d, k).wait_recv()

        for k in range(chunks):
            here(k).wait()

    def finish():
        for d in range(3):
            for k in range(chunks):

                @pl.when((z < 3) & (z >= d))
                def _():
                    up(d, k).wait_send()

                @pl.when((z > 0) & (z + d <= 3))
                def _():
                    down(d, k).wait_send()

    return begin, pass_on, arrive, finish


def sum_scratch():
    return [pltpu.VMEM((2, 4, 128, 1024), BF)] + [pltpu.VMEM((2, 128, 1024), BF)] * 6 + [
        DMA((2, 4)), DMA((2, 4)), DMA((2, 6)), DMA((2, 6)),
    ]


def sum_ops(part, m, out, scratch):
    pair, gs, gr, xs, xr, ys, yr = [ref.at[m] for ref in scratch[:7]]
    s1, r1, s2, r2 = scratch[7:]
    me, core, sib, xn, yn, dg = plane_coords()
    order = (dg, xn, yn, me)
    lo, hi = pl.ds(0, 64), pl.ds(64, 64)

    def to_pair(i):
        other = order[i] + 1 - 2 * core
        return send_to(part.at[m, other], pair.at[i], s1.at[m, i], r1.at[m, i], "ctx", sib)

    def ship(index):
        src, dst, peer = (
            (gs.at[lo], gr.at[lo], xn),
            (gs.at[hi], gr.at[hi], yn),
            (xs.at[lo], xr.at[lo], xn),
            (ys.at[hi], yr.at[hi], yn),
            (ys.at[lo], yr.at[lo], yn),
            (xs.at[hi], xr.at[hi], xn),
        )[index]
        return send_to(src, dst, s2.at[m, index], r2.at[m, index], "ctx", peer)

    def f32(value):
        return value.astype(F32)

    def both(i, rr):
        return f32(part[m, order[i], rr]) + f32(pair[i, rr])

    def begin():
        for i in range(4):
            to_pair(i).start()

    def span(offset, count, visit):
        def one(index):
            visit(pl.ds(offset + index.start, 32))

        by_rows(count, 32, one)

    def diag():
        to_pair(0).wait_recv()

        def add(rr):
            gs[rr] = both(0, rr).astype(BF)

        span(0, 128, add)
        ship(0).start()
        ship(1).start()

    def near():
        to_pair(1).wait_recv()

        def add_x(rr):
            xs[rr] = both(1, rr).astype(BF)

        span(0, 64, add_x)
        ship(2).start()
        to_pair(2).wait_recv()

        def add_y(rr):
            ys[rr] = both(2, rr).astype(BF)

        span(64, 64, add_y)
        ship(3).start()

    def join():
        ship(0).wait_recv()

        def add_y(rr):
            ys[rr] = (both(2, rr) + f32(gr[rr])).astype(BF)

        span(0, 64, add_y)
        ship(4).start()
        ship(1).wait_recv()

        def add_x(rr):
            xs[rr] = (both(1, rr) + f32(gr[rr])).astype(BF)

        span(64, 64, add_x)
        ship(5).start()

    def finish():
        to_pair(3).wait_recv()
        for index in (2, 3, 4, 5):
            ship(index).wait_recv()

        def add(rr):
            place = pl.ds(m * 128 + rr.start, 32)
            out[place] = both(3, rr) + f32(xr[rr]) + f32(yr[rr])

        span(0, 128, add)
        for i in range(4):
            to_pair(i).wait_send()
        for index in range(6):
            ship(index).wait_send()

    return begin, diag, near, join, finish


def fold_scratch(rows):
    return [
        pltpu.VMEM((2, 3, rows, 1024), BF),
        pltpu.VMEM((2, 2, rows, 1024), BF),
        DMA((2, 3, 2)),
        DMA((2, 3, 2)),
    ]


def fold_ops(block, rows, out, scratch):
    got, sent, ss, rs = scratch
    z = lax.axis_index("fsdp")
    half = rows // 2
    places = (z, 3 - z)
    nexts = ((z + 1) % 4, (z + 3) % 4)

    def target(side, q):
        return q if side == 0 else 3 - q

    def piece(ref, h):
        return ref.at[pl.ds(half * h, half)]

    def message(src, side, q, h):
        return send_to(
            piece(src, h), piece(got.at[side, q - 1], h), ss.at[side, q - 1, h], rs.at[side, q - 1, h],
            "fsdp", nexts[side],
        )

    def first(side, q, h):
        return message(block(target(side, q)), side, q, h)

    def later(side, q, h):
        return message(sent.at[side, q - 2], side, q, h)

    def begin():
        for side in (0, 1):

            @pl.when(places[side] == 0)
            def _():
                for q in (3, 2, 1):
                    for h in (0, 1):
                        first(side, q, h).start()

    def relay(at, q, h):
        for side in (0, 1):

            @pl.when(places[side] == at)
            def _():
                later(side, q, h).wait_recv()
                mine = block(target(side, q))

                def add(index):
                    rr = pl.ds(half * h + index.start, 32)
                    total = mine[rr].astype(F32) + got[side, q - 1, rr].astype(F32)
                    sent[side, q - 2, rr] = total.astype(BF)

                by_rows(half, 32, add)
                later(side, q, h).start()

    def step(n):
        for at, q, h in (((1, 3, 0),), ((1, 3, 1), (2, 3, 0)), ((1, 2, 0), (2, 3, 1)), ((1, 2, 1),))[n]:
            relay(at, q, h)

    def finish():
        mine = block(z)
        for side in (0, 1):

            @pl.when(places[side] > 0)
            def _():
                for h in (0, 1):
                    q = places[side]
                    send_to(
                        piece(mine, h), piece(got.at[side, q - 1], h), ss.at[side, q - 1, h],
                        rs.at[side, q - 1, h], "fsdp", nexts[side],
                    ).wait_recv()

        def add_all(sides):
            def add(rr):
                total = mine[rr].astype(F32)
                for side in sides:
                    total = total + got[side, places[side] - 1, rr].astype(F32)
                out[rr] = total.astype(BF)

            by_rows(rows, 32, add)

        @pl.when(z == 0)
        def _():
            add_all((1,))

        @pl.when(z == 3)
        def _():
            add_all((0,))

        @pl.when((z > 0) & (z < 3))
        def _():
            add_all((0, 1))

        for side in (0, 1):
            for at, qs in ((0, (3, 2, 1)), (1, (3, 2)), (2, (3,))):

                @pl.when(places[side] == at)
                def _():
                    for q in qs:
                        for h in (0, 1):
                            first(side, q, h).wait_send()

    return begin, step, finish


def vmem_spec():
    return pl.BlockSpec(memory_space=pltpu.VMEM)


def any_spec():
    return pl.BlockSpec(memory_space=pl.ANY)


def natural_slot(device, k):
    micro, part = k // 2, k % 2
    return micro * 16 + (device if part == 0 else 15 - device)


def remote_params(ident):
    return pltpu.CompilerParams(
        collective_id=ident, has_side_effects=True, vmem_limit_bytes=VMEM_CAP
    )


def line_peers():
    z = lax.axis_index("fsdp")
    return [(z + d) % 4 for d in (1, 2, 3)]


def token_docs(row_ref, m):
    row = jnp.broadcast_to(row_ref[m].astype(F32), (8, 1024))
    return row[0:1], jnp.transpose(row)[:, 0:1]


def front_kernel(
    x_ref, base_ref, qvb_ref, inb_ref, backb_ref, doc_ref, wq_ref, wo_ref, wi_ref, picks_ref, dy_ref,
    h_ref, params_ref, wqc_ref, woc_ref, wic_ref, qkv_ref, of_ref, lse_ref,
    y_ref, h2_ref, stat_ref, disp_ref, hslot_ref, dslot_ref,
    out_ref, small_ref, hs, units, part, zs, zr, os, orr, ol, *sems,
):
    me, core, sib, xn, yn, dg = plane_coords()
    z = lax.axis_index("fsdp")
    peers = line_peers()
    meet((sib, xn, yn), peers)
    small_ref[...] = base_ref[...]
    small_ref[2:4] = qvb_ref[...]
    for e in (0, 1):
        for k in range(4):
            small_ref[9 + 4 * e + k : 10 + 4 * e + k] = inb_ref[e : e + 1, 256 * k : 256 * (k + 1)]
    small_ref[17:19] = backb_ref[...]
    params_ref[z] = small_ref[...]
    copies = []
    for i, peer in enumerate(peers):
        copy = send_to(small_ref, params_ref.at[z], zs.at[i], zr.at[i], "fsdp", peer)
        copy.start()
        copies.append(copy)
    owner = me // 2
    columns = pl.ds(pl.multiple_of(me * 128, 128), 128)
    expert, quarter = me // 4, me % 4

    def wq_slot(where, k):
        return wqc_ref.at[k, pl.ds(pl.multiple_of(where * 256, 256), 256)]

    def wi_own(k):
        return wi_ref.at[expert, :, pl.ds(pl.multiple_of(k * 1024 + quarter * 256, 256), 256)]

    def wi_slot(where, k):
        return wic_ref.at[pl.ds(pl.multiple_of(where * 256, 256), 256), pl.ds(256 * k, 256)]

    q_begin, q_pass, q_arrive, q_finish = line_ops(
        lambda k: wq_ref.at[k, :, columns], wq_slot, 3, sems[:5]
    )
    i_begin, i_pass, i_arrive, i_finish = line_ops(wi_own, wi_slot, 4, sems[5:10])
    begin, relay, diag, done, finish = ring_ops(
        lambda k: hs.at[pl.ds(64 * k, 64)],
        lambda device, k: h_ref.at[natural_slot(device, k)],
        sems[10:19],
    )
    sums = [sum_ops(part, m, out_ref, sems[19:]) for m in (0, 1)]
    q_begin()

    wo_own = wo_ref.at[pl.ds(pl.multiple_of(core * 128, 128), 128)]

    def wo_step(src, side):
        return send_to(
            src, woc_ref, os.at[side], orr.at[side], "fsdp", z + 1 if side == 0 else z - 1
        )

    def wo_both(act):
        @pl.when((z >= owner) & (z < 3))
        def _():
            act(0)

        @pl.when((z <= owner) & (z > 0))
        def _():
            act(1)

    def wo_begin():
        @pl.when(z == owner)
        def _():
            pltpu.make_async_copy(wo_own, woc_ref, ol).start()
            wo_both(lambda side: wo_step(wo_own, side).start())

    def wo_arrive():
        @pl.when(z > owner)
        def _():
            wo_step(woc_ref, 0).wait_recv()

        @pl.when(z < owner)
        def _():
            wo_step(woc_ref, 1).wait_recv()

    def wo_pass(d):
        @pl.when((z == owner + d) | (z == owner - d))
        def _():
            wo_arrive()
            wo_both(lambda side: wo_step(woc_ref, side).start())

    def wo_last():
        @pl.when((z == owner + 3) | (z == owner - 3))
        def _():
            wo_arrive()

        @pl.when(z == owner)
        def _():
            pltpu.make_async_copy(wo_own, woc_ref, ol).wait()

    wo_begin()

    def unit(rr):
        values = x_ref[rr].astype(F32)
        centred = values - jnp.mean(values, -1, keepdims=True)
        spread = jnp.mean(centred * centred, -1, keepdims=True)
        units[rr] = centred * lax.rsqrt(spread + norm_eps)

    by_rows(256, 32, unit)
    for copy in copies:
        copy.wait()

    def full_row(r):
        return jnp.concatenate([params_ref[i, r : r + 1, :] for i in range(4)], axis=1).astype(F32)

    gain, shift = full_row(0), full_row(1)

    def norm(rr):
        hs[rr] = (units[rr] * gain + shift).astype(BF)

    by_rows(256, 32, norm)
    begin(0)
    begin(1)
    q_pass(1)
    relay(0)
    relay(1)
    begin(2)
    begin(3)
    wo_pass(1)
    q_pass(2)
    i_begin()
    diag(0)
    diag(1)
    wo_pass(2)
    done(0)
    done(1)
    q_arrive()
    half = pl.ds(pl.multiple_of(core * 128, 128), 128)
    q_bias = params_ref[owner, 2:3, half].astype(F32)
    v_bias = params_ref[owner, 3:4, half].astype(F32)
    masks = head_masks(256)
    vmasks = head_masks(1024)
    zero = jnp.zeros((), BF)

    def micro(m, carry):
        @pl.when(m == 1)
        def _():
            done(2)
            done(3)

        h = h_ref[pl.ds(16 * m, 16)].reshape(1024, 1024)
        place = pl.ds(pl.multiple_of(m * 1024, 1024), 1024)
        q = (mm(h, wqc_ref[0]) + q_bias).astype(BF)
        k = mm(h, wqc_ref[1]).astype(BF)
        v = (mm(h, wqc_ref[2]) + v_bias).astype(BF)
        qkv_ref[0, place] = q
        qkv_ref[1, place] = k
        qkv_ref[2, place] = v
        vh = [jnp.where(vmasks[j], v, zero) for j in (0, 1)]
        doc_row, doc_col = token_docs(doc_ref, m)
        for i in range(4):
            length = 256 * (i + 1)
            rows = slice(256 * i, 256 * (i + 1))
            qi = q[rows] * jnp.asarray(0.125, BF)
            allowed = allowed_mask(i, doc_col[rows], doc_row[:, :length])
            total = None
            stats = []
            for j in (0, 1):
                s = mm(jnp.where(masks[j], qi, zero), k[:length], NT)
                s = jnp.where(allowed, s, mask_fill)
                top = jnp.max(s, -1, keepdims=True)
                e = jnp.exp(s - top)
                den = jnp.sum(e, -1, keepdims=True)
                p = (e * (1.0 / den)).astype(BF)
                term = mm(p, vh[j][:length])
                total = term if total is None else total + term
                stats.append(top + jnp.log(den))
            at = pl.ds(pl.multiple_of(m * 1024 + 256 * i, 256), 256)
            lse_ref[at] = jnp.where(masks[0], stats[0], stats[1])
            of_ref[at] = total

            @pl.when(m == 0)
            def _():
                if i == 0:
                    relay(2)
                    relay(3)
                if i == 1:
                    i_pass(1, (0,))
                    diag(2)
                if i == 2:
                    i_pass(1, (1,))
                    diag(3)
                if i == 3:
                    wo_last()

            @pl.when(m == 1)
            def _():
                if i == 1:
                    sums[0][3]()
                if i == 3:
                    i_pass(2, (0,))

        for i in range(4):
            at = pl.ds(pl.multiple_of(m * 1024 + 256 * i, 256), 256)
            a = mm(of_ref[at].astype(BF), woc_ref[...]).astype(BF)
            for b in range(4):
                block = 4 * i + b
                dest, side = (block, 0) if block < 8 else (15 - block, 1)
                part[m, dest, 64 * side : 64 * (side + 1)] = a[64 * b : 64 * (b + 1)]

        for n in (0, 1):

            @pl.when(m == n)
            def _():
                for step in sums[n][:3]:
                    step()
                if n == 0:
                    i_pass(1, (2, 3))

        return carry

    lax.fori_loop(0, 2, micro, 0)
    outb, gain2, shift2 = full_row(4), full_row(5), full_row(6)
    router = jnp.concatenate([full_row(7), full_row(8)], axis=0).astype(BF)

    def route(m):
        picked = jnp.broadcast_to(picks_ref[m : m + 1].astype(F32), (8, 128))
        sub = lax.broadcasted_iota(jnp.int32, (8, 128), 0)
        member = jnp.where(sub == 0, 1.0 - picked, picked)
        earlier = lax.broadcasted_iota(jnp.int32, (128, 128), 0)
        later = lax.broadcasted_iota(jnp.int32, (128, 128), 1)
        rank = mm(member.astype(BF), (earlier < later).astype(BF))
        slot = lax.broadcasted_iota(jnp.int32, (CAP, 128), 0).astype(F32)
        for e in (0, 1):
            hit = (rank[e : e + 1] == slot) & (member[e : e + 1] > 0.5)
            disp_ref[m, e] = hit.astype(BF)
        return jnp.transpose(picked)[:, 0:1]

    def second_norm(m):
        pick = route(m)
        base = 128 * m

        def visit(index):
            rr = pl.ds(base + index.start, 32)
            values = x_ref[rr].astype(F32) + (out_ref[rr] + outb)
            y_ref[rr] = values
            centred = values - jnp.mean(values, -1, keepdims=True)
            spread = jnp.mean(centred * centred, -1, keepdims=True)
            h2_ref[rr] = (centred * lax.rsqrt(spread + norm_eps) * gain2 + shift2).astype(BF)

        by_rows(128, 32, visit)
        span = pl.ds(base, 128)
        h2 = h2_ref[span]
        logits = mm(h2, router, NT)
        top = jnp.max(logits, -1, keepdims=True)
        e = jnp.exp(logits - top)
        probs = e / jnp.sum(e, -1, keepdims=True)
        gate = jnp.where(pick > 0.5, probs[:, 1:2], probs[:, 0:1])
        lane = lax.broadcasted_iota(jnp.int32, (128, 128), 1)
        packed = jnp.where(lane == 0, probs[:, 0:1], probs[:, 1:2])
        packed = jnp.where(lane == 2, gate, packed)
        stat_ref[span] = jnp.where(lane == 3, pick, packed)
        du = (gate * dy_ref[span].astype(F32)).astype(BF)
        for which in (0, 1):
            hslot_ref[which, m] = mm(disp_ref[m, which], h2).astype(BF)
            dslot_ref[which, m] = mm(disp_ref[m, which], du).astype(BF)

    i_pass(2, (1,))
    sums[1][3]()
    i_pass(2, (2, 3))
    sums[0][4]()
    second_norm(0)
    sums[1][4]()
    second_norm(1)
    i_arrive()
    wo_both(lambda side: wo_step(woc_ref, side).wait_send())
    q_finish()
    i_finish()
    for k in range(4):
        finish(k)


def front_call(x, small, qv_bias, in_bias, back_bias, docs, w_qkv, w_out, w_in, picks, dy):
    return pl.pallas_call(
        front_kernel,
        out_shape=(
            jax.ShapeDtypeStruct((32, 64, 1024), BF),
            jax.ShapeDtypeStruct((4, SMALL_ROWS, 256), BF),
            jax.ShapeDtypeStruct((3, 1024, 128), BF),
            jax.ShapeDtypeStruct((128, 1024), BF),
            jax.ShapeDtypeStruct((1024, 1024), BF),
            jax.ShapeDtypeStruct((3, 2048, 128), BF),
            jax.ShapeDtypeStruct((2048, 128), F32),
            jax.ShapeDtypeStruct((2048, 128), F32),
            jax.ShapeDtypeStruct((256, 1024), F32),
            jax.ShapeDtypeStruct((256, 1024), BF),
            jax.ShapeDtypeStruct((256, 128), F32),
            jax.ShapeDtypeStruct((2, 2, CAP, 128), BF),
            jax.ShapeDtypeStruct((2, 2, CAP, 1024), BF),
            jax.ShapeDtypeStruct((2, 2, CAP, 1024), BF),
        ),
        in_specs=[vmem_spec()] * 6 + [any_spec()] * 3 + [vmem_spec()] * 2,
        out_specs=[vmem_spec()] * 4 + [any_spec()] + [vmem_spec()] * 9,
        scratch_shapes=[
            pltpu.VMEM((256, 1024), F32),
            pltpu.VMEM((SMALL_ROWS, 256), BF),
            pltpu.VMEM((256, 1024), BF),
            pltpu.VMEM((256, 1024), F32),
            pltpu.VMEM((2, 8, 128, 1024), BF),
            DMA((3,)),
            DMA((3,)),
            DMA((2,)),
            DMA((2,)),
            DMA(()),
        ]
        + line_sems(3)
        + line_sems(4)
        + gather_sems(4)
        + sum_scratch(),
        name="front",
        compiler_params=remote_params(0),
    )(x, small, qv_bias, in_bias, back_bias, docs, w_qkv, w_out, w_in, picks, dy)


def moe_call(h_slots, d_slots, win, w_back, params, y1, h2, stats, dispatch, dy):
    def kernel(
        h_ref, d_ref, wi_ref, wall_ref, params_ref, y_ref, h2_ref, stat_ref, disp_ref, dy_ref,
        gi_ref, gbs_ref, mixed_ref, dy1_ref, da_ref, v_ref,
        o_ref, gib_ref, acc, wb_ref, gba, u_ref, g_ref, rows, gz, slope, dz, part, pair, sent, got,
        ns, nr, fs, fr, ss, sr, ls, s1, r1, s2, r2, *wsems,
    ):
        me, core, sib, xn, yn, dg = plane_coords()
        expert, quarter = me // 4, me % 4
        meet((sib, xn, yn, dg), line_peers())
        w_begin, w_pass, w_arrive, w_finish = line_ops(
            lambda k: wall_ref.at[expert, pl.ds(pl.multiple_of(quarter * 256 + 64 * k, 64), 64)],
            lambda where, k: wb_ref.at[pl.ds(pl.multiple_of(where * 256 + 64 * k, 64), 64)],
            4,
            wsems[:5],
        )
        z_begin, z_step, z_finish = fold_ops(lambda where: gba.at[where], 256, gbs_ref, wsems[5:])
        w_begin()
        peers = (dg, xn, yn)
        wanted = (1 - expert, expert, 1 - expert)
        ins = (h_ref, d_ref)

        def away(t, m, i):
            return send_to(
                ins[t].at[wanted[i], m], rows.at[t, m, me], ns.at[t, m, i], nr.at[t, m, i], "ctx", peers[i]
            )

        def beside(t, m):
            return send_to(
                ins[t].at[expert, m], rows.at[t, m, me], ss.at[t, m], sr.at[t, m], "ctx", sib
            )

        def here(t, m):
            return pltpu.make_async_copy(ins[t].at[expert, m], rows.at[t, m, me], ls.at[t, m])

        def onward(t, m, i):
            block = rows.at[t, m, peers[i]]
            return send_to(block, block, fs.at[t, m, i], fr.at[t, m, i], "ctx", sib)

        for t in (0, 1):
            for m in (0, 1):
                for i in range(3):
                    away(t, m, i).start()
        for t in (0, 1):
            for m in (0, 1):
                beside(t, m).start()
                here(t, m).start()

        def arrive(t, m):
            for i in range(3):
                away(t, m, i).wait_recv()
                onward(t, m, i).start()
            here(t, m).wait()
            beside(t, m).wait_recv()
            for i in range(3):
                onward(t, m, i).wait_recv()

        order = (dg, xn, yn, me)

        def to_pair(t, m, i):
            other = order[i] + 1 - 2 * core
            return send_to(
                part.at[t, m, other], pair.at[t, m, i], s1.at[t, m, i], r1.at[t, m, i], "ctx", sib
            )

        def to_home(t, m, i):
            return send_to(
                sent.at[t, m, i], got.at[t, m, i], s2.at[t, m, i], r2.at[t, m, i], "ctx", order[i]
            )

        def join(t, m):
            for i in range(3):
                to_pair(t, m, i).wait_recv()
                mine = order[i]

                def add(rr):
                    sent[t, m, i, rr] = (
                        part[t, m, mine, rr].astype(F32) + pair[t, m, i, rr].astype(F32)
                    ).astype(BF)

                by_rows(CAP, 16, add)
                to_home(t, m, i).start()

        mine_row = lax.broadcasted_iota(jnp.int32, (8, 256), 0) == me
        in_bias = jnp.concatenate(
            [
                jnp.sum(
                    jnp.where(mine_row, params_ref[i, 9:17, :].astype(F32), 0.0), 0, keepdims=True
                )
                for i in range(4)
            ],
            axis=1,
        )

        def inner_rows(m):
            def visit(half, carry):
                xs = rows[0, m, pl.ds(4 * half, 4)].reshape(4 * CAP, 1024)
                zed = mm(xs, wi_ref[...]) + in_bias
                square = zed * zed
                t = jnp.tanh(zed * (GELU_A + GELU_A * GELU_B * square))
                half_up = 0.5 + 0.5 * t
                place = pl.ds(pl.multiple_of(m * 8 * CAP + half * 4 * CAP, 4 * CAP), 4 * CAP)
                gz[place] = (zed * half_up).astype(BF)
                slope[place] = half_up + 0.5 * zed * (1.0 - t * t) * (
                    GELU_A + 3.0 * GELU_A * GELU_B * square
                )
                return carry

            lax.fori_loop(0, 2, visit, 0)

        def inner(m, carry):
            @pl.when(m == 0)
            def _():
                w_pass(1, (0, 1))

            arrive(0, m)

            @pl.when(m == 0)
            def _():
                w_pass(1, (2,))

            inner_rows(m)

            @pl.when(m == 0)
            def _():
                w_pass(1, (3,))

            return carry

        lax.fori_loop(0, 2, inner, 0)
        w_pass(2, (0, 1))
        arrive(1, 0)
        w_pass(2, (2, 3))
        arrive(1, 1)

        def back_grads(j, carry):
            column = pl.ds(pl.multiple_of(256 * j, 256), 256)
            du = rows[1].reshape(16 * CAP, 1024)
            gba[j] = mm(gz[:, column], du, TN).astype(BF)
            return carry

        lax.fori_loop(0, 4, back_grads, 0)
        z_begin()
        w_arrive()

        def forward(m, carry):
            def visit(half, inner_carry):
                place = pl.ds(pl.multiple_of(m * 8 * CAP + half * 4 * CAP, 4 * CAP), 4 * CAP)
                u = mm(gz[place], wb_ref[...]).astype(BF)
                part[0, m, pl.ds(4 * half, 4)] = u.reshape(4, CAP, 1024)
                return inner_carry

            lax.fori_loop(0, 2, visit, 0)
            for i in range(4):
                to_pair(0, m, i).start()
            join(0, m)
            return carry

        lax.fori_loop(0, 2, forward, 0)
        z_step(0)
        gib_ref[...] = jnp.zeros_like(gib_ref)

        def backward(m, carry):
            def rows_backward(half, inner_carry):
                du = rows[1, m, pl.ds(4 * half, 4)].reshape(4 * CAP, 1024)
                place = pl.ds(pl.multiple_of(m * 8 * CAP + half * 4 * CAP, 4 * CAP), 4 * CAP)
                low = (mm(du, wb_ref[...], NT) * slope[place]).astype(BF)
                dz[place] = low
                gib_ref[...] += jnp.sum(low.astype(F32), 0, keepdims=True)
                dh = mm(low, wi_ref[...], NT).astype(BF)
                part[1, m, pl.ds(4 * half, 4)] = dh.reshape(4, CAP, 1024)
                return inner_carry

            lax.fori_loop(0, 2, rows_backward, 0)
            for i in range(4):
                to_pair(1, m, i).start()
            join(1, m)

            @pl.when(m == 0)
            def _():
                z_step(1)

            return carry

        lax.fori_loop(0, 2, backward, 0)
        z_step(2)

        def weight_grads(j, carry):
            column = pl.ds(pl.multiple_of(256 * j, 256), 256)
            xs = rows[0, :, :, :, column].reshape(16 * CAP, 256)
            gi_ref[column] = mm(xs, dz[...], TN).astype(BF)
            return carry

        lax.fori_loop(0, 4, weight_grads, 0)
        z_step(3)

        def full_row(r):
            return jnp.concatenate(
                [params_ref[i, r : r + 1, :] for i in range(4)], axis=1
            ).astype(F32)

        gain2, router0, router1 = full_row(5), full_row(7), full_row(8)
        bias0, bias1 = full_row(17), full_row(18)
        acc[...] = jnp.zeros_like(acc)

        def home(t, m):
            to_pair(t, m, 3).wait_recv()
            for i in range(3):
                to_home(t, m, i).wait_recv()

            def finish(rr):
                o_ref[expert, t, m, rr] = (
                    part[t, m, me, rr].astype(F32)
                    + pair[t, m, 3, rr].astype(F32)
                    + got[t, m, 1, rr].astype(F32)
                )
                o_ref[1 - expert, t, m, rr] = got[t, m, 0, rr].astype(F32) + got[
                    t, m, 2, rr
                ].astype(F32)

            by_rows(CAP, 16, finish)

        def to_tokens(t, m):
            total = None
            for e in (0, 1):
                value = o_ref[e, t, m]
                for _ in range(3):
                    low = value.astype(BF)
                    term = mm(disp_ref[m, e], low, TN)
                    total = term if total is None else total + term
                    value = value - low.astype(F32)
            return total

        def token_rows(m):
            span = pl.ds(128 * m, 128)
            home(0, m)
            u_ref[...] = to_tokens(0, m)
            home(1, m)
            g_ref[...] = to_tokens(1, m)

            def visit(index):
                rr = pl.ds(128 * m + index.start, 32)
                local = pl.ds(index.start, 32)
                stat = stat_ref[rr]
                p0, p1, gate, pick = (stat[:, i : i + 1] for i in range(4))
                dy = dy_ref[rr].astype(F32)
                values = y_ref[rr]
                u = u_ref[local] + jnp.where(pick > 0.5, bias1, bias0)
                mixed_ref[rr] = (values + gate * u).astype(BF)
                dgate = jnp.sum(dy * u, -1, keepdims=True)
                d0, d1 = dgate * (1.0 - pick), dgate * pick
                mean_grad = p0 * d0 + p1 * d1
                l0, l1 = p0 * (d0 - mean_grad), p1 * (d1 - mean_grad)
                grad = g_ref[local] + (l0 * router0 + l1 * router1)
                h2f = h2_ref[rr].astype(F32)
                centred = values - jnp.mean(values, -1, keepdims=True)
                inv = lax.rsqrt(jnp.mean(centred * centred, -1, keepdims=True) + norm_eps)
                unit = centred * inv
                scaled = grad * gain2
                back = inv * (
                    scaled
                    - jnp.mean(scaled, -1, keepdims=True)
                    - unit * jnp.mean(scaled * unit, -1, keepdims=True)
                )
                dy1 = dy + back
                low = dy1.astype(BF)
                dy1_ref[rr] = dy1
                da_ref[rr] = low
                sums = (
                    low.astype(F32), grad * unit, grad, h2f * l0, h2f * l1,
                )
                for row, term in enumerate(sums):
                    acc[row : row + 1] += jnp.sum(term, 0, keepdims=True)

            by_rows(128, 32, visit)

        token_rows(0)
        token_rows(1)
        for e in (0, 1):
            for m in (0, 1):
                acc[5 + e : 6 + e] += jnp.sum(d_ref[e, m].astype(F32), 0, keepdims=True)
        v_ref[...] = jnp.zeros_like(v_ref)
        for i in range(4):
            v_ref[i, 4:11, :] = acc[0:7, 256 * i : 256 * (i + 1)]
            v_ref[i, pl.ds(11 + me, 1), :] = gib_ref[:, 256 * i : 256 * (i + 1)]
        for t in (0, 1):
            for m in (0, 1):
                for i in range(3):
                    away(t, m, i).wait_send()
                    onward(t, m, i).wait_send()
                    to_home(t, m, i).wait_send()
                for i in range(4):
                    to_pair(t, m, i).wait_send()
                beside(t, m).wait_send()
        w_finish()
        z_finish()

    return pl.pallas_call(
        kernel,
        out_shape=(
            jax.ShapeDtypeStruct((1024, 1024), BF),
            jax.ShapeDtypeStruct((256, 1024), BF),
            jax.ShapeDtypeStruct((256, 1024), BF),
            jax.ShapeDtypeStruct((256, 1024), F32),
            jax.ShapeDtypeStruct((256, 1024), BF),
            jax.ShapeDtypeStruct((4, 24, 256), F32),
        ),
        in_specs=[vmem_spec()] * 3 + [any_spec()] + [vmem_spec()] * 6,
        out_specs=[vmem_spec()] * 6,
        scratch_shapes=[
            pltpu.VMEM((2, 2, 2, CAP, 1024), F32),
            pltpu.VMEM((1, 1024), F32),
            pltpu.VMEM((8, 1024), F32),
            pltpu.VMEM((1024, 1024), BF),
            pltpu.VMEM((4, 256, 1024), BF),
            pltpu.VMEM((128, 1024), F32),
            pltpu.VMEM((128, 1024), F32),
            pltpu.VMEM((2, 2, 8, CAP, 1024), BF),
            pltpu.VMEM((16 * CAP, 1024), BF),
            pltpu.VMEM((16 * CAP, 1024), F32),
            pltpu.VMEM((16 * CAP, 1024), BF),
            pltpu.VMEM((2, 2, 8, CAP, 1024), BF),
            pltpu.VMEM((2, 2, 4, CAP, 1024), BF),
            pltpu.VMEM((2, 2, 3, CAP, 1024), BF),
            pltpu.VMEM((2, 2, 3, CAP, 1024), BF),
        ]
        + [DMA((2, 2, 3))] * 4
        + [DMA((2, 2))] * 3
        + [DMA((2, 2, 4))] * 2
        + [DMA((2, 2, 3))] * 2
        + line_sems(4)
        + fold_scratch(256),
        name="moe",
        compiler_params=remote_params(2),
    )(h_slots, d_slots, win, w_back, params, y1, h2, stats, dispatch, dy)


def final_call(gi, gb, gq, gwo, vectors, gqv, x, dh1, dy1, params):
    def kernel(
        gi_ref, gb_ref, gq_ref, go_ref, base_ref, gqv_ref, x_ref, dh_ref, dy_ref, params_ref,
        oi_ref, ob_ref, oq_ref, oo_ref, ov_ref, ot_ref,
        v_ref, acc, qgot, qsum, vgot, vsum, vall,
        qs, qr, vs, vr, ps, pr, ws, wr, hs, hr, fs, fr, ol, *sems,
    ):
        me, core, sib, xn, yn, dg = plane_coords()
        z = lax.axis_index("fsdp")
        others = [(me + d) % 8 for d in range(1, 8)]
        meet(others, line_peers())
        owner = me // 2

        def vector_copy(d):
            peer = (z + d) % 4
            return send_to(v_ref.at[peer], vgot.at[d - 1], vs.at[d - 1], vr.at[d - 1], "fsdp", peer)

        def q_copy(d):
            peer = (z + d) % 4
            block = gq_ref.at[:, pl.ds(pl.multiple_of(peer * 256, 256), 256)]
            return send_to(block, qgot.at[d - 1], qs.at[d - 1], qr.at[d - 1], "fsdp", peer)

        rows_mine = oo_ref.at[pl.ds(pl.multiple_of(core * 128, 128), 128)]
        rows_sib = oo_ref.at[pl.ds(pl.multiple_of((1 - core) * 128, 128), 128)]

        def half(ref, part):
            return ref.at[pl.ds(64 * part, 64)]

        def o_near(i):
            return send_to(go_ref, rows_mine, ws.at[i], wr, "ctx", (xn, yn)[i])

        def o_half(part):
            block = half(rows_mine, part)
            return send_to(block, block, hs, hr.at[part], "ctx", (yn, xn)[part])

        def o_pair(src):
            return send_to(src, rows_mine, fs, fr, "ctx", sib)

        row, col = me // 4, (me // 2) % 2
        own_row, own_col = z // 2, z % 2
        beside_x = (row == own_row) & (col != own_col)
        beside_y = (row != own_row) & (col == own_col)
        across = (row != own_row) & (col != own_col)

        def o_root():
            @pl.when(z == owner)
            def _():
                for i in (0, 1):
                    o_near(i).start()
                o_pair(go_ref).start()
                pltpu.make_async_copy(go_ref, rows_mine, ol).start()

        def o_relay():
            @pl.when(beside_x)
            def _():
                o_near(0).wait_recv()
                o_half(0).start()
                o_pair(rows_mine).start()

            @pl.when(beside_y)
            def _():
                o_near(1).wait_recv()
                o_half(1).start()
                o_pair(rows_mine).start()

        def o_end():
            @pl.when(across)
            def _():
                o_half(0).wait_recv()
                o_half(1).wait_recv()
                o_pair(rows_mine).start()
                o_pair(rows_mine).wait_send()

            @pl.when(z == owner)
            def _():
                for i in (0, 1):
                    o_near(i).wait_send()
                o_pair(go_ref).wait_send()
                pltpu.make_async_copy(go_ref, rows_mine, ol).wait()

            @pl.when(beside_x)
            def _():
                o_half(0).wait_send()
                o_pair(rows_mine).wait_send()

            @pl.when(beside_y)
            def _():
                o_half(1).wait_send()
                o_pair(rows_mine).wait_send()

            send_to(go_ref, rows_sib, fs, fr, "ctx", sib).wait_recv()

        def own(k):
            if k < 4:
                return gi_ref.at[:, pl.ds(256 * k, 256)]
            return gb_ref.at[pl.ds(64 * (k - 4), 64)]

        def slot(device, k):
            which, part = device // 4, device % 4
            if k < 4:
                column = pl.multiple_of(k * 1024 + part * 256, 256)
                return oi_ref.at[which, :, pl.ds(column, 256)]
            row_at = pl.multiple_of(part * 256 + 64 * (k - 4), 64)
            return ob_ref.at[which, pl.ds(row_at, 64)]

        def qslot(device, k):
            return oq_ref.at[k, :, pl.ds(pl.multiple_of(device * 128, 128), 128)]

        begin, relay, diag, done, finish = ring_ops(own, slot, sems[:9])
        q_begin, q_relay, q_diag, q_done, q_finish = ring_ops(lambda k: qsum.at[k], qslot, sems[9:18])
        for d in (1, 3, 2):
            q_copy(d).start()
        for k in range(8):
            begin(k)
        o_root()
        gain = jnp.concatenate([params_ref[i, 0:1, :] for i in range(4)], axis=1).astype(F32)
        acc[...] = jnp.zeros_like(acc)

        def norm_rows(rr):
            values = x_ref[rr].astype(F32)
            grad = dh_ref[rr]
            centred = values - jnp.mean(values, -1, keepdims=True)
            inv = lax.rsqrt(jnp.mean(centred * centred, -1, keepdims=True) + norm_eps)
            unit = centred * inv
            scaled = grad * gain
            back = inv * (
                scaled
                - jnp.mean(scaled, -1, keepdims=True)
                - unit * jnp.mean(scaled * unit, -1, keepdims=True)
            )
            ot_ref[rr] = dy_ref[rr] + back
            acc[0:1] += jnp.sum(grad * unit, 0, keepdims=True)
            acc[1:2] += jnp.sum(grad, 0, keepdims=True)

        for k in range(4):

            def part(index):
                norm_rows(pl.ds(64 * k + index.start, 32))

            by_rows(64, 32, part)
            relay(k)
        v_ref[...] = base_ref[...]
        for i in range(4):
            v_ref[i, 0:2, :] = acc[0:2, 256 * i : 256 * (i + 1)]
        v_ref[owner, 2:4, pl.ds(pl.multiple_of(core * 128, 128), 128)] = gqv_ref[...]
        for d in (1, 2, 3):
            vector_copy(d).start()

        def plane_vector(i):
            return send_to(vsum, vall.at[i], ps.at[i], pr.at[i], "ctx", others[i])

        relay(4)
        for d in (1, 3, 2):
            q_copy(d).wait_recv()
        for j in range(3):

            def add(rr):
                place = pl.ds(pl.multiple_of(z * 256 + rr.start, 32), 32)
                total = gq_ref[j, place].astype(F32)
                for i in range(3):
                    total = total + qgot[i, j, rr].astype(F32)
                qsum[j, rr] = total.astype(BF)

            by_rows(256, 32, add)
        for k in range(3):
            q_begin(k)
        for d in (1, 2, 3):
            vector_copy(d).wait_recv()
        vsum[...] = v_ref[z] + vgot[0] + vgot[1] + vgot[2]
        for i in range(7):
            plane_vector(i).start()
        relay(5)
        diag(0)
        relay(6)
        diag(1)
        relay(7)
        diag(2)
        o_relay()
        diag(3)
        for k in range(3):
            q_relay(k)
        for k in range(4, 8):
            diag(k)
        for k in range(3):
            q_diag(k)
        o_end()
        for k in range(8):
            done(k)
        for k in range(3):
            q_done(k)
        total = vsum[...]
        for i in range(7):
            plane_vector(i).wait_recv()
            total = total + vall[i]
        ov_ref[...] = total
        for k in range(8):
            finish(k)
        for k in range(3):
            q_finish(k)
        for d in (1, 2, 3):
            vector_copy(d).wait_send()
            q_copy(d).wait_send()
        for i in range(7):
            plane_vector(i).wait_send()

    count = vectors.shape[1]
    return pl.pallas_call(
        kernel,
        out_shape=(
            jax.ShapeDtypeStruct((2, 256, 4096), BF),
            jax.ShapeDtypeStruct((2, 1024, 1024), BF),
            jax.ShapeDtypeStruct((3, 256, 1024), BF),
            jax.ShapeDtypeStruct((256, 1024), BF),
            jax.ShapeDtypeStruct((count, 256), F32),
            jax.ShapeDtypeStruct((256, 1024), F32),
        ),
        in_specs=[vmem_spec()] * 10,
        out_specs=[any_spec()] * 4 + [vmem_spec()] * 2,
        scratch_shapes=[
            pltpu.VMEM((4, count, 256), F32),
            pltpu.VMEM((8, 1024), F32),
            pltpu.VMEM((3, 3, 256, 128), BF),
            pltpu.VMEM((3, 256, 128), BF),
            pltpu.VMEM((3, count, 256), F32),
            pltpu.VMEM((count, 256), F32),
            pltpu.VMEM((7, count, 256), F32),
            DMA((3,)), DMA((3,)), DMA((3,)), DMA((3,)), DMA((7,)), DMA((7,)),
            DMA((2,)), DMA(()), DMA(()), DMA((2,)), DMA(()), DMA(()), DMA(()),
        ]
        + gather_sems(8)
        + gather_sems(3),
        name="final",
        compiler_params=remote_params(6),
    )(gi, gb, gq, gwo, vectors, gqv, x, dh1, dy1, params)


def head_masks(rows):
    lane = lax.broadcasted_iota(jnp.int32, (rows, 128), 1)
    return lane < 64, lane >= 64


def allowed_mask(i, doc_col, doc_row):
    length = 256 * (i + 1)
    qpos = lax.broadcasted_iota(jnp.int32, (256, length), 0) + 256 * i
    kpos = lax.broadcasted_iota(jnp.int32, (256, length), 1)
    return (kpos <= qpos) & (doc_col == doc_row)


def back_kernel(
    da_ref, h_ref, qkv_ref, of_ref, lse_ref, w_ref, wo_ref, doc_ref, gi_ref,
    out_ref, gq_ref, gwo_ref, gqv_ref, gis_ref,
    g_all, dqkv, part, dka, dva, probs, gwo, gwo_low, gwo_got, os, orr, *sems,
):
    me, core, sib, xn, yn, dg = plane_coords()
    meet((sib, xn, yn), line_peers())
    begin, relay, diag, done, finish = ring_ops(
        lambda k: da_ref.at[pl.ds(64 * k, 64)],
        lambda device, k: g_all.at[natural_slot(device, k)],
        sems[:9],
    )
    z_begin, z_step, z_finish = fold_ops(
        lambda where: gi_ref.at[pl.ds(pl.multiple_of(where * 256, 256), 256)],
        256,
        gis_ref,
        sems[9:13],
    )
    sums = [sum_ops(part, m, out_ref, sems[13:]) for m in (0, 1)]
    z = lax.axis_index("fsdp")
    owner = me // 2
    away = (owner - z + 4) % 4

    def to_owner():
        return send_to(gwo_low, gwo_got.at[away - 1], os, orr.at[away - 1], "fsdp", owner)

    masks = head_masks(256)
    zero = jnp.zeros((), BF)
    spans = [slice(128 * i * (i + 1), 128 * (i + 1) * (i + 2)) for i in range(4)]
    begin(0)
    begin(1)
    z_begin()

    def weigh(m, carry):
        place = pl.ds(pl.multiple_of(m * 1024, 1024), 1024)
        q, k = qkv_ref[0, place], qkv_ref[1, place]
        doc_row, doc_col = token_docs(doc_ref, m)
        for i in range(4):
            length = 256 * (i + 1)
            rows = slice(256 * i, 256 * (i + 1))
            qi = q[rows] * jnp.asarray(0.125, BF)
            allowed = allowed_mask(i, doc_col[rows], doc_row[:, :length])
            lse = lse_ref[pl.ds(pl.multiple_of(m * 1024 + 256 * i, 256), 256)]
            for j in (0, 1):
                s = mm(jnp.where(masks[j], qi, zero), k[:length], NT)
                probs[m, j, :, spans[i]] = jnp.exp(
                    jnp.where(allowed, s, mask_fill) - lse[:, 64 * j : 64 * j + 1]
                )

        @pl.when(m == 0)
        def _():
            relay(0)
            relay(1)
            begin(2)
            begin(3)

        return carry

    lax.fori_loop(0, 2, weigh, 0)
    z_step(0)
    diag(0)
    diag(1)
    done(0)
    done(1)
    kmasks = head_masks(1024)

    def micro(m, carry):
        @pl.when(m == 1)
        def _():
            done(2)
            done(3)

        place = pl.ds(pl.multiple_of(m * 1024, 1024), 1024)
        g = g_all[pl.ds(16 * m, 16)].reshape(1024, 1024)
        q, k, v = qkv_ref[0, place], qkv_ref[1, place], qkv_ref[2, place]
        do = mm(g, wo_ref[...], NT).astype(BF)
        term = mm(of_ref[place].astype(BF), g, TN)

        @pl.when(m == 0)
        def _():
            gwo[...] = term

        @pl.when(m == 1)
        def _():
            gwo_low[...] = (gwo[...] + term).astype(BF)

            @pl.when(z != owner)
            def _():
                to_owner().start()

        dka[...] = jnp.zeros_like(dka)
        dva[...] = jnp.zeros_like(dva)
        kh = [jnp.where(kmasks[j], k, zero) for j in (0, 1)]
        for i in range(4):
            length = 256 * (i + 1)
            rows = slice(256 * i, 256 * (i + 1))
            at = pl.ds(pl.multiple_of(m * 1024 + 256 * i, 256), 256)
            qi = q[rows] * jnp.asarray(0.125, BF)
            doi = do[rows]
            prod = doi.astype(F32) * of_ref[at]
            dq = None
            for j in (0, 1):
                qh = jnp.where(masks[j], qi, zero)
                doh = jnp.where(masks[j], doi, zero)
                delta = jnp.sum(jnp.where(masks[j], prod, 0.0), -1, keepdims=True)
                p = probs[m, j, :, spans[i]]
                dp = mm(doh, v[:length], NT)
                ds = (p * (dp - delta)).astype(BF)
                term = mm(ds, kh[j][:length])
                dq = term if dq is None else dq + term
                dka[:, :length] += mm(qh, ds, TN)
                dva[:, :length] += mm(doh, p.astype(BF), TN)
            dqkv[0, at] = (dq * 0.125).astype(BF)

            @pl.when(m == 0)
            def _():
                if i == 0:
                    relay(2)
                if i == 1:
                    relay(3)
                    z_step(1)
                if i == 3:
                    diag(2)
                    diag(3)
                    z_step(2)

            @pl.when(m == 1)
            def _():
                if i == 0:
                    z_step(3)
                if i == 1:
                    sums[0][3]()

        dqkv[1, place] = jnp.transpose(dka[...]).astype(BF)
        dqkv[2, place] = jnp.transpose(dva[...]).astype(BF)
        for i in range(4):
            at = pl.ds(pl.multiple_of(m * 1024 + 256 * i, 256), 256)
            a = mm(dqkv[0, at], w_ref[0], NT) + mm(dqkv[1, at], w_ref[1], NT)
            a = (a + mm(dqkv[2, at], w_ref[2], NT)).astype(BF)
            for b in range(4):
                block = 4 * i + b
                dest, side = (block, 0) if block < 8 else (15 - block, 1)
                part[m, dest, 64 * side : 64 * (side + 1)] = a[64 * b : 64 * (b + 1)]
        for n in (0, 1):

            @pl.when(m == n)
            def _():
                for step in sums[n][:3]:
                    step()

        return carry

    lax.fori_loop(0, 2, micro, 0)
    sums[1][3]()
    for j in range(3):
        gq_ref[j] = jnp.transpose(mm(dqkv[j], h_ref[...].reshape(2048, 1024), TN)).astype(BF)
    gqv_ref[0:1] = jnp.sum(dqkv[0].astype(F32), 0, keepdims=True)
    gqv_ref[1:2] = jnp.sum(dqkv[2].astype(F32), 0, keepdims=True)
    sums[0][4]()
    sums[1][4]()
    z_finish()

    @pl.when(z != owner)
    def _():
        to_owner().wait_send()

    @pl.when(z == owner)
    def _():
        for i in range(3):
            send_to(gwo_low, gwo_got.at[i], os, orr.at[i], "fsdp", (z + 1) % 4).wait_recv()

        def add(rr):
            total = gwo_low[rr].astype(F32)
            for i in range(3):
                total = total + gwo_got[i, rr].astype(F32)
            gwo_ref[rr] = total.astype(BF)

        by_rows(128, 32, add)

    @pl.when(z != owner)
    def _():
        gwo_ref[...] = jnp.zeros_like(gwo_ref)

    for k in range(4):
        finish(k)


def back_call(da, h, qkv, of, lse, wqkv, wout, docs, gi):
    return pl.pallas_call(
        back_kernel,
        out_shape=(
            jax.ShapeDtypeStruct((256, 1024), F32),
            jax.ShapeDtypeStruct((3, 1024, 128), BF),
            jax.ShapeDtypeStruct((128, 1024), BF),
            jax.ShapeDtypeStruct((2, 128), F32),
            jax.ShapeDtypeStruct((256, 1024), BF),
        ),
        in_specs=[vmem_spec()] * 9,
        out_specs=[vmem_spec()] * 5,
        scratch_shapes=[
            pltpu.VMEM((32, 64, 1024), BF),
            pltpu.VMEM((3, 2048, 128), BF),
            pltpu.VMEM((2, 8, 128, 1024), BF),
            pltpu.VMEM((128, 1024), F32),
            pltpu.VMEM((128, 1024), F32),
            pltpu.VMEM((2, 2, 256, 2560), F32),
            pltpu.VMEM((128, 1024), F32),
            pltpu.VMEM((128, 1024), BF),
            pltpu.VMEM((3, 128, 1024), BF),
            DMA(()),
            DMA((3,)),
        ]
        + gather_sems(4)
        + fold_scratch(256)
        + sum_scratch(),
        name="back",
        compiler_params=remote_params(4),
    )(da, h, qkv, of, lse, wqkv, wout, docs, gi)


GELU_A = math.sqrt(2.0 / math.pi)
GELU_B = 0.044715


def widen_call(arrays, kinds, sums):
    count = len(arrays)
    steps = 8
    flat = [array.reshape(-1, array.shape[-1]) for array in arrays]
    sizes = [f.shape[0] // steps for f in flat]
    small = [(256,), (256,), (2, 256), (256,), (256,), (256,), (2, 256), (2, 1024), (2, 256)]

    def kernel(*refs):
        step = pl.program_id(0)
        v_ref, wide, outs = refs[count], refs[count + 1 : 2 * count + 1], refs[2 * count + 1 :]
        for src, dst, size in zip(refs[:count], wide, sizes):
            dst[...] = src[pl.ds(pl.multiple_of(step * size, 16), size)].astype(dst.dtype)

        @pl.when(step == 0)
        def _():
            for index, row in ((0, 0), (1, 1), (3, 4), (4, 5), (5, 6)):
                outs[index][...] = v_ref[row]
            outs[2][...] = v_ref[2:4]
            outs[6][...] = v_ref[7:9]
            for e in (0, 1):
                for k in range(4):
                    outs[7][e : e + 1, 256 * k : 256 * (k + 1)] = v_ref[11 + 4 * e + k : 12 + 4 * e + k]
            outs[8][...] = v_ref[9:11]

    results = pl.pallas_call(
        kernel,
        grid=(steps,),
        out_shape=[jax.ShapeDtypeStruct(f.shape, kind) for f, kind in zip(flat, kinds)]
        + [jax.ShapeDtypeStruct(shape, F32) for shape in small],
        in_specs=[vmem_spec()] * (count + 1),
        out_specs=[pl.BlockSpec((n, f.shape[1]), lambda i: (i, 0)) for n, f in zip(sizes, flat)]
        + [vmem_spec()] * len(small),
        name="widen",
        compiler_params=pltpu.CompilerParams(vmem_limit_bytes=VMEM_CAP),
    )(*flat, sums)
    return [w.reshape(a.shape) for w, a in zip(results[:count], arrays)], results[count:]


def fast_body(
    tokens, doc_ids, routes, cotangent, ln1_gain, ln1_shift, w_qkv, qv_bias, w_out, out_bias,
    ln2_gain, ln2_shift, router, w_in, in_bias, w_back, back_bias,
):
    router_t = jnp.transpose(router)
    rows = {0: ln1_gain[None], 1: ln1_shift[None], 4: out_bias[None], 5: ln2_gain[None]}
    rows |= {6: ln2_shift[None], 7: router_t[0:1], 8: router_t[1:2]}
    row_iota = lax.broadcasted_iota(jnp.int32, (SMALL_ROWS, 256), 0)
    small = jnp.zeros((SMALL_ROWS, 256), BF)
    for index, row in rows.items():
        small = jnp.where(row_iota == index, row, small)
    x_low = tokens[:, 0].reshape(256, 1024)
    picks = routes[:, 0, :, 0]
    dy_low = cotangent[:, 0].reshape(256, 1024)
    hs, params, wqkv_c, wout_c, win_c, qkv, o_full, lse, y1, h2, stats, dispatch, h_slots, d_slots = (
        front_call(x_low, small, qv_bias, in_bias, back_bias, doc_ids, w_qkv, w_out, w_in, picks, dy_low)
    )
    gi, gb_sum, mixed, dy1, da, vectors = moe_call(
        h_slots, d_slots, win_c, w_back, params, y1, h2, stats, dispatch, dy_low
    )
    dh1, gq, gwo, gqv, gi_sum = back_call(
        da, hs, qkv, o_full, lse, wqkv_c, wout_c, doc_ids, gi
    )
    g_in, g_back, g_qkv, g_out, sums, token_grad = final_call(
        gi_sum, gb_sum, gq, gwo, vectors, gqv, x_low, dh1, dy1, params
    )
    (g_in, g_back, g_qkv, g_out, token_grad, mixed), small_grads = widen_call(
        [g_in, g_back, g_qkv, g_out, token_grad, mixed], [F32] * 5 + [BF], sums
    )
    g_one, s_one, g_qv, g_outb, g_two, s_two, g_router, g_inb, g_backb = small_grads
    return (
        mixed.reshape(2, 1, 128, 1024),
        token_grad.reshape(2, 1, 128, 1024),
        g_one, s_one, g_qkv, g_qv, g_out, g_outb, g_two, s_two,
        jnp.transpose(g_router), g_in, g_inb, g_back, g_backb,
    )


def solution(mesh):
    small_plane = mesh.shape["ctx"] == 8 and mesh.shape["fsdp"] == 4
    chosen_body = fast_body if small_plane else body
    placed = (
        P(None, "fsdp", "ctx", None),
        P(None, "fsdp", None),
        P(None, "fsdp", "ctx", None),
        P(None, "fsdp", "ctx", None),
        P("fsdp"),
        P("fsdp"),
        P(None, "fsdp", None),
        P(None, "fsdp"),
        P("fsdp", None),
        P("fsdp"),
        P("fsdp"),
        P("fsdp"),
        P("fsdp", None),
        P(None, "fsdp", None),
        P(None, "fsdp"),
        P(None, "fsdp", None),
        P(None, "fsdp"),
    )
    return jax.shard_map(
        chosen_body,
        mesh=mesh,
        in_specs=placed,
        out_specs=(
            P(None, "fsdp", "ctx", None),
            P(None, "fsdp", "ctx", None),
            P("fsdp"),
            P("fsdp"),
            P(None, "fsdp", None),
            P(None, "fsdp"),
            P("fsdp", None),
            P("fsdp"),
            P("fsdp"),
            P("fsdp"),
            P("fsdp", None),
            P(None, "fsdp", None),
            P(None, "fsdp"),
            P(None, "fsdp", None),
            P(None, "fsdp"),
        ),
        check_vma=False,
    )
```

```python
import math

import jax
import jax.numpy as jnp
from jax import lax
from jax.experimental import pallas as pl
from jax.experimental.pallas import tpu as pltpu
from jax.sharding import PartitionSpec as P

HEADS = 16
HEAD_DIM = 64
CAP = 80


norm_eps = 1e-05
mask_fill = -1e30


def layer_norm(values, gain, shift):
    mean = jnp.mean(values, -1, keepdims=True)
    centred = values - mean
    spread = jnp.mean(centred * centred, -1, keepdims=True)
    return centred * lax.rsqrt(spread + norm_eps) * gain + shift


def natural_position(store_index, tok_rows, ctx_count):
    half = tok_rows // 2
    device = store_index // tok_rows
    slot = store_index % tok_rows
    return jnp.where(
        slot < half, device * half + slot, (2 * ctx_count - 1 - device) * half + slot - half
    )


def visible(query_pos, query_ids, key_pos, key_ids):
    return (key_pos[None, :] <= query_pos[:, None]) & (key_ids[None, :] == query_ids[:, None])


def block_needed(query_pos, query_ids, key_pos, key_ids):
    return (
        (jnp.min(key_pos) <= jnp.max(query_pos))
        & (jnp.max(key_ids) >= jnp.min(query_ids))
        & (jnp.min(key_ids) <= jnp.max(query_ids))
    )


def attend_keys(
    running, query_heads, query_pos, query_ids, key_part, value_part, pos_part, id_part, scale
):
    length = key_part.shape[0]
    stride = math.gcd(length, 512)
    key_heads = key_part.reshape(length, HEADS, HEAD_DIM)
    value_heads = value_part.reshape(length, HEADS, HEAD_DIM)

    def attend_visit_block(block_index, state):
        offset = block_index * stride
        key_blk = lax.dynamic_slice_in_dim(key_heads, offset, stride, 0)
        value_blk = lax.dynamic_slice_in_dim(value_heads, offset, stride, 0)
        key_pos = lax.dynamic_slice_in_dim(pos_part, offset, stride, 0)
        key_ids = lax.dynamic_slice_in_dim(id_part, offset, stride, 0)
        needed = block_needed(query_pos, query_ids, key_pos, key_ids)

        def update(current):
            best, totals, accum = current
            scores = (
                jnp.einsum("qhc,khc->hqk", query_heads, key_blk, preferred_element_type=jnp.float32)
                * scale
            )
            allowed = visible(query_pos, query_ids, key_pos, key_ids)[None]
            scores = jnp.where(allowed, scores, mask_fill)
            new_best = jnp.maximum(best, jnp.max(scores, -1))
            shrink = jnp.exp(best - new_best)
            weights = jnp.where(allowed, jnp.exp(scores - new_best[..., None]), 0.0)
            totals = totals * shrink + jnp.sum(weights, -1)
            addend = jnp.einsum(
                "hqk,khc->qhc",
                weights.astype(jnp.bfloat16),
                value_blk,
                preferred_element_type=jnp.float32,
            )
            accum = accum * jnp.transpose(shrink)[..., None] + addend
            return (new_best, totals, accum)

        def unchanged(current):
            return current

        return lax.cond(needed, update, unchanged, state)

    return lax.fori_loop(0, length // stride, attend_visit_block, running)


def backward_range(
    query_heads,
    grad_heads,
    log_total,
    delta,
    query_pos,
    query_ids,
    key_part,
    value_part,
    pos_part,
    id_part,
    scale,
):
    length = key_part.shape[0]
    stride = math.gcd(length, 512)
    blocks = length // stride
    key_blocks = key_part.reshape(blocks, stride, HEADS, HEAD_DIM)
    value_blocks = value_part.reshape(blocks, stride, HEADS, HEAD_DIM)
    pos_blocks = pos_part.reshape(blocks, stride)
    id_blocks = id_part.reshape(blocks, stride)
    rows = query_heads.shape[0]

    def backward_visit_block(query_acc, block_data):
        key_blk, value_blk, pos_blk, id_blk = block_data
        needed = block_needed(query_pos, query_ids, pos_blk, id_blk)

        def compute(current):
            scores = (
                jnp.einsum("qhc,khc->hqk", query_heads, key_blk, preferred_element_type=jnp.float32)
                * scale
            )
            allowed = visible(query_pos, query_ids, pos_blk, id_blk)[None]
            weights = jnp.where(allowed, jnp.exp(scores - log_total[..., None]), 0.0)
            weight_grad = jnp.einsum(
                "qhc,khc->hqk", grad_heads, value_blk, preferred_element_type=jnp.float32
            )
            score_grad = (weights * (weight_grad - delta[..., None])).astype(jnp.bfloat16)
            current = (
                current
                + jnp.einsum(
                    "hqk,khc->qhc", score_grad, key_blk, preferred_element_type=jnp.float32
                )
                * scale
            )
            terms = ()
            value_term = jnp.einsum(
                "hqk,qhc->khc",
                weights.astype(jnp.bfloat16),
                grad_heads,
                preferred_element_type=jnp.float32,
            )
            key_term = (
                jnp.einsum(
                    "hqk,qhc->khc", score_grad, query_heads, preferred_element_type=jnp.float32
                )
                * scale
            )
            terms = (key_term, value_term)
            return (current, terms)

        def skipped(current):
            terms = ()
            empty = jnp.zeros((stride, HEADS, HEAD_DIM), jnp.float32)
            terms = (empty, empty)
            return (current, terms)

        query_acc, terms = lax.cond(needed, compute, skipped, query_acc)
        terms = (
            terms[0].reshape(stride, HEADS * HEAD_DIM),
            terms[1].reshape(stride, HEADS * HEAD_DIM),
        )
        return (query_acc, terms)

    start_acc = jnp.zeros((rows, HEADS, HEAD_DIM), jnp.float32)
    query_grad, terms = lax.scan(
        backward_visit_block, start_acc, (key_blocks, value_blocks, pos_blocks, id_blocks)
    )
    return (
        query_grad,
        terms[0].reshape(length, HEADS * HEAD_DIM),
        terms[1].reshape(length, HEADS * HEAD_DIM),
    )


def gather_keys(key_rows, value_rows):
    return (
        lax.all_gather(key_rows, "ctx", axis=0, tiled=True),
        lax.all_gather(value_rows, "ctx", axis=0, tiled=True),
    )


def reduce_grads(attn_terms, expert_terms):
    g_one, s_one, g_qkv, g_qv, g_out, g_outb, g_two, s_two, g_router = attn_terms
    g_in, g_inb, g_back, g_backb = expert_terms
    e_in, e_inb, e_back, e_backb = (
        lax.psum_scatter(g_in.astype(jnp.bfloat16), "fsdp", scatter_dimension=1, tiled=True).astype(
            jnp.float32
        ),
        lax.psum_scatter(
            g_inb.astype(jnp.bfloat16), "fsdp", scatter_dimension=1, tiled=True
        ).astype(jnp.float32),
        lax.psum_scatter(
            g_back.astype(jnp.bfloat16), "fsdp", scatter_dimension=1, tiled=True
        ).astype(jnp.float32),
        lax.psum_scatter(
            g_backb.astype(jnp.bfloat16), "fsdp", scatter_dimension=1, tiled=True
        ).astype(jnp.float32),
    )
    a_one, b_one, a_qkv, a_qv, a_out, a_outb, a_two, b_two, a_router = (
        lax.psum_scatter(
            g_one.astype(jnp.bfloat16), "fsdp", scatter_dimension=0, tiled=True
        ).astype(jnp.float32),
        lax.psum_scatter(
            s_one.astype(jnp.bfloat16), "fsdp", scatter_dimension=0, tiled=True
        ).astype(jnp.float32),
        lax.psum_scatter(
            g_qkv.astype(jnp.bfloat16), "fsdp", scatter_dimension=1, tiled=True
        ).astype(jnp.float32),
        lax.psum_scatter(g_qv.astype(jnp.bfloat16), "fsdp", scatter_dimension=1, tiled=True).astype(
            jnp.float32
        ),
        lax.psum_scatter(
            g_out.astype(jnp.bfloat16), "fsdp", scatter_dimension=0, tiled=True
        ).astype(jnp.float32),
        lax.psum_scatter(
            g_outb.astype(jnp.bfloat16), "fsdp", scatter_dimension=0, tiled=True
        ).astype(jnp.float32),
        lax.psum_scatter(
            g_two.astype(jnp.bfloat16), "fsdp", scatter_dimension=0, tiled=True
        ).astype(jnp.float32),
        lax.psum_scatter(
            s_two.astype(jnp.bfloat16), "fsdp", scatter_dimension=0, tiled=True
        ).astype(jnp.float32),
        lax.psum_scatter(
            g_router.astype(jnp.bfloat16), "fsdp", scatter_dimension=0, tiled=True
        ).astype(jnp.float32),
    )
    return (
        lax.psum(a_one.astype(jnp.bfloat16), "ctx").astype(jnp.float32),
        lax.psum(b_one.astype(jnp.bfloat16), "ctx").astype(jnp.float32),
        lax.psum(a_qkv.astype(jnp.bfloat16), "ctx").astype(jnp.float32),
        lax.psum(a_qv.astype(jnp.bfloat16), "ctx").astype(jnp.float32),
        lax.psum(a_out.astype(jnp.bfloat16), "ctx").astype(jnp.float32),
        lax.psum(a_outb.astype(jnp.bfloat16), "ctx").astype(jnp.float32),
        lax.psum(a_two.astype(jnp.bfloat16), "ctx").astype(jnp.float32),
        lax.psum(b_two.astype(jnp.bfloat16), "ctx").astype(jnp.float32),
        lax.psum(a_router.astype(jnp.bfloat16), "ctx").astype(jnp.float32),
        lax.psum(e_in.astype(jnp.bfloat16), "ctx").astype(jnp.float32),
        lax.psum(e_inb.astype(jnp.bfloat16), "ctx").astype(jnp.float32),
        lax.psum(e_back.astype(jnp.bfloat16), "ctx").astype(jnp.float32),
        lax.psum(e_backb.astype(jnp.bfloat16), "ctx").astype(jnp.float32),
    )


def body(
    tokens,
    doc_ids,
    routes,
    cotangent,
    ln1_gain,
    ln1_shift,
    w_qkv,
    qv_bias,
    w_out,
    out_bias,
    ln2_gain,
    ln2_shift,
    router,
    w_in,
    in_bias,
    w_back,
    back_bias,
):
    gain_one, shift_one, proj_all, bias_qv, proj_out, bias_out, gain_two, shift_two, router_full = (
        lax.all_gather(ln1_gain, "fsdp", axis=0, tiled=True),
        lax.all_gather(ln1_shift, "fsdp", axis=0, tiled=True),
        lax.all_gather(w_qkv, "fsdp", axis=1, tiled=True),
        lax.all_gather(qv_bias, "fsdp", axis=1, tiled=True),
        lax.all_gather(w_out, "fsdp", axis=0, tiled=True),
        lax.all_gather(out_bias, "fsdp", axis=0, tiled=True),
        lax.all_gather(ln2_gain, "fsdp", axis=0, tiled=True),
        lax.all_gather(ln2_shift, "fsdp", axis=0, tiled=True),
        lax.all_gather(router, "fsdp", axis=0, tiled=True),
    )
    inner_full, inner_bias, outer_full, outer_bias = (
        lax.all_gather(w_in, "fsdp", axis=1, tiled=True),
        lax.all_gather(in_bias, "fsdp", axis=1, tiled=True),
        lax.all_gather(w_back, "fsdp", axis=1, tiled=True),
        lax.all_gather(back_bias, "fsdp", axis=1, tiled=True),
    )
    gain_one_f = gain_one.astype(jnp.float32)
    shift_one_f = shift_one.astype(jnp.float32)
    bias_qv_f = bias_qv.astype(jnp.float32)
    bias_out_f = bias_out.astype(jnp.float32)
    gain_two_f = gain_two.astype(jnp.float32)
    shift_two_f = shift_two.astype(jnp.float32)
    router_f = router_full.astype(jnp.float32)
    inner_bias_f = inner_bias.astype(jnp.float32)
    outer_bias_f = outer_bias.astype(jnp.float32)
    micro_count = tokens.shape[0]
    tok_rows = tokens.shape[2]
    width = tokens.shape[3]
    stream_len = doc_ids.shape[2]
    ctx_count = lax.axis_size("ctx")
    expert_count = inner_full.shape[0]
    scale = 1.0 / math.sqrt(HEAD_DIM)
    first_row = lax.axis_index("ctx") * tok_rows
    store_pos = natural_position(lax.iota(jnp.int32, stream_len), tok_rows, ctx_count)
    query_pos = lax.dynamic_slice_in_dim(store_pos, first_row, tok_rows, 0)
    expert_iota = lax.iota(jnp.int32, expert_count)
    slot_iota = lax.iota(jnp.int32, CAP)
    outputs = []
    input_grads = []
    totals = None
    for micro in range(micro_count):
        inputs = tokens[micro, 0].astype(jnp.float32)
        ids_store = jnp.take(doc_ids[micro, 0], store_pos)
        query_ids = lax.dynamic_slice_in_dim(ids_store, first_row, tok_rows, 0)
        picks = routes[micro, 0, :, 0]
        upstream = cotangent[micro, 0].astype(jnp.float32)
        h_first, pull_first = jax.vjp(layer_norm, inputs, gain_one_f, shift_one_f)
        h_first_low = h_first.astype(jnp.bfloat16)
        projected = jnp.einsum(
            "td,jde->jte", h_first_low, proj_all, preferred_element_type=jnp.float32
        )
        queries = (projected[0] + bias_qv_f[0]).astype(jnp.bfloat16)
        key_rows = projected[1].astype(jnp.bfloat16)
        value_rows = (projected[2] + bias_qv_f[1]).astype(jnp.bfloat16)
        query_heads = queries.reshape(tok_rows, HEADS, HEAD_DIM)
        start_state = (
            jnp.full((HEADS, tok_rows), mask_fill, jnp.float32),
            jnp.zeros((HEADS, tok_rows), jnp.float32),
            jnp.zeros((tok_rows, HEADS, HEAD_DIM), jnp.float32),
        )
        best, totals_soft, accum = attend_keys(
            start_state,
            query_heads,
            query_pos,
            query_ids,
            lax.all_gather(key_rows, "ctx", axis=0, tiled=True),
            lax.all_gather(value_rows, "ctx", axis=0, tiled=True),
            store_pos,
            ids_store,
            scale,
        )
        log_total = best + jnp.log(totals_soft)
        attended = accum / jnp.transpose(totals_soft)[..., None]
        attended_low = attended.reshape(tok_rows, width).astype(jnp.bfloat16)
        branch = jnp.dot(attended_low, proj_out, preferred_element_type=jnp.float32) + bias_out_f
        middle = inputs + branch
        h_second, pull_second = jax.vjp(layer_norm, middle, gain_two_f, shift_two_f)
        h_second_low = h_second.astype(jnp.bfloat16)
        logits = jnp.dot(h_second_low, router_full, preferred_element_type=jnp.float32)
        probs = jax.nn.softmax(logits, axis=-1)
        chosen = picks[:, None] == expert_iota[None, :]
        chosen_f = chosen.astype(jnp.float32)
        gate = jnp.sum(probs * chosen_f, -1)
        ranks = jnp.cumsum(chosen.astype(jnp.int32), 0) - 1
        dispatch = (jnp.transpose(ranks)[:, None, :] == slot_iota[None, :, None]) & jnp.transpose(
            chosen
        )[:, None, :]
        dispatch_low = dispatch.astype(jnp.bfloat16)
        dispatch_f = dispatch.astype(jnp.float32)
        slot_inputs = jnp.einsum(
            "ect,td->ecd", dispatch_low, h_second_low, preferred_element_type=jnp.float32
        ).astype(jnp.bfloat16)
        inner = (
            jnp.einsum("ecd,edh->ech", slot_inputs, inner_full, preferred_element_type=jnp.float32)
            + inner_bias_f[:, None, :]
        )
        active, pull_gelu = jax.vjp(jax.nn.gelu, inner)
        active_low = active.astype(jnp.bfloat16)
        result = (
            jnp.einsum("ech,ehd->ecd", active_low, outer_full, preferred_element_type=jnp.float32)
            + outer_bias_f[:, None, :]
        )
        expert_sum = jnp.einsum("ect,ecd->td", dispatch_f, result, precision=lax.Precision.HIGHEST)
        output = middle + gate[:, None] * expert_sum
        outputs.append(output.astype(jnp.bfloat16))
        gate_grad = jnp.sum(upstream * expert_sum, -1)
        slot_grad = jnp.einsum(
            "ect,td->ecd", dispatch_f, gate[:, None] * upstream, precision=lax.Precision.HIGHEST
        ).astype(jnp.bfloat16)
        outer_bias_grad = jnp.sum(slot_grad.astype(jnp.float32), 1)
        outer_grad = jnp.einsum(
            "ech,ecd->ehd", active_low, slot_grad, preferred_element_type=jnp.float32
        )
        active_grad = jnp.einsum(
            "ecd,ehd->ech", slot_grad, outer_full, preferred_element_type=jnp.float32
        )
        inner_grad = pull_gelu(active_grad)[0].astype(jnp.bfloat16)
        inner_bias_grad = jnp.sum(inner_grad.astype(jnp.float32), 1)
        inner_w_grad = jnp.einsum(
            "ecd,ech->edh", slot_inputs, inner_grad, preferred_element_type=jnp.float32
        )
        slot_input_grad = jnp.einsum(
            "ech,edh->ecd", inner_grad, inner_full, preferred_element_type=jnp.float32
        )
        second_grad = jnp.einsum(
            "ect,ecd->td", dispatch_f, slot_input_grad, precision=lax.Precision.HIGHEST
        )
        pick_grad = gate_grad[:, None] * chosen_f
        logit_grad = probs * (pick_grad - jnp.sum(probs * pick_grad, -1, keepdims=True))
        router_grad = jnp.einsum(
            "td,te->de",
            h_second_low.astype(jnp.float32),
            logit_grad,
            precision=lax.Precision.HIGHEST,
        )
        second_grad = second_grad + jnp.einsum(
            "te,de->td", logit_grad, router_f, precision=lax.Precision.HIGHEST
        )
        middle_norm_grad, gain_two_grad, shift_two_grad = pull_second(second_grad)
        middle_grad = upstream + middle_norm_grad
        branch_grad = middle_grad.astype(jnp.bfloat16)
        out_bias_grad = jnp.sum(branch_grad.astype(jnp.float32), 0)
        out_grad = jnp.einsum(
            "td,te->de", attended_low, branch_grad, preferred_element_type=jnp.float32
        )
        attended_grad = jnp.einsum(
            "te,de->td", branch_grad, proj_out, preferred_element_type=jnp.float32
        ).astype(jnp.bfloat16)
        grad_heads = attended_grad.reshape(tok_rows, HEADS, HEAD_DIM)
        delta = jnp.transpose(jnp.sum(grad_heads.astype(jnp.float32) * attended, -1))
        key_all, value_all = gather_keys(key_rows, value_rows)
        query_grad, key_terms, value_terms = backward_range(
            query_heads,
            grad_heads,
            log_total,
            delta,
            query_pos,
            query_ids,
            key_all,
            value_all,
            store_pos,
            ids_store,
            scale,
        )
        key_grad, value_grad = (
            lax.psum_scatter(
                key_terms.astype(jnp.bfloat16), "ctx", scatter_dimension=0, tiled=True
            ).astype(jnp.float32),
            lax.psum_scatter(
                value_terms.astype(jnp.bfloat16), "ctx", scatter_dimension=0, tiled=True
            ).astype(jnp.float32),
        )
        query_low = query_grad.reshape(tok_rows, width).astype(jnp.bfloat16)
        key_low = key_grad.astype(jnp.bfloat16)
        value_low = value_grad.astype(jnp.bfloat16)
        stacked_grad = jnp.stack([query_low, key_low, value_low])
        proj_grad = jnp.einsum(
            "td,jte->jde", h_first_low, stacked_grad, preferred_element_type=jnp.float32
        )
        qv_bias_grad = jnp.stack(
            [jnp.sum(query_low.astype(jnp.float32), 0), jnp.sum(value_low.astype(jnp.float32), 0)]
        )
        first_grad = jnp.einsum(
            "jte,jde->td", stacked_grad, proj_all, preferred_element_type=jnp.float32
        )
        input_norm_grad, gain_one_grad, shift_one_grad = pull_first(first_grad)
        input_grads.append(middle_grad + input_norm_grad)
        attn_terms = (
            gain_one_grad,
            shift_one_grad,
            proj_grad,
            qv_bias_grad,
            out_grad,
            out_bias_grad,
            gain_two_grad,
            shift_two_grad,
            router_grad,
        )
        expert_terms = (inner_w_grad, inner_bias_grad, outer_grad, outer_bias_grad)
        local_terms = attn_terms + expert_terms
        totals = local_terms if totals is None else jax.tree.map(jnp.add, totals, local_terms)
    totals = reduce_grads(totals[:9], totals[9:])
    (
        g_one,
        s_one,
        g_qkv,
        g_qv,
        g_out,
        g_outb,
        g_two,
        s_two,
        g_router,
        g_in,
        g_inb,
        g_back,
        g_backb,
    ) = totals
    mixed = jnp.stack(outputs)[:, None]
    token_grad = jnp.stack(input_grads)[:, None]
    return (
        mixed,
        token_grad,
        g_one,
        s_one,
        g_qkv,
        g_qv,
        g_out,
        g_outb,
        g_two,
        s_two,
        g_router,
        g_in,
        g_inb,
        g_back,
        g_backb,
    )


MESH_ID = pl.DeviceIdType.MESH
BF = jnp.bfloat16
F32 = jnp.float32
DMA = pltpu.SemaphoreType.DMA
VMEM_CAP = 60 * 1024 * 1024
SMALL_ROWS = 32
NT = (((1,), (1,)), ((), ()))
TN = (((0,), (0,)), ((), ()))
NN = (((1,), (0,)), ((), ()))


def mm(left, right, dims=NN):
    return lax.dot_general(left, right, dims, preferred_element_type=F32)


def plane_coords():
    me = lax.axis_index("ctx")
    core = me % 2
    col = (me // 2) % 2
    row = me // 4
    sib = me + 1 - 2 * core
    xn = (row * 2 + 1 - col) * 2 + core
    yn = ((1 - row) * 2 + col) * 2 + core
    dg = ((1 - row) * 2 + 1 - col) * 2 + core
    return me, core, sib, xn, yn, dg


def meet(ctx_peers, fsdp_peers=()):
    sem = pltpu.get_barrier_semaphore()
    for peer in ctx_peers:
        pl.semaphore_signal(sem, inc=1, device_id={"ctx": peer}, device_id_type=MESH_ID)
    for peer in fsdp_peers:
        pl.semaphore_signal(sem, inc=1, device_id={"fsdp": peer}, device_id_type=MESH_ID)
    pl.semaphore_wait(sem, len(ctx_peers) + len(fsdp_peers))


def send_to(src, dst, send_sem, recv_sem, axis, peer):
    return pltpu.make_async_remote_copy(
        src_ref=src,
        dst_ref=dst,
        send_sem=send_sem,
        recv_sem=recv_sem,
        device_id={axis: peer},
        device_id_type=MESH_ID,
    )


def gather_sems(chunks):
    return [
        DMA((2, chunks)),
        DMA((2, chunks)),
        DMA((chunks,)),
        DMA((chunks,)),
        DMA((3, chunks)),
        DMA((3, chunks)),
        DMA((chunks,)),
        DMA((chunks,)),
        DMA((chunks,)),
    ]


def line_sems(chunks):
    return [DMA((3, chunks)), DMA((3, chunks)), DMA((3, chunks)), DMA((3, chunks)), DMA((chunks,))]


def by_rows(count, step, visit):
    def one(index, carry):
        visit(pl.ds(pl.multiple_of(index * step, step), step))
        return carry

    lax.fori_loop(0, count // step, one, 0)


def ring_ops(own, slot, sems):
    ns, nr, ds, dr, fs, fr, ss, sr, ls = sems
    me, core, sib, xn, yn, dg = plane_coords()
    near = (xn, yn)

    def away(i, k):
        return send_to(own(k), slot(me, k), ns.at[i, k], nr.at[i, k], "ctx", near[i])

    def beside(k):
        return send_to(own(k), slot(me, k), ss.at[k], sr.at[k], "ctx", sib)

    def here(k):
        return pltpu.make_async_copy(own(k), slot(me, k), ls.at[k])

    def passed(k):
        block = slot(near[k % 2], k)
        return send_to(block, block, ds.at[k], dr.at[k], "ctx", near[1 - k % 2])

    def onward(i, k):
        block = slot((xn, yn, dg)[i], k)
        return send_to(block, block, fs.at[i, k], fr.at[i, k], "ctx", sib)

    def begin(k):
        for i in (0, 1):
            away(i, k).start()
        beside(k).start()
        here(k).start()

    def relay(k):
        for i in (k % 2, 1 - k % 2):
            away(i, k).wait_recv()
            if i == k % 2:
                passed(k).start()
            onward(i, k).start()

    def diag(k):
        passed(k).wait_recv()
        onward(2, k).start()

    def done(k):
        here(k).wait()
        beside(k).wait_recv()
        for i in range(3):
            onward(i, k).wait_recv()

    def finish(k):
        for i in (0, 1):
            away(i, k).wait_send()
        beside(k).wait_send()
        passed(k).wait_send()
        for i in range(3):
            onward(i, k).wait_send()

    return begin, relay, diag, done, finish


def line_ops(own, slot, chunks, sems):
    us, ur, ws, wr, ls = sems
    z = lax.axis_index("fsdp")

    def up(d, k):
        src = own(k) if d == 0 else slot(z - d, k)
        return send_to(src, slot(z - d, k), us.at[d, k], ur.at[d, k], "fsdp", z + 1)

    def down(d, k):
        src = own(k) if d == 0 else slot(z + d, k)
        return send_to(src, slot(z + d, k), ws.at[d, k], wr.at[d, k], "fsdp", z - 1)

    def from_below(d, k):
        return send_to(own(k), slot(z - d - 1, k), us.at[d, k], ur.at[d, k], "fsdp", z - 1)

    def from_above(d, k):
        return send_to(own(k), slot(z + d + 1, k), ws.at[d, k], wr.at[d, k], "fsdp", z + 1)

    def here(k):
        return pltpu.make_async_copy(own(k), slot(z, k), ls.at[k])

    def pass_one(d, k):
        @pl.when((z < 3) & (z >= d))
        def _():
            if d:
                from_below(d - 1, k).wait_recv()
            up(d, k).start()

        @pl.when((z > 0) & (z + d <= 3))
        def _():
            if d:
                from_above(d - 1, k).wait_recv()
            down(d, k).start()

    def pass_on(d, which=None):
        for k in range(chunks) if which is None else which:
            pass_one(d, k)

    def begin():
        for k in range(chunks):
            here(k).start()
        pass_on(0)

    def arrive():
        for d in range(3):
            for k in range(chunks):

                @pl.when(z == 3)
                def _():
                    from_below(d, k).wait_recv()

                @pl.when(z == 0)
                def _():
                    from_above(d, k).wait_recv()

        for k in range(chunks):
            here(k).wait()

    def finish():
        for d in range(3):
            for k in range(chunks):

                @pl.when((z < 3) & (z >= d))
                def _():
                    up(d, k).wait_send()

                @pl.when((z > 0) & (z + d <= 3))
                def _():
                    down(d, k).wait_send()

    return begin, pass_on, arrive, finish


def sum_scratch():
    return [pltpu.VMEM((2, 4, 128, 1024), BF)] + [pltpu.VMEM((2, 128, 1024), BF)] * 6 + [
        DMA((2, 4)), DMA((2, 4)), DMA((2, 6)), DMA((2, 6)),
    ]


def sum_ops(part, m, out, scratch):
    pair, gs, gr, xs, xr, ys, yr = [ref.at[m] for ref in scratch[:7]]
    s1, r1, s2, r2 = scratch[7:]
    me, core, sib, xn, yn, dg = plane_coords()
    order = (dg, xn, yn, me)
    lo, hi = pl.ds(0, 64), pl.ds(64, 64)

    def to_pair(i):
        other = order[i] + 1 - 2 * core
        return send_to(part.at[m, other], pair.at[i], s1.at[m, i], r1.at[m, i], "ctx", sib)

    def ship(index):
        src, dst, peer = (
            (gs.at[lo], gr.at[lo], xn),
            (gs.at[hi], gr.at[hi], yn),
            (xs.at[lo], xr.at[lo], xn),
            (ys.at[hi], yr.at[hi], yn),
            (ys.at[lo], yr.at[lo], yn),
            (xs.at[hi], xr.at[hi], xn),
        )[index]
        return send_to(src, dst, s2.at[m, index], r2.at[m, index], "ctx", peer)

    def f32(value):
        return value.astype(F32)

    def both(i, rr):
        return f32(part[m, order[i], rr]) + f32(pair[i, rr])

    def begin():
        for i in range(4):
            to_pair(i).start()

    def span(offset, count, visit):
        def one(index):
            visit(pl.ds(offset + index.start, 32))

        by_rows(count, 32, one)

    def diag():
        to_pair(0).wait_recv()

        def add(rr):
            gs[rr] = both(0, rr).astype(BF)

        span(0, 128, add)
        ship(0).start()
        ship(1).start()

    def near():
        to_pair(1).wait_recv()

        def add_x(rr):
            xs[rr] = both(1, rr).astype(BF)

        span(0, 64, add_x)
        ship(2).start()
        to_pair(2).wait_recv()

        def add_y(rr):
            ys[rr] = both(2, rr).astype(BF)

        span(64, 64, add_y)
        ship(3).start()

    def join():
        ship(0).wait_recv()

        def add_y(rr):
            ys[rr] = (both(2, rr) + f32(gr[rr])).astype(BF)

        span(0, 64, add_y)
        ship(4).start()
        ship(1).wait_recv()

        def add_x(rr):
            xs[rr] = (both(1, rr) + f32(gr[rr])).astype(BF)

        span(64, 64, add_x)
        ship(5).start()

    def finish():
        to_pair(3).wait_recv()
        for index in (2, 3, 4, 5):
            ship(index).wait_recv()

        def add(rr):
            place = pl.ds(m * 128 + rr.start, 32)
            out[place] = both(3, rr) + f32(xr[rr]) + f32(yr[rr])

        span(0, 128, add)
        for i in range(4):
            to_pair(i).wait_send()
        for index in range(6):
            ship(index).wait_send()

    return begin, diag, near, join, finish


def fold_scratch(rows):
    return [
        pltpu.VMEM((2, 3, rows, 1024), BF),
        pltpu.VMEM((2, 2, rows, 1024), BF),
        DMA((2, 3, 2)),
        DMA((2, 3, 2)),
    ]


def fold_ops(block, rows, out, scratch):
    got, sent, ss, rs = scratch
    z = lax.axis_index("fsdp")
    half = rows // 2
    places = (z, 3 - z)
    nexts = ((z + 1) % 4, (z + 3) % 4)

    def target(side, q):
        return q if side == 0 else 3 - q

    def piece(ref, h):
        return ref.at[pl.ds(half * h, half)]

    def message(src, side, q, h):
        return send_to(
            piece(src, h), piece(got.at[side, q - 1], h), ss.at[side, q - 1, h], rs.at[side, q - 1, h],
            "fsdp", nexts[side],
        )

    def first(side, q, h):
        return message(block(target(side, q)), side, q, h)

    def later(side, q, h):
        return message(sent.at[side, q - 2], side, q, h)

    def begin():
        for side in (0, 1):

            @pl.when(places[side] == 0)
            def _():
                for q in (3, 2, 1):
                    for h in (0, 1):
                        first(side, q, h).start()

    def relay(at, q, h):
        for side in (0, 1):

            @pl.when(places[side] == at)
            def _():
                later(side, q, h).wait_recv()
                mine = block(target(side, q))

                def add(index):
                    rr = pl.ds(half * h + index.start, 32)
                    total = mine[rr].astype(F32) + got[side, q - 1, rr].astype(F32)
                    sent[side, q - 2, rr] = total.astype(BF)

                by_rows(half, 32, add)
                later(side, q, h).start()

    def step(n):
        for at, q, h in (((1, 3, 0),), ((1, 3, 1), (2, 3, 0)), ((1, 2, 0), (2, 3, 1)), ((1, 2, 1),))[n]:
            relay(at, q, h)

    def finish():
        mine = block(z)
        for side in (0, 1):

            @pl.when(places[side] > 0)
            def _():
                for h in (0, 1):
                    q = places[side]
                    send_to(
                        piece(mine, h), piece(got.at[side, q - 1], h), ss.at[side, q - 1, h],
                        rs.at[side, q - 1, h], "fsdp", nexts[side],
                    ).wait_recv()

        def add_all(sides):
            def add(rr):
                total = mine[rr].astype(F32)
                for side in sides:
                    total = total + got[side, places[side] - 1, rr].astype(F32)
                out[rr] = total.astype(BF)

            by_rows(rows, 32, add)

        @pl.when(z == 0)
        def _():
            add_all((1,))

        @pl.when(z == 3)
        def _():
            add_all((0,))

        @pl.when((z > 0) & (z < 3))
        def _():
            add_all((0, 1))

        for side in (0, 1):
            for at, qs in ((0, (3, 2, 1)), (1, (3, 2)), (2, (3,))):

                @pl.when(places[side] == at)
                def _():
                    for q in qs:
                        for h in (0, 1):
                            first(side, q, h).wait_send()

    return begin, step, finish


def vmem_spec():
    return pl.BlockSpec(memory_space=pltpu.VMEM)


def any_spec():
    return pl.BlockSpec(memory_space=pl.ANY)


def natural_slot(device, k):
    micro, part = k // 2, k % 2
    return micro * 16 + (device if part == 0 else 15 - device)


def remote_params(ident):
    return pltpu.CompilerParams(
        collective_id=ident, has_side_effects=True, vmem_limit_bytes=VMEM_CAP
    )


def line_peers():
    z = lax.axis_index("fsdp")
    return [(z + d) % 4 for d in (1, 2, 3)]


def token_docs(row_ref, m):
    row = jnp.broadcast_to(row_ref[m].astype(F32), (8, 1024))
    return row[0:1], jnp.transpose(row)[:, 0:1]


def front_kernel(
    x_ref, base_ref, qvb_ref, router_ref, inb_ref, backb_ref, doc_ref, wq_ref, wo_ref, wi_ref, picks_ref, dy_ref,
    h_ref, params_ref, wqc_ref, woc_ref, wic_ref, qkv_ref, of_ref, lse_ref,
    y_ref, h2_ref, stat_ref, disp_ref, hslot_ref, dslot_ref,
    out_ref, small_ref, hs, units, part, zs, zr, os, orr, ol, *sems,
):
    me, core, sib, xn, yn, dg = plane_coords()
    z = lax.axis_index("fsdp")
    peers = line_peers()
    meet((sib, xn, yn), peers)
    small_ref[...] = base_ref[...]
    small_ref[2:4] = qvb_ref[...]
    small_ref[7:9] = router_ref[...]
    for e in (0, 1):
        for k in range(4):
            small_ref[9 + 4 * e + k : 10 + 4 * e + k] = inb_ref[e : e + 1, 256 * k : 256 * (k + 1)]
    small_ref[17:19] = backb_ref[...]
    params_ref[z] = small_ref[...]
    copies = []
    for i, peer in enumerate(peers):
        copy = send_to(small_ref, params_ref.at[z], zs.at[i], zr.at[i], "fsdp", peer)
        copy.start()
        copies.append(copy)
    owner = me // 2
    columns = pl.ds(pl.multiple_of(me * 128, 128), 128)
    expert, quarter = me // 4, me % 4

    def wq_slot(where, k):
        return wqc_ref.at[k, pl.ds(pl.multiple_of(where * 256, 256), 256)]

    def wi_own(k):
        return wi_ref.at[expert, :, pl.ds(pl.multiple_of(k * 1024 + quarter * 256, 256), 256)]

    def wi_slot(where, k):
        return wic_ref.at[pl.ds(pl.multiple_of(where * 256, 256), 256), pl.ds(256 * k, 256)]

    q_begin, q_pass, q_arrive, q_finish = line_ops(
        lambda k: wq_ref.at[k, :, columns], wq_slot, 3, sems[:5]
    )
    i_begin, i_pass, i_arrive, i_finish = line_ops(wi_own, wi_slot, 4, sems[5:10])
    begin, relay, diag, done, finish = ring_ops(
        lambda k: hs.at[pl.ds(64 * k, 64)],
        lambda device, k: h_ref.at[natural_slot(device, k)],
        sems[10:19],
    )
    sums = [sum_ops(part, m, out_ref, sems[19:]) for m in (0, 1)]
    q_begin()

    wo_own = wo_ref.at[pl.ds(pl.multiple_of(core * 128, 128), 128)]

    def wo_step(src, side):
        return send_to(
            src, woc_ref, os.at[side], orr.at[side], "fsdp", z + 1 if side == 0 else z - 1
        )

    def wo_both(act):
        @pl.when((z >= owner) & (z < 3))
        def _():
            act(0)

        @pl.when((z <= owner) & (z > 0))
        def _():
            act(1)

    def wo_begin():
        @pl.when(z == owner)
        def _():
            pltpu.make_async_copy(wo_own, woc_ref, ol).start()
            wo_both(lambda side: wo_step(wo_own, side).start())

    def wo_arrive():
        @pl.when(z > owner)
        def _():
            wo_step(woc_ref, 0).wait_recv()

        @pl.when(z < owner)
        def _():
            wo_step(woc_ref, 1).wait_recv()

    def wo_pass(d):
        @pl.when((z == owner + d) | (z == owner - d))
        def _():
            wo_arrive()
            wo_both(lambda side: wo_step(woc_ref, side).start())

    def wo_last():
        @pl.when((z == owner + 3) | (z == owner - 3))
        def _():
            wo_arrive()

        @pl.when(z == owner)
        def _():
            pltpu.make_async_copy(wo_own, woc_ref, ol).wait()

    wo_begin()

    def unit(rr):
        values = x_ref[rr].astype(F32)
        centred = values - jnp.mean(values, -1, keepdims=True)
        spread = jnp.mean(centred * centred, -1, keepdims=True)
        units[rr] = centred * lax.rsqrt(spread + norm_eps)

    by_rows(256, 32, unit)
    for copy in copies:
        copy.wait()

    def full_row(r):
        return jnp.concatenate([params_ref[i, r : r + 1, :] for i in range(4)], axis=1).astype(F32)

    gain, shift = full_row(0), full_row(1)

    def norm(rr):
        hs[rr] = (units[rr] * gain + shift).astype(BF)

    by_rows(256, 32, norm)
    begin(0)
    begin(1)
    q_pass(1)
    relay(0)
    relay(1)
    begin(2)
    begin(3)
    wo_pass(1)
    q_pass(2)
    i_begin()
    diag(0)
    diag(1)
    wo_pass(2)
    done(0)
    done(1)
    q_arrive()
    half = pl.ds(pl.multiple_of(core * 128, 128), 128)
    q_bias = params_ref[owner, 2:3, half].astype(F32)
    v_bias = params_ref[owner, 3:4, half].astype(F32)
    masks = head_masks(256)
    vmasks = head_masks(1024)
    zero = jnp.zeros((), BF)

    def micro(m, carry):
        @pl.when(m == 1)
        def _():
            done(2)
            done(3)

        h = h_ref[pl.ds(16 * m, 16)].reshape(1024, 1024)
        place = pl.ds(pl.multiple_of(m * 1024, 1024), 1024)
        q = (mm(h, wqc_ref[0]) + q_bias).astype(BF)
        k = mm(h, wqc_ref[1]).astype(BF)
        v = (mm(h, wqc_ref[2]) + v_bias).astype(BF)
        qkv_ref[0, place] = q
        qkv_ref[1, place] = k
        qkv_ref[2, place] = v
        vh = [jnp.where(vmasks[j], v, zero) for j in (0, 1)]
        doc_row, doc_col = token_docs(doc_ref, m)
        for i in range(4):
            length = 256 * (i + 1)
            rows = slice(256 * i, 256 * (i + 1))
            qi = q[rows] * jnp.asarray(0.125, BF)
            allowed = allowed_mask(i, doc_col[rows], doc_row[:, :length])
            total = None
            stats = []
            for j in (0, 1):
                s = mm(jnp.where(masks[j], qi, zero), k[:length], NT)
                s = jnp.where(allowed, s, mask_fill)
                top = jnp.max(s, -1, keepdims=True)
                e = jnp.exp(s - top)
                den = jnp.sum(e, -1, keepdims=True)
                p = (e * (1.0 / den)).astype(BF)
                term = mm(p, vh[j][:length])
                total = term if total is None else total + term
                stats.append(top + jnp.log(den))
            at = pl.ds(pl.multiple_of(m * 1024 + 256 * i, 256), 256)
            lse_ref[at] = jnp.where(masks[0], stats[0], stats[1])
            of_ref[at] = total

            @pl.when(m == 0)
            def _():
                if i == 0:
                    relay(2)
                    relay(3)
                if i == 1:
                    i_pass(1, (0,))
                    diag(2)
                if i == 2:
                    i_pass(1, (1,))
                    diag(3)
                if i == 3:
                    wo_last()

            @pl.when(m == 1)
            def _():
                if i == 1:
                    sums[0][3]()
                if i == 3:
                    i_pass(2, (0,))

        for i in range(4):
            at = pl.ds(pl.multiple_of(m * 1024 + 256 * i, 256), 256)
            a = mm(of_ref[at].astype(BF), woc_ref[...]).astype(BF)
            for b in range(4):
                block = 4 * i + b
                dest, side = (block, 0) if block < 8 else (15 - block, 1)
                part[m, dest, 64 * side : 64 * (side + 1)] = a[64 * b : 64 * (b + 1)]

        for n in (0, 1):

            @pl.when(m == n)
            def _():
                for step in sums[n][:3]:
                    step()
                if n == 0:
                    i_pass(1, (2, 3))

        return carry

    lax.fori_loop(0, 2, micro, 0)
    outb, gain2, shift2 = full_row(4), full_row(5), full_row(6)
    router = jnp.concatenate([full_row(7), full_row(8)], axis=0).astype(BF)

    def route(m):
        picked = jnp.broadcast_to(picks_ref[m : m + 1].astype(F32), (8, 128))
        sub = lax.broadcasted_iota(jnp.int32, (8, 128), 0)
        member = jnp.where(sub == 0, 1.0 - picked, picked)
        earlier = lax.broadcasted_iota(jnp.int32, (128, 128), 0)
        later = lax.broadcasted_iota(jnp.int32, (128, 128), 1)
        rank = mm(member.astype(BF), (earlier < later).astype(BF))
        slot = lax.broadcasted_iota(jnp.int32, (CAP, 128), 0).astype(F32)
        for e in (0, 1):
            hit = (rank[e : e + 1] == slot) & (member[e : e + 1] > 0.5)
            disp_ref[m, e] = hit.astype(BF)
        return jnp.transpose(picked)[:, 0:1]

    def second_norm(m):
        pick = route(m)
        base = 128 * m

        def visit(index):
            rr = pl.ds(base + index.start, 32)
            values = x_ref[rr].astype(F32) + (out_ref[rr] + outb)
            y_ref[rr] = values
            centred = values - jnp.mean(values, -1, keepdims=True)
            spread = jnp.mean(centred * centred, -1, keepdims=True)
            h2_ref[rr] = (centred * lax.rsqrt(spread + norm_eps) * gain2 + shift2).astype(BF)

        by_rows(128, 32, visit)
        span = pl.ds(base, 128)
        h2 = h2_ref[span]
        logits = mm(h2, router, NT)
        top = jnp.max(logits, -1, keepdims=True)
        e = jnp.exp(logits - top)
        probs = e / jnp.sum(e, -1, keepdims=True)
        gate = jnp.where(pick > 0.5, probs[:, 1:2], probs[:, 0:1])
        lane = lax.broadcasted_iota(jnp.int32, (128, 128), 1)
        packed = jnp.where(lane == 0, probs[:, 0:1], probs[:, 1:2])
        packed = jnp.where(lane == 2, gate, packed)
        stat_ref[span] = jnp.where(lane == 3, pick, packed)
        du = (gate * dy_ref[span].astype(F32)).astype(BF)
        for which in (0, 1):
            hslot_ref[which, m] = mm(disp_ref[m, which], h2).astype(BF)
            dslot_ref[which, m] = mm(disp_ref[m, which], du).astype(BF)

    i_pass(2, (1,))
    sums[1][3]()
    i_pass(2, (2, 3))
    sums[0][4]()
    second_norm(0)
    sums[1][4]()
    second_norm(1)
    i_arrive()
    wo_both(lambda side: wo_step(woc_ref, side).wait_send())
    q_finish()
    i_finish()
    for k in range(4):
        finish(k)


def front_call(x, small, qv_bias, router_t, in_bias, back_bias, docs, w_qkv, w_out, w_in, picks, dy):
    return pl.pallas_call(
        front_kernel,
        out_shape=(
            jax.ShapeDtypeStruct((32, 64, 1024), BF),
            jax.ShapeDtypeStruct((4, SMALL_ROWS, 256), BF),
            jax.ShapeDtypeStruct((3, 1024, 128), BF),
            jax.ShapeDtypeStruct((128, 1024), BF),
            jax.ShapeDtypeStruct((1024, 1024), BF),
            jax.ShapeDtypeStruct((3, 2048, 128), BF),
            jax.ShapeDtypeStruct((2048, 128), F32),
            jax.ShapeDtypeStruct((2048, 128), F32),
            jax.ShapeDtypeStruct((256, 1024), F32),
            jax.ShapeDtypeStruct((256, 1024), BF),
            jax.ShapeDtypeStruct((256, 128), F32),
            jax.ShapeDtypeStruct((2, 2, CAP, 128), BF),
            jax.ShapeDtypeStruct((2, 2, CAP, 1024), BF),
            jax.ShapeDtypeStruct((2, 2, CAP, 1024), BF),
        ),
        in_specs=[vmem_spec()] * 7 + [any_spec()] * 3 + [vmem_spec()] * 2,
        out_specs=[vmem_spec()] * 4 + [any_spec()] + [vmem_spec()] * 9,
        scratch_shapes=[
            pltpu.VMEM((256, 1024), F32),
            pltpu.VMEM((SMALL_ROWS, 256), BF),
            pltpu.VMEM((256, 1024), BF),
            pltpu.VMEM((256, 1024), F32),
            pltpu.VMEM((2, 8, 128, 1024), BF),
            DMA((3,)),
            DMA((3,)),
            DMA((2,)),
            DMA((2,)),
            DMA(()),
        ]
        + line_sems(3)
        + line_sems(4)
        + gather_sems(4)
        + sum_scratch(),
        name="front",
        compiler_params=remote_params(0),
    )(x, small, qv_bias, router_t, in_bias, back_bias, docs, w_qkv, w_out, w_in, picks, dy)


def moe_call(h_slots, d_slots, win, w_back, params, y1, h2, stats, dispatch, dy):
    def kernel(
        h_ref, d_ref, wi_ref, wall_ref, params_ref, y_ref, h2_ref, stat_ref, disp_ref, dy_ref,
        gi_ref, gbs_ref, mixed_ref, dy1_ref, da_ref, v_ref,
        o_ref, gib_ref, acc, wb_ref, gba, u_ref, g_ref, rows, gz, slope, dz, part, pair, sent, got,
        ns, nr, fs, fr, ss, sr, ls, s1, r1, s2, r2, *wsems,
    ):
        me, core, sib, xn, yn, dg = plane_coords()
        expert, quarter = me // 4, me % 4
        meet((sib, xn, yn, dg), line_peers())
        w_begin, w_pass, w_arrive, w_finish = line_ops(
            lambda k: wall_ref.at[expert, pl.ds(pl.multiple_of(quarter * 256 + 64 * k, 64), 64)],
            lambda where, k: wb_ref.at[pl.ds(pl.multiple_of(where * 256 + 64 * k, 64), 64)],
            4,
            wsems[:5],
        )
        z_begin, z_step, z_finish = fold_ops(lambda where: gba.at[where], 256, gbs_ref, wsems[5:])
        w_begin()
        peers = (dg, xn, yn)
        wanted = (1 - expert, expert, 1 - expert)
        ins = (h_ref, d_ref)

        def away(t, m, i):
            return send_to(
                ins[t].at[wanted[i], m], rows.at[t, m, me], ns.at[t, m, i], nr.at[t, m, i], "ctx", peers[i]
            )

        def beside(t, m):
            return send_to(
                ins[t].at[expert, m], rows.at[t, m, me], ss.at[t, m], sr.at[t, m], "ctx", sib
            )

        def here(t, m):
            return pltpu.make_async_copy(ins[t].at[expert, m], rows.at[t, m, me], ls.at[t, m])

        def onward(t, m, i):
            block = rows.at[t, m, peers[i]]
            return send_to(block, block, fs.at[t, m, i], fr.at[t, m, i], "ctx", sib)

        for t in (0, 1):
            for m in (0, 1):
                for i in range(3):
                    away(t, m, i).start()
        for t in (0, 1):
            for m in (0, 1):
                beside(t, m).start()
                here(t, m).start()

        def arrive(t, m):
            for i in range(3):
                away(t, m, i).wait_recv()
                onward(t, m, i).start()
            here(t, m).wait()
            beside(t, m).wait_recv()
            for i in range(3):
                onward(t, m, i).wait_recv()

        order = (dg, xn, yn, me)

        def to_pair(t, m, i):
            other = order[i] + 1 - 2 * core
            return send_to(
                part.at[t, m, other], pair.at[t, m, i], s1.at[t, m, i], r1.at[t, m, i], "ctx", sib
            )

        def to_home(t, m, i):
            return send_to(
                sent.at[t, m, i], got.at[t, m, i], s2.at[t, m, i], r2.at[t, m, i], "ctx", order[i]
            )

        def join(t, m):
            for i in range(3):
                to_pair(t, m, i).wait_recv()
                mine = order[i]

                def add(rr):
                    sent[t, m, i, rr] = (
                        part[t, m, mine, rr].astype(F32) + pair[t, m, i, rr].astype(F32)
                    ).astype(BF)

                by_rows(CAP, 16, add)
                to_home(t, m, i).start()

        mine_row = lax.broadcasted_iota(jnp.int32, (8, 256), 0) == me
        in_bias = jnp.concatenate(
            [
                jnp.sum(
                    jnp.where(mine_row, params_ref[i, 9:17, :].astype(F32), 0.0), 0, keepdims=True
                )
                for i in range(4)
            ],
            axis=1,
        )

        def inner_rows(m):
            def visit(half, carry):
                xs = rows[0, m, pl.ds(4 * half, 4)].reshape(4 * CAP, 1024)
                zed = mm(xs, wi_ref[...]) + in_bias
                square = zed * zed
                t = jnp.tanh(zed * (GELU_A + GELU_A * GELU_B * square))
                half_up = 0.5 + 0.5 * t
                place = pl.ds(pl.multiple_of(m * 8 * CAP + half * 4 * CAP, 4 * CAP), 4 * CAP)
                gz[place] = (zed * half_up).astype(BF)
                slope[place] = half_up + 0.5 * zed * (1.0 - t * t) * (
                    GELU_A + 3.0 * GELU_A * GELU_B * square
                )
                return carry

            lax.fori_loop(0, 2, visit, 0)

        def inner(m, carry):
            @pl.when(m == 0)
            def _():
                w_pass(1, (0, 1))

            arrive(0, m)

            @pl.when(m == 0)
            def _():
                w_pass(1, (2,))

            inner_rows(m)

            @pl.when(m == 0)
            def _():
                w_pass(1, (3,))

            return carry

        lax.fori_loop(0, 2, inner, 0)
        w_pass(2, (0, 1))
        arrive(1, 0)
        w_pass(2, (2, 3))
        arrive(1, 1)

        def back_grads(j, carry):
            column = pl.ds(pl.multiple_of(256 * j, 256), 256)
            du = rows[1].reshape(16 * CAP, 1024)
            gba[j] = mm(gz[:, column], du, TN).astype(BF)
            return carry

        lax.fori_loop(0, 4, back_grads, 0)
        z_begin()
        w_arrive()

        def forward(m, carry):
            def visit(half, inner_carry):
                place = pl.ds(pl.multiple_of(m * 8 * CAP + half * 4 * CAP, 4 * CAP), 4 * CAP)
                u = mm(gz[place], wb_ref[...]).astype(BF)
                part[0, m, pl.ds(4 * half, 4)] = u.reshape(4, CAP, 1024)
                return inner_carry

            lax.fori_loop(0, 2, visit, 0)
            for i in range(4):
                to_pair(0, m, i).start()
            join(0, m)
            return carry

        lax.fori_loop(0, 2, forward, 0)
        z_step(0)
        gib_ref[...] = jnp.zeros_like(gib_ref)

        def backward(m, carry):
            def rows_backward(half, inner_carry):
                du = rows[1, m, pl.ds(4 * half, 4)].reshape(4 * CAP, 1024)
                place = pl.ds(pl.multiple_of(m * 8 * CAP + half * 4 * CAP, 4 * CAP), 4 * CAP)
                low = (mm(du, wb_ref[...], NT) * slope[place]).astype(BF)
                dz[place] = low
                gib_ref[...] += jnp.sum(low.astype(F32), 0, keepdims=True)
                dh = mm(low, wi_ref[...], NT).astype(BF)
                part[1, m, pl.ds(4 * half, 4)] = dh.reshape(4, CAP, 1024)
                return inner_carry

            lax.fori_loop(0, 2, rows_backward, 0)
            for i in range(4):
                to_pair(1, m, i).start()
            join(1, m)

            @pl.when(m == 0)
            def _():
                z_step(1)

            return carry

        lax.fori_loop(0, 2, backward, 0)
        z_step(2)

        def weight_grads(j, carry):
            column = pl.ds(pl.multiple_of(256 * j, 256), 256)
            xs = rows[0, :, :, :, column].reshape(16 * CAP, 256)
            gi_ref[column] = mm(xs, dz[...], TN).astype(BF)
            return carry

        lax.fori_loop(0, 4, weight_grads, 0)
        z_step(3)

        def full_row(r):
            return jnp.concatenate(
                [params_ref[i, r : r + 1, :] for i in range(4)], axis=1
            ).astype(F32)

        gain2, router0, router1 = full_row(5), full_row(7), full_row(8)
        bias0, bias1 = full_row(17), full_row(18)
        acc[...] = jnp.zeros_like(acc)

        def home(t, m):
            to_pair(t, m, 3).wait_recv()
            for i in range(3):
                to_home(t, m, i).wait_recv()

            def finish(rr):
                o_ref[expert, t, m, rr] = (
                    part[t, m, me, rr].astype(F32)
                    + pair[t, m, 3, rr].astype(F32)
                    + got[t, m, 1, rr].astype(F32)
                )
                o_ref[1 - expert, t, m, rr] = got[t, m, 0, rr].astype(F32) + got[
                    t, m, 2, rr
                ].astype(F32)

            by_rows(CAP, 16, finish)

        def to_tokens(t, m):
            total = None
            for e in (0, 1):
                value = o_ref[e, t, m]
                for _ in range(3):
                    low = value.astype(BF)
                    term = mm(disp_ref[m, e], low, TN)
                    total = term if total is None else total + term
                    value = value - low.astype(F32)
            return total

        def token_rows(m):
            span = pl.ds(128 * m, 128)
            home(0, m)
            u_ref[...] = to_tokens(0, m)
            home(1, m)
            g_ref[...] = to_tokens(1, m)

            def visit(index):
                rr = pl.ds(128 * m + index.start, 32)
                local = pl.ds(index.start, 32)
                stat = stat_ref[rr]
                p0, p1, gate, pick = (stat[:, i : i + 1] for i in range(4))
                dy = dy_ref[rr].astype(F32)
                values = y_ref[rr]
                u = u_ref[local] + jnp.where(pick > 0.5, bias1, bias0)
                mixed_ref[rr] = (values + gate * u).astype(BF)
                dgate = jnp.sum(dy * u, -1, keepdims=True)
                d0, d1 = dgate * (1.0 - pick), dgate * pick
                mean_grad = p0 * d0 + p1 * d1
                l0, l1 = p0 * (d0 - mean_grad), p1 * (d1 - mean_grad)
                grad = g_ref[local] + (l0 * router0 + l1 * router1)
                h2f = h2_ref[rr].astype(F32)
                centred = values - jnp.mean(values, -1, keepdims=True)
                inv = lax.rsqrt(jnp.mean(centred * centred, -1, keepdims=True) + norm_eps)
                unit = centred * inv
                scaled = grad * gain2
                back = inv * (
                    scaled
                    - jnp.mean(scaled, -1, keepdims=True)
                    - unit * jnp.mean(scaled * unit, -1, keepdims=True)
                )
                dy1 = dy + back
                low = dy1.astype(BF)
                dy1_ref[rr] = dy1
                da_ref[rr] = low
                sums = (
                    low.astype(F32), grad * unit, grad, h2f * l0, h2f * l1,
                )
                for row, term in enumerate(sums):
                    acc[row : row + 1] += jnp.sum(term, 0, keepdims=True)

            by_rows(128, 32, visit)

        token_rows(0)
        token_rows(1)
        for e in (0, 1):
            for m in (0, 1):
                acc[5 + e : 6 + e] += jnp.sum(d_ref[e, m].astype(F32), 0, keepdims=True)
        v_ref[...] = jnp.zeros_like(v_ref)
        for i in range(4):
            v_ref[i, 4:11, :] = acc[0:7, 256 * i : 256 * (i + 1)]
            v_ref[i, pl.ds(11 + me, 1), :] = gib_ref[:, 256 * i : 256 * (i + 1)]
        for t in (0, 1):
            for m in (0, 1):
                for i in range(3):
                    away(t, m, i).wait_send()
                    onward(t, m, i).wait_send()
                    to_home(t, m, i).wait_send()
                for i in range(4):
                    to_pair(t, m, i).wait_send()
                beside(t, m).wait_send()
        w_finish()
        z_finish()

    return pl.pallas_call(
        kernel,
        out_shape=(
            jax.ShapeDtypeStruct((1024, 1024), BF),
            jax.ShapeDtypeStruct((256, 1024), BF),
            jax.ShapeDtypeStruct((256, 1024), BF),
            jax.ShapeDtypeStruct((256, 1024), F32),
            jax.ShapeDtypeStruct((256, 1024), BF),
            jax.ShapeDtypeStruct((4, 24, 256), F32),
        ),
        in_specs=[vmem_spec()] * 3 + [any_spec()] + [vmem_spec()] * 6,
        out_specs=[vmem_spec()] * 6,
        scratch_shapes=[
            pltpu.VMEM((2, 2, 2, CAP, 1024), F32),
            pltpu.VMEM((1, 1024), F32),
            pltpu.VMEM((8, 1024), F32),
            pltpu.VMEM((1024, 1024), BF),
            pltpu.VMEM((4, 256, 1024), BF),
            pltpu.VMEM((128, 1024), F32),
            pltpu.VMEM((128, 1024), F32),
            pltpu.VMEM((2, 2, 8, CAP, 1024), BF),
            pltpu.VMEM((16 * CAP, 1024), BF),
            pltpu.VMEM((16 * CAP, 1024), F32),
            pltpu.VMEM((16 * CAP, 1024), BF),
            pltpu.VMEM((2, 2, 8, CAP, 1024), BF),
            pltpu.VMEM((2, 2, 4, CAP, 1024), BF),
            pltpu.VMEM((2, 2, 3, CAP, 1024), BF),
            pltpu.VMEM((2, 2, 3, CAP, 1024), BF),
        ]
        + [DMA((2, 2, 3))] * 4
        + [DMA((2, 2))] * 3
        + [DMA((2, 2, 4))] * 2
        + [DMA((2, 2, 3))] * 2
        + line_sems(4)
        + fold_scratch(256),
        name="moe",
        compiler_params=remote_params(2),
    )(h_slots, d_slots, win, w_back, params, y1, h2, stats, dispatch, dy)


def final_call(gi, gb, gq, gwo, vectors, gqv, x, dh1, dy1, params):
    def kernel(
        gi_ref, gb_ref, gq_ref, go_ref, base_ref, gqv_ref, x_ref, dh_ref, dy_ref, params_ref,
        oi_ref, ob_ref, oq_ref, oo_ref, ov_ref, ot_ref,
        v_ref, acc, qgot, qsum, vgot, vsum, vall,
        qs, qr, vs, vr, ps, pr, ws, wr, hs, hr, fs, fr, ol, *sems,
    ):
        me, core, sib, xn, yn, dg = plane_coords()
        z = lax.axis_index("fsdp")
        others = [(me + d) % 8 for d in range(1, 8)]
        meet(others, line_peers())
        owner = me // 2

        def vector_copy(d):
            peer = (z + d) % 4
            return send_to(v_ref.at[peer], vgot.at[d - 1], vs.at[d - 1], vr.at[d - 1], "fsdp", peer)

        def q_copy(d):
            peer = (z + d) % 4
            block = gq_ref.at[:, pl.ds(pl.multiple_of(peer * 256, 256), 256)]
            return send_to(block, qgot.at[d - 1], qs.at[d - 1], qr.at[d - 1], "fsdp", peer)

        rows_mine = oo_ref.at[pl.ds(pl.multiple_of(core * 128, 128), 128)]
        rows_sib = oo_ref.at[pl.ds(pl.multiple_of((1 - core) * 128, 128), 128)]

        def half(ref, part):
            return ref.at[pl.ds(64 * part, 64)]

        def o_near(i):
            return send_to(go_ref, rows_mine, ws.at[i], wr, "ctx", (xn, yn)[i])

        def o_half(part):
            block = half(rows_mine, part)
            return send_to(block, block, hs, hr.at[part], "ctx", (yn, xn)[part])

        def o_pair(src):
            return send_to(src, rows_mine, fs, fr, "ctx", sib)

        row, col = me // 4, (me // 2) % 2
        own_row, own_col = z // 2, z % 2
        beside_x = (row == own_row) & (col != own_col)
        beside_y = (row != own_row) & (col == own_col)
        across = (row != own_row) & (col != own_col)

        def o_root():
            @pl.when(z == owner)
            def _():
                for i in (0, 1):
                    o_near(i).start()
                o_pair(go_ref).start()
                pltpu.make_async_copy(go_ref, rows_mine, ol).start()

        def o_relay():
            @pl.when(beside_x)
            def _():
                o_near(0).wait_recv()
                o_half(0).start()
                o_pair(rows_mine).start()

            @pl.when(beside_y)
            def _():
                o_near(1).wait_recv()
                o_half(1).start()
                o_pair(rows_mine).start()

        def o_end():
            @pl.when(across)
            def _():
                o_half(0).wait_recv()
                o_half(1).wait_recv()
                o_pair(rows_mine).start()
                o_pair(rows_mine).wait_send()

            @pl.when(z == owner)
            def _():
                for i in (0, 1):
                    o_near(i).wait_send()
                o_pair(go_ref).wait_send()
                pltpu.make_async_copy(go_ref, rows_mine, ol).wait()

            @pl.when(beside_x)
            def _():
                o_half(0).wait_send()
                o_pair(rows_mine).wait_send()

            @pl.when(beside_y)
            def _():
                o_half(1).wait_send()
                o_pair(rows_mine).wait_send()

            send_to(go_ref, rows_sib, fs, fr, "ctx", sib).wait_recv()

        def own(k):
            if k < 4:
                return gi_ref.at[:, pl.ds(256 * k, 256)]
            return gb_ref.at[pl.ds(64 * (k - 4), 64)]

        def slot(device, k):
            which, part = device // 4, device % 4
            if k < 4:
                column = pl.multiple_of(k * 1024 + part * 256, 256)
                return oi_ref.at[which, :, pl.ds(column, 256)]
            row_at = pl.multiple_of(part * 256 + 64 * (k - 4), 64)
            return ob_ref.at[which, pl.ds(row_at, 64)]

        def qslot(device, k):
            return oq_ref.at[k, :, pl.ds(pl.multiple_of(device * 128, 128), 128)]

        begin, relay, diag, done, finish = ring_ops(own, slot, sems[:9])
        q_begin, q_relay, q_diag, q_done, q_finish = ring_ops(lambda k: qsum.at[k], qslot, sems[9:18])
        for d in (1, 3, 2):
            q_copy(d).start()
        for k in range(8):
            begin(k)
        o_root()
        gain = jnp.concatenate([params_ref[i, 0:1, :] for i in range(4)], axis=1).astype(F32)
        acc[...] = jnp.zeros_like(acc)

        def norm_rows(rr):
            values = x_ref[rr].astype(F32)
            grad = dh_ref[rr]
            centred = values - jnp.mean(values, -1, keepdims=True)
            inv = lax.rsqrt(jnp.mean(centred * centred, -1, keepdims=True) + norm_eps)
            unit = centred * inv
            scaled = grad * gain
            back = inv * (
                scaled
                - jnp.mean(scaled, -1, keepdims=True)
                - unit * jnp.mean(scaled * unit, -1, keepdims=True)
            )
            ot_ref[rr] = dy_ref[rr] + back
            acc[0:1] += jnp.sum(grad * unit, 0, keepdims=True)
            acc[1:2] += jnp.sum(grad, 0, keepdims=True)

        for k in range(4):

            def part(index):
                norm_rows(pl.ds(64 * k + index.start, 32))

            by_rows(64, 32, part)
            relay(k)
        v_ref[...] = base_ref[...]
        for i in range(4):
            v_ref[i, 0:2, :] = acc[0:2, 256 * i : 256 * (i + 1)]
        v_ref[owner, 2:4, pl.ds(pl.multiple_of(core * 128, 128), 128)] = gqv_ref[...]
        for d in (1, 2, 3):
            vector_copy(d).start()

        def plane_vector(i):
            return send_to(vsum, vall.at[i], ps.at[i], pr.at[i], "ctx", others[i])

        relay(4)
        for d in (1, 3, 2):
            q_copy(d).wait_recv()
        for j in range(3):

            def add(rr):
                place = pl.ds(pl.multiple_of(z * 256 + rr.start, 32), 32)
                total = gq_ref[j, place].astype(F32)
                for i in range(3):
                    total = total + qgot[i, j, rr].astype(F32)
                qsum[j, rr] = total.astype(BF)

            by_rows(256, 32, add)
        for k in range(3):
            q_begin(k)
        for d in (1, 2, 3):
            vector_copy(d).wait_recv()
        vsum[...] = v_ref[z] + vgot[0] + vgot[1] + vgot[2]
        for i in range(7):
            plane_vector(i).start()
        relay(5)
        diag(0)
        relay(6)
        diag(1)
        relay(7)
        diag(2)
        o_relay()
        diag(3)
        for k in range(3):
            q_relay(k)
        for k in range(4, 8):
            diag(k)
        for k in range(3):
            q_diag(k)
        o_end()
        for k in range(8):
            done(k)
        for k in range(3):
            q_done(k)
        total = vsum[...]
        for i in range(7):
            plane_vector(i).wait_recv()
            total = total + vall[i]
        ov_ref[...] = total
        for k in range(8):
            finish(k)
        for k in range(3):
            q_finish(k)
        for d in (1, 2, 3):
            vector_copy(d).wait_send()
            q_copy(d).wait_send()
        for i in range(7):
            plane_vector(i).wait_send()

    count = vectors.shape[1]
    return pl.pallas_call(
        kernel,
        out_shape=(
            jax.ShapeDtypeStruct((2, 256, 4096), BF),
            jax.ShapeDtypeStruct((2, 1024, 1024), BF),
            jax.ShapeDtypeStruct((3, 256, 1024), BF),
            jax.ShapeDtypeStruct((256, 1024), BF),
            jax.ShapeDtypeStruct((count, 256), F32),
            jax.ShapeDtypeStruct((256, 1024), F32),
        ),
        in_specs=[vmem_spec()] * 10,
        out_specs=[any_spec()] * 4 + [vmem_spec()] * 2,
        scratch_shapes=[
            pltpu.VMEM((4, count, 256), F32),
            pltpu.VMEM((8, 1024), F32),
            pltpu.VMEM((3, 3, 256, 128), BF),
            pltpu.VMEM((3, 256, 128), BF),
            pltpu.VMEM((3, count, 256), F32),
            pltpu.VMEM((count, 256), F32),
            pltpu.VMEM((7, count, 256), F32),
            DMA((3,)), DMA((3,)), DMA((3,)), DMA((3,)), DMA((7,)), DMA((7,)),
            DMA((2,)), DMA(()), DMA(()), DMA((2,)), DMA(()), DMA(()), DMA(()),
        ]
        + gather_sems(8)
        + gather_sems(3),
        name="final",
        compiler_params=remote_params(6),
    )(gi, gb, gq, gwo, vectors, gqv, x, dh1, dy1, params)


def head_masks(rows):
    lane = lax.broadcasted_iota(jnp.int32, (rows, 128), 1)
    return lane < 64, lane >= 64


def allowed_mask(i, doc_col, doc_row):
    length = 256 * (i + 1)
    qpos = lax.broadcasted_iota(jnp.int32, (256, length), 0) + 256 * i
    kpos = lax.broadcasted_iota(jnp.int32, (256, length), 1)
    return (kpos <= qpos) & (doc_col == doc_row)


def back_kernel(
    da_ref, h_ref, qkv_ref, of_ref, lse_ref, w_ref, wo_ref, doc_ref, gi_ref,
    out_ref, gq_ref, gwo_ref, gqv_ref, gis_ref,
    g_all, dqkv, part, dka, dva, probs, gwo, gwo_low, gwo_got, os, orr, *sems,
):
    me, core, sib, xn, yn, dg = plane_coords()
    meet((sib, xn, yn), line_peers())
    begin, relay, diag, done, finish = ring_ops(
        lambda k: da_ref.at[pl.ds(64 * k, 64)],
        lambda device, k: g_all.at[natural_slot(device, k)],
        sems[:9],
    )
    z_begin, z_step, z_finish = fold_ops(
        lambda where: gi_ref.at[pl.ds(pl.multiple_of(where * 256, 256), 256)],
        256,
        gis_ref,
        sems[9:13],
    )
    sums = [sum_ops(part, m, out_ref, sems[13:]) for m in (0, 1)]
    z = lax.axis_index("fsdp")
    owner = me // 2
    away = (owner - z + 4) % 4

    def to_owner():
        return send_to(gwo_low, gwo_got.at[away - 1], os, orr.at[away - 1], "fsdp", owner)

    masks = head_masks(256)
    zero = jnp.zeros((), BF)
    spans = [slice(128 * i * (i + 1), 128 * (i + 1) * (i + 2)) for i in range(4)]
    begin(0)
    begin(1)
    z_begin()

    def weigh(m, carry):
        place = pl.ds(pl.multiple_of(m * 1024, 1024), 1024)
        q, k = qkv_ref[0, place], qkv_ref[1, place]
        doc_row, doc_col = token_docs(doc_ref, m)
        for i in range(4):
            length = 256 * (i + 1)
            rows = slice(256 * i, 256 * (i + 1))
            qi = q[rows] * jnp.asarray(0.125, BF)
            allowed = allowed_mask(i, doc_col[rows], doc_row[:, :length])
            lse = lse_ref[pl.ds(pl.multiple_of(m * 1024 + 256 * i, 256), 256)]
            for j in (0, 1):
                s = mm(jnp.where(masks[j], qi, zero), k[:length], NT)
                probs[m, j, :, spans[i]] = jnp.exp(
                    jnp.where(allowed, s, mask_fill) - lse[:, 64 * j : 64 * j + 1]
                )

        @pl.when(m == 0)
        def _():
            relay(0)
            relay(1)
            begin(2)
            begin(3)

        return carry

    lax.fori_loop(0, 2, weigh, 0)
    z_step(0)
    diag(0)
    diag(1)
    done(0)
    done(1)
    kmasks = head_masks(1024)

    def micro(m, carry):
        @pl.when(m == 1)
        def _():
            done(2)
            done(3)

        place = pl.ds(pl.multiple_of(m * 1024, 1024), 1024)
        g = g_all[pl.ds(16 * m, 16)].reshape(1024, 1024)
        q, k, v = qkv_ref[0, place], qkv_ref[1, place], qkv_ref[2, place]
        do = mm(g, wo_ref[...], NT).astype(BF)
        term = mm(of_ref[place].astype(BF), g, TN)

        @pl.when(m == 0)
        def _():
            gwo[...] = term

        @pl.when(m == 1)
        def _():
            gwo_low[...] = (gwo[...] + term).astype(BF)

            @pl.when(z != owner)
            def _():
                to_owner().start()

        dka[...] = jnp.zeros_like(dka)
        dva[...] = jnp.zeros_like(dva)
        kh = [jnp.where(kmasks[j], k, zero) for j in (0, 1)]
        for i in range(4):
            length = 256 * (i + 1)
            rows = slice(256 * i, 256 * (i + 1))
            at = pl.ds(pl.multiple_of(m * 1024 + 256 * i, 256), 256)
            qi = q[rows] * jnp.asarray(0.125, BF)
            doi = do[rows]
            prod = doi.astype(F32) * of_ref[at]
            dq = None
            for j in (0, 1):
                qh = jnp.where(masks[j], qi, zero)
                doh = jnp.where(masks[j], doi, zero)
                delta = jnp.sum(jnp.where(masks[j], prod, 0.0), -1, keepdims=True)
                p = probs[m, j, :, spans[i]]
                dp = mm(doh, v[:length], NT)
                ds = (p * (dp - delta)).astype(BF)
                term = mm(ds, kh[j][:length])
                dq = term if dq is None else dq + term
                dka[:, :length] += mm(qh, ds, TN)
                dva[:, :length] += mm(doh, p.astype(BF), TN)
            dqkv[0, at] = (dq * 0.125).astype(BF)

            @pl.when(m == 0)
            def _():
                if i == 0:
                    relay(2)
                if i == 1:
                    relay(3)
                    z_step(1)
                if i == 3:
                    diag(2)
                    diag(3)
                    z_step(2)

            @pl.when(m == 1)
            def _():
                if i == 0:
                    z_step(3)
                if i == 1:
                    sums[0][3]()

        dqkv[1, place] = jnp.transpose(dka[...]).astype(BF)
        dqkv[2, place] = jnp.transpose(dva[...]).astype(BF)
        for i in range(4):
            at = pl.ds(pl.multiple_of(m * 1024 + 256 * i, 256), 256)
            a = mm(dqkv[0, at], w_ref[0], NT) + mm(dqkv[1, at], w_ref[1], NT)
            a = (a + mm(dqkv[2, at], w_ref[2], NT)).astype(BF)
            for b in range(4):
                block = 4 * i + b
                dest, side = (block, 0) if block < 8 else (15 - block, 1)
                part[m, dest, 64 * side : 64 * (side + 1)] = a[64 * b : 64 * (b + 1)]
        for n in (0, 1):

            @pl.when(m == n)
            def _():
                for step in sums[n][:3]:
                    step()

        return carry

    lax.fori_loop(0, 2, micro, 0)
    sums[1][3]()
    for j in range(3):
        gq_ref[j] = jnp.transpose(mm(dqkv[j], h_ref[...].reshape(2048, 1024), TN)).astype(BF)
    gqv_ref[0:1] = jnp.sum(dqkv[0].astype(F32), 0, keepdims=True)
    gqv_ref[1:2] = jnp.sum(dqkv[2].astype(F32), 0, keepdims=True)
    sums[0][4]()
    sums[1][4]()
    z_finish()

    @pl.when(z != owner)
    def _():
        to_owner().wait_send()

    @pl.when(z == owner)
    def _():
        for i in range(3):
            send_to(gwo_low, gwo_got.at[i], os, orr.at[i], "fsdp", (z + 1) % 4).wait_recv()

        def add(rr):
            total = gwo_low[rr].astype(F32)
            for i in range(3):
                total = total + gwo_got[i, rr].astype(F32)
            gwo_ref[rr] = total.astype(BF)

        by_rows(128, 32, add)

    @pl.when(z != owner)
    def _():
        gwo_ref[...] = jnp.zeros_like(gwo_ref)

    for k in range(4):
        finish(k)


def back_call(da, h, qkv, of, lse, wqkv, wout, docs, gi):
    return pl.pallas_call(
        back_kernel,
        out_shape=(
            jax.ShapeDtypeStruct((256, 1024), F32),
            jax.ShapeDtypeStruct((3, 1024, 128), BF),
            jax.ShapeDtypeStruct((128, 1024), BF),
            jax.ShapeDtypeStruct((2, 128), F32),
            jax.ShapeDtypeStruct((256, 1024), BF),
        ),
        in_specs=[vmem_spec()] * 9,
        out_specs=[vmem_spec()] * 5,
        scratch_shapes=[
            pltpu.VMEM((32, 64, 1024), BF),
            pltpu.VMEM((3, 2048, 128), BF),
            pltpu.VMEM((2, 8, 128, 1024), BF),
            pltpu.VMEM((128, 1024), F32),
            pltpu.VMEM((128, 1024), F32),
            pltpu.VMEM((2, 2, 256, 2560), F32),
            pltpu.VMEM((128, 1024), F32),
            pltpu.VMEM((128, 1024), BF),
            pltpu.VMEM((3, 128, 1024), BF),
            DMA(()),
            DMA((3,)),
        ]
        + gather_sems(4)
        + fold_scratch(256)
        + sum_scratch(),
        name="back",
        compiler_params=remote_params(4),
    )(da, h, qkv, of, lse, wqkv, wout, docs, gi)


GELU_A = math.sqrt(2.0 / math.pi)
GELU_B = 0.044715


def widen_call(arrays, kinds, sums):
    count = len(arrays)
    steps = 8
    flat = [array.reshape(-1, array.shape[-1]) for array in arrays]
    sizes = [f.shape[0] // steps for f in flat]
    small = [(256,), (256,), (2, 256), (256,), (256,), (256,), (2, 256), (2, 1024), (2, 256)]

    def kernel(*refs):
        step = pl.program_id(0)
        v_ref, wide, outs = refs[count], refs[count + 1 : 2 * count + 1], refs[2 * count + 1 :]
        for src, dst, size in zip(refs[:count], wide, sizes):
            dst[...] = src[pl.ds(pl.multiple_of(step * size, 16), size)].astype(dst.dtype)

        @pl.when(step == 0)
        def _():
            for index, row in ((0, 0), (1, 1), (3, 4), (4, 5), (5, 6)):
                outs[index][...] = v_ref[row]
            outs[2][...] = v_ref[2:4]
            outs[6][...] = v_ref[7:9]
            for e in (0, 1):
                for k in range(4):
                    outs[7][e : e + 1, 256 * k : 256 * (k + 1)] = v_ref[11 + 4 * e + k : 12 + 4 * e + k]
            outs[8][...] = v_ref[9:11]

    results = pl.pallas_call(
        kernel,
        grid=(steps,),
        out_shape=[jax.ShapeDtypeStruct(f.shape, kind) for f, kind in zip(flat, kinds)]
        + [jax.ShapeDtypeStruct(shape, F32) for shape in small],
        in_specs=[vmem_spec()] * (count + 1),
        out_specs=[pl.BlockSpec((n, f.shape[1]), lambda i: (i, 0)) for n, f in zip(sizes, flat)]
        + [vmem_spec()] * len(small),
        name="widen",
        compiler_params=pltpu.CompilerParams(vmem_limit_bytes=VMEM_CAP),
    )(*flat, sums)
    return [w.reshape(a.shape) for w, a in zip(results[:count], arrays)], results[count:]


def fast_body(
    tokens, doc_ids, routes, cotangent, ln1_gain, ln1_shift, w_qkv, qv_bias, w_out, out_bias,
    ln2_gain, ln2_shift, router, w_in, in_bias, w_back, back_bias,
):
    router_t = jnp.transpose(router)
    rows = {0: ln1_gain[None], 1: ln1_shift[None], 4: out_bias[None], 5: ln2_gain[None]}
    rows |= {6: ln2_shift[None]}
    row_iota = lax.broadcasted_iota(jnp.int32, (SMALL_ROWS, 256), 0)
    small = jnp.zeros((SMALL_ROWS, 256), BF)
    for index, row in rows.items():
        small = jnp.where(row_iota == index, row, small)
    x_low = tokens[:, 0].reshape(256, 1024)
    picks = routes[:, 0, :, 0]
    dy_low = cotangent[:, 0].reshape(256, 1024)
    hs, params, wqkv_c, wout_c, win_c, qkv, o_full, lse, y1, h2, stats, dispatch, h_slots, d_slots = (
        front_call(x_low, small, qv_bias, router_t, in_bias, back_bias, doc_ids, w_qkv, w_out, w_in, picks, dy_low)
    )
    gi, gb_sum, mixed, dy1, da, vectors = moe_call(
        h_slots, d_slots, win_c, w_back, params, y1, h2, stats, dispatch, dy_low
    )
    dh1, gq, gwo, gqv, gi_sum = back_call(
        da, hs, qkv, o_full, lse, wqkv_c, wout_c, doc_ids, gi
    )
    g_in, g_back, g_qkv, g_out, sums, token_grad = final_call(
        gi_sum, gb_sum, gq, gwo, vectors, gqv, x_low, dh1, dy1, params
    )
    (g_in, g_back, g_qkv, g_out, token_grad, mixed), small_grads = widen_call(
        [g_in, g_back, g_qkv, g_out, token_grad, mixed], [F32] * 5 + [BF], sums
    )
    g_one, s_one, g_qv, g_outb, g_two, s_two, g_router, g_inb, g_backb = small_grads
    return (
        mixed.reshape(2, 1, 128, 1024),
        token_grad.reshape(2, 1, 128, 1024),
        g_one, s_one, g_qkv, g_qv, g_out, g_outb, g_two, s_two,
        jnp.transpose(g_router), g_in, g_inb, g_back, g_backb,
    )


def solution(mesh):
    small_plane = mesh.shape["ctx"] == 8 and mesh.shape["fsdp"] == 4
    chosen_body = fast_body if small_plane else body
    placed = (
        P(None, "fsdp", "ctx", None),
        P(None, "fsdp", None),
        P(None, "fsdp", "ctx", None),
        P(None, "fsdp", "ctx", None),
        P("fsdp"),
        P("fsdp"),
        P(None, "fsdp", None),
        P(None, "fsdp"),
        P("fsdp", None),
        P("fsdp"),
        P("fsdp"),
        P("fsdp"),
        P("fsdp", None),
        P(None, "fsdp", None),
        P(None, "fsdp"),
        P(None, "fsdp", None),
        P(None, "fsdp"),
    )
    return jax.shard_map(
        chosen_body,
        mesh=mesh,
        in_specs=placed,
        out_specs=(
            P(None, "fsdp", "ctx", None),
            P(None, "fsdp", "ctx", None),
            P("fsdp"),
            P("fsdp"),
            P(None, "fsdp", None),
            P(None, "fsdp"),
            P("fsdp", None),
            P("fsdp"),
            P("fsdp"),
            P("fsdp"),
            P("fsdp", None),
            P(None, "fsdp", None),
            P(None, "fsdp"),
            P(None, "fsdp", None),
            P(None, "fsdp"),
        ),
        check_vma=False,
    )
```
